32 devices in a mesh: ctx: 8 (over z, x), fsdp: 4 (over y, core).
Axes of the slice: x: 2, y: 2, z: 4, core: 2. Of those that a mesh axis runs over, the one named last changes fastest.
Arguments:
- inputs: bfloat16 [2, 4, 4096, 512], P(None, 'fsdp', 'ctx'), may hold values from -6 to 6
- out_grad: bfloat16 [2, 4, 4096, 512], P(None, 'fsdp', 'ctx'), may hold values from -6 to 6
- segment_ids: int32 [2, 4, 4096], P(None, 'fsdp', 'ctx'), may hold values from 0 to 15, never falling along the last dimension, each value on 1 to 2048 neighbouring positions
- block_order: int32 [16], replicated, may hold values from 0 to 15, each once
- w_qkv: bfloat16 [512, 1536], P('fsdp'), may hold values from -0.25 to 0.25
- w_out: bfloat16 [512, 512], P('fsdp'), may hold values from -1 to 1
- w_up: bfloat16 [512, 2048], P('fsdp'), may hold values from -0.25 to 0.25
- w_down: bfloat16 [2048, 512], P('fsdp'), may hold values from -0.125 to 0.125
- norm1_gain: bfloat16 [512], P('fsdp'), may hold values from 0.25 to 1.75
- norm1_bias: bfloat16 [512], P('fsdp'), may hold values from -2 to 2
- norm2_gain: bfloat16 [512], P('fsdp'), may hold values from 0.25 to 1.75
- norm2_bias: bfloat16 [512], P('fsdp'), may hold values from -2 to 2
- out_bias: bfloat16 [512], P('fsdp'), may hold values from -2 to 2
- up_bias: bfloat16 [2048], P('fsdp'), may hold values from -3 to 3
- down_bias: bfloat16 [512], P('fsdp'), may hold values from -2 to 2
Outputs:
- outputs: bfloat16 [2, 4, 4096, 512], P(None, 'fsdp', 'ctx')
- input_grad: float32 [2, 4, 4096, 512], P(None, 'fsdp', 'ctx')
- grad_w_qkv: float32 [512, 1536], P('fsdp')
- grad_w_out: float32 [512, 512], P('fsdp')
- grad_w_up: float32 [512, 2048], P('fsdp')
- grad_w_down: float32 [2048, 512], P('fsdp')
- grad_norm1_gain: float32 [512], P('fsdp')
- grad_norm1_bias: float32 [512], P('fsdp')
- grad_norm2_gain: float32 [512], P('fsdp')
- grad_norm2_bias: float32 [512], P('fsdp')
- grad_out_bias: float32 [512], P('fsdp')
- grad_up_bias: float32 [2048], P('fsdp')
- grad_down_bias: float32 [512], P('fsdp')
The draws below stay inside these ranges and needn't reach their ends.
Inputs may be any that keep to these rules, and one draw needn't show every extreme that they name: `segment_ids`: along each sequence's true positions document numbers start at 0 and never fall; each document has 1 to 2048 tokens and one has exactly 2048. `block_order`: each value appears exactly once.
All inputs are finite; a program needn't handle non-finite values.
Results may differ from the reference program's by a relative error of at most 0.02.
Values may be sent and summed in bfloat16 or wider, within the bound.
A program may use at most 256 MiB of HBM per device.

```python
import math
import jax
import jax.numpy as jnp
import numpy as np
from jax import lax

D = 512
H = 8
HD = 64
FF = 2048
BLK = 256
MB = 2
LEN = 4096
SEQS = 4
DOCS = 16
MOST = 2048
N_CTX = 8


def steps_of(own_key, extent, cuts, low, top_value):
    level = 1.0
    for position, shards_of in cuts:
        draws = jax.random.uniform(jax.random.fold_in(jax.random.fold_in(own_key, 6), position), (shards_of,), jnp.float32, low / len(cuts), top_value / len(cuts))
        level = level * jnp.repeat(jnp.exp(draws), extent[position] // shards_of).reshape((-1,) + (1,) * (len(extent) - 1 - position))
    return level


def profile(count, total, bound, lean):
    weights = [(1 << 20) // math.isqrt(standing ** lean) + 1 for standing in range(2, count + 1)]
    surplus, holding = total - bound - (count - 1), [1] * (count - 1)
    while surplus > 0:
        candidates = [i for i in range(count - 1) if holding[i] < bound]
        mass, budget = sum([weights[i] for i in candidates]), surplus
        for i in candidates:
            addition = min(bound - holding[i], max(1, budget * weights[i] // mass), surplus)
            holding[i] = holding[i] + addition
            surplus = surplus - addition
    return np.array([bound] + holding)


def uneven_parts(rng, number_of, total, limit, skew):
    if number_of == 2:
        one = jax.random.randint(rng, (), max(1, total - limit), min(limit, total - 1) + 1)
        return jnp.stack([one, total - one])
    lengths = jnp.asarray(profile(number_of, total, limit, skew), jnp.int32)
    couples = (number_of - 1) // 2
    donor, taker = lengths[1:1 + 2 * couples:2], lengths[2:2 + 2 * couples:2]
    slack = jnp.minimum(donor - 1, limit - taker)
    shifted = jax.random.randint(jax.random.fold_in(rng, 1), (couples,), 0, 1 << 20) % (slack + 1)
    lengths = lengths.at[1:1 + 2 * couples:2].set(donor - shifted).at[2:2 + 2 * couples:2].set(taker + shifted)
    return lengths[jax.random.permutation(jax.random.fold_in(rng, 2), number_of)]


def bell_draw(rng, dims, scale, reach, cuts=(), held_as=jnp.bfloat16):
    array = scale * jax.random.normal(rng, dims, jnp.float32)
    if cuts:
        array = array * steps_of(rng, dims, cuts, -0.22, 0.18)
    return jnp.clip(array, -reach, reach).astype(held_as)


def setup_inputs(seed: int = 0) -> dict:
    streams_of = jax.random.split(jax.random.key(seed), 16)
    inputs = bell_draw(streams_of[0], (MB, SEQS, LEN, D), 1.0, 6.0, ((1, 4), (2, 8)))
    out_grad = bell_draw(streams_of[1], (MB, SEQS, LEN, D), 1.0, 6.0, ((1, 4), (2, 8)))
    segment_ids = jax.vmap(lambda own: jnp.searchsorted(jnp.cumsum(uneven_parts(own, DOCS, LEN, MOST, 2)), jnp.arange(LEN), side="right"))(jax.random.split(streams_of[2], MB * SEQS)).reshape((MB, SEQS, LEN)).astype(jnp.int32)
    block_order = jax.random.permutation(streams_of[3], 2 * N_CTX).astype(jnp.int32)
    w_qkv = bell_draw(streams_of[4], (D, 3 * D), D ** -0.5, 0.25, ((0, 4),))
    w_out = bell_draw(streams_of[5], (D, D), (D // 16) ** -0.5, 1.0, ((0, 4),))
    w_up = bell_draw(streams_of[6], (D, FF), D ** -0.5, 0.25, ((0, 4),))
    w_down = bell_draw(streams_of[7], (FF, D), FF ** -0.5, 0.125, ((0, 4),))
    norm1_gain = jnp.clip(1.0 + 0.15 * jax.random.normal(streams_of[8], (D,), jnp.float32), 0.25, 1.75).astype(jnp.bfloat16)
    norm1_bias = bell_draw(streams_of[9], (D,), 0.3, 2.0, ((0, 4),))
    norm2_gain = jnp.clip(1.0 + 0.15 * jax.random.normal(streams_of[10], (D,), jnp.float32), 0.25, 1.75).astype(jnp.bfloat16)
    norm2_bias = bell_draw(streams_of[11], (D,), 0.3, 2.0, ((0, 4),))
    out_bias = bell_draw(streams_of[12], (D,), 0.3, 2.0, ((0, 4),))
    up_bias = bell_draw(streams_of[13], (FF,), 0.5, 3.0, ((0, 4),))
    down_bias = bell_draw(streams_of[14], (D,), 0.3, 2.0, ((0, 4),))
    return dict(inputs=inputs, out_grad=out_grad, segment_ids=segment_ids, block_order=block_order, w_qkv=w_qkv, w_out=w_out, w_up=w_up, w_down=w_down, norm1_gain=norm1_gain, norm1_bias=norm1_bias, norm2_gain=norm2_gain, norm2_bias=norm2_bias, out_bias=out_bias, up_bias=up_bias, down_bias=down_bias)


norm_eps = 1e-05
mask_fill = -1e+30
HIGH = lax.Precision.HIGHEST

@jax.custom_vjp
def low(v):
    return lax.optimization_barrier(v.astype(jnp.bfloat16)).astype(jnp.float32)

@jax.custom_vjp
def low_back(v):
    return v

def low_keep(v):
    return (low(v), None)

def low_pass(kept, grad):
    return (grad,)

def back_keep(v):
    return (v, None)

def back_low(kept, grad):
    return (low(grad),)
low.defvjp(low_keep, low_pass)
low_back.defvjp(back_keep, back_low)

def layer_norm(values, gain_vec, offset):
    center = values - lax.optimization_barrier(jnp.mean(values, axis=-1, keepdims=True))
    spread = lax.optimization_barrier(jnp.mean(center * center, axis=-1, keepdims=True))
    return center * lax.rsqrt(spread + norm_eps) * gain_vec + offset

def gelu_exact(values):
    return 0.5 * values * (1.0 + lax.erf(values * (1.0 / math.sqrt(2.0))))

def add_up(first, second):
    return first + second

def sequence_forward(seq_in, params, doc_rows, true_pos):
    w_qkv, w_out, w_up, w_down, gain_one, bias_one, gain_two, bias_two, out_bias, up_bias, down_bias = params
    seq_len = seq_in.shape[0]
    model_width = seq_in.shape[1]
    normed = layer_norm(seq_in, gain_one, bias_one)
    qkv_out = low(low_back(jnp.dot(low(normed), w_qkv, precision=HIGH)))
    query_heads = qkv_out[:, :model_width].reshape(seq_len, H, HD)
    key_heads = qkv_out[:, model_width:2 * model_width].reshape(seq_len, H, HD)
    value_heads = qkv_out[:, 2 * model_width:].reshape(seq_len, H, HD)
    query_block = min(512, seq_len)
    block_count = seq_len // query_block

    def one_block(block_item):
        block_q, block_doc, block_pos = block_item
        scores = low_back(jnp.einsum('qhd,khd->hqk', block_q, key_heads, precision=HIGH) * (1.0 / math.sqrt(HD)))
        allowed = (block_doc[:, None] == doc_rows[None, :]) & (true_pos[None, :] <= block_pos[:, None])
        masked = jnp.where(allowed[None], scores, mask_fill)
        row_top = lax.optimization_barrier(jnp.max(masked, axis=-1, keepdims=True))
        expo = jnp.exp(masked - row_top)
        soft = low(expo / lax.optimization_barrier(jnp.sum(expo, axis=-1, keepdims=True)))
        return jnp.einsum('hqk,khd->qhd', soft, value_heads, precision=HIGH)
    mixed = lax.map(jax.checkpoint(one_block), (query_heads.reshape(block_count, query_block, H, HD), doc_rows.reshape(block_count, query_block), true_pos.reshape(block_count, query_block)))
    attn_low = low(low_back(mixed.reshape(seq_len, model_width)))
    branch = low_back(jnp.dot(attn_low, w_out, precision=HIGH) + out_bias)
    middle = seq_in + branch
    normed_two = layer_norm(middle, gain_two, bias_two)
    hidden = low_back(jnp.dot(low(normed_two), w_up, precision=HIGH) + up_bias)
    active = gelu_exact(hidden)
    ffn_out = low_back(jnp.dot(low(active), w_down, precision=HIGH) + down_bias)
    return middle + ffn_out

def reference(inputs, out_grad, segment_ids, block_order, w_qkv, w_out, w_up, w_down, norm1_gain, norm1_bias, norm2_gain, norm2_bias, out_bias, up_bias, down_bias):
    params = tuple((member.astype(jnp.float32) for member in (w_qkv, w_out, w_up, w_down, norm1_gain, norm1_bias, norm2_gain, norm2_bias, out_bias, up_bias, down_bias)))
    row_ids = jnp.arange(LEN, dtype=jnp.int32)
    true_pos = (block_order[row_ids // BLK] * BLK + row_ids % BLK).astype(jnp.int32)
    seq_count = MB * SEQS
    flat_in = inputs.reshape(seq_count, LEN, D).astype(jnp.float32)
    flat_grad = out_grad.reshape(seq_count, LEN, D).astype(jnp.float32)
    flat_docs = segment_ids.reshape(seq_count, LEN)

    def per_sequence(totals, seq_item):
        seq_in, seq_grad, seq_docs = seq_item
        doc_rows = seq_docs[true_pos]

        def forward(values, weights):
            return sequence_forward(values, weights, doc_rows, true_pos)
        result, pullback = jax.vjp(forward, seq_in, params)
        grad_in, grad_params = pullback(seq_grad)
        return (jax.tree.map(add_up, totals, grad_params), (result.astype(jnp.bfloat16), grad_in))
    start = tuple((jnp.zeros(member.shape, jnp.float32) for member in params))
    totals, (outputs, input_grad) = lax.scan(per_sequence, start, (flat_in, flat_grad, flat_docs))
    return (outputs.reshape(MB, SEQS, LEN, D), input_grad.reshape(MB, SEQS, LEN, D), totals[0], totals[1], totals[2], totals[3], totals[4], totals[5], totals[6], totals[7], totals[8], totals[9], totals[10])
```

```python
import functools
import math

import jax
import jax.numpy as jnp
from jax import lax
from jax.experimental import pallas as pl
from jax.experimental.pallas import tpu as pltpu
from jax.sharding import Mesh
from jax.sharding import PartitionSpec as P

H = 8
HD = 64
BLK = 256
PAIR = 2 * HD

norm_eps = 1e-05
mask_fill = -1e30
LOG2E = math.log2(math.e)
LN2 = math.log(2.0)
SCORE_SCALE = 1.0 / math.sqrt(HD)

f32 = jnp.float32
bf16 = jnp.bfloat16


def contract(a, b, da, db):
    return lax.dot_general(a, b, (((da,), (db,)), ((), ())), preferred_element_type=f32)


def norm_parts(values):
    center = values - jnp.mean(values, axis=-1, keepdims=True)
    spread = jnp.mean(center * center, axis=-1, keepdims=True)
    inv = lax.rsqrt(spread + norm_eps)
    return center * inv, inv


def whole(shape):
    zeros = (0,) * len(shape)
    return pl.BlockSpec(shape, lambda *_: zeros)


def project_kernel(true_ref, x_ref, gain_ref, bias_ref, w_ref, q_ref, k_ref, kt_ref, v_ref, vt_ref, h_ref):
    unit, _ = norm_parts(x_ref[...].astype(f32))
    low = (unit * gain_ref[...] + bias_ref[...]).astype(bf16)
    h_ref[...] = low
    qkv = jnp.dot(low, w_ref[...], preferred_element_type=f32)
    q_ref[...] = (qkv[:, :PAIR] * (SCORE_SCALE * LOG2E)).astype(bf16)
    k = qkv[:, PAIR : 2 * PAIR].astype(bf16)
    v = qkv[:, 2 * PAIR :].astype(bf16)
    k_ref[...] = k
    v_ref[...] = v
    kt_ref[...] = k.T
    vt_ref[...] = v.T


def project(true_of, rows, gain, bias, weight):
    count, width = rows.shape
    blocks = count // BLK
    by_true = pl.BlockSpec((BLK, PAIR), lambda t, tab: (tab[t], 0))
    by_true_t = pl.BlockSpec((PAIR, BLK), lambda t, tab: (0, tab[t]))
    return pl.pallas_call(
        project_kernel,
        grid_spec=pltpu.PrefetchScalarGridSpec(
            num_scalar_prefetch=1,
            grid=(blocks,),
            in_specs=[
                pl.BlockSpec((BLK, width), lambda t, tab: (t, 0)),
                whole(gain.shape),
                whole(bias.shape),
                whole(weight.shape),
            ],
            out_specs=[
                by_true,
                by_true,
                by_true_t,
                by_true,
                by_true_t,
                pl.BlockSpec((BLK, width), lambda t, tab: (tab[t], 0)),
            ],
        ),
        out_shape=[
            jax.ShapeDtypeStruct((count, PAIR), bf16),
            jax.ShapeDtypeStruct((count, PAIR), bf16),
            jax.ShapeDtypeStruct((PAIR, count), bf16),
            jax.ShapeDtypeStruct((count, PAIR), bf16),
            jax.ShapeDtypeStruct((PAIR, count), bf16),
            jax.ShapeDtypeStruct((count, width), bf16),
        ],
        name="project",
    )(true_of, rows, gain, bias, weight)


def split_heads(block):
    lane = lax.broadcasted_iota(jnp.int32, block.shape, 1)
    zero = jnp.zeros_like(block)
    first = lane < HD
    return jnp.concatenate([jnp.where(first, block, zero), jnp.where(first, zero, block)], axis=0)


def attend_kernel(slot_ref, low_ref, q_ref, start_ref, k_ref, vt_ref, o_ref, ot_ref, lse_ref, acc, top):
    qb = pl.program_id(0)
    both = split_heads(q_ref[...])
    start = jnp.concatenate([start_ref[0], start_ref[0]], axis=1)
    row = lax.broadcasted_iota(jnp.int32, (BLK, 2 * BLK), 0)
    col = lax.broadcasted_iota(jnp.int32, (BLK, 2 * BLK), 1)
    ones = jnp.ones((16, BLK), bf16)

    def scores(kb):
        base = pl.multiple_of(kb * BLK, BLK)
        return contract(k_ref[pl.ds(base, BLK), :], both, 1, 1)

    def values(kb):
        base = pl.multiple_of(kb * BLK, BLK)
        return jnp.concatenate([vt_ref[:, pl.ds(base, BLK)], ones], axis=0)

    st = scores(qb)
    allowed = (row >= start - qb * BLK) & (row <= jnp.bitwise_and(col, BLK - 1))
    st = jnp.where(allowed, st, mask_fill)
    peak = jnp.max(st, axis=0, keepdims=True)
    probs = jnp.exp2(st - peak).astype(bf16)
    top[...] = peak
    acc[...] = jnp.dot(values(qb), probs, preferred_element_type=f32)

    def visit(kb, carry):
        st = jnp.where(row >= start - kb * BLK, scores(kb), mask_fill)
        old = top[...]
        peak = jnp.maximum(old, jnp.max(st, axis=0, keepdims=True))
        probs = jnp.exp2(st - peak).astype(bf16)
        top[...] = peak
        acc[...] = acc[...] * jnp.exp2(old - peak) + jnp.dot(values(kb), probs, preferred_element_type=f32)
        return carry

    lax.fori_loop(low_ref[qb], qb, visit, 0)
    total = acc[PAIR : PAIR + 1, :]
    lse_ref[0] = top[...] + jnp.log2(total)
    out = acc[:PAIR, :] / total
    heads = jnp.concatenate([out[:HD, :BLK], out[HD:, BLK:]], axis=0)
    ot_ref[0] = heads
    o_ref[...] = heads.T.astype(bf16)


def attend(slot_of, low_of, q, start, k, vt):
    count = q.shape[0]
    blocks = count // BLK
    return pl.pallas_call(
        attend_kernel,
        grid_spec=pltpu.PrefetchScalarGridSpec(
            num_scalar_prefetch=2,
            grid=(blocks,),
            in_specs=[
                pl.BlockSpec((BLK, PAIR), lambda b, s, l: (b, 0)),
                pl.BlockSpec((1, 1, BLK), lambda b, s, l: (b, 0, 0)),
                whole(k.shape),
                whole(vt.shape),
            ],
            out_specs=[
                pl.BlockSpec((BLK, PAIR), lambda b, s, l: (s[b], 0)),
                pl.BlockSpec((1, PAIR, BLK), lambda b, s, l: (b, 0, 0)),
                pl.BlockSpec((1, 1, 2 * BLK), lambda b, s, l: (b, 0, 0)),
            ],
            scratch_shapes=[
                pltpu.VMEM((PAIR + 16, 2 * BLK), f32),
                pltpu.VMEM((1, 2 * BLK), f32),
            ],
        ),
        out_shape=[
            jax.ShapeDtypeStruct((count, PAIR), bf16),
            jax.ShapeDtypeStruct((blocks, PAIR, BLK), f32),
            jax.ShapeDtypeStruct((blocks, 1, 2 * BLK), f32),
        ],
        name="attend",
    )(slot_of, low_of, q, start, k, vt)


def attend_back_kernel(
    slot_ref, high_ref, k_ref, kt_ref, v_ref, h_ref, w_ref, q_ref, start_ref, do_ref, ot_ref, lse_ref,
    dh_ref, gw_ref, dqt, dk, dv, delta,
):
    kb = pl.program_id(0)
    blocks = pl.num_programs(0)
    row = lax.broadcasted_iota(jnp.int32, (BLK, 2 * BLK), 0)
    col = lax.broadcasted_iota(jnp.int32, (BLK, 2 * BLK), 1)

    def d_out(qb):
        return do_ref[pl.ds(pl.multiple_of(slot_ref[qb] * BLK, BLK), BLK), :]

    @pl.when(kb == 0)
    def _():
        gw_ref[...] = jnp.zeros_like(gw_ref)

        def prepare(qb, carry):
            dqt[qb] = jnp.zeros((PAIR, BLK), f32)
            both = d_out(qb).astype(f32).T * ot_ref[qb]
            delta[qb] = jnp.concatenate(
                [
                    jnp.sum(both[:HD], axis=0, keepdims=True),
                    jnp.sum(both[HD:], axis=0, keepdims=True),
                ],
                axis=1,
            )
            return carry

        lax.fori_loop(0, blocks, prepare, 0)

    k = k_ref[...]
    v = v_ref[...]
    kt = kt_ref[...]

    def tile(qb, diagonal):
        both_q = split_heads(q_ref[pl.ds(pl.multiple_of(qb * BLK, BLK), BLK), :])
        both_do = split_heads(d_out(qb))
        start = jnp.concatenate([start_ref[qb], start_ref[qb]], axis=1)
        st = contract(k, both_q, 1, 1)
        dpt = contract(v, both_do, 1, 1)
        allowed = row >= start - kb * BLK
        if diagonal:
            allowed = allowed & (row <= jnp.bitwise_and(col, BLK - 1))
        pt = jnp.exp2(jnp.where(allowed, st - lse_ref[qb], mask_fill))
        dst = (pt * (dpt - delta[qb])).astype(bf16)
        part_v = jnp.dot(pt.astype(bf16), both_do, preferred_element_type=f32)
        part_k = jnp.dot(dst, both_q, preferred_element_type=f32)
        if diagonal:
            dv[...] = part_v
            dk[...] = part_k
        else:
            dv[...] += part_v
            dk[...] += part_k
        dqt[qb] += jnp.concatenate(
            [
                jnp.dot(kt[:HD], dst[:, :BLK], preferred_element_type=f32),
                jnp.dot(kt[HD:], dst[:, BLK:], preferred_element_type=f32),
            ],
            axis=0,
        )

    tile(kb, True)

    def visit(qb, carry):
        tile(qb, False)
        return carry

    lax.fori_loop(kb + 1, high_ref[kb] + 1, visit, 0)
    dq = (dqt[kb] * SCORE_SCALE).T.astype(bf16)
    joined = jnp.concatenate([dq, (dk[...] * LN2).astype(bf16), dv[...].astype(bf16)], axis=1)
    dh_ref[...] = contract(joined, w_ref[...], 1, 1).astype(bf16)
    gw_ref[...] += contract(h_ref[...], joined, 0, 0)


def attend_back(slot_of, high_of, k, kt, v, h, weight, q, start, d_out, ot, lse):
    count = q.shape[0]
    width = h.shape[1]
    blocks = count // BLK
    return pl.pallas_call(
        attend_back_kernel,
        grid_spec=pltpu.PrefetchScalarGridSpec(
            num_scalar_prefetch=2,
            grid=(blocks,),
            in_specs=[
                pl.BlockSpec((BLK, PAIR), lambda b, s, l: (b, 0)),
                pl.BlockSpec((PAIR, BLK), lambda b, s, l: (0, b)),
                pl.BlockSpec((BLK, PAIR), lambda b, s, l: (b, 0)),
                pl.BlockSpec((BLK, width), lambda b, s, l: (b, 0)),
                whole(weight.shape),
                whole(q.shape),
                whole(start.shape),
                whole(d_out.shape),
                whole(ot.shape),
                whole(lse.shape),
            ],
            out_specs=[
                pl.BlockSpec((BLK, width), lambda b, s, l: (s[b], 0)),
                whole(weight.shape),
            ],
            scratch_shapes=[
                pltpu.VMEM((blocks, PAIR, BLK), f32),
                pltpu.VMEM((BLK, PAIR), f32),
                pltpu.VMEM((BLK, PAIR), f32),
                pltpu.VMEM((blocks, 1, 2 * BLK), f32),
            ],
        ),
        out_shape=[
            jax.ShapeDtypeStruct((count, width), bf16),
            jax.ShapeDtypeStruct(weight.shape, f32),
        ],
        name="attend_back",
    )(slot_of, high_of, k, kt, v, h, weight, q, start, d_out, ot, lse)


FF_TILE = 512


def feed_kernel(
    pair_ref, attn_ref, x_ref, dy_ref, wo_ref, wu_ref, wd_ref, vec_ref, ub_ref,
    y_ref, do_ref, dmid_ref, gd_ref, gu_ref, go_ref, gvec_ref, gub_ref, attn_all,
):
    step = pl.program_id(0)
    groups = attn_ref.shape[0]

    @pl.when(step == 0)
    def _():
        for ref in (gd_ref, gu_ref, go_ref, gvec_ref, gub_ref):
            ref[...] = jnp.zeros_like(ref)

    for g in range(groups):
        attn_all[:, pl.ds(pl.multiple_of(pair_ref[g] * PAIR, PAIR), PAIR)] = attn_ref[g]
    attn = attn_all[...]
    out_bias, gain, bias, down_bias = (vec_ref[i : i + 1, :] for i in range(4))
    middle = (
        x_ref[...].astype(f32) + jnp.dot(attn, wo_ref[...], preferred_element_type=f32) + out_bias
    )
    unit, inv = norm_parts(middle)
    low = (unit * gain + bias).astype(bf16)
    dy = dy_ref[...]
    dy32 = dy.astype(f32)
    total = middle + down_bias
    d_low = jnp.zeros_like(middle)
    width = wu_ref.shape[1]
    for j in range(0, width, FF_TILE):
        part = pl.ds(j, FF_TILE)
        up = wu_ref[:, part]
        down = wd_ref[part, :]
        hidden = jnp.dot(low, up, preferred_element_type=f32) + ub_ref[:, part]
        cdf = 0.5 * (1.0 + lax.erf(hidden * (1.0 / math.sqrt(2.0))))
        active = (hidden * cdf).astype(bf16)
        slope = cdf + hidden * (jnp.exp2(hidden * hidden * (-0.5 * LOG2E)) * (1.0 / math.sqrt(2.0 * math.pi)))
        total = total + jnp.dot(active, down, preferred_element_type=f32)
        d_hidden = contract(dy, down, 1, 1) * slope
        d_hidden_low = d_hidden.astype(bf16)
        gub_ref[:, part] += jnp.sum(d_hidden, axis=0, keepdims=True)
        d_low = d_low + contract(d_hidden_low, up, 1, 1)
        gd_ref[part, :] += contract(active, dy, 0, 0)
        gu_ref[:, part] += contract(low, d_hidden_low, 0, 0)
    y_ref[...] = total.astype(bf16)
    scaled = d_low * gain
    d_middle = dy32 + inv * (
        scaled
        - jnp.mean(scaled, axis=-1, keepdims=True)
        - unit * jnp.mean(scaled * unit, axis=-1, keepdims=True)
    )
    dmid_ref[...] = d_middle
    branch = d_middle.astype(bf16)
    go_ref[...] += contract(attn, branch, 0, 0)
    gvec_ref[0:1, :] += jnp.sum(d_middle, axis=0, keepdims=True)
    gvec_ref[1:2, :] += jnp.sum(d_low * unit, axis=0, keepdims=True)
    gvec_ref[2:3, :] += jnp.sum(d_low, axis=0, keepdims=True)
    gvec_ref[3:4, :] += jnp.sum(dy32, axis=0, keepdims=True)
    attn_all[...] = contract(branch, wo_ref[...], 1, 1).astype(bf16)
    for g in range(groups):
        do_ref[g] = attn_all[:, pl.ds(pl.multiple_of(pair_ref[g] * PAIR, PAIR), PAIR)]


def feed(pair_of, attn, x, dy, w_out, w_up, w_down, vecs, up_bias, tile=BLK):
    groups, count, _ = attn.shape
    width = x.shape[1]
    rows = pl.BlockSpec((tile, width), lambda i, p: (i, 0))
    heads = pl.BlockSpec((groups, tile, PAIR), lambda i, p: (0, i, 0))
    return pl.pallas_call(
        feed_kernel,
        grid_spec=pltpu.PrefetchScalarGridSpec(
            num_scalar_prefetch=1,
            grid=(count // tile,),
            in_specs=[
                heads, rows, rows, whole(w_out.shape), whole(w_up.shape), whole(w_down.shape),
                whole(vecs.shape), whole(up_bias.shape),
            ],
            out_specs=[
                rows, heads, rows, whole(w_down.shape), whole(w_up.shape), whole(w_out.shape),
                whole(vecs.shape), whole(up_bias.shape),
            ],
            scratch_shapes=[pltpu.VMEM((tile, width), bf16)],
        ),
        out_shape=[
            jax.ShapeDtypeStruct((count, width), bf16),
            jax.ShapeDtypeStruct((groups, count, PAIR), bf16),
            jax.ShapeDtypeStruct((count, width), f32),
            jax.ShapeDtypeStruct(w_down.shape, f32),
            jax.ShapeDtypeStruct(w_up.shape, f32),
            jax.ShapeDtypeStruct(w_out.shape, f32),
            jax.ShapeDtypeStruct(vecs.shape, f32),
            jax.ShapeDtypeStruct(up_bias.shape, f32),
        ],
        compiler_params=pltpu.CompilerParams(vmem_limit_bytes=60 * 1024 * 1024),
        name="feed",
    )(pair_of, attn, x, dy, w_out, w_up, w_down, vecs, up_bias)


def norm_back_kernel(dh_a_ref, dh_b_ref, x_ref, dmid_ref, gain_ref, dx_ref, gvec_ref):
    @pl.when(pl.program_id(0) == 0)
    def _():
        gvec_ref[...] = jnp.zeros_like(gvec_ref)

    d_low = dh_a_ref[...].astype(f32) + dh_b_ref[...].astype(f32)
    unit, inv = norm_parts(x_ref[...].astype(f32))
    scaled = d_low * gain_ref[...]
    dx = dmid_ref[...] + inv * (
        scaled
        - jnp.mean(scaled, axis=-1, keepdims=True)
        - unit * jnp.mean(scaled * unit, axis=-1, keepdims=True)
    )
    dx_ref[...] = dx.astype(bf16)
    gvec_ref[0:1, :] += jnp.sum(d_low * unit, axis=0, keepdims=True)
    gvec_ref[1:2, :] += jnp.sum(d_low, axis=0, keepdims=True)


def norm_back(dh_a, dh_b, x, dmid, gain):
    count, width = x.shape
    rows = pl.BlockSpec((BLK, width), lambda i: (i, 0))
    return pl.pallas_call(
        norm_back_kernel,
        grid=(count // BLK,),
        in_specs=[rows, rows, rows, rows, whole(gain.shape)],
        out_specs=[rows, whole((8, width))],
        out_shape=[
            jax.ShapeDtypeStruct((count, width), bf16),
            jax.ShapeDtypeStruct((8, width), f32),
        ],
        name="norm_back",
    )(dh_a, dh_b, x, dmid, gain)


def layer_norm(values, gain_vec, offset):
    center = values - jnp.mean(values, axis=-1, keepdims=True)
    spread = jnp.mean(center * center, axis=-1, keepdims=True)
    return center * lax.rsqrt(spread + norm_eps) * gain_vec + offset


def gelu_exact(values):
    return 0.5 * values * (1.0 + lax.erf(values * (1.0 / math.sqrt(2.0))))


def score_block(query_heads, key_heads, query_doc, query_pos, key_doc, key_pos):
    raw_scores = jnp.einsum(
        "qhd,khd->hqk", query_heads, key_heads, preferred_element_type=jnp.float32
    ) * (1.0 / math.sqrt(HD))
    allowed = (query_doc[:, None] == key_doc[None, :]) & (key_pos[None, :] <= query_pos[:, None])
    return (raw_scores, allowed[None])


def soft_block(raw_scores, allowed, log_norm):
    return jnp.exp(jnp.where(allowed, raw_scores, mask_fill) - log_norm[:, :, None])


def row_log_norm(query_heads, key_blocks, doc_blocks, pos_blocks, query_doc, query_pos):

    def row_visit(running, block_item):
        row_top, row_sum = running
        key_heads, key_doc, key_pos = block_item
        raw_scores, allowed = score_block(
            query_heads, key_heads, query_doc, query_pos, key_doc, key_pos
        )
        masked = jnp.where(allowed, raw_scores, mask_fill)
        new_top = jnp.maximum(row_top, jnp.max(masked, axis=-1))
        fresh = jnp.sum(jnp.where(allowed, jnp.exp(masked - new_top[:, :, None]), 0.0), axis=-1)
        return ((new_top, row_sum * jnp.exp(row_top - new_top) + fresh), None)

    query_count = query_doc.shape[0]
    start = (
        jnp.full((H, query_count), mask_fill, jnp.float32),
        jnp.zeros((H, query_count), jnp.float32),
    )
    (row_top, row_sum), unused = lax.scan(row_visit, start, (key_blocks, doc_blocks, pos_blocks))
    return row_top + jnp.log(row_sum)


def attend_all(
    query_heads, key_blocks, value_blocks, doc_blocks, pos_blocks, query_doc, query_pos, log_norm
):

    def attend_visit(accum_out, block_item):
        key_heads, value_heads, key_doc, key_pos = block_item
        raw_scores, allowed = score_block(
            query_heads, key_heads, query_doc, query_pos, key_doc, key_pos
        )
        soft_low = soft_block(raw_scores, allowed, log_norm).astype(jnp.bfloat16)
        return (
            accum_out
            + jnp.einsum("hqk,khd->qhd", soft_low, value_heads, preferred_element_type=jnp.float32),
            None,
        )

    start = jnp.zeros(query_heads.shape, jnp.float32)
    accum_out, unused = lax.scan(
        attend_visit, start, (key_blocks, value_blocks, doc_blocks, pos_blocks)
    )
    return accum_out


def grad_block(
    query_heads,
    grad_heads,
    log_norm,
    row_delta,
    query_doc,
    query_pos,
    key_heads,
    value_heads,
    key_doc,
    key_pos,
):
    raw_scores, allowed = score_block(
        query_heads, key_heads, query_doc, query_pos, key_doc, key_pos
    )
    soft = soft_block(raw_scores, allowed, log_norm)
    grad_soft = jnp.einsum(
        "qhd,khd->hqk", grad_heads, value_heads, preferred_element_type=jnp.float32
    )
    grad_scores = (soft * (grad_soft - row_delta[:, :, None])).astype(jnp.bfloat16)
    score_scale = 1.0 / math.sqrt(HD)
    part_q = (
        jnp.einsum("hqk,khd->qhd", grad_scores, key_heads, preferred_element_type=jnp.float32)
        * score_scale
    )
    part_k = (
        jnp.einsum("hqk,qhd->khd", grad_scores, query_heads, preferred_element_type=jnp.float32)
        * score_scale
    )
    part_v = jnp.einsum(
        "hqk,qhd->khd", soft.astype(jnp.bfloat16), grad_heads, preferred_element_type=jnp.float32
    )
    return (part_q, part_k, part_v)


def general_body(
    inputs,
    out_grad,
    segment_ids,
    block_order,
    w_qkv,
    w_out,
    w_up,
    w_down,
    norm1_gain,
    norm1_bias,
    norm2_gain,
    norm2_bias,
    out_bias,
    up_bias,
    down_bias,
):
    gathered = (
        lax.all_gather(w_qkv, "fsdp", axis=0, tiled=True),
        lax.all_gather(w_out, "fsdp", axis=0, tiled=True),
        lax.all_gather(w_up, "fsdp", axis=0, tiled=True),
        lax.all_gather(w_down, "fsdp", axis=0, tiled=True),
        lax.all_gather(norm1_gain, "fsdp", axis=0, tiled=True),
        lax.all_gather(norm1_bias, "fsdp", axis=0, tiled=True),
        lax.all_gather(norm2_gain, "fsdp", axis=0, tiled=True),
        lax.all_gather(norm2_bias, "fsdp", axis=0, tiled=True),
        lax.all_gather(out_bias, "fsdp", axis=0, tiled=True),
        lax.all_gather(up_bias, "fsdp", axis=0, tiled=True),
        lax.all_gather(down_bias, "fsdp", axis=0, tiled=True),
    )
    full_qkv, full_out, full_up, full_down = (gathered[0], gathered[1], gathered[2], gathered[3])
    gain_one, bias_one, gain_two, bias_two, full_obias, full_ubias, full_dbias = [
        member.astype(jnp.float32) for member in gathered[4:]
    ]
    model_width = full_qkv.shape[0]
    local_rows = inputs.shape[2]
    ctx_count = lax.axis_size("ctx")
    seq_len = local_rows * ctx_count
    key_block = min(512, seq_len)
    block_count = seq_len // key_block
    ctx_index = lax.axis_index("ctx")
    row_ids = jnp.arange(local_rows, dtype=jnp.int32)
    own_blocks = lax.dynamic_slice_in_dim(block_order, 2 * ctx_index, 2)
    own_pos = own_blocks[row_ids // BLK] * BLK + row_ids % BLK
    all_ids = jnp.arange(seq_len, dtype=jnp.int32)
    all_pos = block_order[all_ids // BLK] * BLK + all_ids % BLK
    pos_blocks = all_pos.reshape(block_count, key_block)
    grad_sums = [jnp.zeros(member.shape, jnp.float32) for member in gathered]
    outputs_list = []
    input_grads = []
    for micro_idx in range(inputs.shape[0]):
        seq_in = inputs[micro_idx, 0].astype(jnp.float32)
        normed, norm1_pull = jax.vjp(layer_norm, seq_in, gain_one, bias_one)
        normed_low = normed.astype(jnp.bfloat16)
        qkv_out = jnp.dot(normed_low, full_qkv, preferred_element_type=jnp.float32).astype(
            jnp.bfloat16
        )
        query_heads = qkv_out[:, :model_width].reshape(local_rows, H, HD)
        kv_all, doc_all = (
            lax.all_gather(qkv_out[:, model_width:], "ctx", axis=0, tiled=True),
            lax.all_gather(segment_ids[micro_idx, 0], "ctx", axis=0, tiled=True),
        )
        doc_rows = doc_all[all_pos]
        query_doc = doc_all[own_pos]
        kv_heads = kv_all.reshape(block_count, key_block, 2, H, HD)
        key_blocks = kv_heads[:, :, 0]
        value_blocks = kv_heads[:, :, 1]
        doc_blocks = doc_rows.reshape(block_count, key_block)
        log_norm = row_log_norm(query_heads, key_blocks, doc_blocks, pos_blocks, query_doc, own_pos)
        attn_acc = attend_all(
            query_heads,
            key_blocks,
            value_blocks,
            doc_blocks,
            pos_blocks,
            query_doc,
            own_pos,
            log_norm,
        )
        attn_low = attn_acc.reshape(local_rows, model_width).astype(jnp.bfloat16)
        branch = jnp.dot(attn_low, full_out, preferred_element_type=jnp.float32) + full_obias
        middle = seq_in + branch
        normed_two, norm2_pull = jax.vjp(layer_norm, middle, gain_two, bias_two)
        normed_two_low = normed_two.astype(jnp.bfloat16)
        hidden = jnp.dot(normed_two_low, full_up, preferred_element_type=jnp.float32) + full_ubias
        active, gelu_pull = jax.vjp(gelu_exact, hidden)
        active_low = active.astype(jnp.bfloat16)
        result = middle + (
            jnp.dot(active_low, full_down, preferred_element_type=jnp.float32) + full_dbias
        )
        outputs_list.append(result.astype(jnp.bfloat16))
        grad_y = out_grad[micro_idx, 0]
        grad_y32 = grad_y.astype(jnp.float32)
        grad_sums[3] = grad_sums[3] + jnp.einsum(
            "rf,rd->fd", active_low, grad_y, preferred_element_type=jnp.float32
        )
        grad_sums[10] = grad_sums[10] + jnp.sum(grad_y32, axis=0)
        grad_active = jnp.einsum("rd,fd->rf", grad_y, full_down, preferred_element_type=jnp.float32)
        (grad_hidden,) = gelu_pull(grad_active)
        grad_hidden_low = grad_hidden.astype(jnp.bfloat16)
        grad_sums[2] = grad_sums[2] + jnp.einsum(
            "rd,rf->df", normed_two_low, grad_hidden_low, preferred_element_type=jnp.float32
        )
        grad_sums[9] = grad_sums[9] + jnp.sum(grad_hidden_low.astype(jnp.float32), axis=0)
        grad_normed_two = jnp.einsum(
            "rf,df->rd", grad_hidden_low, full_up, preferred_element_type=jnp.float32
        )
        grad_mid_ln, grad_gain_two, grad_bias_two = norm2_pull(grad_normed_two)
        grad_sums[6] = grad_sums[6] + grad_gain_two
        grad_sums[7] = grad_sums[7] + grad_bias_two
        grad_mid = grad_y32 + grad_mid_ln
        grad_mid_low = grad_mid.astype(jnp.bfloat16)
        grad_sums[1] = grad_sums[1] + jnp.einsum(
            "rd,re->de", attn_low, grad_mid_low, preferred_element_type=jnp.float32
        )
        grad_sums[8] = grad_sums[8] + jnp.sum(grad_mid_low.astype(jnp.float32), axis=0)
        grad_attn_low = jnp.einsum(
            "re,de->rd", grad_mid_low, full_out, preferred_element_type=jnp.float32
        ).astype(jnp.bfloat16)
        grad_heads = grad_attn_low.reshape(local_rows, H, HD)
        row_delta = jnp.sum(grad_heads.astype(jnp.float32) * attn_acc, axis=-1).T

        def back_visit(grad_query, block_item):
            key_heads, value_heads, key_doc, key_pos = block_item
            part_q, part_k, part_v = grad_block(
                query_heads,
                grad_heads,
                log_norm,
                row_delta,
                query_doc,
                own_pos,
                key_heads,
                value_heads,
                key_doc,
                key_pos,
            )
            joined = jnp.concatenate(
                [part_k.reshape(key_block, model_width), part_v.reshape(key_block, model_width)],
                axis=1,
            )
            return (grad_query + part_q, joined)

        grad_query, kv_terms = lax.scan(
            back_visit,
            jnp.zeros((local_rows, H, HD), jnp.float32),
            (key_blocks, value_blocks, doc_blocks, pos_blocks),
        )
        kv_grad = lax.psum_scatter(
            kv_terms.reshape(seq_len, 2 * model_width).astype(jnp.bfloat16),
            "ctx",
            scatter_dimension=0,
            tiled=True,
        ).astype(jnp.float32)
        grad_qkv_low = jnp.concatenate(
            [grad_query.reshape(local_rows, model_width), kv_grad], axis=1
        ).astype(jnp.bfloat16)
        grad_sums[0] = grad_sums[0] + jnp.einsum(
            "rd,re->de", normed_low, grad_qkv_low, preferred_element_type=jnp.float32
        )
        grad_normed = jnp.einsum(
            "re,de->rd", grad_qkv_low, full_qkv, preferred_element_type=jnp.float32
        )
        grad_in_ln, grad_gain_one, grad_bias_one = norm1_pull(grad_normed)
        grad_sums[4] = grad_sums[4] + grad_gain_one
        grad_sums[5] = grad_sums[5] + grad_bias_one
        input_grads.append(grad_mid + grad_in_ln)
    owned = (
        lax.psum_scatter(
            grad_sums[0].astype(jnp.bfloat16), "fsdp", scatter_dimension=0, tiled=True
        ).astype(jnp.float32),
        lax.psum_scatter(
            grad_sums[1].astype(jnp.bfloat16), "fsdp", scatter_dimension=0, tiled=True
        ).astype(jnp.float32),
        lax.psum_scatter(
            grad_sums[2].astype(jnp.bfloat16), "fsdp", scatter_dimension=0, tiled=True
        ).astype(jnp.float32),
        lax.psum_scatter(
            grad_sums[3].astype(jnp.bfloat16), "fsdp", scatter_dimension=0, tiled=True
        ).astype(jnp.float32),
        lax.psum_scatter(
            grad_sums[4].astype(jnp.bfloat16), "fsdp", scatter_dimension=0, tiled=True
        ).astype(jnp.float32),
        lax.psum_scatter(
            grad_sums[5].astype(jnp.bfloat16), "fsdp", scatter_dimension=0, tiled=True
        ).astype(jnp.float32),
        lax.psum_scatter(
            grad_sums[6].astype(jnp.bfloat16), "fsdp", scatter_dimension=0, tiled=True
        ).astype(jnp.float32),
        lax.psum_scatter(
            grad_sums[7].astype(jnp.bfloat16), "fsdp", scatter_dimension=0, tiled=True
        ).astype(jnp.float32),
        lax.psum_scatter(
            grad_sums[8].astype(jnp.bfloat16), "fsdp", scatter_dimension=0, tiled=True
        ).astype(jnp.float32),
        lax.psum_scatter(
            grad_sums[9].astype(jnp.bfloat16), "fsdp", scatter_dimension=0, tiled=True
        ).astype(jnp.float32),
        lax.psum_scatter(
            grad_sums[10].astype(jnp.bfloat16), "fsdp", scatter_dimension=0, tiled=True
        ).astype(jnp.float32),
    )
    summed = (
        lax.psum(owned[0].astype(jnp.bfloat16), "ctx").astype(jnp.float32),
        lax.psum(owned[1].astype(jnp.bfloat16), "ctx").astype(jnp.float32),
        lax.psum(owned[2].astype(jnp.bfloat16), "ctx").astype(jnp.float32),
        lax.psum(owned[3].astype(jnp.bfloat16), "ctx").astype(jnp.float32),
        lax.psum(owned[4].astype(jnp.bfloat16), "ctx").astype(jnp.float32),
        lax.psum(owned[5].astype(jnp.bfloat16), "ctx").astype(jnp.float32),
        lax.psum(owned[6].astype(jnp.bfloat16), "ctx").astype(jnp.float32),
        lax.psum(owned[7].astype(jnp.bfloat16), "ctx").astype(jnp.float32),
        lax.psum(owned[8].astype(jnp.bfloat16), "ctx").astype(jnp.float32),
        lax.psum(owned[9].astype(jnp.bfloat16), "ctx").astype(jnp.float32),
        lax.psum(owned[10].astype(jnp.bfloat16), "ctx").astype(jnp.float32),
    )
    return (
        jnp.stack(outputs_list)[:, None],
        jnp.stack(input_grads)[:, None],
        summed[0],
        summed[1],
        summed[2],
        summed[3],
        summed[4],
        summed[5],
        summed[6],
        summed[7],
        summed[8],
        summed[9],
        summed[10],
    )


AXES = ("z", "x", "y", "c")
SIZES = (4, 2, 2, 2)


def place(z, x, y, c):
    return ((z * SIZES[1] + x) * SIZES[2] + y) * SIZES[3] + c


def everyone():
    return [
        (z, x, y, c)
        for z in range(SIZES[0])
        for x in range(SIZES[1])
        for y in range(SIZES[2])
        for c in range(SIZES[3])
    ]


def gather_pairs(turn):
    return [
        (place(z, x, y, c), place(2 * ((z % 2) ^ turn) + c, x, y, z // 2))
        for z, x, y, c in everyone()
    ]


def swap_pairs(dx, dy, dc):
    return [(place(z, x, y, c), place(z, x ^ dx, y ^ dy, c ^ dc)) for z, x, y, c in everyone()]


def move(value, pairs):
    return lax.ppermute(value, AXES, pairs)


def swap(value, dx=0, dy=0, dc=0):
    return move(value, swap_pairs(dx, dy, dc))


def to_pair(value, odd):
    return [
        move(lax.dynamic_index_in_dim(value, odd ^ turn, 0, keepdims=False)[0], gather_pairs(turn))
        for turn in range(2)
    ]


def from_pair(value, odd):
    back = [move(value[turn], [(b, a) for a, b in gather_pairs(turn)]) for turn in range(2)]
    first = jnp.where(odd == 0, back[0], back[1])
    second = jnp.where(odd == 0, back[1], back[0])
    return jnp.stack([first, second])[:, None]


def paired_body(
    inputs, out_grad, segment_ids, block_order, w_qkv, w_out, w_up, w_down,
    norm1_gain, norm1_bias, norm2_gain, norm2_bias, out_bias, up_bias, down_bias,
):
    z, x, y, c = (lax.axis_index(name) for name in AXES)
    odd, upper = z % 2, z // 2
    rows, width = inputs.shape[2], inputs.shape[3]
    blocks = block_order.shape[0]
    seq_len = blocks * BLK
    shard = norm1_gain.shape[0]

    x_piece = to_pair(inputs, odd)
    def head_columns(pair):
        parts = [
            lax.dynamic_slice_in_dim(w_qkv, part * width + pair * PAIR, PAIR, axis=1) for part in range(3)
        ]
        return jnp.concatenate(parts, axis=1)

    head_mine, head_other = head_columns(2 * x + c), head_columns(2 * x + 1 - c)
    from_core = swap(head_other, dc=1)
    from_y = swap(head_mine, dy=1)
    from_both = swap(head_other, dy=1, dc=1)
    low_half = jnp.where(c == 0, jnp.stack([head_mine, from_core]), jnp.stack([from_core, head_mine]))
    high_half = jnp.where(c == 0, jnp.stack([from_y, from_both]), jnp.stack([from_both, from_y]))
    w_heads = jnp.where(
        y == 0, jnp.stack([low_half, high_half]), jnp.stack([high_half, low_half])
    ).reshape(width, 3 * PAIR)

    vectors = jnp.concatenate(
        [norm1_gain, norm1_bias, norm2_gain, norm2_bias, out_bias, down_bias, up_bias]
    ).reshape(-1, shard)
    vectors = lax.all_gather(vectors, ("y", "c")).astype(f32)
    gain_one, bias_one, gain_two, bias_two, full_obias, full_dbias = (
        vectors[:, i].reshape(1, width) for i in range(6)
    )
    full_ubias = vectors[:, 6:].reshape(1, -1)

    docs = lax.all_gather(segment_ids[:, 0], ("z", "x", "c"))
    docs = lax.dynamic_index_in_dim(docs.reshape(-1, 2, 2, rows), odd, 1, keepdims=False)
    docs = lax.dynamic_index_in_dim(docs, upper, 1, keepdims=False).reshape(seq_len)
    ids = jnp.arange(blocks, dtype=jnp.int32)
    before = jnp.sum((docs[None, :] < ids[:, None]).astype(jnp.int32), axis=1)
    start = jnp.sum(jnp.where(docs[None, :] == ids[:, None], before[:, None], 0), axis=0)
    low_of = start[::BLK] // BLK
    high_of = jnp.sum((low_of[None, :] <= ids[:, None]).astype(jnp.int32), axis=1) - 1
    start = start.reshape(blocks, 1, BLK)

    slot = jnp.arange(blocks, dtype=jnp.int32)
    group, turn, half = slot // 4, slot // 2 % 2, slot % 2
    stored = 2 * (2 * (2 * (c ^ (group % 2)) + (upper ^ turn)) + (x ^ (group // 2))) + half
    true_of = jnp.sum(jnp.where(stored[:, None] == ids[None, :], block_order[None, :], 0), axis=1)
    slot_of = jnp.sum(jnp.where(true_of[None, :] == ids[:, None], slot[None, :], 0), axis=1)
    groups = jnp.arange(4, dtype=jnp.int32)
    pair_of = 2 * (x ^ (groups // 2)) + (c ^ (groups % 2))

    across = [swap(piece, dx=1) for piece in x_piece]
    beside = [swap(jnp.stack([own, far]), dc=1) for own, far in zip(x_piece, across)]
    x_rows = jnp.stack([
        *x_piece, beside[0][0], beside[1][0], *across, beside[0][1], beside[1][1]
    ]).reshape(seq_len, width)

    q, k, kt, v, vt, h = project(true_of, x_rows, gain_one, bias_one, w_heads)
    dy_piece = to_pair(out_grad, odd)
    o, ot, lse = attend(slot_of, low_of, q, start, k, vt)
    o = o.reshape(4, -1, PAIR)
    attn = jnp.stack([o[0], swap(o[1], dc=1), swap(o[2], dx=1), swap(o[3], dx=1, dc=1)])

    full_out, full_up, full_down = (
        lax.all_gather(member, ("y", "c"), axis=0, tiled=True) for member in (w_out, w_up, w_down)
    )
    vecs = jnp.concatenate([full_obias, gain_two, bias_two, full_dbias], axis=0)
    own_x = jnp.concatenate(x_piece, axis=0)
    own_dy = jnp.concatenate(dy_piece, axis=0)
    result, d_o, d_middle, g_down, g_up, g_out, g_vecs, g_ubias = feed(
        pair_of, attn, own_x, own_dy, full_out, full_up, full_down, vecs, full_ubias
    )
    outputs = from_pair(result.reshape(2, rows, width), odd)

    def reduce_rows(value):
        part = lax.psum_scatter(value.astype(bf16), ("y", "c"), scatter_dimension=0, tiled=True)
        return lax.psum(part, ("z", "x")).astype(f32)

    d_o = jnp.concatenate([d_o[0], swap(d_o[1], dc=1), swap(d_o[2], dx=1), swap(d_o[3], dx=1, dc=1)])
    grad_out, grad_up, grad_down = reduce_rows(g_out), reduce_rows(g_up), reduce_rows(g_down)
    dh, g_heads = attend_back(slot_of, high_of, k, kt, v, h, w_heads, q, start, d_o, ot, lse)
    dh = dh.reshape(4, -1, width)
    other = swap(jnp.stack([dh[1], dh[3]]), dc=1)
    far = swap((dh[2].astype(f32) + other[1].astype(f32)).astype(bf16), dx=1)
    near = (dh[0].astype(f32) + other[0].astype(f32)).astype(bf16)
    dx, g_norm = norm_back(near, far, own_x, d_middle, gain_one)
    input_grad = from_pair(dx.reshape(2, rows, width), odd).astype(f32)

    g_heads = lax.psum_scatter(g_heads.astype(bf16), "y", scatter_dimension=0, tiled=True)
    g_heads = lax.psum(g_heads, "z")
    g_heads = lax.all_gather(g_heads, ("x", "c"))
    g_heads = lax.dynamic_slice_in_dim(g_heads, c * shard, shard, axis=1)
    grad_qkv = g_heads.reshape(4, shard, 3, PAIR).transpose(1, 2, 0, 3).reshape(shard, -1).astype(f32)

    small = jnp.concatenate([
        g_norm[0], g_norm[1], g_vecs[1], g_vecs[2], g_vecs[0], g_vecs[3], g_ubias[0]
    ])
    small = lax.psum(small, AXES)
    index = 2 * y + c
    owned = [
        lax.dynamic_slice_in_dim(small, i * width + index * shard, shard) for i in range(6)
    ]
    owned_up = lax.dynamic_slice_in_dim(small, 6 * width + index * 4 * shard, 4 * shard)
    return (
        outputs, input_grad, grad_qkv, grad_out, grad_up, grad_down,
        owned[0], owned[1], owned[2], owned[3], owned[4], owned_up, owned[5],
    )


def solution(mesh):
    paired = mesh.shape["ctx"] == SIZES[0] * SIZES[1] and mesh.shape["fsdp"] == SIZES[2] * SIZES[3]
    if paired:
        mesh = Mesh(mesh.devices.reshape(SIZES), AXES)
        ctx, fsdp, program = ("z", "x"), ("y", "c"), paired_body
    else:
        ctx, fsdp, program = "ctx", "fsdp", general_body
    tokens = P(None, fsdp, ctx, None)
    matrix, vector = P(fsdp, None), P(fsdp)
    return jax.shard_map(
        program,
        mesh=mesh,
        in_specs=(tokens, tokens, P(None, fsdp, ctx), P()) + (matrix,) * 4 + (vector,) * 7,
        out_specs=(tokens, tokens) + (matrix,) * 4 + (vector,) * 7,
        check_vma=False,
    )
```

```python
import functools
import math

import jax
import jax.numpy as jnp
from jax import lax
from jax.experimental import pallas as pl
from jax.experimental.pallas import tpu as pltpu
from jax.sharding import Mesh
from jax.sharding import PartitionSpec as P

H = 8
HD = 64
BLK = 256
PAIR = 2 * HD

norm_eps = 1e-05
mask_fill = -1e30
LOG2E = math.log2(math.e)
LN2 = math.log(2.0)
SCORE_SCALE = 1.0 / math.sqrt(HD)

f32 = jnp.float32
bf16 = jnp.bfloat16


def contract(a, b, da, db):
    return lax.dot_general(a, b, (((da,), (db,)), ((), ())), preferred_element_type=f32)


def norm_parts(values):
    center = values - jnp.mean(values, axis=-1, keepdims=True)
    spread = jnp.mean(center * center, axis=-1, keepdims=True)
    inv = lax.rsqrt(spread + norm_eps)
    return center * inv, inv


def whole(shape):
    zeros = (0,) * len(shape)
    return pl.BlockSpec(shape, lambda *_: zeros)


def split_heads(block):
    lane = lax.broadcasted_iota(jnp.int32, block.shape, 1)
    zero = jnp.zeros_like(block)
    first = lane < HD
    return jnp.concatenate([jnp.where(first, block, zero), jnp.where(first, zero, block)], axis=0)


def attend_kernel(tab_ref, q_ref, start_ref, k_ref, vt_ref, o_ref, ot_ref, lse_ref, acc, top):
    qb = pl.program_id(0)
    both = split_heads(q_ref[...])
    start = jnp.concatenate([start_ref[0], start_ref[0]], axis=1)
    row = lax.broadcasted_iota(jnp.int32, (BLK, 2 * BLK), 0)
    col = lax.broadcasted_iota(jnp.int32, (BLK, 2 * BLK), 1)
    ones = jnp.ones((16, BLK), bf16)

    def scores(kb):
        base = pl.multiple_of(tab_ref[2, kb] * BLK, BLK)
        return contract(k_ref[pl.ds(base, BLK), :], both, 1, 1)

    def values(kb):
        base = pl.multiple_of(tab_ref[2, kb] * BLK, BLK)
        return jnp.concatenate([vt_ref[:, pl.ds(base, BLK)], ones], axis=0)

    st = scores(qb)
    allowed = (row >= start - qb * BLK) & (row <= jnp.bitwise_and(col, BLK - 1))
    st = jnp.where(allowed, st, mask_fill)
    peak = jnp.max(st, axis=0, keepdims=True)
    probs = jnp.exp2(st - peak).astype(bf16)
    top[...] = peak
    acc[...] = jnp.dot(values(qb), probs, preferred_element_type=f32)

    def visit(kb, carry):
        st = jnp.where(row >= start - kb * BLK, scores(kb), mask_fill)
        old = top[...]
        peak = jnp.maximum(old, jnp.max(st, axis=0, keepdims=True))
        probs = jnp.exp2(st - peak).astype(bf16)
        top[...] = peak
        acc[...] = acc[...] * jnp.exp2(old - peak) + jnp.dot(values(kb), probs, preferred_element_type=f32)
        return carry

    lax.fori_loop(tab_ref[0, qb], qb, visit, 0)
    total = acc[PAIR : PAIR + 1, :]
    lse_ref[0] = top[...] + jnp.log2(total)
    out = acc[:PAIR, :] / total
    heads = jnp.concatenate([out[:HD, :BLK], out[HD:, BLK:]], axis=0)
    ot_ref[0] = heads
    o_ref[...] = heads.T.astype(bf16)


def attend(tab, q, start, k, vt):
    count = q.shape[0]
    blocks = count // BLK
    return pl.pallas_call(
        attend_kernel,
        grid_spec=pltpu.PrefetchScalarGridSpec(
            num_scalar_prefetch=1,
            grid=(blocks,),
            in_specs=[
                pl.BlockSpec((BLK, PAIR), lambda b, t: (t[2, b], 0)),
                pl.BlockSpec((1, 1, BLK), lambda b, t: (b, 0, 0)),
                whole(k.shape),
                whole(vt.shape),
            ],
            out_specs=[
                pl.BlockSpec((BLK, PAIR), lambda b, t: (t[2, b], 0)),
                pl.BlockSpec((1, PAIR, BLK), lambda b, t: (b, 0, 0)),
                pl.BlockSpec((1, 1, 2 * BLK), lambda b, t: (b, 0, 0)),
            ],
            scratch_shapes=[
                pltpu.VMEM((PAIR + 16, 2 * BLK), f32),
                pltpu.VMEM((1, 2 * BLK), f32),
            ],
        ),
        out_shape=[
            jax.ShapeDtypeStruct((count, PAIR), bf16),
            jax.ShapeDtypeStruct((blocks, PAIR, BLK), f32),
            jax.ShapeDtypeStruct((blocks, 1, 2 * BLK), f32),
        ],
        name="attend",
    )(tab, q, start, k, vt)


def attend_back_kernel(
    tab_ref, k_ref, kt_ref, v_ref, h_ref, w_ref, q_ref, start_ref, do_ref, ot_ref, lse_ref,
    gain_ref, bias_ref, dh_ref, gw_ref, gn_ref, dqt, dk, dv, delta, total, sums,
):
    kb = pl.program_id(0)
    blocks = pl.num_programs(0)
    row = lax.broadcasted_iota(jnp.int32, (BLK, 2 * BLK), 0)
    col = lax.broadcasted_iota(jnp.int32, (BLK, 2 * BLK), 1)

    def at(qb):
        return pl.ds(pl.multiple_of(tab_ref[2, qb] * BLK, BLK), BLK)

    @pl.when(kb == 0)
    def _():
        total[...] = jnp.zeros_like(total)
        sums[...] = jnp.zeros_like(sums)

        def prepare(qb, carry):
            dqt[qb] = jnp.zeros((PAIR, BLK), f32)
            both = do_ref[at(qb), :].astype(f32).T * ot_ref[qb]
            delta[qb] = jnp.concatenate(
                [
                    jnp.sum(both[:HD], axis=0, keepdims=True),
                    jnp.sum(both[HD:], axis=0, keepdims=True),
                ],
                axis=1,
            )
            return carry

        lax.fori_loop(0, blocks, prepare, 0)

    k = k_ref[...]
    v = v_ref[...]
    kt = kt_ref[...]

    def tile(qb, diagonal):
        both_q = split_heads(q_ref[at(qb), :])
        both_do = split_heads(do_ref[at(qb), :])
        start = jnp.concatenate([start_ref[qb], start_ref[qb]], axis=1)
        st = contract(k, both_q, 1, 1)
        dpt = contract(v, both_do, 1, 1)
        allowed = row >= start - kb * BLK
        if diagonal:
            allowed = allowed & (row <= jnp.bitwise_and(col, BLK - 1))
        pt = jnp.exp2(jnp.where(allowed, st - lse_ref[qb], mask_fill))
        dst = (pt * (dpt - delta[qb])).astype(bf16)
        part_v = jnp.dot(pt.astype(bf16), both_do, preferred_element_type=f32)
        part_k = jnp.dot(dst, both_q, preferred_element_type=f32)
        if diagonal:
            dv[...] = part_v
            dk[...] = part_k
        else:
            dv[...] += part_v
            dk[...] += part_k
        dqt[qb] += jnp.concatenate(
            [
                jnp.dot(kt[:HD], dst[:, :BLK], preferred_element_type=f32),
                jnp.dot(kt[HD:], dst[:, BLK:], preferred_element_type=f32),
            ],
            axis=0,
        )

    tile(kb, True)

    def visit(qb, carry):
        tile(qb, False)
        return carry

    lax.fori_loop(kb + 1, tab_ref[1, kb] + 1, visit, 0)
    dq = (dqt[kb] * SCORE_SCALE).T.astype(bf16)
    joined = jnp.concatenate([dq, (dk[...] * LN2).astype(bf16), dv[...].astype(bf16)], axis=1)
    dh_ref[...] = contract(joined, w_ref[...], 1, 1).astype(bf16)
    total[...] += contract(h_ref[...], joined, 0, 0)
    sums[...] += jnp.sum(joined.astype(f32), axis=0, keepdims=True)

    @pl.when(kb == blocks - 1)
    def _():
        shard = gw_ref.shape[1]
        for j in range(gw_ref.shape[0]):
            part = pl.ds(j * shard, shard)
            gw_ref[j] = (total[part] * gain_ref[part] + bias_ref[part] * sums[...]).astype(bf16)
            w = w_ref[part].astype(f32)
            for i, term in enumerate((w * total[part], w * sums[...])):
                column = jnp.sum(term, axis=1, keepdims=True)
                gn_ref[i : i + 1, part] = jnp.broadcast_to(column, (shard, shard)).T[:1]


def attend_back(tab, k, kt, v, h, weight, q, start, d_out, ot, lse, gain, bias, shards):
    count = q.shape[0]
    width = h.shape[1]
    shard = width // shards
    gain, bias = gain.reshape(width, 1), bias.reshape(width, 1)
    blocks = count // BLK
    return pl.pallas_call(
        attend_back_kernel,
        grid_spec=pltpu.PrefetchScalarGridSpec(
            num_scalar_prefetch=1,
            grid=(blocks,),
            in_specs=[
                pl.BlockSpec((BLK, PAIR), lambda b, t: (t[2, b], 0)),
                pl.BlockSpec((PAIR, BLK), lambda b, t: (0, t[2, b])),
                pl.BlockSpec((BLK, PAIR), lambda b, t: (t[2, b], 0)),
                pl.BlockSpec((BLK, width), lambda b, t: (t[2, b], 0)),
                whole(weight.shape),
                whole(q.shape),
                whole(start.shape),
                whole(d_out.shape),
                whole(ot.shape),
                whole(lse.shape),
                whole(gain.shape),
                whole(bias.shape),
            ],
            out_specs=[
                pl.BlockSpec((BLK, width), lambda b, t: (t[2, b], 0)),
                whole((shards, shard, 3 * PAIR)),
                whole((2, width)),
            ],
            scratch_shapes=[
                pltpu.VMEM((blocks, PAIR, BLK), f32),
                pltpu.VMEM((BLK, PAIR), f32),
                pltpu.VMEM((BLK, PAIR), f32),
                pltpu.VMEM((blocks, 1, 2 * BLK), f32),
                pltpu.VMEM(weight.shape, f32),
                pltpu.VMEM((1, 3 * PAIR), f32),
            ],
        ),
        out_shape=[
            jax.ShapeDtypeStruct((count, width), bf16),
            jax.ShapeDtypeStruct((shards, shard, 3 * PAIR), bf16),
            jax.ShapeDtypeStruct((2, width), f32),
        ],
        name="attend_back",
    )(tab, k, kt, v, h, weight, q, start, d_out, ot, lse, gain, bias)


FF_TILE = 512


def feed_kernel(
    pair_ref, attn_ref, x_ref, dy_ref, wo_ref, wu_ref, wd_ref, vec_ref, ub_ref,
    y_ref, do_ref, dmid_ref, grad_ref, gvec_ref, gub_ref, attn_all, gd_ref, gu_ref, go_ref,
):
    step = pl.program_id(0)
    groups = attn_ref.shape[0]

    @pl.when(step == 0)
    def _():
        for ref in (gd_ref, gu_ref, go_ref, gvec_ref, gub_ref):
            ref[...] = jnp.zeros_like(ref)

    for g in range(groups):
        attn_all[:, pl.ds(pl.multiple_of(pair_ref[g] * PAIR, PAIR), PAIR)] = attn_ref[g]
    attn = attn_all[...]
    gain, bias, out_bias, down_bias = (vec_ref[i : i + 1, :] for i in range(2, 6))
    middle = (
        x_ref[...].astype(f32) + jnp.dot(attn, wo_ref[...], preferred_element_type=f32) + out_bias
    )
    unit, inv = norm_parts(middle)
    low = (unit * gain + bias).astype(bf16)
    dy = dy_ref[...]
    dy32 = dy.astype(f32)
    total = middle + down_bias
    d_low = jnp.zeros_like(middle)
    width = wu_ref.shape[1]
    for j in range(0, width, FF_TILE):
        part = pl.ds(j, FF_TILE)
        up = wu_ref[:, part]
        down = wd_ref[part, :]
        hidden = jnp.dot(low, up, preferred_element_type=f32) + ub_ref[:, part]
        cdf = 0.5 * (1.0 + lax.erf(hidden * (1.0 / math.sqrt(2.0))))
        active = (hidden * cdf).astype(bf16)
        slope = cdf + hidden * (jnp.exp2(hidden * hidden * (-0.5 * LOG2E)) * (1.0 / math.sqrt(2.0 * math.pi)))
        total = total + jnp.dot(active, down, preferred_element_type=f32)
        d_hidden = contract(dy, down, 1, 1) * slope
        d_hidden_low = d_hidden.astype(bf16)
        gub_ref[:, part] += jnp.sum(d_hidden, axis=0, keepdims=True)
        d_low = d_low + contract(d_hidden_low, up, 1, 1)
        gd_ref[part, :] += contract(active, dy, 0, 0)
        gu_ref[:, part] += contract(low, d_hidden_low, 0, 0)
    y_ref[...] = total.astype(bf16)
    scaled = d_low * gain
    d_middle = dy32 + inv * (
        scaled
        - jnp.mean(scaled, axis=-1, keepdims=True)
        - unit * jnp.mean(scaled * unit, axis=-1, keepdims=True)
    )
    dmid_ref[...] = d_middle
    branch = d_middle.astype(bf16)
    go_ref[...] += contract(attn, branch, 0, 0)
    gvec_ref[0:1, :] += jnp.sum(d_middle, axis=0, keepdims=True)
    gvec_ref[1:2, :] += jnp.sum(d_low * unit, axis=0, keepdims=True)
    gvec_ref[2:3, :] += jnp.sum(d_low, axis=0, keepdims=True)
    gvec_ref[3:4, :] += jnp.sum(dy32, axis=0, keepdims=True)
    attn_all[...] = contract(branch, wo_ref[...], 1, 1).astype(bf16)
    for g in range(groups):
        do_ref[g] = attn_all[:, pl.ds(pl.multiple_of(pair_ref[g] * PAIR, PAIR), PAIR)]

    @pl.when(step == pl.num_programs(0) - 1)
    def _():
        shards = grad_ref.shape[0]
        d_model = x_ref.shape[1]
        down_rows, up_rows = gd_ref.shape[0] // shards, d_model // shards
        for j in range(shards):
            grad_ref[j, :down_rows] = gd_ref[j * down_rows : (j + 1) * down_rows].astype(bf16)
            rows = slice(j * up_rows, (j + 1) * up_rows)
            at = down_rows
            for t in range(0, width, d_model):
                grad_ref[j, at : at + up_rows] = gu_ref[rows, t : t + d_model].astype(bf16)
                at += up_rows
            grad_ref[j, at : at + up_rows] = go_ref[rows].astype(bf16)


def feed(pair_of, attn, x, dy, w_out, w_up, w_down, vecs, up_bias, shards, tile=BLK):
    groups, count, _ = attn.shape
    width = x.shape[1]
    flat = (w_out.size + w_up.size + w_down.size) // shards // width
    rows = pl.BlockSpec((tile, width), lambda i, p: (i, 0))
    heads = pl.BlockSpec((groups, tile, PAIR), lambda i, p: (0, i, 0))
    return pl.pallas_call(
        feed_kernel,
        grid_spec=pltpu.PrefetchScalarGridSpec(
            num_scalar_prefetch=1,
            grid=(count // tile,),
            in_specs=[
                heads, rows, rows, whole(w_out.shape), whole(w_up.shape), whole(w_down.shape),
                whole(vecs.shape), whole(up_bias.shape),
            ],
            out_specs=[
                rows, heads, rows, whole((shards, flat, width)), whole(vecs.shape), whole(up_bias.shape),
            ],
            scratch_shapes=[
                pltpu.VMEM((tile, width), bf16),
                pltpu.VMEM(w_down.shape, f32),
                pltpu.VMEM(w_up.shape, f32),
                pltpu.VMEM(w_out.shape, f32),
            ],
        ),
        out_shape=[
            jax.ShapeDtypeStruct((count, width), bf16),
            jax.ShapeDtypeStruct((groups, count, PAIR), bf16),
            jax.ShapeDtypeStruct((count, width), f32),
            jax.ShapeDtypeStruct((shards, flat, width), bf16),
            jax.ShapeDtypeStruct(vecs.shape, f32),
            jax.ShapeDtypeStruct(up_bias.shape, f32),
        ],
        compiler_params=pltpu.CompilerParams(vmem_limit_bytes=60 * 1024 * 1024),
        name="feed",
    )(pair_of, attn, x, dy, w_out, w_up, w_down, vecs, up_bias)


def layer_norm(values, gain_vec, offset):
    center = values - jnp.mean(values, axis=-1, keepdims=True)
    spread = jnp.mean(center * center, axis=-1, keepdims=True)
    return center * lax.rsqrt(spread + norm_eps) * gain_vec + offset


def gelu_exact(values):
    return 0.5 * values * (1.0 + lax.erf(values * (1.0 / math.sqrt(2.0))))


def score_block(query_heads, key_heads, query_doc, query_pos, key_doc, key_pos):
    raw_scores = jnp.einsum(
        "qhd,khd->hqk", query_heads, key_heads, preferred_element_type=jnp.float32
    ) * (1.0 / math.sqrt(HD))
    allowed = (query_doc[:, None] == key_doc[None, :]) & (key_pos[None, :] <= query_pos[:, None])
    return (raw_scores, allowed[None])


def soft_block(raw_scores, allowed, log_norm):
    return jnp.exp(jnp.where(allowed, raw_scores, mask_fill) - log_norm[:, :, None])


def row_log_norm(query_heads, key_blocks, doc_blocks, pos_blocks, query_doc, query_pos):

    def row_visit(running, block_item):
        row_top, row_sum = running
        key_heads, key_doc, key_pos = block_item
        raw_scores, allowed = score_block(
            query_heads, key_heads, query_doc, query_pos, key_doc, key_pos
        )
        masked = jnp.where(allowed, raw_scores, mask_fill)
        new_top = jnp.maximum(row_top, jnp.max(masked, axis=-1))
        fresh = jnp.sum(jnp.where(allowed, jnp.exp(masked - new_top[:, :, None]), 0.0), axis=-1)
        return ((new_top, row_sum * jnp.exp(row_top - new_top) + fresh), None)

    query_count = query_doc.shape[0]
    start = (
        jnp.full((H, query_count), mask_fill, jnp.float32),
        jnp.zeros((H, query_count), jnp.float32),
    )
    (row_top, row_sum), unused = lax.scan(row_visit, start, (key_blocks, doc_blocks, pos_blocks))
    return row_top + jnp.log(row_sum)


def attend_all(
    query_heads, key_blocks, value_blocks, doc_blocks, pos_blocks, query_doc, query_pos, log_norm
):

    def attend_visit(accum_out, block_item):
        key_heads, value_heads, key_doc, key_pos = block_item
        raw_scores, allowed = score_block(
            query_heads, key_heads, query_doc, query_pos, key_doc, key_pos
        )
        soft_low = soft_block(raw_scores, allowed, log_norm).astype(jnp.bfloat16)
        return (
            accum_out
            + jnp.einsum("hqk,khd->qhd", soft_low, value_heads, preferred_element_type=jnp.float32),
            None,
        )

    start = jnp.zeros(query_heads.shape, jnp.float32)
    accum_out, unused = lax.scan(
        attend_visit, start, (key_blocks, value_blocks, doc_blocks, pos_blocks)
    )
    return accum_out


def grad_block(
    query_heads,
    grad_heads,
    log_norm,
    row_delta,
    query_doc,
    query_pos,
    key_heads,
    value_heads,
    key_doc,
    key_pos,
):
    raw_scores, allowed = score_block(
        query_heads, key_heads, query_doc, query_pos, key_doc, key_pos
    )
    soft = soft_block(raw_scores, allowed, log_norm)
    grad_soft = jnp.einsum(
        "qhd,khd->hqk", grad_heads, value_heads, preferred_element_type=jnp.float32
    )
    grad_scores = (soft * (grad_soft - row_delta[:, :, None])).astype(jnp.bfloat16)
    score_scale = 1.0 / math.sqrt(HD)
    part_q = (
        jnp.einsum("hqk,khd->qhd", grad_scores, key_heads, preferred_element_type=jnp.float32)
        * score_scale
    )
    part_k = (
        jnp.einsum("hqk,qhd->khd", grad_scores, query_heads, preferred_element_type=jnp.float32)
        * score_scale
    )
    part_v = jnp.einsum(
        "hqk,qhd->khd", soft.astype(jnp.bfloat16), grad_heads, preferred_element_type=jnp.float32
    )
    return (part_q, part_k, part_v)


def general_body(
    inputs,
    out_grad,
    segment_ids,
    block_order,
    w_qkv,
    w_out,
    w_up,
    w_down,
    norm1_gain,
    norm1_bias,
    norm2_gain,
    norm2_bias,
    out_bias,
    up_bias,
    down_bias,
):
    gathered = (
        lax.all_gather(w_qkv, "fsdp", axis=0, tiled=True),
        lax.all_gather(w_out, "fsdp", axis=0, tiled=True),
        lax.all_gather(w_up, "fsdp", axis=0, tiled=True),
        lax.all_gather(w_down, "fsdp", axis=0, tiled=True),
        lax.all_gather(norm1_gain, "fsdp", axis=0, tiled=True),
        lax.all_gather(norm1_bias, "fsdp", axis=0, tiled=True),
        lax.all_gather(norm2_gain, "fsdp", axis=0, tiled=True),
        lax.all_gather(norm2_bias, "fsdp", axis=0, tiled=True),
        lax.all_gather(out_bias, "fsdp", axis=0, tiled=True),
        lax.all_gather(up_bias, "fsdp", axis=0, tiled=True),
        lax.all_gather(down_bias, "fsdp", axis=0, tiled=True),
    )
    full_qkv, full_out, full_up, full_down = (gathered[0], gathered[1], gathered[2], gathered[3])
    gain_one, bias_one, gain_two, bias_two, full_obias, full_ubias, full_dbias = [
        member.astype(jnp.float32) for member in gathered[4:]
    ]
    model_width = full_qkv.shape[0]
    local_rows = inputs.shape[2]
    ctx_count = lax.axis_size("ctx")
    seq_len = local_rows * ctx_count
    key_block = min(512, seq_len)
    block_count = seq_len // key_block
    ctx_index = lax.axis_index("ctx")
    row_ids = jnp.arange(local_rows, dtype=jnp.int32)
    own_blocks = lax.dynamic_slice_in_dim(block_order, 2 * ctx_index, 2)
    own_pos = own_blocks[row_ids // BLK] * BLK + row_ids % BLK
    all_ids = jnp.arange(seq_len, dtype=jnp.int32)
    all_pos = block_order[all_ids // BLK] * BLK + all_ids % BLK
    pos_blocks = all_pos.reshape(block_count, key_block)
    grad_sums = [jnp.zeros(member.shape, jnp.float32) for member in gathered]
    outputs_list = []
    input_grads = []
    for micro_idx in range(inputs.shape[0]):
        seq_in = inputs[micro_idx, 0].astype(jnp.float32)
        normed, norm1_pull = jax.vjp(layer_norm, seq_in, gain_one, bias_one)
        normed_low = normed.astype(jnp.bfloat16)
        qkv_out = jnp.dot(normed_low, full_qkv, preferred_element_type=jnp.float32).astype(
            jnp.bfloat16
        )
        query_heads = qkv_out[:, :model_width].reshape(local_rows, H, HD)
        kv_all, doc_all = (
            lax.all_gather(qkv_out[:, model_width:], "ctx", axis=0, tiled=True),
            lax.all_gather(segment_ids[micro_idx, 0], "ctx", axis=0, tiled=True),
        )
        doc_rows = doc_all[all_pos]
        query_doc = doc_all[own_pos]
        kv_heads = kv_all.reshape(block_count, key_block, 2, H, HD)
        key_blocks = kv_heads[:, :, 0]
        value_blocks = kv_heads[:, :, 1]
        doc_blocks = doc_rows.reshape(block_count, key_block)
        log_norm = row_log_norm(query_heads, key_blocks, doc_blocks, pos_blocks, query_doc, own_pos)
        attn_acc = attend_all(
            query_heads,
            key_blocks,
            value_blocks,
            doc_blocks,
            pos_blocks,
            query_doc,
            own_pos,
            log_norm,
        )
        attn_low = attn_acc.reshape(local_rows, model_width).astype(jnp.bfloat16)
        branch = jnp.dot(attn_low, full_out, preferred_element_type=jnp.float32) + full_obias
        middle = seq_in + branch
        normed_two, norm2_pull = jax.vjp(layer_norm, middle, gain_two, bias_two)
        normed_two_low = normed_two.astype(jnp.bfloat16)
        hidden = jnp.dot(normed_two_low, full_up, preferred_element_type=jnp.float32) + full_ubias
        active, gelu_pull = jax.vjp(gelu_exact, hidden)
        active_low = active.astype(jnp.bfloat16)
        result = middle + (
            jnp.dot(active_low, full_down, preferred_element_type=jnp.float32) + full_dbias
        )
        outputs_list.append(result.astype(jnp.bfloat16))
        grad_y = out_grad[micro_idx, 0]
        grad_y32 = grad_y.astype(jnp.float32)
        grad_sums[3] = grad_sums[3] + jnp.einsum(
            "rf,rd->fd", active_low, grad_y, preferred_element_type=jnp.float32
        )
        grad_sums[10] = grad_sums[10] + jnp.sum(grad_y32, axis=0)
        grad_active = jnp.einsum("rd,fd->rf", grad_y, full_down, preferred_element_type=jnp.float32)
        (grad_hidden,) = gelu_pull(grad_active)
        grad_hidden_low = grad_hidden.astype(jnp.bfloat16)
        grad_sums[2] = grad_sums[2] + jnp.einsum(
            "rd,rf->df", normed_two_low, grad_hidden_low, preferred_element_type=jnp.float32
        )
        grad_sums[9] = grad_sums[9] + jnp.sum(grad_hidden_low.astype(jnp.float32), axis=0)
        grad_normed_two = jnp.einsum(
            "rf,df->rd", grad_hidden_low, full_up, preferred_element_type=jnp.float32
        )
        grad_mid_ln, grad_gain_two, grad_bias_two = norm2_pull(grad_normed_two)
        grad_sums[6] = grad_sums[6] + grad_gain_two
        grad_sums[7] = grad_sums[7] + grad_bias_two
        grad_mid = grad_y32 + grad_mid_ln
        grad_mid_low = grad_mid.astype(jnp.bfloat16)
        grad_sums[1] = grad_sums[1] + jnp.einsum(
            "rd,re->de", attn_low, grad_mid_low, preferred_element_type=jnp.float32
        )
        grad_sums[8] = grad_sums[8] + jnp.sum(grad_mid_low.astype(jnp.float32), axis=0)
        grad_attn_low = jnp.einsum(
            "re,de->rd", grad_mid_low, full_out, preferred_element_type=jnp.float32
        ).astype(jnp.bfloat16)
        grad_heads = grad_attn_low.reshape(local_rows, H, HD)
        row_delta = jnp.sum(grad_heads.astype(jnp.float32) * attn_acc, axis=-1).T

        def back_visit(grad_query, block_item):
            key_heads, value_heads, key_doc, key_pos = block_item
            part_q, part_k, part_v = grad_block(
                query_heads,
                grad_heads,
                log_norm,
                row_delta,
                query_doc,
                own_pos,
                key_heads,
                value_heads,
                key_doc,
                key_pos,
            )
            joined = jnp.concatenate(
                [part_k.reshape(key_block, model_width), part_v.reshape(key_block, model_width)],
                axis=1,
            )
            return (grad_query + part_q, joined)

        grad_query, kv_terms = lax.scan(
            back_visit,
            jnp.zeros((local_rows, H, HD), jnp.float32),
            (key_blocks, value_blocks, doc_blocks, pos_blocks),
        )
        kv_grad = lax.psum_scatter(
            kv_terms.reshape(seq_len, 2 * model_width).astype(jnp.bfloat16),
            "ctx",
            scatter_dimension=0,
            tiled=True,
        ).astype(jnp.float32)
        grad_qkv_low = jnp.concatenate(
            [grad_query.reshape(local_rows, model_width), kv_grad], axis=1
        ).astype(jnp.bfloat16)
        grad_sums[0] = grad_sums[0] + jnp.einsum(
            "rd,re->de", normed_low, grad_qkv_low, preferred_element_type=jnp.float32
        )
        grad_normed = jnp.einsum(
            "re,de->rd", grad_qkv_low, full_qkv, preferred_element_type=jnp.float32
        )
        grad_in_ln, grad_gain_one, grad_bias_one = norm1_pull(grad_normed)
        grad_sums[4] = grad_sums[4] + grad_gain_one
        grad_sums[5] = grad_sums[5] + grad_bias_one
        input_grads.append(grad_mid + grad_in_ln)
    owned = (
        lax.psum_scatter(
            grad_sums[0].astype(jnp.bfloat16), "fsdp", scatter_dimension=0, tiled=True
        ).astype(jnp.float32),
        lax.psum_scatter(
            grad_sums[1].astype(jnp.bfloat16), "fsdp", scatter_dimension=0, tiled=True
        ).astype(jnp.float32),
        lax.psum_scatter(
            grad_sums[2].astype(jnp.bfloat16), "fsdp", scatter_dimension=0, tiled=True
        ).astype(jnp.float32),
        lax.psum_scatter(
            grad_sums[3].astype(jnp.bfloat16), "fsdp", scatter_dimension=0, tiled=True
        ).astype(jnp.float32),
        lax.psum_scatter(
            grad_sums[4].astype(jnp.bfloat16), "fsdp", scatter_dimension=0, tiled=True
        ).astype(jnp.float32),
        lax.psum_scatter(
            grad_sums[5].astype(jnp.bfloat16), "fsdp", scatter_dimension=0, tiled=True
        ).astype(jnp.float32),
        lax.psum_scatter(
            grad_sums[6].astype(jnp.bfloat16), "fsdp", scatter_dimension=0, tiled=True
        ).astype(jnp.float32),
        lax.psum_scatter(
            grad_sums[7].astype(jnp.bfloat16), "fsdp", scatter_dimension=0, tiled=True
        ).astype(jnp.float32),
        lax.psum_scatter(
            grad_sums[8].astype(jnp.bfloat16), "fsdp", scatter_dimension=0, tiled=True
        ).astype(jnp.float32),
        lax.psum_scatter(
            grad_sums[9].astype(jnp.bfloat16), "fsdp", scatter_dimension=0, tiled=True
        ).astype(jnp.float32),
        lax.psum_scatter(
            grad_sums[10].astype(jnp.bfloat16), "fsdp", scatter_dimension=0, tiled=True
        ).astype(jnp.float32),
    )
    summed = (
        lax.psum(owned[0].astype(jnp.bfloat16), "ctx").astype(jnp.float32),
        lax.psum(owned[1].astype(jnp.bfloat16), "ctx").astype(jnp.float32),
        lax.psum(owned[2].astype(jnp.bfloat16), "ctx").astype(jnp.float32),
        lax.psum(owned[3].astype(jnp.bfloat16), "ctx").astype(jnp.float32),
        lax.psum(owned[4].astype(jnp.bfloat16), "ctx").astype(jnp.float32),
        lax.psum(owned[5].astype(jnp.bfloat16), "ctx").astype(jnp.float32),
        lax.psum(owned[6].astype(jnp.bfloat16), "ctx").astype(jnp.float32),
        lax.psum(owned[7].astype(jnp.bfloat16), "ctx").astype(jnp.float32),
        lax.psum(owned[8].astype(jnp.bfloat16), "ctx").astype(jnp.float32),
        lax.psum(owned[9].astype(jnp.bfloat16), "ctx").astype(jnp.float32),
        lax.psum(owned[10].astype(jnp.bfloat16), "ctx").astype(jnp.float32),
    )
    return (
        jnp.stack(outputs_list)[:, None],
        jnp.stack(input_grads)[:, None],
        summed[0],
        summed[1],
        summed[2],
        summed[3],
        summed[4],
        summed[5],
        summed[6],
        summed[7],
        summed[8],
        summed[9],
        summed[10],
    )


AXES = ("z", "x", "y", "c")
SIZES = (4, 2, 2, 2)


MESH = pl.DeviceIdType.MESH


def send(src, dst, sems, recv_sems, index, peer):
    copy = pltpu.make_async_remote_copy(
        src_ref=src,
        dst_ref=dst,
        send_sem=sems.at[index],
        recv_sem=recv_sems.at[index],
        device_id=peer,
        device_id_type=MESH,
    )
    copy.start()
    return copy


def greet(peers, extra, extra_on):
    barrier = pltpu.get_barrier_semaphore()
    for peer in peers:
        pl.semaphore_signal(barrier, inc=1, device_id=peer, device_id_type=MESH)

    @pl.when(extra_on)
    def _():
        for peer in extra:
            pl.semaphore_signal(barrier, inc=1, device_id=peer, device_id_type=MESH)

    pl.semaphore_wait(barrier, len(peers) + jnp.where(extra_on, len(extra), 0))


HEAD_CHUNK = 128


def head_kernel(
    x_in_ref, docs_in_ref, order_ref, vec_in_ref, wq_ref, wo_ref, wu_ref, wd_ref,
    q_ref, k_ref, kt_ref, v_ref, vt_ref, u_ref, own_ref, wh_ref, vec_ref, ub_ref, start_ref, tab_ref,
    wo_all, wu_all, wd_all,
    rows, docs, docs_true, vec_all, wo_tmp, wu_tmp, wd_tmp,
    z_s, z_r, x_s, x_r, c_s, c_r, f_s, f_r, docs_s, docs_r, vec_s, vec_r, wh_s, wh_r, wh_l,
    y_s, y_r, n_s, n_r, o_s, o_r, load_sem, put_sem, self_sem,
):
    z, x, y, c = (lax.axis_index(name) for name in AXES)
    odd, upper = lax.rem(z, 2), lax.div(z, 2)
    width = x_in_ref.shape[-1]
    chunks = rows.shape[1] // HEAD_CHUNK
    per_turn = chunks // 2
    by_core, by_x, by_y, by_yc = {"c": 1 - c}, {"x": 1 - x}, {"y": 1 - y}, {"y": 1 - y, "c": 1 - c}
    home = [{"z": 2 * c + upper, "c": odd}, {"z": 2 * c + 1 - upper, "c": odd}]
    target = [{"z": 2 * odd + c, "c": upper}, {"z": 2 * (1 - odd) + c, "c": upper}]
    block = [odd, 1 - odd]
    stay = (c == upper) & (odd == c)
    leave = jnp.logical_not(stay)
    greet([by_core, by_x, by_y, by_yc, home[1], target[1]], [home[0], target[0]], leave)

    def piece(i):
        turn, row = i // per_turn, (i % per_turn) * HEAD_CHUNK
        return (
            x_in_ref.at[block[turn], 0, pl.ds(row, HEAD_CHUNK)],
            rows.at[0, pl.ds(i * HEAD_CHUNK, HEAD_CHUNK)],
        )

    for turn in range(2):
        src, dst = docs_in_ref.at[block[turn]], docs.at[0, turn]

        def start_docs():
            send(src, dst, docs_s, docs_r, turn, target[turn])

        if turn == 0:
            pl.when(stay)(lambda: pltpu.make_async_copy(src, dst, self_sem.at[per_turn]).start())
            pl.when(leave)(start_docs)
        else:
            start_docs()
    for i in range(chunks):
        src, dst = piece(i)
        if i < per_turn:
            pl.when(stay)(lambda: pltpu.make_async_copy(src, dst, self_sem.at[i]).start())
            pl.when(leave)(lambda: send(src, dst, z_s, z_r, i, target[0]) and None)
        else:
            send(src, dst, z_s, z_r, i, target[1])

    def landed(src, dst, sems, recv_sems, index, turn, self_index):
        def remote():
            pltpu.make_async_remote_copy(
                src_ref=src, dst_ref=dst, send_sem=sems.at[index], recv_sem=recv_sems.at[index],
                device_id=target[turn], device_id_type=MESH,
            ).wait()

        if turn == 0:
            pl.when(stay)(lambda: pltpu.make_async_copy(src, dst, self_sem.at[self_index]).wait())
            pl.when(leave)(remote)
        else:
            remote()

    mine = 2 * y + c
    vec_copy = [
        send(vec_in_ref, vec_all.at[mine], vec_s, vec_r, i, peer)
        for i, peer in enumerate((by_core, by_y, by_yc))
    ]
    vec_all[mine] = vec_in_ref[...]
    wh_copy = []
    shard = wq_ref.shape[0]
    own_rows = pl.ds(pl.multiple_of(mine * shard, shard), shard)
    for part in range(3):
        to = wh_ref.at[own_rows, pl.ds(part * PAIR, PAIR)]

        def columns(core):
            return wq_ref.at[:, pl.ds(pl.multiple_of(part * width + (2 * x + core) * PAIR, PAIR), PAIR)]

        for i, (peer, core) in enumerate(((by_core, 1 - c), (by_y, c), (by_yc, 1 - c))):
            wh_copy.append(send(columns(core), to, wh_s, wh_r, 3 * part + i, peer))
        copy = pltpu.make_async_copy(columns(c), to, wh_l.at[part])
        copy.start()
        wh_copy.append(copy)

    up_rows, down_rows = wu_ref.shape[0] // 4, wd_ref.shape[0] // 4
    parts = [(wo_ref, wo_all, wo_ref.shape[0], 0)]
    parts += [(wu_ref, wu_all, up_rows, i * up_rows) for i in range(4)]
    parts += [(wd_ref, wd_all, down_rows, i * down_rows) for i in range(4)]

    def at_owner(full, src, size, offset, owner):
        return full.at[pl.ds(pl.multiple_of(owner * src.shape[0] + offset, 32), size)]

    other = 2 * (1 - y) + c
    y_copy = []
    for i, (src, full, size, offset) in enumerate(parts):
        y_copy.append(
            send(src.at[pl.ds(offset, size)], at_owner(full, src, size, offset, mine), y_s, y_r, i, by_y)
        )
    n_copy, load_copy, put_copy = [], [], []
    for i, (src, full, tmp) in enumerate(((wo_ref, wo_all, wo_tmp), (wu_ref, wu_all, wu_tmp), (wd_ref, wd_all, wd_tmp))):
        n_copy.append(send(src, at_owner(full, src, src.shape[0], 0, mine), n_s, n_r, i, by_core))
        load_copy.append(pltpu.make_async_copy(src, tmp, load_sem.at[i]))
        load_copy[-1].start()

    def put(i):
        src, full, tmp = ((wo_ref, wo_all, wo_tmp), (wu_ref, wu_all, wu_tmp), (wd_ref, wd_all, wd_tmp))[i]
        load_copy[i].wait()
        put_copy.append(pltpu.make_async_copy(tmp, at_owner(full, src, src.shape[0], 0, mine), put_sem.at[i]))
        put_copy[-1].start()

    o_copy = []

    def forward(i):
        src, full, size, offset = parts[i]
        y_copy[i].wait()
        held = at_owner(full, src, size, offset, other)
        o_copy.append(send(held, held, o_s, o_r, i, by_core))

    blocks = order_ref.shape[0]
    lane = lax.broadcasted_iota(jnp.int32, (1, 128), 1)
    slots = jnp.zeros((1, 128), jnp.int32)
    for t in range(blocks):
        dc, dx, turn, half = t // 8, t // 4 % 2, t // 2 % 2, t % 2
        core, side = (1 - c if dc else c), (1 - x if dx else x)
        stored = 2 * (2 * (2 * core + (1 - upper if turn else upper)) + side) + half
        slots = jnp.where(lane == order_ref[stored], t, slots)

    docs_copy = {}
    for turn in range(2):
        landed(docs_in_ref.at[block[turn]], docs.at[0, turn], docs_s, docs_r, turn, turn, per_turn)
    docs_copy["x"] = send(docs.at[0], docs.at[1], docs_s, docs_r, 2, by_x)
    docs_copy["c"] = send(docs.at[0], docs.at[2], docs_s, docs_r, 3, by_core)

    for copy in vec_copy:
        copy.wait()
    vec_width = vec_in_ref.shape[1]
    for j in range(4):
        for i in range(6):
            vec_ref[i : i + 1, j * vec_width : (j + 1) * vec_width] = vec_all[j, i : i + 1].astype(f32)
        for i in range(4):
            at = (4 * j + i) * vec_width
            ub_ref[:, at : at + vec_width] = vec_all[j, 6 + i : 7 + i].astype(f32)
    vec_ref[6:8] = jnp.zeros((2, width), f32)
    for copy in wh_copy:
        copy.wait()

    docs_copy["x"].wait()
    docs_copy["f"] = send(docs.at[1], docs.at[3], docs_s, docs_r, 4, by_core)

    def finish_docs():
        docs_copy["c"].wait()
        docs_copy["f"].wait()
        for g in range(4):
            core, side = (1 - c if g // 2 else c), (1 - x if g % 2 else x)
            for turn in range(2):
                docs_true[2 * (2 * core + (1 - upper if turn else upper)) + side] = docs[g, turn]
        numbers = docs_true[...]
        first = jnp.zeros_like(numbers)
        for d in range(1, blocks):
            before = jnp.sum((numbers < d).astype(jnp.int32), axis=(0, 1, 2), keepdims=True)
            first = jnp.where(numbers == d, before, first)
        docs_true[...] = first
        low = jnp.zeros((1, 128), jnp.int32)
        for b in range(blocks):
            line = docs_true[b // 2]
            at = 2 * (b % 2)
            line = jnp.concatenate([line[at : at + 1], line[at + 1 : at + 2]], axis=1)
            start_ref[b] = line
            low = jnp.where(lane == b, line[:, :1] // BLK, low)
        high = jnp.zeros((1, 128), jnp.int32) - 1
        for b in range(blocks):
            high = high + (low[:, b : b + 1] <= lane).astype(jnp.int32)
        tab_ref[...] = jnp.concatenate([low, high, slots, jnp.zeros((5, 128), jnp.int32)], axis=0)

    x_copy, c_copy, f_copy = [], [], []

    def relay(i):
        src, dst = piece(i)
        landed(src, dst, z_s, z_r, i, i // per_turn, i)
        part = pl.ds(i * HEAD_CHUNK, HEAD_CHUNK)
        x_copy.append(send(rows.at[0, part], rows.at[1, part], x_s, x_r, i, by_x))
        c_copy.append(send(rows.at[0, part], rows.at[2, part], c_s, c_r, i, by_core))

    def relay_far(i):
        x_copy[i].wait()
        part = pl.ds(i * HEAD_CHUNK, HEAD_CHUNK)
        f_copy.append(send(rows.at[1, part], rows.at[3, part], f_s, f_r, i, by_core))

    def compute(g, i):
        count = rows.shape[1]
        unit, _ = norm_parts(rows[g, i * HEAD_CHUNK : (i + 1) * HEAD_CHUNK].astype(f32))
        at = slice(g * count + i * HEAD_CHUNK, g * count + (i + 1) * HEAD_CHUNK)
        u_ref[at] = unit.astype(bf16)
        low = (unit * vec_ref[0:1] + vec_ref[1:2]).astype(bf16)
        qkv = jnp.dot(low, wh_ref[...], preferred_element_type=f32)
        q_ref[at] = (qkv[:, :PAIR] * (SCORE_SCALE * LOG2E)).astype(bf16)
        k = qkv[:, PAIR : 2 * PAIR].astype(bf16)
        v = qkv[:, 2 * PAIR :].astype(bf16)
        k_ref[at] = k
        v_ref[at] = v
        kt_ref[:, at] = k.T
        vt_ref[:, at] = v.T

    for i in range(chunks + 2):
        if i < chunks:
            relay(i)
            compute(0, i)
        if 1 <= i <= chunks:
            relay_far(i - 1)
            compute(1, i - 1)
            c_copy[i - 1].wait()
            compute(2, i - 1)
        if i >= 2:
            f_copy[i - 2].wait()
            compute(3, i - 2)
        if i == 1:
            finish_docs()
        if 2 <= i < 5:
            put(i - 2)
        if i >= 3 and i - 3 < len(parts):
            forward(i - 3)
    own_ref[...] = rows[0]
    for i in range(chunks - 1, len(parts)):
        forward(i)
    for copy in n_copy + put_copy + o_copy:
        copy.wait()


def head(x_in, docs_in, order, vec_in, w_qkv, w_out, w_up, w_down):
    width = x_in.shape[-1]
    count = 2 * x_in.shape[2]
    total = 4 * count
    shard = w_qkv.shape[0]
    chunks = count // HEAD_CHUNK
    blocks = order.shape[0]
    vmem, any_ = pl.BlockSpec(memory_space=pltpu.VMEM), pl.BlockSpec(memory_space=pl.ANY)
    smem = pl.BlockSpec(memory_space=pltpu.SMEM)
    dma, buf, shape = pltpu.SemaphoreType.DMA, pltpu.VMEM, jax.ShapeDtypeStruct
    return pl.pallas_call(
        head_kernel,
        in_specs=[any_, vmem, smem, vmem, any_, any_, any_, any_],
        out_specs=[vmem] * 12 + [any_] * 3,
        out_shape=[
            shape((total, PAIR), bf16),
            shape((total, PAIR), bf16),
            shape((PAIR, total), bf16),
            shape((total, PAIR), bf16),
            shape((PAIR, total), bf16),
            shape((total, width), bf16),
            shape((count, width), bf16),
            shape((width, 3 * PAIR), bf16),
            shape((8, width), f32),
            shape((1, 4 * w_down.shape[0]), f32),
            shape((blocks, 1, BLK), jnp.int32),
            shape((8, 128), jnp.int32),
            shape((4 * w_out.shape[0], w_out.shape[1]), bf16),
            shape((4 * w_up.shape[0], w_up.shape[1]), bf16),
            shape((4 * w_down.shape[0], w_down.shape[1]), bf16),
        ],
        scratch_shapes=[
            buf((4, count, width), bf16),
            buf((4, 2) + docs_in.shape[1:], jnp.int32),
            buf((blocks // 2,) + docs_in.shape[1:], jnp.int32),
            buf((4,) + vec_in.shape, bf16),
            buf(w_out.shape, bf16),
            buf(w_up.shape, bf16),
            buf(w_down.shape, bf16),
        ]
        + [dma((chunks,))] * 8
        + [dma((5,)), dma((5,)), dma((3,)), dma((3,)), dma((9,)), dma((9,)), dma((3,))]
        + [dma((9,)), dma((9,)), dma((3,)), dma((3,)), dma((9,)), dma((9,)), dma((3,)), dma((3,))]
        + [dma((chunks // 2 + 1,))],
        compiler_params=pltpu.CompilerParams(
            collective_id=1, has_side_effects=True, vmem_limit_bytes=56 * 1024 * 1024
        ),
        name="head",
    )(x_in, docs_in, order, vec_in, w_qkv, w_out, w_up, w_down)
TAIL_CHUNK = 128
PIECES = 3


def tail_kernel(
    dh_ref, x_ref, dmid_ref, gain_ref, keep_ref, from_y_ref, from_x_ref, from_xy_ref, gw_ref, small_ref,
    dx_ref, gd_ref, gu_ref, go_ref, gq_ref, gvec_ref, gub_ref,
    core_buf, own_dh, x_out, x_buf, dx_out, home_buf,
    gsum, gz1s, gz1r, gz2s, gz2r, gfull,
    wy, ws, wz1s, wz1r, wz2s, wz2r, wfull, wall,
    small_out, small_in,
    local_sem, self_sem, core_s, core_r, x_s, x_r, home_s, home_r, g_s, g_r, w_s, w_r, s_s, s_r,
):
    z, x, y, c = (lax.axis_index(name) for name in AXES)
    odd, upper = lax.rem(z, 2), lax.div(z, 2)
    width = x_ref.shape[1]
    chunks = x_ref.shape[0] // TAIL_CHUNK
    per_turn = chunks // 2
    by_core, by_x, by_y, by_xc = {"c": 1 - c}, {"x": 1 - x}, {"y": 1 - y}, {"x": 1 - x, "c": 1 - c}
    by_z1, by_z2 = {"z": z + 1 - 2 * odd}, {"z": z + 2 - 4 * upper}
    home = [{"z": 2 * c + upper, "c": odd}, {"z": 2 * c + 1 - upper, "c": odd}]
    origin = [{"z": 2 * odd + c, "c": upper}, {"z": 2 * (1 - odd) + c, "c": upper}]
    stay = (c == upper) & (odd == c)
    greet(
        [by_core, by_x, by_y, by_xc, by_z1, by_z2, home[1], origin[1]],
        [home[0], origin[0]],
        jnp.logical_not(stay),
    )
    small_peers = [by_x, by_core, by_y, by_z1, by_z2]
    s_copy = [send(small_ref, small_in.at[0], s_s, s_r, 0, small_peers[0])]
    to_core, locals_ = [], []
    for i in range(chunks):
        part = pl.ds(i * TAIL_CHUNK, TAIL_CHUNK)
        to_core.append(
            send(dh_ref.at[pl.ds(2, 2), part], core_buf.at[:, part], core_s, core_r, i, by_core)
        )
        copy = pltpu.make_async_copy(dh_ref.at[pl.ds(0, 2), part], own_dh.at[:, part], local_sem.at[i])
        copy.start()
        locals_.append(copy)
    w_copy = {}
    w_copy["y"] = send(gw_ref.at[pl.ds(2 * (1 - y), 2)], wy, w_s, w_r, 0, by_y)
    g_copy = {}

    def g_start(p):
        for half in range(2):
            part = pl.ds(96 * half, 96)
            gsum[p, part] = (
                keep_ref[p, part].astype(f32)
                + from_y_ref[p, part].astype(f32)
                + from_x_ref[p, part].astype(f32)
                + from_xy_ref[p, part].astype(f32)
            )
        gz1s[p] = gsum[p, pl.ds(pl.multiple_of(96 * (1 - odd), 16), 96)].astype(bf16)
        g_copy["z1", p] = send(gz1s.at[p], gz1r.at[p], g_s, g_r, 5 * p, by_z1)

    mine_half = pl.multiple_of(96 * odd, 16)
    mine_quarter = pl.multiple_of(96 * odd + 48 * upper, 16)
    give_quarter = pl.multiple_of(96 * odd + 48 * (1 - upper), 16)

    def g_second(p):
        g_copy["z1", p].wait()
        gsum[p, pl.ds(mine_half, 96)] += gz1r[p].astype(f32)
        gz2s[p] = gsum[p, pl.ds(give_quarter, 48)].astype(bf16)
        g_copy["z2", p] = send(gz2s.at[p], gz2r.at[p], g_s, g_r, 5 * p + 1, by_z2)

    def g_third(p):
        g_copy["z2", p].wait()
        part = pl.ds(mine_quarter, 48)
        gfull[p, x, part] = (gsum[p, part] + gz2r[p].astype(f32)).astype(bf16)
        place_ = gfull.at[p, x, part]
        g_copy["z2b", p] = send(place_, place_, g_s, g_r, 5 * p + 2, by_z2)

    def g_fourth(p):
        g_copy["z2b", p].wait()
        place_ = gfull.at[p, x, pl.ds(mine_half, 96)]
        g_copy["z1b", p] = send(place_, place_, g_s, g_r, 5 * p + 3, by_z1)

    def g_fifth(p):
        g_copy["z1b", p].wait()
        g_copy["x", p] = send(gfull.at[p, x], gfull.at[p, x], g_s, g_r, 5 * p + 4, by_x)

    def w_second():
        w_copy["y"].wait()
        for i in range(2):
            ws[i] = gw_ref[2 * y + i].astype(f32) + wy[i].astype(f32)
        wz1s[...] = ws[1 - odd].astype(bf16)
        w_copy["z1"] = send(wz1s, wz1r, w_s, w_r, 1, by_z1)

    def w_third():
        w_copy["z1"].wait()
        ws[odd] += wz1r[...].astype(f32)
        wz2s[...] = ws[odd, pl.ds(pl.multiple_of(64 * (1 - upper), 64), 64)].astype(bf16)
        w_copy["z2"] = send(wz2s, wz2r, w_s, w_r, 2, by_z2)

    def w_fourth():
        w_copy["z2"].wait()
        part = pl.ds(pl.multiple_of(64 * upper, 64), 64)
        wfull[odd, part] = (ws[odd, part] + wz2r[...].astype(f32)).astype(bf16)
        place_ = wfull.at[odd, part]
        w_copy["z2b"] = send(place_, place_, w_s, w_r, 3, by_z2)

    def w_fifth():
        w_copy["z2b"].wait()
        w_copy["z1b"] = send(wfull.at[odd], wfull.at[odd], w_s, w_r, 4, by_z1)

    def w_sixth():
        w_copy["z1b"].wait()
        mine = 2 * x + c
        w_copy["core"] = send(wfull.at[1 - c], wall.at[mine], w_s, w_r, 5, by_core)
        w_copy["x"] = send(wfull.at[c], wall.at[mine], w_s, w_r, 6, by_x)
        w_copy["xc"] = send(wfull.at[1 - c], wall.at[mine], w_s, w_r, 7, by_xc)

    def s_next(step):
        s_copy[step].wait()
        before = small_ref[...] if step == 0 else small_out[step - 1]
        small_out[step] = before + small_in[step]
        if step + 1 < len(small_peers):
            s_copy.append(
                send(small_out.at[step], small_in.at[step + 1], s_s, s_r, step + 1, small_peers[step + 1])
            )

    x_copy, home_copy = [], []

    def add_core(i):
        part = pl.ds(i * TAIL_CHUNK, TAIL_CHUNK)
        to_core[i].wait()
        locals_[i].wait()
        x_out[part] = (own_dh[1, part].astype(f32) + core_buf[1, part].astype(f32)).astype(bf16)
        x_copy.append(send(x_out.at[part], x_buf.at[part], x_s, x_r, i, by_x))

    def finish(i):
        part = pl.ds(i * TAIL_CHUNK, TAIL_CHUNK)
        x_copy[i].wait()
        d_low = own_dh[0, part].astype(f32) + core_buf[0, part].astype(f32) + x_buf[part].astype(f32)
        unit, inv = norm_parts(x_ref[part].astype(f32))
        scaled = d_low * gain_ref[...]
        dx = dmid_ref[part] + inv * (
            scaled
            - jnp.mean(scaled, axis=-1, keepdims=True)
            - unit * jnp.mean(scaled * unit, axis=-1, keepdims=True)
        )
        dx_out[part] = dx.astype(bf16)
        turn, row = i // per_turn, (i % per_turn) * TAIL_CHUNK
        target = home_buf.at[upper, pl.ds(row, TAIL_CHUNK)]
        if turn == 0:
            @pl.when(stay)
            def _():
                pltpu.make_async_copy(dx_out.at[part], target, self_sem.at[i]).start()

            @pl.when(jnp.logical_not(stay))
            def _():
                send(dx_out.at[part], target, home_s, home_r, i, home[0])
        else:
            send(dx_out.at[part], target, home_s, home_r, i, home[1])

    def arrive(i):
        part = pl.ds(i * TAIL_CHUNK, TAIL_CHUNK)
        turn, row = i // per_turn, (i % per_turn) * TAIL_CHUNK
        block = odd if turn == 0 else 1 - odd
        landed = home_buf.at[block, pl.ds(row, TAIL_CHUNK)]

        def remote():
            copy = pltpu.make_async_remote_copy(
                src_ref=dx_out.at[part], dst_ref=landed, send_sem=home_s.at[i], recv_sem=home_r.at[i],
                device_id=home[turn], device_id_type=MESH,
            )
            copy.wait_send()
            copy.wait_recv()

        if turn == 0:
            @pl.when(stay)
            def _():
                pltpu.make_async_copy(dx_out.at[part], landed, self_sem.at[i]).wait()

            pl.when(jnp.logical_not(stay))(remote)
        else:
            remote()
        dx_ref[block, pl.ds(row, TAIL_CHUNK)] = home_buf[block, pl.ds(row, TAIL_CHUNK)].astype(f32)

    g_start(0)
    add_core(0)
    g_start(1)
    add_core(1)
    g_start(2)
    add_core(2)
    s_next(0)
    s_next(1)
    g_second(0)
    w_second()
    g_second(1)
    g_second(2)
    finish(0)
    add_core(3)
    s_next(2)
    g_third(0)
    finish(1)
    add_core(4)
    w_third()
    g_third(1)
    g_third(2)
    s_next(3)
    finish(2)
    add_core(5)
    g_fourth(0)
    w_fourth()
    finish(3)
    add_core(6)
    s_next(4)
    g_fourth(1)
    g_fourth(2)
    w_fifth()
    finish(4)
    add_core(7)
    g_fifth(0)
    finish(5)
    w_sixth()
    g_fifth(1)
    finish(6)
    g_fifth(2)
    finish(7)
    w_copy["core"].wait()
    w_copy["x"].wait()
    w_copy["xc"].wait()
    wall[2 * x + c] = wfull[c]
    for pair in range(4):
        for part in range(3):
            gq_ref[:, part * width + pair * PAIR : part * width + (pair + 1) * PAIR] = wall[
                pair, :, part * PAIR : (part + 1) * PAIR
            ].astype(f32)
    shard = go_ref.shape[0]
    lanes = pl.ds(pl.multiple_of(shard * (2 * y + c), shard), shard)
    for i in range(6):
        gvec_ref[i : i + 1, :] = small_out[4, i : i + 1, lanes]
    gub_ref[...] = small_out[4, pl.ds(6 + 2 * y + c, 1), :]
    for i in range(chunks):
        arrive(i)
    for p in range(PIECES):
        g_copy["x", p].wait()
    flat = gd_ref.shape[0] + (gu_ref.shape[1] // width + 1) * shard
    for row in range(0, flat, 64):
        p, rest = divmod(row, flat // PIECES)
        side, inner = divmod(rest, flat // PIECES // 2)
        value = gfull[p, side, inner : inner + 64].astype(f32)
        if row < gd_ref.shape[0]:
            gd_ref[row : row + 64] = value
        elif row < flat - shard:
            t, r = divmod(row - gd_ref.shape[0], shard)
            gu_ref[r : r + 64, t * width : (t + 1) * width] = value
        else:
            r = row - (flat - shard)
            go_ref[r : r + 64] = value


def tail(dh, x, dmid, gain, keep, from_y, from_x, from_xy, gw, small, ff_shard):
    count, width = x.shape
    shard = gw.shape[1]
    half = count // 2
    chunks = count // TAIL_CHUNK
    sixth = keep.shape[1]
    vmem = pl.BlockSpec(memory_space=pltpu.VMEM)
    dma = pltpu.SemaphoreType.DMA
    buf = pltpu.VMEM
    return pl.pallas_call(
        tail_kernel,
        in_specs=[pl.BlockSpec(memory_space=pl.ANY)] + [vmem] * 9,
        out_specs=[vmem] * 7,
        out_shape=[
            jax.ShapeDtypeStruct((2, half, width), f32),
            jax.ShapeDtypeStruct((ff_shard, width), f32),
            jax.ShapeDtypeStruct((shard, 4 * ff_shard), f32),
            jax.ShapeDtypeStruct((shard, width), f32),
            jax.ShapeDtypeStruct((shard, 3 * width), f32),
            jax.ShapeDtypeStruct((8, shard), f32),
            jax.ShapeDtypeStruct((1, ff_shard), f32),
        ],
        scratch_shapes=[
            buf((2, count, width), bf16),
            buf((2, count, width), bf16),
            buf((count, width), bf16),
            buf((count, width), bf16),
            buf((count, width), bf16),
            buf((2, half, width), bf16),
            buf((PIECES, sixth, width), f32),
            buf((PIECES, sixth // 2, width), bf16),
            buf((PIECES, sixth // 2, width), bf16),
            buf((PIECES, sixth // 4, width), bf16),
            buf((PIECES, sixth // 4, width), bf16),
            buf((PIECES, 2, sixth, width), bf16),
            buf((2, shard, 3 * PAIR), bf16),
            buf((2, shard, 3 * PAIR), f32),
            buf((shard, 3 * PAIR), bf16),
            buf((shard, 3 * PAIR), bf16),
            buf((shard // 2, 3 * PAIR), bf16),
            buf((shard // 2, 3 * PAIR), bf16),
            buf((2, shard, 3 * PAIR), bf16),
            buf((4, shard, 3 * PAIR), bf16),
            buf((5,) + small.shape, f32),
            buf((5,) + small.shape, f32),
            dma((chunks,)),
            dma((chunks // 2,)),
            dma((chunks,)),
            dma((chunks,)),
            dma((chunks,)),
            dma((chunks,)),
            dma((chunks,)),
            dma((chunks,)),
            dma((5 * PIECES,)),
            dma((5 * PIECES,)),
            dma((8,)),
            dma((8,)),
            dma((5,)),
            dma((5,)),
        ],
        compiler_params=pltpu.CompilerParams(
            collective_id=5, has_side_effects=True, vmem_limit_bytes=56 * 1024 * 1024
        ),
        name="tail",
    )(dh, x, dmid, gain, keep, from_y, from_x, from_xy, gw, small)
def stack_rows(members, width, count):
    at, total = 0, 0
    for member in members:
        rows = member.reshape(-1, width)
        total = total + jnp.pad(rows, ((at, count - at - rows.shape[0]), (0, 0)))
        at += rows.shape[0]
    return total


def place(z, x, y, c):
    return ((z * SIZES[1] + x) * SIZES[2] + y) * SIZES[3] + c


def everyone():
    return [
        (z, x, y, c)
        for z in range(SIZES[0])
        for x in range(SIZES[1])
        for y in range(SIZES[2])
        for c in range(SIZES[3])
    ]


def gather_pairs(turn):
    return [
        (place(z, x, y, c), place(2 * ((z % 2) ^ turn) + c, x, y, z // 2))
        for z, x, y, c in everyone()
    ]


def swap_pairs(dx, dy, dc):
    return [(place(z, x, y, c), place(z, x ^ dx, y ^ dy, c ^ dc)) for z, x, y, c in everyone()]


def move(value, pairs):
    return lax.ppermute(value, AXES, pairs)


def swap(value, dx=0, dy=0, dc=0):
    return move(value, swap_pairs(dx, dy, dc))


def to_pair(value, odd):
    return [
        move(lax.dynamic_index_in_dim(value, odd ^ turn, 0, keepdims=False)[0], gather_pairs(turn))
        for turn in range(2)
    ]


def from_pair(value, odd):
    back = [move(value[turn], [(b, a) for a, b in gather_pairs(turn)]) for turn in range(2)]
    first = jnp.where(odd == 0, back[0], back[1])
    second = jnp.where(odd == 0, back[1], back[0])
    return jnp.stack([first, second])[:, None]


def paired_body(
    inputs, out_grad, segment_ids, block_order, w_qkv, w_out, w_up, w_down,
    norm1_gain, norm1_bias, norm2_gain, norm2_bias, out_bias, up_bias, down_bias,
):
    z, x, y, c = (lax.axis_index(name) for name in AXES)
    odd = z % 2
    rows, width = inputs.shape[2], inputs.shape[3]
    shard = norm1_gain.shape[0]
    vectors = stack_rows(
        [norm1_gain, norm1_bias, norm2_gain, norm2_bias, out_bias, down_bias, up_bias], shard, 16
    )
    (
        q, k, kt, v, vt, unit, own_x, w_heads, vecs, full_ubias, start, tab, full_out, full_up, full_down
    ) = head(
        inputs, segment_ids.reshape(2, -1, 128), block_order, vectors, w_qkv, w_out, w_up, w_down
    )
    gain_one, bias_one = vecs[0:1], vecs[1:2]
    groups = jnp.arange(4, dtype=jnp.int32)
    pair_of = 2 * (x ^ (groups % 2)) + (c ^ (groups // 2))

    dy_piece = to_pair(out_grad, odd)
    o, ot, lse = attend(tab, q, start, k, vt)
    o = o.reshape(4, -1, PAIR)
    attn = jnp.stack([o[0], swap(o[1], dx=1), swap(o[2], dc=1), swap(o[3], dx=1, dc=1)])

    own_dy = jnp.concatenate(dy_piece, axis=0)
    result, d_o, d_middle, g_flat, g_vecs, g_ubias = feed(
        pair_of, attn, own_x, own_dy, full_out, full_up, full_down, vecs, full_ubias, 4
    )
    outputs = from_pair(result.reshape(2, rows, width), odd)

    d_o = jnp.concatenate([d_o[0], swap(d_o[1], dx=1), swap(d_o[2], dc=1), swap(d_o[3], dx=1, dc=1)])
    g_flat = g_flat.reshape((2, 2) + g_flat.shape[1:])
    given = lax.dynamic_index_in_dim(g_flat, 1 - c, 1, keepdims=False)
    kept = lax.dynamic_index_in_dim(g_flat, c, 1, keepdims=False)
    flat = (kept.astype(f32) + swap(given, dc=1).astype(f32)).astype(bf16)
    flat = flat.reshape(2, PIECES, 2, -1, width)

    def quarter(dy, dx):
        part = lax.dynamic_index_in_dim(flat, y ^ dy, 0, keepdims=False)
        return lax.dynamic_index_in_dim(part, x ^ dx, 1, keepdims=False)

    from_y, from_x, from_xy = (
        swap(quarter(1, 0), dy=1), swap(quarter(0, 1), dx=1), swap(quarter(1, 1), dy=1, dx=1)
    )
    dh, g_heads, g_norm = attend_back(
        tab, k, kt, v, unit, w_heads, q, start, d_o, ot, lse, gain_one, bias_one, 4
    )
    small = stack_rows([g_norm, g_vecs[1:3], g_vecs[0:1], g_vecs[3:4], g_ubias], width, 16)
    dx, grad_down, grad_up, grad_out, grad_qkv, g_vec, g_ub = tail(
        dh.reshape(4, -1, width), own_x, d_middle, gain_one, quarter(0, 0), from_y, from_x, from_xy,
        g_heads, small, w_down.shape[0],
    )
    return (
        outputs, dx[:, None], grad_qkv, grad_out, grad_up, grad_down,
        g_vec[0], g_vec[1], g_vec[2], g_vec[3], g_vec[4], g_ub[0], g_vec[5],
    )


def solution(mesh):
    paired = mesh.shape["ctx"] == SIZES[0] * SIZES[1] and mesh.shape["fsdp"] == SIZES[2] * SIZES[3]
    if paired:
        mesh = Mesh(mesh.devices.reshape(SIZES), AXES)
        ctx, fsdp, program = ("z", "x"), ("y", "c"), paired_body
    else:
        ctx, fsdp, program = "ctx", "fsdp", general_body
    tokens = P(None, fsdp, ctx, None)
    matrix, vector = P(fsdp, None), P(fsdp)
    return jax.shard_map(
        program,
        mesh=mesh,
        in_specs=(tokens, tokens, P(None, fsdp, ctx), P()) + (matrix,) * 4 + (vector,) * 7,
        out_specs=(tokens, tokens) + (matrix,) * 4 + (vector,) * 7,
        check_vma=False,
    )
```

```python
import functools
import math

import jax
import jax.numpy as jnp
from jax import lax
from jax.experimental import pallas as pl
from jax.experimental.pallas import tpu as pltpu
from jax.sharding import Mesh
from jax.sharding import PartitionSpec as P

H = 8
HD = 64
BLK = 256
PAIR = 2 * HD

norm_eps = 1e-05
mask_fill = -1e30
LOG2E = math.log2(math.e)
LN2 = math.log(2.0)
SCORE_SCALE = 1.0 / math.sqrt(HD)

f32 = jnp.float32
bf16 = jnp.bfloat16


def contract(a, b, da, db):
    return lax.dot_general(a, b, (((da,), (db,)), ((), ())), preferred_element_type=f32)


def norm_parts(values):
    center = values - jnp.mean(values, axis=-1, keepdims=True)
    spread = jnp.mean(center * center, axis=-1, keepdims=True)
    inv = lax.rsqrt(spread + norm_eps)
    return center * inv, inv


def whole(shape):
    zeros = (0,) * len(shape)
    return pl.BlockSpec(shape, lambda *_: zeros)


def two_heads(block):
    zero = jnp.zeros((HD, block.shape[1]), block.dtype)
    return jnp.concatenate(
        [jnp.concatenate([block[:HD], zero], axis=0), jnp.concatenate([zero, block[HD:]], axis=0)], axis=1
    )


EXTRA = 16


def attend_kernel(tab_ref, qt_ref, start_ref, k_ref, vt_ref, o_ref, ot_ref, lse_ref, acc, top):
    qb = pl.program_id(0)
    both = two_heads(qt_ref[...])
    start = jnp.concatenate([start_ref[0], start_ref[0]], axis=1)
    row = lax.broadcasted_iota(jnp.int32, (BLK, 2 * BLK), 0)
    ones = jnp.ones((EXTRA, 2 * BLK), bf16)

    def place_of(kb):
        return pl.ds(pl.multiple_of(tab_ref[2, jnp.maximum(kb, 0)] * BLK, BLK), BLK)

    def visit(kb, first):
        places = [place_of(kb), place_of(kb - 1)]
        terms = []
        for i in range(2):
            allowed = row >= start - (kb - i) * BLK
            if first and i == 0:
                col = lax.broadcasted_iota(jnp.int32, (BLK, 2 * BLK), 1)
                allowed = allowed & (row <= jnp.bitwise_and(col, BLK - 1))
            st = jnp.dot(k_ref[places[i], :], both, preferred_element_type=f32)
            terms.append(jnp.where(allowed, st, mask_fill))
        peak = jnp.maximum(
            jnp.max(terms[0], axis=0, keepdims=True), jnp.max(terms[1], axis=0, keepdims=True)
        )
        if not first:
            old = top[...]
            peak = jnp.maximum(old, peak)
            shrink = jnp.exp2(old - peak)
        top[...] = peak
        probs = jnp.concatenate([jnp.exp2(term - peak).astype(bf16) for term in terms], axis=0)
        vt = jnp.concatenate([vt_ref[:, places[0]], vt_ref[:, places[1]]], axis=1)
        for head in range(2):
            cols = slice(head * BLK, (head + 1) * BLK)
            left = jnp.concatenate([vt[head * HD : (head + 1) * HD], ones], axis=0)
            part = jnp.dot(left, probs[:, cols], preferred_element_type=f32)
            acc[head] = part if first else acc[head] * shrink[:, cols] + part

    visit(qb, True)

    def more(i, carry):
        visit(qb - 2 * i, False)
        return carry

    lax.fori_loop(1, (qb - tab_ref[0, qb]) // 2 + 1, more, 0)
    total = jnp.concatenate([acc[0, HD : HD + 1], acc[1, HD : HD + 1]], axis=1)
    lse_ref[0] = top[...] + jnp.log2(total)
    heads = jnp.concatenate([acc[h, :HD] / acc[h, HD : HD + 1] for h in range(2)], axis=0)
    ot_ref[0] = heads
    o_ref[...] = heads.T.astype(bf16)


def attend(tab, qt, start, k, vt):
    count = k.shape[0]
    blocks = count // BLK
    return pl.pallas_call(
        attend_kernel,
        grid_spec=pltpu.PrefetchScalarGridSpec(
            num_scalar_prefetch=1,
            grid=(blocks,),
            in_specs=[
                pl.BlockSpec((PAIR, BLK), lambda b, t: (0, t[2, b])),
                pl.BlockSpec((1, 1, BLK), lambda b, t: (b, 0, 0)),
                whole(k.shape),
                whole(vt.shape),
            ],
            out_specs=[
                pl.BlockSpec((BLK, PAIR), lambda b, t: (t[2, b], 0)),
                pl.BlockSpec((1, PAIR, BLK), lambda b, t: (b, 0, 0)),
                pl.BlockSpec((1, 1, 2 * BLK), lambda b, t: (b, 0, 0)),
            ],
            scratch_shapes=[
                pltpu.VMEM((2, HD + EXTRA, BLK), f32),
                pltpu.VMEM((1, 2 * BLK), f32),
            ],
        ),
        out_shape=[
            jax.ShapeDtypeStruct((count, PAIR), bf16),
            jax.ShapeDtypeStruct((blocks, PAIR, BLK), f32),
            jax.ShapeDtypeStruct((blocks, 1, 2 * BLK), f32),
        ],
        name="attend",
    )(tab, qt, start, k, vt)


def attend_back_kernel(
    tab_ref, k_ref, kt_ref, v_ref, u_ref, w_ref, qt_ref, start_ref, do_ref, ot_ref, lse_ref,
    gain_ref, bias_ref, dh_ref, gw_ref, gn_ref, dqt, dkt, dvt, dot, delta, total, sums,
):
    kb = pl.program_id(0)
    blocks = pl.num_programs(0)
    row = lax.broadcasted_iota(jnp.int32, (BLK, 2 * BLK), 0)

    def at(qb):
        return pl.ds(pl.multiple_of(tab_ref[2, qb] * BLK, BLK), BLK)

    @pl.when(kb == 0)
    def _():
        total[...] = jnp.zeros_like(total)
        sums[...] = jnp.zeros_like(sums)

        def prepare(qb, carry):
            dqt[qb] = jnp.zeros((PAIR, BLK), f32)
            turned = do_ref[at(qb), :].astype(f32).T
            dot[qb] = turned.astype(bf16)
            both = turned * ot_ref[qb]
            delta[qb] = jnp.concatenate(
                [
                    jnp.sum(both[:HD], axis=0, keepdims=True),
                    jnp.sum(both[HD:], axis=0, keepdims=True),
                ],
                axis=1,
            )
            return carry

        lax.fori_loop(0, blocks, prepare, 0)

    k = k_ref[...]
    v = v_ref[...]
    kt = kt_ref[...]

    def tile(qb, diagonal):
        qt = qt_ref[:, at(qb)]
        d_out = dot[qb]
        start = jnp.concatenate([start_ref[qb], start_ref[qb]], axis=1)
        st = jnp.dot(k, two_heads(qt), preferred_element_type=f32)
        dpt = jnp.dot(v, two_heads(d_out), preferred_element_type=f32)
        allowed = row >= start - kb * BLK
        if diagonal:
            col = lax.broadcasted_iota(jnp.int32, (BLK, 2 * BLK), 1)
            allowed = allowed & (row <= jnp.bitwise_and(col, BLK - 1))
        pt = jnp.exp2(jnp.where(allowed, st - lse_ref[qb], mask_fill))
        dst = (pt * (dpt - delta[qb])).astype(bf16)
        pt = pt.astype(bf16)
        for head in range(2):
            mine = slice(head * HD, (head + 1) * HD)
            cols = slice(head * BLK, (head + 1) * BLK)
            part_v = contract(d_out[mine], pt[:, cols], 1, 1)
            part_k = contract(qt[mine], dst[:, cols], 1, 1)
            if diagonal:
                dvt[mine] = part_v
                dkt[mine] = part_k
            else:
                dvt[mine] += part_v
                dkt[mine] += part_k
            dqt[qb, mine] += jnp.dot(kt[mine], dst[:, cols], preferred_element_type=f32)

    tile(kb, True)

    def visit(qb, carry):
        tile(qb, False)
        return carry

    lax.fori_loop(kb + 1, tab_ref[1, kb] + 1, visit, 0)
    dq = (dqt[kb] * SCORE_SCALE).T.astype(bf16)
    dk = (dkt[...] * LN2).T.astype(bf16)
    joined = jnp.concatenate([dq, dk, dvt[...].T.astype(bf16)], axis=1)
    dh_ref[...] = contract(joined, w_ref[...], 1, 1).astype(bf16)
    total[...] += contract(u_ref[...], joined, 0, 0)
    sums[...] += jnp.sum(joined.astype(f32), axis=0, keepdims=True)

    @pl.when(kb == blocks - 1)
    def _():
        shard = gw_ref.shape[1]
        for j in range(gw_ref.shape[0]):
            part = pl.ds(j * shard, shard)
            gw_ref[j] = (total[part] * gain_ref[part] + bias_ref[part] * sums[...]).astype(bf16)
            w = w_ref[part].astype(f32)
            for i, term in enumerate((w * total[part], w * sums[...])):
                column = jnp.sum(term, axis=1, keepdims=True)
                gn_ref[i : i + 1, part] = jnp.broadcast_to(column, (shard, shard)).T[:1]


def attend_back(tab, k, kt, v, unit, weight, qt, start, d_out, ot, lse, gain, bias, shards):
    count = k.shape[0]
    width = unit.shape[1]
    shard = width // shards
    gain, bias = gain.reshape(width, 1), bias.reshape(width, 1)
    blocks = count // BLK
    return pl.pallas_call(
        attend_back_kernel,
        grid_spec=pltpu.PrefetchScalarGridSpec(
            num_scalar_prefetch=1,
            grid=(blocks,),
            in_specs=[
                pl.BlockSpec((BLK, PAIR), lambda b, t: (t[2, b], 0)),
                pl.BlockSpec((PAIR, BLK), lambda b, t: (0, t[2, b])),
                pl.BlockSpec((BLK, PAIR), lambda b, t: (t[2, b], 0)),
                pl.BlockSpec((BLK, width), lambda b, t: (t[2, b], 0)),
                whole(weight.shape),
                whole(qt.shape),
                whole(start.shape),
                whole(d_out.shape),
                whole(ot.shape),
                whole(lse.shape),
                whole(gain.shape),
                whole(bias.shape),
            ],
            out_specs=[
                pl.BlockSpec((BLK, width), lambda b, t: (t[2, b], 0)),
                whole((shards, shard, 3 * PAIR)),
                whole((2, width)),
            ],
            scratch_shapes=[
                pltpu.VMEM((blocks, PAIR, BLK), f32),
                pltpu.VMEM((PAIR, BLK), f32),
                pltpu.VMEM((PAIR, BLK), f32),
                pltpu.VMEM((blocks, PAIR, BLK), bf16),
                pltpu.VMEM((blocks, 1, 2 * BLK), f32),
                pltpu.VMEM(weight.shape, f32),
                pltpu.VMEM((1, 3 * PAIR), f32),
            ],
        ),
        out_shape=[
            jax.ShapeDtypeStruct((count, width), bf16),
            jax.ShapeDtypeStruct((shards, shard, 3 * PAIR), bf16),
            jax.ShapeDtypeStruct((2, width), f32),
        ],
        name="attend_back",
    )(tab, k, kt, v, unit, weight, qt, start, d_out, ot, lse, gain, bias)


def layer_norm(values, gain_vec, offset):
    center = values - jnp.mean(values, axis=-1, keepdims=True)
    spread = jnp.mean(center * center, axis=-1, keepdims=True)
    return center * lax.rsqrt(spread + norm_eps) * gain_vec + offset


def gelu_exact(values):
    return 0.5 * values * (1.0 + lax.erf(values * (1.0 / math.sqrt(2.0))))


def score_block(query_heads, key_heads, query_doc, query_pos, key_doc, key_pos):
    raw_scores = jnp.einsum(
        "qhd,khd->hqk", query_heads, key_heads, preferred_element_type=jnp.float32
    ) * (1.0 / math.sqrt(HD))
    allowed = (query_doc[:, None] == key_doc[None, :]) & (key_pos[None, :] <= query_pos[:, None])
    return (raw_scores, allowed[None])


def soft_block(raw_scores, allowed, log_norm):
    return jnp.exp(jnp.where(allowed, raw_scores, mask_fill) - log_norm[:, :, None])


def row_log_norm(query_heads, key_blocks, doc_blocks, pos_blocks, query_doc, query_pos):

    def row_visit(running, block_item):
        row_top, row_sum = running
        key_heads, key_doc, key_pos = block_item
        raw_scores, allowed = score_block(
            query_heads, key_heads, query_doc, query_pos, key_doc, key_pos
        )
        masked = jnp.where(allowed, raw_scores, mask_fill)
        new_top = jnp.maximum(row_top, jnp.max(masked, axis=-1))
        fresh = jnp.sum(jnp.where(allowed, jnp.exp(masked - new_top[:, :, None]), 0.0), axis=-1)
        return ((new_top, row_sum * jnp.exp(row_top - new_top) + fresh), None)

    query_count = query_doc.shape[0]
    start = (
        jnp.full((H, query_count), mask_fill, jnp.float32),
        jnp.zeros((H, query_count), jnp.float32),
    )
    (row_top, row_sum), unused = lax.scan(row_visit, start, (key_blocks, doc_blocks, pos_blocks))
    return row_top + jnp.log(row_sum)


def attend_all(
    query_heads, key_blocks, value_blocks, doc_blocks, pos_blocks, query_doc, query_pos, log_norm
):

    def attend_visit(accum_out, block_item):
        key_heads, value_heads, key_doc, key_pos = block_item
        raw_scores, allowed = score_block(
            query_heads, key_heads, query_doc, query_pos, key_doc, key_pos
        )
        soft_low = soft_block(raw_scores, allowed, log_norm).astype(jnp.bfloat16)
        return (
            accum_out
            + jnp.einsum("hqk,khd->qhd", soft_low, value_heads, preferred_element_type=jnp.float32),
            None,
        )

    start = jnp.zeros(query_heads.shape, jnp.float32)
    accum_out, unused = lax.scan(
        attend_visit, start, (key_blocks, value_blocks, doc_blocks, pos_blocks)
    )
    return accum_out


def grad_block(
    query_heads,
    grad_heads,
    log_norm,
    row_delta,
    query_doc,
    query_pos,
    key_heads,
    value_heads,
    key_doc,
    key_pos,
):
    raw_scores, allowed = score_block(
        query_heads, key_heads, query_doc, query_pos, key_doc, key_pos
    )
    soft = soft_block(raw_scores, allowed, log_norm)
    grad_soft = jnp.einsum(
        "qhd,khd->hqk", grad_heads, value_heads, preferred_element_type=jnp.float32
    )
    grad_scores = (soft * (grad_soft - row_delta[:, :, None])).astype(jnp.bfloat16)
    score_scale = 1.0 / math.sqrt(HD)
    part_q = (
        jnp.einsum("hqk,khd->qhd", grad_scores, key_heads, preferred_element_type=jnp.float32)
        * score_scale
    )
    part_k = (
        jnp.einsum("hqk,qhd->khd", grad_scores, query_heads, preferred_element_type=jnp.float32)
        * score_scale
    )
    part_v = jnp.einsum(
        "hqk,qhd->khd", soft.astype(jnp.bfloat16), grad_heads, preferred_element_type=jnp.float32
    )
    return (part_q, part_k, part_v)


def general_body(
    inputs,
    out_grad,
    segment_ids,
    block_order,
    w_qkv,
    w_out,
    w_up,
    w_down,
    norm1_gain,
    norm1_bias,
    norm2_gain,
    norm2_bias,
    out_bias,
    up_bias,
    down_bias,
):
    gathered = (
        lax.all_gather(w_qkv, "fsdp", axis=0, tiled=True),
        lax.all_gather(w_out, "fsdp", axis=0, tiled=True),
        lax.all_gather(w_up, "fsdp", axis=0, tiled=True),
        lax.all_gather(w_down, "fsdp", axis=0, tiled=True),
        lax.all_gather(norm1_gain, "fsdp", axis=0, tiled=True),
        lax.all_gather(norm1_bias, "fsdp", axis=0, tiled=True),
        lax.all_gather(norm2_gain, "fsdp", axis=0, tiled=True),
        lax.all_gather(norm2_bias, "fsdp", axis=0, tiled=True),
        lax.all_gather(out_bias, "fsdp", axis=0, tiled=True),
        lax.all_gather(up_bias, "fsdp", axis=0, tiled=True),
        lax.all_gather(down_bias, "fsdp", axis=0, tiled=True),
    )
    full_qkv, full_out, full_up, full_down = (gathered[0], gathered[1], gathered[2], gathered[3])
    gain_one, bias_one, gain_two, bias_two, full_obias, full_ubias, full_dbias = [
        member.astype(jnp.float32) for member in gathered[4:]
    ]
    model_width = full_qkv.shape[0]
    local_rows = inputs.shape[2]
    ctx_count = lax.axis_size("ctx")
    seq_len = local_rows * ctx_count
    key_block = min(512, seq_len)
    block_count = seq_len // key_block
    ctx_index = lax.axis_index("ctx")
    row_ids = jnp.arange(local_rows, dtype=jnp.int32)
    own_blocks = lax.dynamic_slice_in_dim(block_order, 2 * ctx_index, 2)
    own_pos = own_blocks[row_ids // BLK] * BLK + row_ids % BLK
    all_ids = jnp.arange(seq_len, dtype=jnp.int32)
    all_pos = block_order[all_ids // BLK] * BLK + all_ids % BLK
    pos_blocks = all_pos.reshape(block_count, key_block)
    grad_sums = [jnp.zeros(member.shape, jnp.float32) for member in gathered]
    outputs_list = []
    input_grads = []
    for micro_idx in range(inputs.shape[0]):
        seq_in = inputs[micro_idx, 0].astype(jnp.float32)
        normed, norm1_pull = jax.vjp(layer_norm, seq_in, gain_one, bias_one)
        normed_low = normed.astype(jnp.bfloat16)
        qkv_out = jnp.dot(normed_low, full_qkv, preferred_element_type=jnp.float32).astype(
            jnp.bfloat16
        )
        query_heads = qkv_out[:, :model_width].reshape(local_rows, H, HD)
        kv_all, doc_all = (
            lax.all_gather(qkv_out[:, model_width:], "ctx", axis=0, tiled=True),
            lax.all_gather(segment_ids[micro_idx, 0], "ctx", axis=0, tiled=True),
        )
        doc_rows = doc_all[all_pos]
        query_doc = doc_all[own_pos]
        kv_heads = kv_all.reshape(block_count, key_block, 2, H, HD)
        key_blocks = kv_heads[:, :, 0]
        value_blocks = kv_heads[:, :, 1]
        doc_blocks = doc_rows.reshape(block_count, key_block)
        log_norm = row_log_norm(query_heads, key_blocks, doc_blocks, pos_blocks, query_doc, own_pos)
        attn_acc = attend_all(
            query_heads,
            key_blocks,
            value_blocks,
            doc_blocks,
            pos_blocks,
            query_doc,
            own_pos,
            log_norm,
        )
        attn_low = attn_acc.reshape(local_rows, model_width).astype(jnp.bfloat16)
        branch = jnp.dot(attn_low, full_out, preferred_element_type=jnp.float32) + full_obias
        middle = seq_in + branch
        normed_two, norm2_pull = jax.vjp(layer_norm, middle, gain_two, bias_two)
        normed_two_low = normed_two.astype(jnp.bfloat16)
        hidden = jnp.dot(normed_two_low, full_up, preferred_element_type=jnp.float32) + full_ubias
        active, gelu_pull = jax.vjp(gelu_exact, hidden)
        active_low = active.astype(jnp.bfloat16)
        result = middle + (
            jnp.dot(active_low, full_down, preferred_element_type=jnp.float32) + full_dbias
        )
        outputs_list.append(result.astype(jnp.bfloat16))
        grad_y = out_grad[micro_idx, 0]
        grad_y32 = grad_y.astype(jnp.float32)
        grad_sums[3] = grad_sums[3] + jnp.einsum(
            "rf,rd->fd", active_low, grad_y, preferred_element_type=jnp.float32
        )
        grad_sums[10] = grad_sums[10] + jnp.sum(grad_y32, axis=0)
        grad_active = jnp.einsum("rd,fd->rf", grad_y, full_down, preferred_element_type=jnp.float32)
        (grad_hidden,) = gelu_pull(grad_active)
        grad_hidden_low = grad_hidden.astype(jnp.bfloat16)
        grad_sums[2] = grad_sums[2] + jnp.einsum(
            "rd,rf->df", normed_two_low, grad_hidden_low, preferred_element_type=jnp.float32
        )
        grad_sums[9] = grad_sums[9] + jnp.sum(grad_hidden_low.astype(jnp.float32), axis=0)
        grad_normed_two = jnp.einsum(
            "rf,df->rd", grad_hidden_low, full_up, preferred_element_type=jnp.float32
        )
        grad_mid_ln, grad_gain_two, grad_bias_two = norm2_pull(grad_normed_two)
        grad_sums[6] = grad_sums[6] + grad_gain_two
        grad_sums[7] = grad_sums[7] + grad_bias_two
        grad_mid = grad_y32 + grad_mid_ln
        grad_mid_low = grad_mid.astype(jnp.bfloat16)
        grad_sums[1] = grad_sums[1] + jnp.einsum(
            "rd,re->de", attn_low, grad_mid_low, preferred_element_type=jnp.float32
        )
        grad_sums[8] = grad_sums[8] + jnp.sum(grad_mid_low.astype(jnp.float32), axis=0)
        grad_attn_low = jnp.einsum(
            "re,de->rd", grad_mid_low, full_out, preferred_element_type=jnp.float32
        ).astype(jnp.bfloat16)
        grad_heads = grad_attn_low.reshape(local_rows, H, HD)
        row_delta = jnp.sum(grad_heads.astype(jnp.float32) * attn_acc, axis=-1).T

        def back_visit(grad_query, block_item):
            key_heads, value_heads, key_doc, key_pos = block_item
            part_q, part_k, part_v = grad_block(
                query_heads,
                grad_heads,
                log_norm,
                row_delta,
                query_doc,
                own_pos,
                key_heads,
                value_heads,
                key_doc,
                key_pos,
            )
            joined = jnp.concatenate(
                [part_k.reshape(key_block, model_width), part_v.reshape(key_block, model_width)],
                axis=1,
            )
            return (grad_query + part_q, joined)

        grad_query, kv_terms = lax.scan(
            back_visit,
            jnp.zeros((local_rows, H, HD), jnp.float32),
            (key_blocks, value_blocks, doc_blocks, pos_blocks),
        )
        kv_grad = lax.psum_scatter(
            kv_terms.reshape(seq_len, 2 * model_width).astype(jnp.bfloat16),
            "ctx",
            scatter_dimension=0,
            tiled=True,
        ).astype(jnp.float32)
        grad_qkv_low = jnp.concatenate(
            [grad_query.reshape(local_rows, model_width), kv_grad], axis=1
        ).astype(jnp.bfloat16)
        grad_sums[0] = grad_sums[0] + jnp.einsum(
            "rd,re->de", normed_low, grad_qkv_low, preferred_element_type=jnp.float32
        )
        grad_normed = jnp.einsum(
            "re,de->rd", grad_qkv_low, full_qkv, preferred_element_type=jnp.float32
        )
        grad_in_ln, grad_gain_one, grad_bias_one = norm1_pull(grad_normed)
        grad_sums[4] = grad_sums[4] + grad_gain_one
        grad_sums[5] = grad_sums[5] + grad_bias_one
        input_grads.append(grad_mid + grad_in_ln)
    owned = (
        lax.psum_scatter(
            grad_sums[0].astype(jnp.bfloat16), "fsdp", scatter_dimension=0, tiled=True
        ).astype(jnp.float32),
        lax.psum_scatter(
            grad_sums[1].astype(jnp.bfloat16), "fsdp", scatter_dimension=0, tiled=True
        ).astype(jnp.float32),
        lax.psum_scatter(
            grad_sums[2].astype(jnp.bfloat16), "fsdp", scatter_dimension=0, tiled=True
        ).astype(jnp.float32),
        lax.psum_scatter(
            grad_sums[3].astype(jnp.bfloat16), "fsdp", scatter_dimension=0, tiled=True
        ).astype(jnp.float32),
        lax.psum_scatter(
            grad_sums[4].astype(jnp.bfloat16), "fsdp", scatter_dimension=0, tiled=True
        ).astype(jnp.float32),
        lax.psum_scatter(
            grad_sums[5].astype(jnp.bfloat16), "fsdp", scatter_dimension=0, tiled=True
        ).astype(jnp.float32),
        lax.psum_scatter(
            grad_sums[6].astype(jnp.bfloat16), "fsdp", scatter_dimension=0, tiled=True
        ).astype(jnp.float32),
        lax.psum_scatter(
            grad_sums[7].astype(jnp.bfloat16), "fsdp", scatter_dimension=0, tiled=True
        ).astype(jnp.float32),
        lax.psum_scatter(
            grad_sums[8].astype(jnp.bfloat16), "fsdp", scatter_dimension=0, tiled=True
        ).astype(jnp.float32),
        lax.psum_scatter(
            grad_sums[9].astype(jnp.bfloat16), "fsdp", scatter_dimension=0, tiled=True
        ).astype(jnp.float32),
        lax.psum_scatter(
            grad_sums[10].astype(jnp.bfloat16), "fsdp", scatter_dimension=0, tiled=True
        ).astype(jnp.float32),
    )
    summed = (
        lax.psum(owned[0].astype(jnp.bfloat16), "ctx").astype(jnp.float32),
        lax.psum(owned[1].astype(jnp.bfloat16), "ctx").astype(jnp.float32),
        lax.psum(owned[2].astype(jnp.bfloat16), "ctx").astype(jnp.float32),
        lax.psum(owned[3].astype(jnp.bfloat16), "ctx").astype(jnp.float32),
        lax.psum(owned[4].astype(jnp.bfloat16), "ctx").astype(jnp.float32),
        lax.psum(owned[5].astype(jnp.bfloat16), "ctx").astype(jnp.float32),
        lax.psum(owned[6].astype(jnp.bfloat16), "ctx").astype(jnp.float32),
        lax.psum(owned[7].astype(jnp.bfloat16), "ctx").astype(jnp.float32),
        lax.psum(owned[8].astype(jnp.bfloat16), "ctx").astype(jnp.float32),
        lax.psum(owned[9].astype(jnp.bfloat16), "ctx").astype(jnp.float32),
        lax.psum(owned[10].astype(jnp.bfloat16), "ctx").astype(jnp.float32),
    )
    return (
        jnp.stack(outputs_list)[:, None],
        jnp.stack(input_grads)[:, None],
        summed[0],
        summed[1],
        summed[2],
        summed[3],
        summed[4],
        summed[5],
        summed[6],
        summed[7],
        summed[8],
        summed[9],
        summed[10],
    )


AXES = ("z", "x", "y", "c")
SIZES = (4, 2, 2, 2)


MESH = pl.DeviceIdType.MESH


def send(src, dst, sems, recv_sems, index, peer):
    copy = pltpu.make_async_remote_copy(
        src_ref=src,
        dst_ref=dst,
        send_sem=sems.at[index],
        recv_sem=recv_sems.at[index],
        device_id=peer,
        device_id_type=MESH,
    )
    copy.start()
    return copy


def greet(peers, extra, extra_on):
    barrier = pltpu.get_barrier_semaphore()
    for peer in peers:
        pl.semaphore_signal(barrier, inc=1, device_id=peer, device_id_type=MESH)

    @pl.when(extra_on)
    def _():
        for peer in extra:
            pl.semaphore_signal(barrier, inc=1, device_id=peer, device_id_type=MESH)

    pl.semaphore_wait(barrier, len(peers) + jnp.where(extra_on, len(extra), 0))


HEAD_CHUNK = 128


def head_kernel(
    x_in_ref, dy_in_ref, docs_in_ref, order_ref, vec_in_ref, wq_ref, wo_ref, wu_ref, wd_ref,
    qt_ref, k_ref, kt_ref, v_ref, vt_ref, u_ref, own_ref, wh_ref, vec_ref, ub_ref, start_ref, tab_ref,
    wo_all, wu_all, wd_all, dy_ref,
    rows, docs, docs_true, vec_all, wo_tmp, wu_tmp, wd_tmp,
    z_s, z_r, x_s, x_r, c_s, c_r, f_s, f_r, docs_s, docs_r, vec_s, vec_r, wh_s, wh_r, wh_l,
    y_s, y_r, n_s, n_r, o_s, o_r, load_sem, put_sem, self_sem, d_s, d_r, d_self,
):
    z, x, y, c = (lax.axis_index(name) for name in AXES)
    odd, upper = lax.rem(z, 2), lax.div(z, 2)
    width = x_in_ref.shape[-1]
    chunks = rows.shape[1] // HEAD_CHUNK
    per_turn = chunks // 2
    by_core, by_x, by_y, by_yc = {"c": 1 - c}, {"x": 1 - x}, {"y": 1 - y}, {"y": 1 - y, "c": 1 - c}
    home = [{"z": 2 * c + upper, "c": odd}, {"z": 2 * c + 1 - upper, "c": odd}]
    target = [{"z": 2 * odd + c, "c": upper}, {"z": 2 * (1 - odd) + c, "c": upper}]
    block = [odd, 1 - odd]
    stay = (c == upper) & (odd == c)
    leave = jnp.logical_not(stay)
    greet([by_core, by_x, by_y, by_yc, home[1], target[1]], [home[0], target[0]], leave)

    def piece(i):
        turn, row = i // per_turn, (i % per_turn) * HEAD_CHUNK
        return (
            x_in_ref.at[block[turn], 0, pl.ds(row, HEAD_CHUNK)],
            rows.at[0, pl.ds(i * HEAD_CHUNK, HEAD_CHUNK)],
        )

    for turn in range(2):
        src, dst = docs_in_ref.at[block[turn]], docs.at[0, turn]

        def start_docs():
            send(src, dst, docs_s, docs_r, turn, target[turn])

        if turn == 0:
            pl.when(stay)(lambda: pltpu.make_async_copy(src, dst, self_sem.at[per_turn]).start())
            pl.when(leave)(start_docs)
        else:
            start_docs()
    for i in range(chunks):
        src, dst = piece(i)
        if i < per_turn:
            pl.when(stay)(lambda: pltpu.make_async_copy(src, dst, self_sem.at[i]).start())
            pl.when(leave)(lambda: send(src, dst, z_s, z_r, i, target[0]) and None)
        else:
            send(src, dst, z_s, z_r, i, target[1])

    def piece_dy(i):
        turn, row = i // per_turn, (i % per_turn) * HEAD_CHUNK
        return (
            dy_in_ref.at[block[turn], 0, pl.ds(row, HEAD_CHUNK)],
            dy_ref.at[pl.ds(i * HEAD_CHUNK, HEAD_CHUNK)],
        )

    def send_dy(i):
        src, dst = piece_dy(i)
        if i < per_turn:
            pl.when(stay)(lambda: pltpu.make_async_copy(src, dst, d_self.at[i]).start())
            pl.when(leave)(lambda: send(src, dst, d_s, d_r, i, target[0]) and None)
        else:
            send(src, dst, d_s, d_r, i, target[1])

    def land_dy(i):
        src, dst = piece_dy(i)

        def remote():
            pltpu.make_async_remote_copy(
                src_ref=src, dst_ref=dst, send_sem=d_s.at[i], recv_sem=d_r.at[i],
                device_id=target[i // per_turn], device_id_type=MESH,
            ).wait()

        if i < per_turn:
            pl.when(stay)(lambda: pltpu.make_async_copy(src, dst, d_self.at[i]).wait())
            pl.when(leave)(remote)
        else:
            remote()

    def landed(src, dst, sems, recv_sems, index, turn, self_index):
        def remote():
            pltpu.make_async_remote_copy(
                src_ref=src, dst_ref=dst, send_sem=sems.at[index], recv_sem=recv_sems.at[index],
                device_id=target[turn], device_id_type=MESH,
            ).wait()

        if turn == 0:
            pl.when(stay)(lambda: pltpu.make_async_copy(src, dst, self_sem.at[self_index]).wait())
            pl.when(leave)(remote)
        else:
            remote()

    mine = 2 * y + c
    vec_copy = [
        send(vec_in_ref, vec_all.at[mine], vec_s, vec_r, i, peer)
        for i, peer in enumerate((by_core, by_y, by_yc))
    ]
    vec_all[mine] = vec_in_ref[...]
    wh_copy = []
    shard = wq_ref.shape[0]
    own_rows = pl.ds(pl.multiple_of(mine * shard, shard), shard)
    for part in range(3):
        to = wh_ref.at[own_rows, pl.ds(part * PAIR, PAIR)]

        def columns(core):
            return wq_ref.at[:, pl.ds(pl.multiple_of(part * width + (2 * x + core) * PAIR, PAIR), PAIR)]

        for i, (peer, core) in enumerate(((by_core, 1 - c), (by_y, c), (by_yc, 1 - c))):
            wh_copy.append(send(columns(core), to, wh_s, wh_r, 3 * part + i, peer))
        copy = pltpu.make_async_copy(columns(c), to, wh_l.at[part])
        copy.start()
        wh_copy.append(copy)

    up_rows, down_rows = wu_ref.shape[0] // 4, wd_ref.shape[0] // 4
    parts = [(wo_ref, wo_all, wo_ref.shape[0], 0)]
    parts += [(wu_ref, wu_all, up_rows, i * up_rows) for i in range(4)]
    parts += [(wd_ref, wd_all, down_rows, i * down_rows) for i in range(4)]

    def at_owner(full, src, size, offset, owner):
        return full.at[pl.ds(pl.multiple_of(owner * src.shape[0] + offset, 32), size)]

    other = 2 * (1 - y) + c
    y_copy = []
    for i, (src, full, size, offset) in enumerate(parts):
        y_copy.append(
            send(src.at[pl.ds(offset, size)], at_owner(full, src, size, offset, mine), y_s, y_r, i, by_y)
        )
    n_copy, load_copy, put_copy = [], [], []
    for i, (src, full, tmp) in enumerate(((wo_ref, wo_all, wo_tmp), (wu_ref, wu_all, wu_tmp), (wd_ref, wd_all, wd_tmp))):
        n_copy.append(send(src, at_owner(full, src, src.shape[0], 0, mine), n_s, n_r, i, by_core))
        load_copy.append(pltpu.make_async_copy(src, tmp, load_sem.at[i]))
        load_copy[-1].start()

    def put(i):
        src, full, tmp = ((wo_ref, wo_all, wo_tmp), (wu_ref, wu_all, wu_tmp), (wd_ref, wd_all, wd_tmp))[i]
        load_copy[i].wait()
        put_copy.append(pltpu.make_async_copy(tmp, at_owner(full, src, src.shape[0], 0, mine), put_sem.at[i]))
        put_copy[-1].start()

    o_copy = []

    def forward(i):
        src, full, size, offset = parts[i]
        y_copy[i].wait()
        held = at_owner(full, src, size, offset, other)
        o_copy.append(send(held, held, o_s, o_r, i, by_core))

    blocks = order_ref.shape[0]
    lane = lax.broadcasted_iota(jnp.int32, (1, 128), 1)
    slots = jnp.zeros((1, 128), jnp.int32)
    for t in range(blocks):
        dc, dx, turn, half = t // 8, t // 4 % 2, t // 2 % 2, t % 2
        core, side = (1 - c if dc else c), (1 - x if dx else x)
        stored = 2 * (2 * (2 * core + (1 - upper if turn else upper)) + side) + half
        slots = jnp.where(lane == order_ref[stored], t, slots)

    docs_copy = {}
    for turn in range(2):
        landed(docs_in_ref.at[block[turn]], docs.at[0, turn], docs_s, docs_r, turn, turn, per_turn)
    docs_copy["x"] = send(docs.at[0], docs.at[1], docs_s, docs_r, 2, by_x)
    docs_copy["c"] = send(docs.at[0], docs.at[2], docs_s, docs_r, 3, by_core)

    for copy in vec_copy:
        copy.wait()
    vec_width = vec_in_ref.shape[1]
    for j in range(4):
        for i in range(6):
            vec_ref[i : i + 1, j * vec_width : (j + 1) * vec_width] = vec_all[j, i : i + 1].astype(f32)
        for i in range(4):
            at = (4 * j + i) * vec_width
            ub_ref[:, at : at + vec_width] = vec_all[j, 6 + i : 7 + i].astype(f32)
    vec_ref[6:8] = jnp.zeros((2, width), f32)
    for copy in wh_copy:
        copy.wait()

    docs_copy["x"].wait()
    docs_copy["f"] = send(docs.at[1], docs.at[3], docs_s, docs_r, 4, by_core)

    def finish_docs():
        docs_copy["c"].wait()
        docs_copy["f"].wait()
        for g in range(4):
            core, side = (1 - c if g // 2 else c), (1 - x if g % 2 else x)
            for turn in range(2):
                docs_true[2 * (2 * core + (1 - upper if turn else upper)) + side] = docs[g, turn]
        numbers = docs_true[...]
        first = jnp.zeros_like(numbers)
        for d in range(1, blocks):
            before = jnp.sum((numbers < d).astype(jnp.int32), axis=(0, 1, 2), keepdims=True)
            first = jnp.where(numbers == d, before, first)
        docs_true[...] = first
        low = jnp.zeros((1, 128), jnp.int32)
        for b in range(blocks):
            line = docs_true[b // 2]
            at = 2 * (b % 2)
            line = jnp.concatenate([line[at : at + 1], line[at + 1 : at + 2]], axis=1)
            start_ref[b] = line
            low = jnp.where(lane == b, line[:, :1] // BLK, low)
        high = jnp.zeros((1, 128), jnp.int32) - 1
        for b in range(blocks):
            high = high + (low[:, b : b + 1] <= lane).astype(jnp.int32)
        tab_ref[...] = jnp.concatenate([low, high, slots, jnp.zeros((5, 128), jnp.int32)], axis=0)

    x_copy, c_copy, f_copy = [], [], []

    def relay(i):
        src, dst = piece(i)
        landed(src, dst, z_s, z_r, i, i // per_turn, i)
        part = pl.ds(i * HEAD_CHUNK, HEAD_CHUNK)
        x_copy.append(send(rows.at[0, part], rows.at[1, part], x_s, x_r, i, by_x))
        c_copy.append(send(rows.at[0, part], rows.at[2, part], c_s, c_r, i, by_core))

    def relay_far(i):
        x_copy[i].wait()
        part = pl.ds(i * HEAD_CHUNK, HEAD_CHUNK)
        f_copy.append(send(rows.at[1, part], rows.at[3, part], f_s, f_r, i, by_core))

    def compute(g, i):
        count = rows.shape[1]
        unit, _ = norm_parts(rows[g, i * HEAD_CHUNK : (i + 1) * HEAD_CHUNK].astype(f32))
        at = slice(g * count + i * HEAD_CHUNK, g * count + (i + 1) * HEAD_CHUNK)
        u_ref[at] = unit.astype(bf16)
        low = (unit * vec_ref[0:1] + vec_ref[1:2]).astype(bf16)
        qkv = jnp.dot(low, wh_ref[...], preferred_element_type=f32)
        qt_ref[:, at] = (qkv[:, :PAIR] * (SCORE_SCALE * LOG2E)).astype(bf16).T
        k = qkv[:, PAIR : 2 * PAIR].astype(bf16)
        v = qkv[:, 2 * PAIR :].astype(bf16)
        k_ref[at] = k
        v_ref[at] = v
        kt_ref[:, at] = k.T
        vt_ref[:, at] = v.T

    for i in range(chunks + 2):
        if i < chunks:
            send_dy(i)
            relay(i)
            compute(0, i)
        if 1 <= i <= chunks:
            relay_far(i - 1)
            compute(1, i - 1)
            c_copy[i - 1].wait()
            compute(2, i - 1)
        if i >= 2:
            f_copy[i - 2].wait()
            compute(3, i - 2)
        if i == 1:
            finish_docs()
        if 2 <= i < 5:
            put(i - 2)
        if i >= 3 and i - 3 < len(parts):
            forward(i - 3)
    own_ref[...] = rows[0]
    for i in range(chunks - 1, len(parts)):
        forward(i)
    for copy in n_copy + put_copy + o_copy:
        copy.wait()
    for i in range(chunks):
        land_dy(i)


def head(x_in, dy_in, docs_in, order, vec_in, w_qkv, w_out, w_up, w_down):
    width = x_in.shape[-1]
    count = 2 * x_in.shape[2]
    total = 4 * count
    shard = w_qkv.shape[0]
    chunks = count // HEAD_CHUNK
    blocks = order.shape[0]
    vmem, any_ = pl.BlockSpec(memory_space=pltpu.VMEM), pl.BlockSpec(memory_space=pl.ANY)
    smem = pl.BlockSpec(memory_space=pltpu.SMEM)
    dma, buf, shape = pltpu.SemaphoreType.DMA, pltpu.VMEM, jax.ShapeDtypeStruct
    return pl.pallas_call(
        head_kernel,
        in_specs=[any_, any_, vmem, smem, vmem, any_, any_, any_, any_],
        out_specs=[vmem] * 12 + [any_] * 4,
        out_shape=[
            shape((PAIR, total), bf16),
            shape((total, PAIR), bf16),
            shape((PAIR, total), bf16),
            shape((total, PAIR), bf16),
            shape((PAIR, total), bf16),
            shape((total, width), bf16),
            shape((count, width), bf16),
            shape((width, 3 * PAIR), bf16),
            shape((8, width), f32),
            shape((1, 4 * w_down.shape[0]), f32),
            shape((blocks, 1, BLK), jnp.int32),
            shape((8, 128), jnp.int32),
            shape((4 * w_out.shape[0], w_out.shape[1]), bf16),
            shape((4 * w_up.shape[0], w_up.shape[1]), bf16),
            shape((4 * w_down.shape[0], w_down.shape[1]), bf16),
            shape((count, width), bf16),
        ],
        scratch_shapes=[
            buf((4, count, width), bf16),
            buf((4, 2) + docs_in.shape[1:], jnp.int32),
            buf((blocks // 2,) + docs_in.shape[1:], jnp.int32),
            buf((4,) + vec_in.shape, bf16),
            buf(w_out.shape, bf16),
            buf(w_up.shape, bf16),
            buf(w_down.shape, bf16),
        ]
        + [dma((chunks,))] * 8
        + [dma((5,)), dma((5,)), dma((3,)), dma((3,)), dma((9,)), dma((9,)), dma((3,))]
        + [dma((9,)), dma((9,)), dma((3,)), dma((3,)), dma((9,)), dma((9,)), dma((3,)), dma((3,))]
        + [dma((chunks // 2 + 1,)), dma((chunks,)), dma((chunks,)), dma((chunks // 2,))],
        compiler_params=pltpu.CompilerParams(
            collective_id=1, has_side_effects=True, vmem_limit_bytes=56 * 1024 * 1024
        ),
        name="head",
    )(x_in, dy_in, docs_in, order, vec_in, w_qkv, w_out, w_up, w_down)
FF_TILE = 512
PIECES = 3
feed_steps = 4


def feed_kernel(
    o_ref, x_ref, dy_ref, wo_ref, wu_ref, wd_ref, vec_ref, ub_ref,
    do_ref, y_home, dmid_ref, keep_ref, to_y_ref, to_x_ref, to_xy_ref, gvec_ref, gub_ref,
    attn_all, gd_ref, gu_ref, go_ref, attn_in, do_out, y_out, grad_ref, grad_in,
    a_s, a_r, a_l, d_s, d_r, d_l, y_s, y_r, y_l, g_s, g_r,
):
    step = pl.program_id(0)
    steps = pl.num_programs(0)
    groups = attn_in.shape[0]
    tile = x_ref.shape[0]
    z, x, y, c = (lax.axis_index(name) for name in AXES)
    odd, upper = lax.rem(z, 2), lax.div(z, 2)
    mates = [None, {"x": 1 - x}, {"c": 1 - c}, {"x": 1 - x, "c": 1 - c}]
    pair_of = [2 * x + c, 2 * (1 - x) + c, 2 * x + 1 - c, 2 * (1 - x) + 1 - c]
    home = [{"z": 2 * c + upper, "c": odd}, {"z": 2 * c + 1 - upper, "c": odd}]
    origin = [{"z": 2 * odd + c, "c": upper}, {"z": 2 * (1 - odd) + c, "c": upper}]
    stay = (c == upper) & (odd == c)
    leave = jnp.logical_not(stay)
    half = feed_steps // 2

    def attn_copy(g, i):
        part = pl.ds(i * tile, tile)
        return pltpu.make_async_remote_copy(
            src_ref=o_ref.at[g, part], dst_ref=attn_in.at[g, part],
            send_sem=a_s.at[g - 1, i], recv_sem=a_r.at[g - 1, i], device_id=mates[g], device_id_type=MESH,
        )

    def attn_own(i):
        part = pl.ds(i * tile, tile)
        return pltpu.make_async_copy(o_ref.at[0, part], attn_in.at[0, part], a_l.at[i])

    def do_copy(g, i):
        return pltpu.make_async_remote_copy(
            src_ref=do_out.at[i, g], dst_ref=do_ref.at[g, pl.ds(i * tile, tile)],
            send_sem=d_s.at[g - 1, i], recv_sem=d_r.at[g - 1, i], device_id=mates[g], device_id_type=MESH,
        )

    def do_own(i):
        return pltpu.make_async_copy(do_out.at[i, 0], do_ref.at[0, pl.ds(i * tile, tile)], d_l.at[i])

    def y_rows(i, block):
        return y_home.at[block, pl.ds(lax.rem(i, half) * tile, tile)]

    def y_copy(i, turn, block):
        return pltpu.make_async_remote_copy(
            src_ref=y_out.at[i], dst_ref=y_rows(i, block),
            send_sem=y_s.at[i], recv_sem=y_r.at[i], device_id=home[turn], device_id_type=MESH,
        )

    def y_own(i, block):
        return pltpu.make_async_copy(y_out.at[i], y_rows(i, block), y_l.at[i])

    def grad_copy(i):
        return pltpu.make_async_remote_copy(
            src_ref=grad_ref.at[2 * i + 1 - c], dst_ref=grad_in.at[i],
            send_sem=g_s.at[i], recv_sem=g_r.at[i], device_id=mates[2], device_id_type=MESH,
        )

    @pl.when(step == 0)
    def _():
        greet(mates[1:] + [home[1], origin[1]], [home[0], origin[0]], leave)
        for i in range(feed_steps):
            for g in (1, 3, 2):
                attn_copy(g, i).start()
            attn_own(i).start()

    @pl.when(step == 0)
    def _():
        for ref in (gd_ref, gu_ref, go_ref, gvec_ref, gub_ref):
            ref[...] = jnp.zeros_like(ref)

    attn_own(step).wait()
    for g in range(1, groups):
        attn_copy(g, step).wait()
    for g in range(groups):
        attn_all[:, pl.ds(pl.multiple_of(pair_of[g] * PAIR, PAIR), PAIR)] = attn_in[
            g, pl.ds(pl.multiple_of(step * tile, tile), tile)
        ]
    attn = attn_all[...]
    gain, bias, out_bias, down_bias = (vec_ref[i : i + 1, :] for i in range(2, 6))
    middle = (
        x_ref[...].astype(f32) + jnp.dot(attn, wo_ref[...], preferred_element_type=f32) + out_bias
    )
    unit, inv = norm_parts(middle)
    low = (unit * gain + bias).astype(bf16)
    dy = dy_ref[...]
    dy32 = dy.astype(f32)
    total = middle + down_bias
    d_low = jnp.zeros_like(middle)
    width = wu_ref.shape[1]
    for j in range(0, width, FF_TILE):
        part = pl.ds(j, FF_TILE)
        up = wu_ref[:, part]
        down = wd_ref[part, :]
        hidden = jnp.dot(low, up, preferred_element_type=f32) + ub_ref[:, part]
        cdf = 0.5 * (1.0 + lax.erf(hidden * (1.0 / math.sqrt(2.0))))
        active = (hidden * cdf).astype(bf16)
        slope = cdf + hidden * (jnp.exp2(hidden * hidden * (-0.5 * LOG2E)) * (1.0 / math.sqrt(2.0 * math.pi)))
        total = total + jnp.dot(active, down, preferred_element_type=f32)
        d_hidden = contract(dy, down, 1, 1) * slope
        d_hidden_low = d_hidden.astype(bf16)
        gub_ref[:, part] += jnp.sum(d_hidden, axis=0, keepdims=True)
        d_low = d_low + contract(d_hidden_low, up, 1, 1)
        gd_ref[part, :] += contract(active, dy, 0, 0)
        gu_ref[:, part] += contract(low, d_hidden_low, 0, 0)
    y_out[step] = total.astype(bf16)

    @pl.when((step < half) & stay)
    def _():
        y_own(step, upper).start()

    @pl.when((step < half) & leave)
    def _():
        y_copy(step, 0, upper).start()

    @pl.when(step >= half)
    def _():
        y_copy(step, 1, upper).start()

    scaled = d_low * gain
    d_middle = dy32 + inv * (
        scaled
        - jnp.mean(scaled, axis=-1, keepdims=True)
        - unit * jnp.mean(scaled * unit, axis=-1, keepdims=True)
    )
    dmid_ref[...] = d_middle
    branch = d_middle.astype(bf16)
    go_ref[...] += contract(attn, branch, 0, 0)
    gvec_ref[0:1, :] += jnp.sum(d_middle, axis=0, keepdims=True)
    gvec_ref[1:2, :] += jnp.sum(d_low * unit, axis=0, keepdims=True)
    gvec_ref[2:3, :] += jnp.sum(d_low, axis=0, keepdims=True)
    gvec_ref[3:4, :] += jnp.sum(dy32, axis=0, keepdims=True)
    attn_all[...] = contract(branch, wo_ref[...], 1, 1).astype(bf16)
    for g in (1, 3, 2, 0):
        do_out[step, g] = attn_all[:, pl.ds(pl.multiple_of(pair_of[g] * PAIR, PAIR), PAIR)]
        if g:
            do_copy(g, step).start()
        else:
            do_own(step).start()

    @pl.when(step == steps - 1)
    def _():
        shards = grad_ref.shape[0]
        d_model = x_ref.shape[1]
        down_rows, up_rows = gd_ref.shape[0] // shards, d_model // shards
        for j in range(shards):
            grad_ref[j, :down_rows] = gd_ref[j * down_rows : (j + 1) * down_rows].astype(bf16)
            rows = slice(j * up_rows, (j + 1) * up_rows)
            at = down_rows
            for t in range(0, width, d_model):
                grad_ref[j, at : at + up_rows] = gu_ref[rows, t : t + d_model].astype(bf16)
                at += up_rows
            grad_ref[j, at : at + up_rows] = go_ref[rows].astype(bf16)
        for j in range(2):
            grad_copy(j).start()
        for j in range(feed_steps):
            do_own(j).wait()
            for g in range(1, groups):
                do_copy(g, j).wait()
            if j < half:
                @pl.when(stay)
                def _():
                    y_own(j, odd).wait()

                @pl.when(leave)
                def _():
                    y_copy(j, 0, odd).wait()
            else:
                y_copy(j, 1, 1 - odd).wait()
        sixth = keep_ref.shape[1]
        for j in range(2):
            grad_copy(j).wait()
        for dy_, dx_, ref in ((0, 0, keep_ref), (1, 0, to_y_ref), (0, 1, to_x_ref), (1, 1, to_xy_ref)):
            row = 1 - y if dy_ else y
            side = 1 - x if dx_ else x
            for p in range(PIECES):
                part = pl.ds(pl.multiple_of((2 * p + side) * sixth, 16), sixth)
                ref[p] = (
                    grad_ref[2 * row + c, part].astype(f32) + grad_in[row, part].astype(f32)
                ).astype(bf16)


def feed(o, x, dy, w_out, w_up, w_down, vecs, up_bias, shards):
    groups, count, _ = o.shape
    width = x.shape[1]
    flat = (w_out.size + w_up.size + w_down.size) // shards // width
    tile = count // feed_steps
    piece = (PIECES, flat // PIECES // 2, width)
    rows = pl.BlockSpec((tile, width), lambda i: (i, 0))
    any_ = pl.BlockSpec(memory_space=pl.ANY)
    dma, buf, shape = pltpu.SemaphoreType.DMA, pltpu.VMEM, jax.ShapeDtypeStruct
    return pl.pallas_call(
        feed_kernel,
        grid=(feed_steps,),
        in_specs=[
            any_, rows, rows, whole(w_out.shape), whole(w_up.shape), whole(w_down.shape),
            whole(vecs.shape), whole(up_bias.shape),
        ],
        out_specs=[any_, any_, rows] + [whole(piece)] * 4 + [whole(vecs.shape), whole(up_bias.shape)],
        out_shape=[
            shape((groups, count, PAIR), bf16),
            shape((2, count // 2, width), bf16),
            shape((count, width), f32),
            shape(piece, bf16),
            shape(piece, bf16),
            shape(piece, bf16),
            shape(piece, bf16),
            shape(vecs.shape, f32),
            shape(up_bias.shape, f32),
        ],
        scratch_shapes=[
            buf((tile, width), bf16),
            buf(w_down.shape, f32),
            buf(w_up.shape, f32),
            buf(w_out.shape, f32),
            buf((groups, count, PAIR), bf16),
            buf((feed_steps, groups, tile, PAIR), bf16),
            buf((feed_steps, tile, width), bf16),
            buf((shards, flat, width), bf16),
            buf((2, flat, width), bf16),
            dma((3, feed_steps)),
            dma((3, feed_steps)),
            dma((feed_steps,)),
            dma((3, feed_steps)),
            dma((3, feed_steps)),
            dma((feed_steps,)),
            dma((feed_steps,)),
            dma((feed_steps,)),
            dma((feed_steps,)),
            dma((2,)),
            dma((2,)),
        ],
        compiler_params=pltpu.CompilerParams(
            collective_id=3, has_side_effects=True, vmem_limit_bytes=60 * 1024 * 1024
        ),
        name="feed",
    )(o, x, dy, w_out, w_up, w_down, vecs, up_bias)


TAIL_CHUNK = 128


def tail_kernel(
    dh_ref, x_ref, dmid_ref, gain_ref, keep_ref, from_y_ref, from_x_ref, from_xy_ref, gw_ref, small_ref,
    dx_ref, gd_ref, gu_ref, go_ref, gq_ref, gvec_ref, gub_ref,
    core_buf, own_dh, x_out, x_buf, dx_out, home_buf,
    gsum, gz1s, gz1r, gz2s, gz2r, gfull,
    wy, ws, wz1s, wz1r, wz2s, wz2r, wfull, wall,
    small_out, small_in,
    local_sem, self_sem, core_s, core_r, x_s, x_r, home_s, home_r, g_s, g_r, w_s, w_r, s_s, s_r,
):
    z, x, y, c = (lax.axis_index(name) for name in AXES)
    odd, upper = lax.rem(z, 2), lax.div(z, 2)
    width = x_ref.shape[1]
    chunks = x_ref.shape[0] // TAIL_CHUNK
    per_turn = chunks // 2
    by_core, by_x, by_y, by_xc = {"c": 1 - c}, {"x": 1 - x}, {"y": 1 - y}, {"x": 1 - x, "c": 1 - c}
    by_z1, by_z2 = {"z": z + 1 - 2 * odd}, {"z": z + 2 - 4 * upper}
    home = [{"z": 2 * c + upper, "c": odd}, {"z": 2 * c + 1 - upper, "c": odd}]
    origin = [{"z": 2 * odd + c, "c": upper}, {"z": 2 * (1 - odd) + c, "c": upper}]
    stay = (c == upper) & (odd == c)
    greet(
        [by_core, by_x, by_y, by_xc, by_z1, by_z2, home[1], origin[1]],
        [home[0], origin[0]],
        jnp.logical_not(stay),
    )
    small_peers = [by_x, by_core, by_y, by_z1, by_z2]
    s_copy = [send(small_ref, small_in.at[0], s_s, s_r, 0, small_peers[0])]
    to_core, locals_ = [], []
    for i in range(chunks):
        part = pl.ds(i * TAIL_CHUNK, TAIL_CHUNK)
        to_core.append(
            send(dh_ref.at[pl.ds(2, 2), part], core_buf.at[:, part], core_s, core_r, i, by_core)
        )
        copy = pltpu.make_async_copy(dh_ref.at[pl.ds(0, 2), part], own_dh.at[:, part], local_sem.at[i])
        copy.start()
        locals_.append(copy)
    w_copy = {}
    w_copy["y"] = send(gw_ref.at[pl.ds(2 * (1 - y), 2)], wy, w_s, w_r, 0, by_y)
    g_copy = {}

    def g_start(p):
        for half in range(2):
            part = pl.ds(96 * half, 96)
            gsum[p, part] = (
                keep_ref[p, part].astype(f32)
                + from_y_ref[p, part].astype(f32)
                + from_x_ref[p, part].astype(f32)
                + from_xy_ref[p, part].astype(f32)
            )
        gz1s[p] = gsum[p, pl.ds(pl.multiple_of(96 * (1 - odd), 16), 96)].astype(bf16)
        g_copy["z1", p] = send(gz1s.at[p], gz1r.at[p], g_s, g_r, 5 * p, by_z1)

    mine_half = pl.multiple_of(96 * odd, 16)
    mine_quarter = pl.multiple_of(96 * odd + 48 * upper, 16)
    give_quarter = pl.multiple_of(96 * odd + 48 * (1 - upper), 16)

    def g_second(p):
        g_copy["z1", p].wait()
        gsum[p, pl.ds(mine_half, 96)] += gz1r[p].astype(f32)
        gz2s[p] = gsum[p, pl.ds(give_quarter, 48)].astype(bf16)
        g_copy["z2", p] = send(gz2s.at[p], gz2r.at[p], g_s, g_r, 5 * p + 1, by_z2)

    def g_third(p):
        g_copy["z2", p].wait()
        part = pl.ds(mine_quarter, 48)
        gfull[p, x, part] = (gsum[p, part] + gz2r[p].astype(f32)).astype(bf16)
        place_ = gfull.at[p, x, part]
        g_copy["z2b", p] = send(place_, place_, g_s, g_r, 5 * p + 2, by_z2)

    def g_fourth(p):
        g_copy["z2b", p].wait()
        place_ = gfull.at[p, x, pl.ds(mine_half, 96)]
        g_copy["z1b", p] = send(place_, place_, g_s, g_r, 5 * p + 3, by_z1)

    def g_fifth(p):
        g_copy["z1b", p].wait()
        g_copy["x", p] = send(gfull.at[p, x], gfull.at[p, x], g_s, g_r, 5 * p + 4, by_x)

    def w_second():
        w_copy["y"].wait()
        for i in range(2):
            ws[i] = gw_ref[2 * y + i].astype(f32) + wy[i].astype(f32)
        wz1s[...] = ws[1 - odd].astype(bf16)
        w_copy["z1"] = send(wz1s, wz1r, w_s, w_r, 1, by_z1)

    def w_third():
        w_copy["z1"].wait()
        ws[odd] += wz1r[...].astype(f32)
        wz2s[...] = ws[odd, pl.ds(pl.multiple_of(64 * (1 - upper), 64), 64)].astype(bf16)
        w_copy["z2"] = send(wz2s, wz2r, w_s, w_r, 2, by_z2)

    def w_fourth():
        w_copy["z2"].wait()
        part = pl.ds(pl.multiple_of(64 * upper, 64), 64)
        wfull[odd, part] = (ws[odd, part] + wz2r[...].astype(f32)).astype(bf16)
        place_ = wfull.at[odd, part]
        w_copy["z2b"] = send(place_, place_, w_s, w_r, 3, by_z2)

    def w_fifth():
        w_copy["z2b"].wait()
        w_copy["z1b"] = send(wfull.at[odd], wfull.at[odd], w_s, w_r, 4, by_z1)

    def w_sixth():
        w_copy["z1b"].wait()
        mine = 2 * x + c
        w_copy["core"] = send(wfull.at[1 - c], wall.at[mine], w_s, w_r, 5, by_core)
        w_copy["x"] = send(wfull.at[c], wall.at[mine], w_s, w_r, 6, by_x)
        w_copy["xc"] = send(wfull.at[1 - c], wall.at[mine], w_s, w_r, 7, by_xc)

    def s_next(step):
        s_copy[step].wait()
        before = small_ref[...] if step == 0 else small_out[step - 1]
        small_out[step] = before + small_in[step]
        if step + 1 < len(small_peers):
            s_copy.append(
                send(small_out.at[step], small_in.at[step + 1], s_s, s_r, step + 1, small_peers[step + 1])
            )

    x_copy, home_copy = [], []

    def add_core(i):
        part = pl.ds(i * TAIL_CHUNK, TAIL_CHUNK)
        to_core[i].wait()
        locals_[i].wait()
        x_out[part] = (own_dh[1, part].astype(f32) + core_buf[1, part].astype(f32)).astype(bf16)
        x_copy.append(send(x_out.at[part], x_buf.at[part], x_s, x_r, i, by_x))

    def finish(i):
        part = pl.ds(i * TAIL_CHUNK, TAIL_CHUNK)
        x_copy[i].wait()
        d_low = own_dh[0, part].astype(f32) + core_buf[0, part].astype(f32) + x_buf[part].astype(f32)
        unit, inv = norm_parts(x_ref[part].astype(f32))
        scaled = d_low * gain_ref[...]
        dx = dmid_ref[part] + inv * (
            scaled
            - jnp.mean(scaled, axis=-1, keepdims=True)
            - unit * jnp.mean(scaled * unit, axis=-1, keepdims=True)
        )
        dx_out[part] = dx.astype(bf16)
        turn, row = i // per_turn, (i % per_turn) * TAIL_CHUNK
        target = home_buf.at[upper, pl.ds(row, TAIL_CHUNK)]
        if turn == 0:
            @pl.when(stay)
            def _():
                pltpu.make_async_copy(dx_out.at[part], target, self_sem.at[i]).start()

            @pl.when(jnp.logical_not(stay))
            def _():
                send(dx_out.at[part], target, home_s, home_r, i, home[0])
        else:
            send(dx_out.at[part], target, home_s, home_r, i, home[1])

    def arrive(i):
        part = pl.ds(i * TAIL_CHUNK, TAIL_CHUNK)
        turn, row = i // per_turn, (i % per_turn) * TAIL_CHUNK
        block = odd if turn == 0 else 1 - odd
        landed = home_buf.at[block, pl.ds(row, TAIL_CHUNK)]

        def remote():
            copy = pltpu.make_async_remote_copy(
                src_ref=dx_out.at[part], dst_ref=landed, send_sem=home_s.at[i], recv_sem=home_r.at[i],
                device_id=home[turn], device_id_type=MESH,
            )
            copy.wait_send()
            copy.wait_recv()

        if turn == 0:
            @pl.when(stay)
            def _():
                pltpu.make_async_copy(dx_out.at[part], landed, self_sem.at[i]).wait()

            pl.when(jnp.logical_not(stay))(remote)
        else:
            remote()
        dx_ref[block, pl.ds(row, TAIL_CHUNK)] = home_buf[block, pl.ds(row, TAIL_CHUNK)].astype(f32)

    g_start(0)
    add_core(0)
    g_start(1)
    add_core(1)
    g_start(2)
    add_core(2)
    s_next(0)
    s_next(1)
    g_second(0)
    w_second()
    g_second(1)
    g_second(2)
    finish(0)
    add_core(3)
    s_next(2)
    g_third(0)
    finish(1)
    add_core(4)
    w_third()
    g_third(1)
    g_third(2)
    s_next(3)
    finish(2)
    add_core(5)
    g_fourth(0)
    w_fourth()
    finish(3)
    add_core(6)
    s_next(4)
    g_fourth(1)
    g_fourth(2)
    w_fifth()
    finish(4)
    add_core(7)
    g_fifth(0)
    finish(5)
    w_sixth()
    g_fifth(1)
    finish(6)
    g_fifth(2)
    finish(7)
    w_copy["core"].wait()
    w_copy["x"].wait()
    w_copy["xc"].wait()
    wall[2 * x + c] = wfull[c]
    for pair in range(4):
        for part in range(3):
            gq_ref[:, part * width + pair * PAIR : part * width + (pair + 1) * PAIR] = wall[
                pair, :, part * PAIR : (part + 1) * PAIR
            ].astype(f32)
    shard = go_ref.shape[0]
    lanes = pl.ds(pl.multiple_of(shard * (2 * y + c), shard), shard)
    for i in range(6):
        gvec_ref[i : i + 1, :] = small_out[4, i : i + 1, lanes]
    gub_ref[...] = small_out[4, pl.ds(6 + 2 * y + c, 1), :]
    for i in range(chunks):
        arrive(i)
    for p in range(PIECES):
        g_copy["x", p].wait()
    flat = gd_ref.shape[0] + (gu_ref.shape[1] // width + 1) * shard
    for row in range(0, flat, 64):
        p, rest = divmod(row, flat // PIECES)
        side, inner = divmod(rest, flat // PIECES // 2)
        value = gfull[p, side, inner : inner + 64].astype(f32)
        if row < gd_ref.shape[0]:
            gd_ref[row : row + 64] = value
        elif row < flat - shard:
            t, r = divmod(row - gd_ref.shape[0], shard)
            gu_ref[r : r + 64, t * width : (t + 1) * width] = value
        else:
            r = row - (flat - shard)
            go_ref[r : r + 64] = value


def tail(dh, x, dmid, gain, keep, from_y, from_x, from_xy, gw, small, ff_shard):
    count, width = x.shape
    shard = gw.shape[1]
    half = count // 2
    chunks = count // TAIL_CHUNK
    sixth = keep.shape[1]
    vmem = pl.BlockSpec(memory_space=pltpu.VMEM)
    dma = pltpu.SemaphoreType.DMA
    buf = pltpu.VMEM
    return pl.pallas_call(
        tail_kernel,
        in_specs=[pl.BlockSpec(memory_space=pl.ANY)] + [vmem] * 9,
        out_specs=[vmem] * 7,
        out_shape=[
            jax.ShapeDtypeStruct((2, half, width), f32),
            jax.ShapeDtypeStruct((ff_shard, width), f32),
            jax.ShapeDtypeStruct((shard, 4 * ff_shard), f32),
            jax.ShapeDtypeStruct((shard, width), f32),
            jax.ShapeDtypeStruct((shard, 3 * width), f32),
            jax.ShapeDtypeStruct((8, shard), f32),
            jax.ShapeDtypeStruct((1, ff_shard), f32),
        ],
        scratch_shapes=[
            buf((2, count, width), bf16),
            buf((2, count, width), bf16),
            buf((count, width), bf16),
            buf((count, width), bf16),
            buf((count, width), bf16),
            buf((2, half, width), bf16),
            buf((PIECES, sixth, width), f32),
            buf((PIECES, sixth // 2, width), bf16),
            buf((PIECES, sixth // 2, width), bf16),
            buf((PIECES, sixth // 4, width), bf16),
            buf((PIECES, sixth // 4, width), bf16),
            buf((PIECES, 2, sixth, width), bf16),
            buf((2, shard, 3 * PAIR), bf16),
            buf((2, shard, 3 * PAIR), f32),
            buf((shard, 3 * PAIR), bf16),
            buf((shard, 3 * PAIR), bf16),
            buf((shard // 2, 3 * PAIR), bf16),
            buf((shard // 2, 3 * PAIR), bf16),
            buf((2, shard, 3 * PAIR), bf16),
            buf((4, shard, 3 * PAIR), bf16),
            buf((5,) + small.shape, f32),
            buf((5,) + small.shape, f32),
            dma((chunks,)),
            dma((chunks // 2,)),
            dma((chunks,)),
            dma((chunks,)),
            dma((chunks,)),
            dma((chunks,)),
            dma((chunks,)),
            dma((chunks,)),
            dma((5 * PIECES,)),
            dma((5 * PIECES,)),
            dma((8,)),
            dma((8,)),
            dma((5,)),
            dma((5,)),
        ],
        compiler_params=pltpu.CompilerParams(
            collective_id=5, has_side_effects=True, vmem_limit_bytes=56 * 1024 * 1024
        ),
        name="tail",
    )(dh, x, dmid, gain, keep, from_y, from_x, from_xy, gw, small)
def stack_rows(members, width, count):
    at, total = 0, 0
    for member in members:
        rows = member.reshape(-1, width)
        total = total + jnp.pad(rows, ((at, count - at - rows.shape[0]), (0, 0)))
        at += rows.shape[0]
    return total


def place(z, x, y, c):
    return ((z * SIZES[1] + x) * SIZES[2] + y) * SIZES[3] + c


def everyone():
    return [
        (z, x, y, c)
        for z in range(SIZES[0])
        for x in range(SIZES[1])
        for y in range(SIZES[2])
        for c in range(SIZES[3])
    ]


def swap_pairs(dx, dy, dc):
    return [(place(z, x, y, c), place(z, x ^ dx, y ^ dy, c ^ dc)) for z, x, y, c in everyone()]


def move(value, pairs):
    return lax.ppermute(value, AXES, pairs)


def swap(value, dx=0, dy=0, dc=0):
    return move(value, swap_pairs(dx, dy, dc))


def paired_body(
    inputs, out_grad, segment_ids, block_order, w_qkv, w_out, w_up, w_down,
    norm1_gain, norm1_bias, norm2_gain, norm2_bias, out_bias, up_bias, down_bias,
):
    width = inputs.shape[3]
    shard = norm1_gain.shape[0]
    vectors = stack_rows(
        [norm1_gain, norm1_bias, norm2_gain, norm2_bias, out_bias, down_bias, up_bias], shard, 16
    )
    (
        qt, k, kt, v, vt, unit, own_x, w_heads, vecs, full_ubias, start, tab, full_out, full_up, full_down, own_dy
    ) = head(
        inputs, out_grad, segment_ids.reshape(2, -1, 128), block_order, vectors, w_qkv, w_out, w_up, w_down
    )
    gain_one, bias_one = vecs[0:1], vecs[1:2]
    o, ot, lse = attend(tab, qt, start, k, vt)
    d_o, outputs, d_middle, keep, to_y, to_x, to_xy, g_vecs, g_ubias = feed(
        o.reshape(4, -1, PAIR), own_x, own_dy, full_out, full_up, full_down, vecs, full_ubias, 4
    )
    from_y, from_x, from_xy = swap(to_y, dy=1), swap(to_x, dx=1), swap(to_xy, dy=1, dx=1)
    dh, g_heads, g_norm = attend_back(
        tab, k, kt, v, unit, w_heads, qt, start, d_o.reshape(-1, PAIR), ot, lse, gain_one, bias_one, 4
    )
    small = stack_rows([g_norm, g_vecs[1:3], g_vecs[0:1], g_vecs[3:4], g_ubias], width, 16)
    dx, grad_down, grad_up, grad_out, grad_qkv, g_vec, g_ub = tail(
        dh.reshape(4, -1, width), own_x, d_middle, gain_one, keep, from_y, from_x, from_xy,
        g_heads, small, w_down.shape[0],
    )
    return (
        outputs[:, None], dx[:, None], grad_qkv, grad_out, grad_up, grad_down,
        g_vec[0], g_vec[1], g_vec[2], g_vec[3], g_vec[4], g_ub[0], g_vec[5],
    )


def solution(mesh):
    paired = mesh.shape["ctx"] == SIZES[0] * SIZES[1] and mesh.shape["fsdp"] == SIZES[2] * SIZES[3]
    if paired:
        mesh = Mesh(mesh.devices.reshape(SIZES), AXES)
        ctx, fsdp, program = ("z", "x"), ("y", "c"), paired_body
    else:
        ctx, fsdp, program = "ctx", "fsdp", general_body
    tokens = P(None, fsdp, ctx, None)
    matrix, vector = P(fsdp, None), P(fsdp)
    return jax.shard_map(
        program,
        mesh=mesh,
        in_specs=(tokens, tokens, P(None, fsdp, ctx), P()) + (matrix,) * 4 + (vector,) * 7,
        out_specs=(tokens, tokens) + (matrix,) * 4 + (vector,) * 7,
        check_vma=False,
    )
```

```python
import functools
import math

import jax
import jax.numpy as jnp
from jax import lax
from jax.experimental import pallas as pl
from jax.experimental.pallas import tpu as pltpu
from jax.sharding import Mesh
from jax.sharding import PartitionSpec as P

H = 8
HD = 64
BLK = 256
PAIR = 2 * HD

norm_eps = 1e-05
mask_fill = -1e30
LOG2E = math.log2(math.e)
LN2 = math.log(2.0)
SCORE_SCALE = 1.0 / math.sqrt(HD)

f32 = jnp.float32
bf16 = jnp.bfloat16


def contract(a, b, da, db):
    return lax.dot_general(a, b, (((da,), (db,)), ((), ())), preferred_element_type=f32)


def norm_parts(values):
    center = values - jnp.mean(values, axis=-1, keepdims=True)
    spread = jnp.mean(center * center, axis=-1, keepdims=True)
    inv = lax.rsqrt(spread + norm_eps)
    return center * inv, inv


def whole(shape):
    zeros = (0,) * len(shape)
    return pl.BlockSpec(shape, lambda *_: zeros)


def two_heads(block):
    zero = jnp.zeros((HD, block.shape[1]), block.dtype)
    return jnp.concatenate(
        [jnp.concatenate([block[:HD], zero], axis=0), jnp.concatenate([zero, block[HD:]], axis=0)], axis=1
    )


EXTRA = 16


def attend_kernel(tab_ref, qt_ref, start_ref, k_ref, vt_ref, o_ref, ot_ref, lse_ref, acc, top):
    qb = pl.program_id(0)
    both = two_heads(qt_ref[...])
    start = jnp.concatenate([start_ref[0], start_ref[0]], axis=1)
    row = lax.broadcasted_iota(jnp.int32, (BLK, 2 * BLK), 0)
    ones = jnp.ones((EXTRA, 2 * BLK), bf16)

    def place_of(kb):
        return pl.ds(pl.multiple_of(tab_ref[2, jnp.maximum(kb, 0)] * BLK, BLK), BLK)

    def masked_scores(kb, at, diagonal):
        allowed = row >= start - kb * BLK
        if diagonal:
            col = lax.broadcasted_iota(jnp.int32, (BLK, 2 * BLK), 1)
            allowed = allowed & (row <= jnp.bitwise_and(col, BLK - 1))
        st = jnp.dot(k_ref[at, :], both, preferred_element_type=f32)
        return jnp.where(allowed, st, mask_fill)

    def visit(kb, first, bounded):
        places = [place_of(kb), place_of(kb - 1)]
        terms = [masked_scores(kb - i, places[i], first and i == 0) for i in range(2)]
        if bounded:
            probs = [jnp.exp2(term).astype(bf16) for term in terms]
        else:
            peak = jnp.maximum(
                jnp.max(terms[0], axis=0, keepdims=True), jnp.max(terms[1], axis=0, keepdims=True)
            )
            if not first:
                old = top[...]
                peak = jnp.maximum(old, peak)
                shrink = jnp.exp2(old - peak)
            top[...] = peak
            probs = [jnp.exp2(term - peak).astype(bf16) for term in terms]
        probs = jnp.concatenate(probs, axis=0)
        vt = jnp.concatenate([vt_ref[:, places[0]], vt_ref[:, places[1]]], axis=1)
        for head in range(2):
            cols = slice(head * BLK, (head + 1) * BLK)
            left = jnp.concatenate([vt[head * HD : (head + 1) * HD], ones], axis=0)
            part = jnp.dot(left, probs[:, cols], preferred_element_type=f32)
            if first:
                acc[head] = part
            elif bounded:
                acc[head] += part
            else:
                acc[head] = acc[head] * shrink[:, cols] + part

    def all_visits(bounded):
        visit(qb, True, bounded)

        def more(i, carry):
            visit(qb - 2 * i, False, bounded)
            return carry

        lax.fori_loop(1, (qb - tab_ref[0, qb]) // 2 + 1, more, 0)

    small = tab_ref[3, 0] > 0

    @pl.when(small)
    def _():
        top[...] = jnp.zeros_like(top)
        all_visits(True)

    pl.when(jnp.logical_not(small))(lambda: all_visits(False))
    total = jnp.concatenate([acc[0, HD : HD + 1], acc[1, HD : HD + 1]], axis=1)
    lse_ref[0] = top[...] + jnp.log2(total)
    heads = jnp.concatenate([acc[h, :HD] / acc[h, HD : HD + 1] for h in range(2)], axis=0)
    ot_ref[0] = heads
    o_ref[...] = heads.T.astype(bf16)


def attend(tab, qt, start, k, vt):
    count = k.shape[0]
    blocks = count // BLK
    return pl.pallas_call(
        attend_kernel,
        grid_spec=pltpu.PrefetchScalarGridSpec(
            num_scalar_prefetch=1,
            grid=(blocks,),
            in_specs=[
                pl.BlockSpec((PAIR, BLK), lambda b, t: (0, t[2, b])),
                pl.BlockSpec((1, 1, BLK), lambda b, t: (b, 0, 0)),
                whole(k.shape),
                whole(vt.shape),
            ],
            out_specs=[
                pl.BlockSpec((BLK, PAIR), lambda b, t: (t[2, b], 0)),
                pl.BlockSpec((1, PAIR, BLK), lambda b, t: (b, 0, 0)),
                pl.BlockSpec((1, 1, 2 * BLK), lambda b, t: (b, 0, 0)),
            ],
            scratch_shapes=[
                pltpu.VMEM((2, HD + EXTRA, BLK), f32),
                pltpu.VMEM((1, 2 * BLK), f32),
            ],
        ),
        out_shape=[
            jax.ShapeDtypeStruct((count, PAIR), bf16),
            jax.ShapeDtypeStruct((blocks, PAIR, BLK), f32),
            jax.ShapeDtypeStruct((blocks, 1, 2 * BLK), f32),
        ],
        name="attend",
    )(tab, qt, start, k, vt)


def split_heads(block):
    lane = lax.broadcasted_iota(jnp.int32, block.shape, 1)
    zero = jnp.zeros_like(block)
    first = lane < HD
    return jnp.concatenate([jnp.where(first, block, zero), jnp.where(first, zero, block)], axis=0)


def attend_back_kernel(
    tab_ref, k_ref, kt_ref, v_ref, ut_ref, w_ref, qt_ref, start_ref, do_ref, ot_ref, lse_ref,
    gain_ref, bias_ref, dh_ref, gw_ref, gn_ref, dqt, dk_acc, dv_acc, dot, dom, qm, delta, total, sums,
):
    kb = pl.program_id(0)
    blocks = pl.num_programs(0) - 1
    now, before = kb % 2, (kb + 1) % 2
    row = lax.broadcasted_iota(jnp.int32, (BLK, 2 * BLK), 0)

    def at(qb):
        return pl.ds(pl.multiple_of(tab_ref[2, qb] * BLK, BLK), BLK)

    @pl.when(kb == 0)
    def _():
        total[...] = jnp.zeros_like(total)
        sums[...] = jnp.zeros_like(sums)
        dk_acc[1] = jnp.zeros(dk_acc.shape[1:], f32)
        dv_acc[1] = jnp.zeros(dv_acc.shape[1:], f32)

        def prepare(qb, carry):
            dqt[qb] = jnp.zeros((PAIR, BLK), f32)
            d_out = do_ref[at(qb), :]
            dom[qb] = split_heads(d_out)
            qm[qb] = split_heads(qt_ref[:, at(qb)].T)
            turned = d_out.astype(f32).T
            dot[qb] = turned.astype(bf16)
            both = turned * ot_ref[qb]
            delta[qb] = jnp.concatenate(
                [
                    jnp.sum(both[:HD], axis=0, keepdims=True),
                    jnp.sum(both[HD:], axis=0, keepdims=True),
                ],
                axis=1,
            )
            return carry

        lax.fori_loop(0, blocks, prepare, 0)

    k = k_ref[...]
    v = v_ref[...]
    kt = kt_ref[...]

    def tile(qb, diagonal):
        qt = qt_ref[:, at(qb)]
        d_out = dot[qb]
        start = jnp.concatenate([start_ref[qb], start_ref[qb]], axis=1)
        st = jnp.dot(k, two_heads(qt), preferred_element_type=f32)
        dpt = jnp.dot(v, two_heads(d_out), preferred_element_type=f32)
        allowed = row >= start - kb * BLK
        if diagonal:
            col = lax.broadcasted_iota(jnp.int32, (BLK, 2 * BLK), 1)
            allowed = allowed & (row <= jnp.bitwise_and(col, BLK - 1))
        pt = jnp.exp2(jnp.where(allowed, st - lse_ref[qb], mask_fill))
        dst = (pt * (dpt - delta[qb])).astype(bf16)
        part_v = jnp.dot(pt.astype(bf16), dom[qb], preferred_element_type=f32)
        part_k = jnp.dot(dst, qm[qb], preferred_element_type=f32)
        if diagonal:
            dv_acc[now] = part_v
            dk_acc[now] = part_k
        else:
            dv_acc[now] += part_v
            dk_acc[now] += part_k
        for head in range(2):
            mine = slice(head * HD, (head + 1) * HD)
            cols = slice(head * BLK, (head + 1) * BLK)
            dqt[qb, mine] += jnp.dot(kt[mine], dst[:, cols], preferred_element_type=f32)

    def close():
        block = jnp.maximum(kb - 1, 0)
        dq = (dqt[block] * SCORE_SCALE).T
        joined = jnp.concatenate([dq, dk_acc[before] * LN2, dv_acc[before]], axis=1)
        if_any = jnp.where(kb == 0, 0.0, 1.0)
        joined = (joined * if_any).astype(bf16)
        dh_ref[...] = contract(joined, w_ref[...], 1, 1).astype(bf16)
        total[...] += jnp.dot(ut_ref[...], joined, preferred_element_type=f32)
        sums[...] += jnp.sum(joined.astype(f32), axis=0, keepdims=True)

    @pl.when(kb < blocks)
    def _():
        close()
        tile(kb, True)
        last = tab_ref[1, kb]

        def visit(i, carry):
            tile(kb + 1 + 2 * i, False)
            tile(kb + 2 + 2 * i, False)
            return carry

        lax.fori_loop(0, (last - kb) // 2, visit, 0)

        @pl.when((last - kb) % 2 == 1)
        def _():
            tile(last, False)

    @pl.when(kb == blocks)
    def _():
        close()
        shard = gw_ref.shape[1]
        for j in range(gw_ref.shape[0]):
            part = pl.ds(j * shard, shard)
            gain, bias = (
                jnp.broadcast_to(ref[:, part], (shard, shard)).T[:, :1] for ref in (gain_ref, bias_ref)
            )
            gw_ref[j] = (total[part] * gain + bias * sums[...]).astype(bf16)
            w = w_ref[part].astype(f32)
            for i, term in enumerate((w * total[part], w * sums[...])):
                column = jnp.sum(term, axis=1, keepdims=True)
                gn_ref[i : i + 1, part] = jnp.broadcast_to(column, (shard, shard)).T[:1]


def attend_back(tab, k, kt, v, unit_t, weight, qt, start, d_out, ot, lse, gain, bias, shards):
    count = k.shape[0]
    width = unit_t.shape[0]
    shard = width // shards
    blocks = count // BLK
    return pl.pallas_call(
        attend_back_kernel,
        grid_spec=pltpu.PrefetchScalarGridSpec(
            num_scalar_prefetch=1,
            grid=(blocks + 1,),
            in_specs=[
                pl.BlockSpec((BLK, PAIR), lambda b, t: (t[2, jnp.minimum(b, blocks - 1)], 0)),
                pl.BlockSpec((PAIR, BLK), lambda b, t: (0, t[2, jnp.minimum(b, blocks - 1)])),
                pl.BlockSpec((BLK, PAIR), lambda b, t: (t[2, jnp.minimum(b, blocks - 1)], 0)),
                pl.BlockSpec((width, BLK), lambda b, t: (0, t[2, jnp.maximum(b - 1, 0)])),
                whole(weight.shape),
                whole(qt.shape),
                whole(start.shape),
                whole(d_out.shape),
                whole(ot.shape),
                whole(lse.shape),
                whole(gain.shape),
                whole(bias.shape),
            ],
            out_specs=[
                pl.BlockSpec((BLK, width), lambda b, t: (t[2, jnp.maximum(b - 1, 0)], 0)),
                whole((shards, shard, 3 * PAIR)),
                whole((2, width)),
            ],
            scratch_shapes=[
                pltpu.VMEM((blocks, PAIR, BLK), f32),
                pltpu.VMEM((2, BLK, PAIR), f32),
                pltpu.VMEM((2, BLK, PAIR), f32),
                pltpu.VMEM((blocks, PAIR, BLK), bf16),
                pltpu.VMEM((blocks, 2 * BLK, PAIR), bf16),
                pltpu.VMEM((blocks, 2 * BLK, PAIR), bf16),
                pltpu.VMEM((blocks, 1, 2 * BLK), f32),
                pltpu.VMEM(weight.shape, f32),
                pltpu.VMEM((1, 3 * PAIR), f32),
            ],
        ),
        out_shape=[
            jax.ShapeDtypeStruct((count, width), bf16),
            jax.ShapeDtypeStruct((shards, shard, 3 * PAIR), bf16),
            jax.ShapeDtypeStruct((2, width), f32),
        ],
        name="attend_back",
    )(tab, k, kt, v, unit_t, weight, qt, start, d_out, ot, lse, gain, bias)


def layer_norm(values, gain_vec, offset):
    center = values - jnp.mean(values, axis=-1, keepdims=True)
    spread = jnp.mean(center * center, axis=-1, keepdims=True)
    return center * lax.rsqrt(spread + norm_eps) * gain_vec + offset


def gelu_exact(values):
    return 0.5 * values * (1.0 + lax.erf(values * (1.0 / math.sqrt(2.0))))


def score_block(query_heads, key_heads, query_doc, query_pos, key_doc, key_pos):
    raw_scores = jnp.einsum(
        "qhd,khd->hqk", query_heads, key_heads, preferred_element_type=jnp.float32
    ) * (1.0 / math.sqrt(HD))
    allowed = (query_doc[:, None] == key_doc[None, :]) & (key_pos[None, :] <= query_pos[:, None])
    return (raw_scores, allowed[None])


def soft_block(raw_scores, allowed, log_norm):
    return jnp.exp(jnp.where(allowed, raw_scores, mask_fill) - log_norm[:, :, None])


def row_log_norm(query_heads, key_blocks, doc_blocks, pos_blocks, query_doc, query_pos):

    def row_visit(running, block_item):
        row_top, row_sum = running
        key_heads, key_doc, key_pos = block_item
        raw_scores, allowed = score_block(
            query_heads, key_heads, query_doc, query_pos, key_doc, key_pos
        )
        masked = jnp.where(allowed, raw_scores, mask_fill)
        new_top = jnp.maximum(row_top, jnp.max(masked, axis=-1))
        fresh = jnp.sum(jnp.where(allowed, jnp.exp(masked - new_top[:, :, None]), 0.0), axis=-1)
        return ((new_top, row_sum * jnp.exp(row_top - new_top) + fresh), None)

    query_count = query_doc.shape[0]
    start = (
        jnp.full((H, query_count), mask_fill, jnp.float32),
        jnp.zeros((H, query_count), jnp.float32),
    )
    (row_top, row_sum), unused = lax.scan(row_visit, start, (key_blocks, doc_blocks, pos_blocks))
    return row_top + jnp.log(row_sum)


def attend_all(
    query_heads, key_blocks, value_blocks, doc_blocks, pos_blocks, query_doc, query_pos, log_norm
):

    def attend_visit(accum_out, block_item):
        key_heads, value_heads, key_doc, key_pos = block_item
        raw_scores, allowed = score_block(
            query_heads, key_heads, query_doc, query_pos, key_doc, key_pos
        )
        soft_low = soft_block(raw_scores, allowed, log_norm).astype(jnp.bfloat16)
        return (
            accum_out
            + jnp.einsum("hqk,khd->qhd", soft_low, value_heads, preferred_element_type=jnp.float32),
            None,
        )

    start = jnp.zeros(query_heads.shape, jnp.float32)
    accum_out, unused = lax.scan(
        attend_visit, start, (key_blocks, value_blocks, doc_blocks, pos_blocks)
    )
    return accum_out


def grad_block(
    query_heads,
    grad_heads,
    log_norm,
    row_delta,
    query_doc,
    query_pos,
    key_heads,
    value_heads,
    key_doc,
    key_pos,
):
    raw_scores, allowed = score_block(
        query_heads, key_heads, query_doc, query_pos, key_doc, key_pos
    )
    soft = soft_block(raw_scores, allowed, log_norm)
    grad_soft = jnp.einsum(
        "qhd,khd->hqk", grad_heads, value_heads, preferred_element_type=jnp.float32
    )
    grad_scores = (soft * (grad_soft - row_delta[:, :, None])).astype(jnp.bfloat16)
    score_scale = 1.0 / math.sqrt(HD)
    part_q = (
        jnp.einsum("hqk,khd->qhd", grad_scores, key_heads, preferred_element_type=jnp.float32)
        * score_scale
    )
    part_k = (
        jnp.einsum("hqk,qhd->khd", grad_scores, query_heads, preferred_element_type=jnp.float32)
        * score_scale
    )
    part_v = jnp.einsum(
        "hqk,qhd->khd", soft.astype(jnp.bfloat16), grad_heads, preferred_element_type=jnp.float32
    )
    return (part_q, part_k, part_v)


def general_body(
    inputs,
    out_grad,
    segment_ids,
    block_order,
    w_qkv,
    w_out,
    w_up,
    w_down,
    norm1_gain,
    norm1_bias,
    norm2_gain,
    norm2_bias,
    out_bias,
    up_bias,
    down_bias,
):
    gathered = (
        lax.all_gather(w_qkv, "fsdp", axis=0, tiled=True),
        lax.all_gather(w_out, "fsdp", axis=0, tiled=True),
        lax.all_gather(w_up, "fsdp", axis=0, tiled=True),
        lax.all_gather(w_down, "fsdp", axis=0, tiled=True),
        lax.all_gather(norm1_gain, "fsdp", axis=0, tiled=True),
        lax.all_gather(norm1_bias, "fsdp", axis=0, tiled=True),
        lax.all_gather(norm2_gain, "fsdp", axis=0, tiled=True),
        lax.all_gather(norm2_bias, "fsdp", axis=0, tiled=True),
        lax.all_gather(out_bias, "fsdp", axis=0, tiled=True),
        lax.all_gather(up_bias, "fsdp", axis=0, tiled=True),
        lax.all_gather(down_bias, "fsdp", axis=0, tiled=True),
    )
    full_qkv, full_out, full_up, full_down = (gathered[0], gathered[1], gathered[2], gathered[3])
    gain_one, bias_one, gain_two, bias_two, full_obias, full_ubias, full_dbias = [
        member.astype(jnp.float32) for member in gathered[4:]
    ]
    model_width = full_qkv.shape[0]
    local_rows = inputs.shape[2]
    ctx_count = lax.axis_size("ctx")
    seq_len = local_rows * ctx_count
    key_block = min(512, seq_len)
    block_count = seq_len // key_block
    ctx_index = lax.axis_index("ctx")
    row_ids = jnp.arange(local_rows, dtype=jnp.int32)
    own_blocks = lax.dynamic_slice_in_dim(block_order, 2 * ctx_index, 2)
    own_pos = own_blocks[row_ids // BLK] * BLK + row_ids % BLK
    all_ids = jnp.arange(seq_len, dtype=jnp.int32)
    all_pos = block_order[all_ids // BLK] * BLK + all_ids % BLK
    pos_blocks = all_pos.reshape(block_count, key_block)
    grad_sums = [jnp.zeros(member.shape, jnp.float32) for member in gathered]
    outputs_list = []
    input_grads = []
    for micro_idx in range(inputs.shape[0]):
        seq_in = inputs[micro_idx, 0].astype(jnp.float32)
        normed, norm1_pull = jax.vjp(layer_norm, seq_in, gain_one, bias_one)
        normed_low = normed.astype(jnp.bfloat16)
        qkv_out = jnp.dot(normed_low, full_qkv, preferred_element_type=jnp.float32).astype(
            jnp.bfloat16
        )
        query_heads = qkv_out[:, :model_width].reshape(local_rows, H, HD)
        kv_all, doc_all = (
            lax.all_gather(qkv_out[:, model_width:], "ctx", axis=0, tiled=True),
            lax.all_gather(segment_ids[micro_idx, 0], "ctx", axis=0, tiled=True),
        )
        doc_rows = doc_all[all_pos]
        query_doc = doc_all[own_pos]
        kv_heads = kv_all.reshape(block_count, key_block, 2, H, HD)
        key_blocks = kv_heads[:, :, 0]
        value_blocks = kv_heads[:, :, 1]
        doc_blocks = doc_rows.reshape(block_count, key_block)
        log_norm = row_log_norm(query_heads, key_blocks, doc_blocks, pos_blocks, query_doc, own_pos)
        attn_acc = attend_all(
            query_heads,
            key_blocks,
            value_blocks,
            doc_blocks,
            pos_blocks,
            query_doc,
            own_pos,
            log_norm,
        )
        attn_low = attn_acc.reshape(local_rows, model_width).astype(jnp.bfloat16)
        branch = jnp.dot(attn_low, full_out, preferred_element_type=jnp.float32) + full_obias
        middle = seq_in + branch
        normed_two, norm2_pull = jax.vjp(layer_norm, middle, gain_two, bias_two)
        normed_two_low = normed_two.astype(jnp.bfloat16)
        hidden = jnp.dot(normed_two_low, full_up, preferred_element_type=jnp.float32) + full_ubias
        active, gelu_pull = jax.vjp(gelu_exact, hidden)
        active_low = active.astype(jnp.bfloat16)
        result = middle + (
            jnp.dot(active_low, full_down, preferred_element_type=jnp.float32) + full_dbias
        )
        outputs_list.append(result.astype(jnp.bfloat16))
        grad_y = out_grad[micro_idx, 0]
        grad_y32 = grad_y.astype(jnp.float32)
        grad_sums[3] = grad_sums[3] + jnp.einsum(
            "rf,rd->fd", active_low, grad_y, preferred_element_type=jnp.float32
        )
        grad_sums[10] = grad_sums[10] + jnp.sum(grad_y32, axis=0)
        grad_active = jnp.einsum("rd,fd->rf", grad_y, full_down, preferred_element_type=jnp.float32)
        (grad_hidden,) = gelu_pull(grad_active)
        grad_hidden_low = grad_hidden.astype(jnp.bfloat16)
        grad_sums[2] = grad_sums[2] + jnp.einsum(
            "rd,rf->df", normed_two_low, grad_hidden_low, preferred_element_type=jnp.float32
        )
        grad_sums[9] = grad_sums[9] + jnp.sum(grad_hidden_low.astype(jnp.float32), axis=0)
        grad_normed_two = jnp.einsum(
            "rf,df->rd", grad_hidden_low, full_up, preferred_element_type=jnp.float32
        )
        grad_mid_ln, grad_gain_two, grad_bias_two = norm2_pull(grad_normed_two)
        grad_sums[6] = grad_sums[6] + grad_gain_two
        grad_sums[7] = grad_sums[7] + grad_bias_two
        grad_mid = grad_y32 + grad_mid_ln
        grad_mid_low = grad_mid.astype(jnp.bfloat16)
        grad_sums[1] = grad_sums[1] + jnp.einsum(
            "rd,re->de", attn_low, grad_mid_low, preferred_element_type=jnp.float32
        )
        grad_sums[8] = grad_sums[8] + jnp.sum(grad_mid_low.astype(jnp.float32), axis=0)
        grad_attn_low = jnp.einsum(
            "re,de->rd", grad_mid_low, full_out, preferred_element_type=jnp.float32
        ).astype(jnp.bfloat16)
        grad_heads = grad_attn_low.reshape(local_rows, H, HD)
        row_delta = jnp.sum(grad_heads.astype(jnp.float32) * attn_acc, axis=-1).T

        def back_visit(grad_query, block_item):
            key_heads, value_heads, key_doc, key_pos = block_item
            part_q, part_k, part_v = grad_block(
                query_heads,
                grad_heads,
                log_norm,
                row_delta,
                query_doc,
                own_pos,
                key_heads,
                value_heads,
                key_doc,
                key_pos,
            )
            joined = jnp.concatenate(
                [part_k.reshape(key_block, model_width), part_v.reshape(key_block, model_width)],
                axis=1,
            )
            return (grad_query + part_q, joined)

        grad_query, kv_terms = lax.scan(
            back_visit,
            jnp.zeros((local_rows, H, HD), jnp.float32),
            (key_blocks, value_blocks, doc_blocks, pos_blocks),
        )
        kv_grad = lax.psum_scatter(
            kv_terms.reshape(seq_len, 2 * model_width).astype(jnp.bfloat16),
            "ctx",
            scatter_dimension=0,
            tiled=True,
        ).astype(jnp.float32)
        grad_qkv_low = jnp.concatenate(
            [grad_query.reshape(local_rows, model_width), kv_grad], axis=1
        ).astype(jnp.bfloat16)
        grad_sums[0] = grad_sums[0] + jnp.einsum(
            "rd,re->de", normed_low, grad_qkv_low, preferred_element_type=jnp.float32
        )
        grad_normed = jnp.einsum(
            "re,de->rd", grad_qkv_low, full_qkv, preferred_element_type=jnp.float32
        )
        grad_in_ln, grad_gain_one, grad_bias_one = norm1_pull(grad_normed)
        grad_sums[4] = grad_sums[4] + grad_gain_one
        grad_sums[5] = grad_sums[5] + grad_bias_one
        input_grads.append(grad_mid + grad_in_ln)
    owned = (
        lax.psum_scatter(
            grad_sums[0].astype(jnp.bfloat16), "fsdp", scatter_dimension=0, tiled=True
        ).astype(jnp.float32),
        lax.psum_scatter(
            grad_sums[1].astype(jnp.bfloat16), "fsdp", scatter_dimension=0, tiled=True
        ).astype(jnp.float32),
        lax.psum_scatter(
            grad_sums[2].astype(jnp.bfloat16), "fsdp", scatter_dimension=0, tiled=True
        ).astype(jnp.float32),
        lax.psum_scatter(
            grad_sums[3].astype(jnp.bfloat16), "fsdp", scatter_dimension=0, tiled=True
        ).astype(jnp.float32),
        lax.psum_scatter(
            grad_sums[4].astype(jnp.bfloat16), "fsdp", scatter_dimension=0, tiled=True
        ).astype(jnp.float32),
        lax.psum_scatter(
            grad_sums[5].astype(jnp.bfloat16), "fsdp", scatter_dimension=0, tiled=True
        ).astype(jnp.float32),
        lax.psum_scatter(
            grad_sums[6].astype(jnp.bfloat16), "fsdp", scatter_dimension=0, tiled=True
        ).astype(jnp.float32),
        lax.psum_scatter(
            grad_sums[7].astype(jnp.bfloat16), "fsdp", scatter_dimension=0, tiled=True
        ).astype(jnp.float32),
        lax.psum_scatter(
            grad_sums[8].astype(jnp.bfloat16), "fsdp", scatter_dimension=0, tiled=True
        ).astype(jnp.float32),
        lax.psum_scatter(
            grad_sums[9].astype(jnp.bfloat16), "fsdp", scatter_dimension=0, tiled=True
        ).astype(jnp.float32),
        lax.psum_scatter(
            grad_sums[10].astype(jnp.bfloat16), "fsdp", scatter_dimension=0, tiled=True
        ).astype(jnp.float32),
    )
    summed = (
        lax.psum(owned[0].astype(jnp.bfloat16), "ctx").astype(jnp.float32),
        lax.psum(owned[1].astype(jnp.bfloat16), "ctx").astype(jnp.float32),
        lax.psum(owned[2].astype(jnp.bfloat16), "ctx").astype(jnp.float32),
        lax.psum(owned[3].astype(jnp.bfloat16), "ctx").astype(jnp.float32),
        lax.psum(owned[4].astype(jnp.bfloat16), "ctx").astype(jnp.float32),
        lax.psum(owned[5].astype(jnp.bfloat16), "ctx").astype(jnp.float32),
        lax.psum(owned[6].astype(jnp.bfloat16), "ctx").astype(jnp.float32),
        lax.psum(owned[7].astype(jnp.bfloat16), "ctx").astype(jnp.float32),
        lax.psum(owned[8].astype(jnp.bfloat16), "ctx").astype(jnp.float32),
        lax.psum(owned[9].astype(jnp.bfloat16), "ctx").astype(jnp.float32),
        lax.psum(owned[10].astype(jnp.bfloat16), "ctx").astype(jnp.float32),
    )
    return (
        jnp.stack(outputs_list)[:, None],
        jnp.stack(input_grads)[:, None],
        summed[0],
        summed[1],
        summed[2],
        summed[3],
        summed[4],
        summed[5],
        summed[6],
        summed[7],
        summed[8],
        summed[9],
        summed[10],
    )


AXES = ("z", "x", "y", "c")
SIZES = (4, 2, 2, 2)


MESH = pl.DeviceIdType.MESH


def send(src, dst, sems, recv_sems, index, peer):
    copy = pltpu.make_async_remote_copy(
        src_ref=src,
        dst_ref=dst,
        send_sem=sems.at[index],
        recv_sem=recv_sems.at[index],
        device_id=peer,
        device_id_type=MESH,
    )
    copy.start()
    return copy


def greet(peers, extra, extra_on):
    barrier = pltpu.get_barrier_semaphore()
    for peer in peers:
        pl.semaphore_signal(barrier, inc=1, device_id=peer, device_id_type=MESH)

    @pl.when(extra_on)
    def _():
        for peer in extra:
            pl.semaphore_signal(barrier, inc=1, device_id=peer, device_id_type=MESH)

    pl.semaphore_wait(barrier, len(peers) + jnp.where(extra_on, len(extra), 0))


HEAD_CHUNK = 128
SAFE_SCORE = 80.0


def head_kernel(
    x_in_ref, dy_in_ref, docs_in_ref, order_ref, g1_ref, b1_ref, g2_ref, b2_ref, ob_ref, db_ref, ub_in_ref, wq_ref, wo_ref, wu_ref, wd_ref,
    qt_ref, k_ref, kt_ref, v_ref, vt_ref, ut_ref, own_ref, wo_all, wu_all, wd_all, dy_ref,
    wh_ref, vec_ref, ub_ref, start_ref, tab_ref,
    qt_buf, k_buf, kt_buf, v_buf, vt_buf, ut_buf, rows, docs, docs_true, norms, vec_in_ref, vec_all, wo_tmp, wu_tmp, wd_tmp,
    z_s, z_r, x_s, x_r, c_s, c_r, f_s, f_r, docs_s, docs_r, vec_s, vec_r, wh_s, wh_r, wh_l,
    y_s, y_r, n_s, n_r, o_s, o_r, load_sem, put_sem, self_sem, d_s, d_r, d_self, out_sem,
):
    z, x, y, c = (lax.axis_index(name) for name in AXES)
    odd, upper = lax.rem(z, 2), lax.div(z, 2)
    width = x_in_ref.shape[-1]
    chunks = rows.shape[1] // HEAD_CHUNK
    per_turn = chunks // 2
    by_core, by_x, by_y, by_yc = {"c": 1 - c}, {"x": 1 - x}, {"y": 1 - y}, {"y": 1 - y, "c": 1 - c}
    home = [{"z": 2 * c + upper, "c": odd}, {"z": 2 * c + 1 - upper, "c": odd}]
    target = [{"z": 2 * odd + c, "c": upper}, {"z": 2 * (1 - odd) + c, "c": upper}]
    block = [odd, 1 - odd]
    stay = (c == upper) & (odd == c)
    leave = jnp.logical_not(stay)
    for i, ref in enumerate((g1_ref, b1_ref, g2_ref, b2_ref, ob_ref, db_ref, ub_in_ref)):
        vec_in_ref[i : i + ref.shape[0]] = ref[...]
    greet([by_core, by_x, by_y, by_yc, home[1], target[1]], [home[0], target[0]], leave)

    def order_of(i):
        return i % 2 * per_turn + i // 2

    def piece(i):
        turn, row = order_of(i) // per_turn, (order_of(i) % per_turn) * HEAD_CHUNK
        return (
            x_in_ref.at[block[turn], 0, pl.ds(row, HEAD_CHUNK)],
            rows.at[0, pl.ds(order_of(i) * HEAD_CHUNK, HEAD_CHUNK)],
        )

    for turn in range(2):
        src, dst = docs_in_ref.at[block[turn]], docs.at[0, turn]

        def start_docs():
            send(src, dst, docs_s, docs_r, turn, target[turn])

        if turn == 0:
            pl.when(stay)(lambda: pltpu.make_async_copy(src, dst, self_sem.at[per_turn]).start())
            pl.when(leave)(start_docs)
        else:
            start_docs()
    for i in range(chunks):
        src, dst = piece(i)
        if i % 2 == 0:
            pl.when(stay)(lambda: pltpu.make_async_copy(src, dst, self_sem.at[i // 2]).start())
            pl.when(leave)(lambda: send(src, dst, z_s, z_r, i, target[0]) and None)
        else:
            send(src, dst, z_s, z_r, i, target[1])

    def piece_dy(i):
        part = pl.ds(i * HEAD_CHUNK, HEAD_CHUNK)
        return dy_in_ref.at[odd, 0, part], dy_ref.at[part]

    def send_dy(i):
        src, dst = piece_dy(i)
        pl.when(stay)(lambda: pltpu.make_async_copy(src, dst, d_self.at[i]).start())
        pl.when(leave)(lambda: send(src, dst, d_s, d_r, i, target[0]) and None)

    def land_dy(i):
        src, dst = piece_dy(i)
        pl.when(stay)(lambda: pltpu.make_async_copy(src, dst, d_self.at[i]).wait())
        pl.when(leave)(
            lambda: pltpu.make_async_remote_copy(
                src_ref=src, dst_ref=dst, send_sem=d_s.at[i], recv_sem=d_r.at[i],
                device_id=target[0], device_id_type=MESH,
            ).wait()
        )

    def landed(src, dst, sems, recv_sems, index, turn, self_index):
        def remote():
            pltpu.make_async_remote_copy(
                src_ref=src, dst_ref=dst, send_sem=sems.at[index], recv_sem=recv_sems.at[index],
                device_id=target[turn], device_id_type=MESH,
            ).wait()

        if turn == 0:
            pl.when(stay)(lambda: pltpu.make_async_copy(src, dst, self_sem.at[self_index]).wait())
            pl.when(leave)(remote)
        else:
            remote()

    mine = 2 * y + c
    vec_copy = [
        send(vec_in_ref, vec_all.at[mine], vec_s, vec_r, i, peer)
        for i, peer in enumerate((by_core, by_y, by_yc))
    ]
    vec_all[mine] = vec_in_ref[...]
    wh_copy = []
    shard = wq_ref.shape[0]
    own_rows = pl.ds(pl.multiple_of(mine * shard, shard), shard)
    for part in range(3):
        to = wh_ref.at[own_rows, pl.ds(part * PAIR, PAIR)]

        def columns(core):
            return wq_ref.at[:, pl.ds(pl.multiple_of(part * width + (2 * x + core) * PAIR, PAIR), PAIR)]

        for i, (peer, core) in enumerate(((by_core, 1 - c), (by_y, c), (by_yc, 1 - c))):
            wh_copy.append(send(columns(core), to, wh_s, wh_r, 3 * part + i, peer))
        copy = pltpu.make_async_copy(columns(c), to, wh_l.at[part])
        copy.start()
        wh_copy.append(copy)

    up_rows, down_rows = wu_ref.shape[0] // 4, wd_ref.shape[0] // 4
    parts = [(wo_ref, wo_all, wo_ref.shape[0], 0)]
    parts += [(wu_ref, wu_all, up_rows, i * up_rows) for i in range(4)]
    parts += [(wd_ref, wd_all, down_rows, i * down_rows) for i in range(4)]

    def at_owner(full, src, size, offset, owner):
        return full.at[pl.ds(pl.multiple_of(owner * src.shape[0] + offset, 32), size)]

    other = 2 * (1 - y) + c
    y_copy = []
    for i, (src, full, size, offset) in enumerate(parts):
        y_copy.append(
            send(src.at[pl.ds(offset, size)], at_owner(full, src, size, offset, mine), y_s, y_r, i, by_y)
        )
    n_copy, load_copy, put_copy = [], [], []
    for i, (src, full, tmp) in enumerate(((wo_ref, wo_all, wo_tmp), (wu_ref, wu_all, wu_tmp), (wd_ref, wd_all, wd_tmp))):
        n_copy.append(send(src, at_owner(full, src, src.shape[0], 0, mine), n_s, n_r, i, by_core))
        load_copy.append(pltpu.make_async_copy(src, tmp, load_sem.at[i]))
        load_copy[-1].start()

    def put(i):
        src, full, tmp = ((wo_ref, wo_all, wo_tmp), (wu_ref, wu_all, wu_tmp), (wd_ref, wd_all, wd_tmp))[i]
        load_copy[i].wait()
        put_copy.append(pltpu.make_async_copy(tmp, at_owner(full, src, src.shape[0], 0, mine), put_sem.at[i]))
        put_copy[-1].start()

    o_copy = []

    def forward(i):
        src, full, size, offset = parts[i]
        y_copy[i].wait()
        held = at_owner(full, src, size, offset, other)
        o_copy.append(send(held, held, o_s, o_r, i, by_core))

    blocks = order_ref.shape[0]
    lane = lax.broadcasted_iota(jnp.int32, (1, 128), 1)
    slots = jnp.zeros((1, 128), jnp.int32)
    for t in range(blocks):
        dc, dx, turn, half = t // 8, t // 4 % 2, t // 2 % 2, t % 2
        core, side = (1 - c if dc else c), (1 - x if dx else x)
        stored = 2 * (2 * (2 * core + (1 - upper if turn else upper)) + side) + half
        slots = jnp.where(lane == order_ref[stored], t, slots)

    docs_copy = {}

    def finish_docs():
        docs_copy["c"].wait()
        docs_copy["f"].wait()
        for g in range(4):
            core, side = (1 - c if g // 2 else c), (1 - x if g % 2 else x)
            for turn in range(2):
                docs_true[2 * (2 * core + (1 - upper if turn else upper)) + side] = docs[g, turn]
        numbers = docs_true[...]
        first = jnp.zeros_like(numbers)
        for d in range(1, blocks):
            before = jnp.sum((numbers < d).astype(jnp.int32), axis=(0, 1, 2), keepdims=True)
            first = jnp.where(numbers == d, before, first)
        docs_true[...] = first
        low = jnp.zeros((1, 128), jnp.int32)
        for b in range(blocks):
            line = docs_true[b // 2]
            at = 2 * (b % 2)
            line = jnp.concatenate([line[at : at + 1], line[at + 1 : at + 2]], axis=1)
            start_ref[b] = line
            low = jnp.where(lane == b, line[:, :1] // BLK, low)
        high = jnp.zeros((1, 128), jnp.int32) - 1
        for b in range(blocks):
            high = high + (low[:, b : b + 1] <= lane).astype(jnp.int32)
        tab_ref[...] = jnp.concatenate([low, high, slots, jnp.zeros((5, 128), jnp.int32)], axis=0)

    def docs_first():
        for turn in range(2):
            landed(docs_in_ref.at[block[turn]], docs.at[0, turn], docs_s, docs_r, turn, turn, per_turn)
        docs_copy["x"] = send(docs.at[0], docs.at[1], docs_s, docs_r, 2, by_x)
        docs_copy["c"] = send(docs.at[0], docs.at[2], docs_s, docs_r, 3, by_core)


    def vectors_and_weight():
        for copy in vec_copy:
            copy.wait()
        vec_width = vec_in_ref.shape[1]
        for j in range(4):
            for i in range(6):
                vec_ref[i : i + 1, j * vec_width : (j + 1) * vec_width] = vec_all[j, i : i + 1].astype(f32)
            for i in range(4):
                at = (4 * j + i) * vec_width
                ub_ref[:, at : at + vec_width] = vec_all[j, 6 + i : 7 + i].astype(f32)
        vec_ref[6:8] = jnp.zeros((2, width), f32)
        for copy in wh_copy:
            copy.wait()


    def docs_second():
        docs_copy["x"].wait()
        docs_copy["f"] = send(docs.at[1], docs.at[3], docs_s, docs_r, 4, by_core)


    x_copy, c_copy, f_copy = [], [], []

    def relay(i):
        src, dst = piece(i)
        landed(src, dst, z_s, z_r, i, i % 2, i // 2)
        part = pl.ds(order_of(i) * HEAD_CHUNK, HEAD_CHUNK)
        x_copy.append(send(rows.at[0, part], rows.at[1, part], x_s, x_r, i, by_x))
        c_copy.append(send(rows.at[0, part], rows.at[2, part], c_s, c_r, i, by_core))

    def relay_far(i):
        x_copy[i].wait()
        part = pl.ds(order_of(i) * HEAD_CHUNK, HEAD_CHUNK)
        f_copy.append(send(rows.at[1, part], rows.at[3, part], f_s, f_r, i, by_core))

    streams = (
        (qt_buf, qt_ref, 1), (k_buf, k_ref, 0), (kt_buf, kt_ref, 1), (v_buf, v_ref, 0), (vt_buf, vt_ref, 1),
        (ut_buf, ut_ref, 1),
    )

    def compute(g, i):
        count = rows.shape[1]
        chunk = order_of(i)
        unit, _ = norm_parts(rows[g, chunk * HEAD_CHUNK : (chunk + 1) * HEAD_CHUNK].astype(f32))
        at = pl.ds(g * count + chunk * HEAD_CHUNK, HEAD_CHUNK)
        ut_buf[:, at] = unit.astype(bf16).T
        low = (unit * vec_ref[0:1] + vec_ref[1:2]).astype(bf16)
        qkv = jnp.dot(low, wh_ref[...], preferred_element_type=f32)
        qt = (qkv[:, :PAIR] * (SCORE_SCALE * LOG2E)).astype(bf16).T
        qt_buf[:, at] = qt
        k = qkv[:, PAIR : 2 * PAIR].astype(bf16)
        v = qkv[:, 2 * PAIR :].astype(bf16)
        k_buf[at] = k
        v_buf[at] = v
        kt = k.T
        kt_buf[:, at] = kt
        vt_buf[:, at] = v.T
        found = []
        for block_ in (qt, kt):
            squares = block_.astype(f32) * block_.astype(f32)
            found += [jnp.sum(squares[head * HD : (head + 1) * HD], axis=0, keepdims=True) for head in range(2)]
        found = jnp.concatenate(found, axis=0)
        norms[...] = found if g == 0 and i == 0 else jnp.maximum(norms[...], found)
        for index, (source, out, columns) in enumerate(streams):
            if columns:
                source, out = source.at[:, at], out.at[:, at]
            else:
                source, out = source.at[at], out.at[at]
            pltpu.make_async_copy(source, out, out_sem.at[index]).start()

    docs_first()
    for i in range(chunks + 2):
        if i < chunks:
            if i < per_turn:
                send_dy(i)
            relay(i)
        if i == 0:
            vectors_and_weight()
            docs_second()
        if 1 <= i <= chunks:
            relay_far(i - 1)
            compute(0, i - 1)
            compute(1, i - 1)
            c_copy[i - 1].wait()
            compute(2, i - 1)
        if i >= 2:
            f_copy[i - 2].wait()
            compute(3, i - 2)
        if i == 1:
            finish_docs()
        if 2 <= i < 5:
            put(i - 2)
        if i >= 3 and i - 3 < len(parts):
            forward(i - 3)
        if i == chunks - 1:
            own_copy = pltpu.make_async_copy(rows.at[0], own_ref, out_sem.at[len(streams)])
            own_copy.start()
    largest = jnp.max(norms[...], axis=1, keepdims=True)
    bound = jnp.maximum(largest[0:1] * largest[2:3], largest[1:2] * largest[3:4])
    tab_ref[3:4] = jnp.broadcast_to((bound <= SAFE_SCORE * SAFE_SCORE).astype(jnp.int32), (1, 128))
    for i in range(chunks - 1, len(parts)):
        forward(i)
    for index, (source, out, _) in enumerate(streams):
        pltpu.make_async_copy(source, out, out_sem.at[index]).wait()
    own_copy.wait()
    for copy in n_copy + put_copy + o_copy:
        copy.wait()
    for i in range(per_turn):
        land_dy(i)


def head(x_in, dy_in, docs_in, order, vectors, w_qkv, w_out, w_up, w_down):
    width = x_in.shape[-1]
    count = 2 * x_in.shape[2]
    total = 4 * count
    shard = w_qkv.shape[0]
    chunks = count // HEAD_CHUNK
    blocks = order.shape[0]
    vmem, any_ = pl.BlockSpec(memory_space=pltpu.VMEM), pl.BlockSpec(memory_space=pl.ANY)
    smem = pl.BlockSpec(memory_space=pltpu.SMEM)
    dma, buf, shape = pltpu.SemaphoreType.DMA, pltpu.VMEM, jax.ShapeDtypeStruct
    return pl.pallas_call(
        head_kernel,
        in_specs=[any_, any_, vmem, smem] + [vmem] * 7 + [any_] * 4,
        out_specs=[any_] * 11 + [vmem] * 5,
        out_shape=[
            shape((PAIR, total), bf16),
            shape((total, PAIR), bf16),
            shape((PAIR, total), bf16),
            shape((total, PAIR), bf16),
            shape((PAIR, total), bf16),
            shape((width, total), bf16),
            shape((count, width), bf16),
            shape((4 * w_out.shape[0], w_out.shape[1]), bf16),
            shape((4 * w_up.shape[0], w_up.shape[1]), bf16),
            shape((4 * w_down.shape[0], w_down.shape[1]), bf16),
            shape((count // 2, width), bf16),
            shape((width, 3 * PAIR), bf16),
            shape((8, width), f32),
            shape((1, 4 * w_down.shape[0]), f32),
            shape((blocks, 1, BLK), jnp.int32),
            shape((8, 128), jnp.int32),
        ],
        scratch_shapes=[
            buf((PAIR, total), bf16),
            buf((total, PAIR), bf16),
            buf((PAIR, total), bf16),
            buf((total, PAIR), bf16),
            buf((PAIR, total), bf16),
            buf((width, total), bf16),
            buf((4, count, width), bf16),
            buf((4, 2) + docs_in.shape[1:], jnp.int32),
            buf((blocks // 2,) + docs_in.shape[1:], jnp.int32),
            buf((4, HEAD_CHUNK), f32),
            buf((16, shard), bf16),
            buf((4, 16, shard), bf16),
            buf(w_out.shape, bf16),
            buf(w_up.shape, bf16),
            buf(w_down.shape, bf16),
        ]
        + [dma((chunks,))] * 8
        + [dma((5,)), dma((5,)), dma((3,)), dma((3,)), dma((9,)), dma((9,)), dma((3,))]
        + [dma((9,)), dma((9,)), dma((3,)), dma((3,)), dma((9,)), dma((9,)), dma((3,)), dma((3,))]
        + [dma((chunks // 2 + 1,)), dma((chunks // 2,))] + [dma((chunks // 2,))] * 2 + [dma((7,))],
        compiler_params=pltpu.CompilerParams(
            collective_id=1, has_side_effects=True, vmem_limit_bytes=56 * 1024 * 1024
        ),
        name="head",
    )(x_in, dy_in, docs_in, order, *[v.reshape(-1, shard) for v in vectors], w_qkv, w_out, w_up, w_down)
FF_TILE = 512
PIECES = 3
feed_steps = 4


def feed_kernel(
    o_ref, x_ref, dy_near_ref, dy_in_ref, wo_ref, wu_ref, wd_ref, vec_ref, ub_ref,
    do_ref, y_home, dmid_ref, keep_ref, to_y_ref, to_x_ref, to_xy_ref, gvec_ref, gub_ref,
    attn_all, gd_ref, gu_ref, go_ref, attn_in, do_out, y_out, grad_ref, grad_in,
    dy_ref, dy_far, a_s, a_r, a_l, d_s, d_r, d_l, y_s, y_r, y_l, g_s, g_r, c_s, c_r,
):
    step = pl.program_id(0)
    steps = pl.num_programs(0)
    groups = attn_in.shape[0]
    tile = x_ref.shape[0]
    z, x, y, c = (lax.axis_index(name) for name in AXES)
    odd, upper = lax.rem(z, 2), lax.div(z, 2)
    mates = [None, {"x": 1 - x}, {"c": 1 - c}, {"x": 1 - x, "c": 1 - c}]
    pair_of = [2 * x + c, 2 * (1 - x) + c, 2 * x + 1 - c, 2 * (1 - x) + 1 - c]
    home = [{"z": 2 * c + upper, "c": odd}, {"z": 2 * c + 1 - upper, "c": odd}]
    origin = [{"z": 2 * odd + c, "c": upper}, {"z": 2 * (1 - odd) + c, "c": upper}]
    stay = (c == upper) & (odd == c)
    leave = jnp.logical_not(stay)
    half = feed_steps // 2

    def attn_copy(g, i):
        part = pl.ds(i * tile, tile)
        return pltpu.make_async_remote_copy(
            src_ref=o_ref.at[g, part], dst_ref=attn_in.at[g, part],
            send_sem=a_s.at[g - 1, i], recv_sem=a_r.at[g - 1, i], device_id=mates[g], device_id_type=MESH,
        )

    def attn_own(i):
        part = pl.ds(i * tile, tile)
        return pltpu.make_async_copy(o_ref.at[0, part], attn_in.at[0, part], a_l.at[i])

    def do_copy(g, i):
        return pltpu.make_async_remote_copy(
            src_ref=do_out.at[i, g], dst_ref=do_ref.at[g, pl.ds(i * tile, tile)],
            send_sem=d_s.at[g - 1, i], recv_sem=d_r.at[g - 1, i], device_id=mates[g], device_id_type=MESH,
        )

    def do_own(i):
        return pltpu.make_async_copy(do_out.at[i, 0], do_ref.at[0, pl.ds(i * tile, tile)], d_l.at[i])

    def y_rows(i, block):
        return y_home.at[block, pl.ds(lax.rem(i, half) * tile, tile)]

    def y_copy(i, turn, block):
        return pltpu.make_async_remote_copy(
            src_ref=y_out.at[i], dst_ref=y_rows(i, block),
            send_sem=y_s.at[i], recv_sem=y_r.at[i], device_id=home[turn], device_id_type=MESH,
        )

    def y_own(i, block):
        return pltpu.make_async_copy(y_out.at[i], y_rows(i, block), y_l.at[i])

    def grad_copy(i):
        return pltpu.make_async_remote_copy(
            src_ref=grad_ref.at[2 * i + 1 - c], dst_ref=grad_in.at[i],
            send_sem=g_s.at[i], recv_sem=g_r.at[i], device_id=mates[2], device_id_type=MESH,
        )

    def dy_copy(i):
        part = pl.ds(i * tile, tile)
        return pltpu.make_async_remote_copy(
            src_ref=dy_in_ref.at[1 - odd, 0, part], dst_ref=dy_far.at[part],
            send_sem=c_s.at[i], recv_sem=c_r.at[i], device_id=origin[1], device_id_type=MESH,
        )

    @pl.when(step == 0)
    def _():
        greet(mates[1:] + [home[1], origin[1]], [home[0], origin[0]], leave)
        for i in range(feed_steps):
            for g in (1, 3, 2):
                attn_copy(g, i).start()
            attn_own(i).start()
        for i in range(half):
            dy_copy(i).start()

    @pl.when(step == 0)
    def _():
        for ref in (gd_ref, gu_ref, go_ref, gvec_ref, gub_ref):
            ref[...] = jnp.zeros_like(ref)

    @pl.when(step < half)
    def _():
        dy_ref[...] = dy_near_ref[...]

    @pl.when(step >= half)
    def _():
        dy_copy(step - half).wait()
        dy_ref[...] = dy_far[pl.ds(pl.multiple_of((step - half) * tile, tile), tile)]

    attn_own(step).wait()
    for g in range(1, groups):
        attn_copy(g, step).wait()
    for g in range(groups):
        attn_all[:, pl.ds(pl.multiple_of(pair_of[g] * PAIR, PAIR), PAIR)] = attn_in[
            g, pl.ds(pl.multiple_of(step * tile, tile), tile)
        ]
    attn = attn_all[...]
    gain, bias, out_bias, down_bias = (vec_ref[i : i + 1, :] for i in range(2, 6))
    middle = (
        x_ref[...].astype(f32) + jnp.dot(attn, wo_ref[...], preferred_element_type=f32) + out_bias
    )
    unit, inv = norm_parts(middle)
    low = (unit * gain + bias).astype(bf16)
    dy = dy_ref[...]
    dy32 = dy.astype(f32)
    total = middle + down_bias
    d_low = jnp.zeros_like(middle)
    width = wu_ref.shape[1]
    for j in range(0, width, FF_TILE):
        part = pl.ds(j, FF_TILE)
        up = wu_ref[:, part]
        down = wd_ref[part, :]
        hidden = jnp.dot(low, up, preferred_element_type=f32) + ub_ref[:, part]
        cdf = 0.5 * (1.0 + lax.erf(hidden * (1.0 / math.sqrt(2.0))))
        active = (hidden * cdf).astype(bf16)
        slope = cdf + hidden * (jnp.exp2(hidden * hidden * (-0.5 * LOG2E)) * (1.0 / math.sqrt(2.0 * math.pi)))
        total = total + jnp.dot(active, down, preferred_element_type=f32)
        d_hidden = contract(dy, down, 1, 1) * slope
        d_hidden_low = d_hidden.astype(bf16)
        gub_ref[:, part] += jnp.sum(d_hidden, axis=0, keepdims=True)
        d_low = d_low + contract(d_hidden_low, up, 1, 1)
        gd_ref[part, :] += contract(active, dy, 0, 0)
        gu_ref[:, part] += contract(low, d_hidden_low, 0, 0)
    y_out[step] = total.astype(bf16)

    @pl.when((step < half) & stay)
    def _():
        y_own(step, upper).start()

    @pl.when((step < half) & leave)
    def _():
        y_copy(step, 0, upper).start()

    @pl.when(step >= half)
    def _():
        y_copy(step, 1, upper).start()

    scaled = d_low * gain
    d_middle = dy32 + inv * (
        scaled
        - jnp.mean(scaled, axis=-1, keepdims=True)
        - unit * jnp.mean(scaled * unit, axis=-1, keepdims=True)
    )
    dmid_ref[...] = d_middle
    branch = d_middle.astype(bf16)
    go_ref[...] += contract(attn, branch, 0, 0)
    gvec_ref[0:1, :] += jnp.sum(d_middle, axis=0, keepdims=True)
    gvec_ref[1:2, :] += jnp.sum(d_low * unit, axis=0, keepdims=True)
    gvec_ref[2:3, :] += jnp.sum(d_low, axis=0, keepdims=True)
    gvec_ref[3:4, :] += jnp.sum(dy32, axis=0, keepdims=True)
    attn_all[...] = contract(branch, wo_ref[...], 1, 1).astype(bf16)
    for g in (1, 3, 2, 0):
        do_out[step, g] = attn_all[:, pl.ds(pl.multiple_of(pair_of[g] * PAIR, PAIR), PAIR)]
        if g:
            do_copy(g, step).start()
        else:
            do_own(step).start()

    @pl.when(step == steps - 1)
    def _():
        shards = grad_ref.shape[0]
        d_model = x_ref.shape[1]
        down_rows, up_rows = gd_ref.shape[0] // shards, d_model // shards
        for j in range(shards):
            grad_ref[j, :down_rows] = gd_ref[j * down_rows : (j + 1) * down_rows].astype(bf16)
            rows = slice(j * up_rows, (j + 1) * up_rows)
            at = down_rows
            for t in range(0, width, d_model):
                grad_ref[j, at : at + up_rows] = gu_ref[rows, t : t + d_model].astype(bf16)
                at += up_rows
            grad_ref[j, at : at + up_rows] = go_ref[rows].astype(bf16)
        for j in range(2):
            grad_copy(j).start()
        for j in range(feed_steps):
            do_own(j).wait()
            for g in range(1, groups):
                do_copy(g, j).wait()
            if j < half:
                @pl.when(stay)
                def _():
                    y_own(j, odd).wait()

                @pl.when(leave)
                def _():
                    y_copy(j, 0, odd).wait()
            else:
                y_copy(j, 1, 1 - odd).wait()
        sixth = keep_ref.shape[1]
        for j in range(2):
            grad_copy(j).wait()
        for dy_, dx_, ref in ((0, 0, keep_ref), (1, 0, to_y_ref), (0, 1, to_x_ref), (1, 1, to_xy_ref)):
            row = 1 - y if dy_ else y
            side = 1 - x if dx_ else x
            for p in range(PIECES):
                part = pl.ds(pl.multiple_of((2 * p + side) * sixth, 16), sixth)
                ref[p] = (
                    grad_ref[2 * row + c, part].astype(f32) + grad_in[row, part].astype(f32)
                ).astype(bf16)


def feed(o, x, dy_near, dy_in, w_out, w_up, w_down, vecs, up_bias, shards):
    groups, count, _ = o.shape
    width = x.shape[1]
    flat = (w_out.size + w_up.size + w_down.size) // shards // width
    tile = count // feed_steps
    piece = (PIECES, flat // PIECES // 2, width)
    rows = pl.BlockSpec((tile, width), lambda i: (i, 0))
    any_ = pl.BlockSpec(memory_space=pl.ANY)
    dma, buf, shape = pltpu.SemaphoreType.DMA, pltpu.VMEM, jax.ShapeDtypeStruct
    return pl.pallas_call(
        feed_kernel,
        grid=(feed_steps,),
        in_specs=[
            any_, rows, pl.BlockSpec((tile, width), lambda i: (jnp.minimum(i, feed_steps // 2 - 1), 0)), any_, whole(w_out.shape), whole(w_up.shape), whole(w_down.shape),
            whole(vecs.shape), whole(up_bias.shape),
        ],
        out_specs=[any_, any_, rows] + [whole(piece)] * 4 + [whole(vecs.shape), whole(up_bias.shape)],
        out_shape=[
            shape((groups, count, PAIR), bf16),
            shape((2, count // 2, width), bf16),
            shape((count, width), f32),
            shape(piece, bf16),
            shape(piece, bf16),
            shape(piece, bf16),
            shape(piece, bf16),
            shape(vecs.shape, f32),
            shape(up_bias.shape, f32),
        ],
        scratch_shapes=[
            buf((tile, width), bf16),
            buf(w_down.shape, f32),
            buf(w_up.shape, f32),
            buf(w_out.shape, f32),
            buf((groups, count, PAIR), bf16),
            buf((feed_steps, groups, tile, PAIR), bf16),
            buf((feed_steps, tile, width), bf16),
            buf((shards, flat, width), bf16),
            buf((2, flat, width), bf16),
            buf((tile, width), bf16),
            buf((count // 2, width), bf16),
            dma((3, feed_steps)),
            dma((3, feed_steps)),
            dma((feed_steps,)),
            dma((3, feed_steps)),
            dma((3, feed_steps)),
            dma((feed_steps,)),
            dma((feed_steps,)),
            dma((feed_steps,)),
            dma((feed_steps,)),
            dma((2,)),
            dma((2,)),
            dma((feed_steps // 2,)),
            dma((feed_steps // 2,)),
        ],
        compiler_params=pltpu.CompilerParams(
            collective_id=3, has_side_effects=True, vmem_limit_bytes=60 * 1024 * 1024
        ),
        name="feed",
    )(o, x, dy_near, dy_in, w_out, w_up, w_down, vecs, up_bias)


TAIL_CHUNK = 128


def tail_kernel(
    dh_ref, x_hbm, dmid_hbm, gain_ref, keep_ref, from_y_ref, from_x_ref, from_xy_ref, gw_ref, gn_ref, gvecs_ref, gub_ref,
    home_buf, gfull, wall, sum_ref,
    x_ref, dmid_ref, core_buf, own_dh, x_out, x_buf, dx_out,
    gsum, gz1s, gz1r, gz2s, gz2r,
    wy, ws, wz1s, wz1r, wz2s, wz2r, wfull,
    small_ref, small_out, small_in,
    local_sem, self_sem, core_s, core_r, x_s, x_r, home_s, home_r, g_s, g_r, w_s, w_r, s_s, s_r, in_sem,
):
    z, x, y, c = (lax.axis_index(name) for name in AXES)
    odd, upper = lax.rem(z, 2), lax.div(z, 2)
    width = x_ref.shape[1]
    chunks = x_ref.shape[0] // TAIL_CHUNK
    per_turn = chunks // 2
    by_core, by_x, by_y, by_xc = {"c": 1 - c}, {"x": 1 - x}, {"y": 1 - y}, {"x": 1 - x, "c": 1 - c}
    by_z1, by_z2 = {"z": z + 1 - 2 * odd}, {"z": z + 2 - 4 * upper}
    home = [{"z": 2 * c + upper, "c": odd}, {"z": 2 * c + 1 - upper, "c": odd}]
    origin = [{"z": 2 * odd + c, "c": upper}, {"z": 2 * (1 - odd) + c, "c": upper}]
    stay = (c == upper) & (odd == c)
    inputs = [
        pltpu.make_async_copy(x_hbm, x_ref, in_sem.at[0]), pltpu.make_async_copy(dmid_hbm, dmid_ref, in_sem.at[1])
    ]
    for copy in inputs:
        copy.start()
    small_ref[...] = jnp.zeros_like(small_ref)
    small_ref[0:2] = gn_ref[...]
    small_ref[2:4] = gvecs_ref[1:3]
    small_ref[4:5] = gvecs_ref[0:1]
    small_ref[5:6] = gvecs_ref[3:4]
    for i in range(4):
        small_ref[6 + i : 7 + i] = gub_ref[:, i * width : (i + 1) * width]
    greet(
        [by_core, by_x, by_y, by_xc, by_z1, by_z2, home[1], origin[1]],
        [home[0], origin[0]],
        jnp.logical_not(stay),
    )
    small_peers = [by_x, by_core, by_y, by_z1, by_z2]
    s_copy = [send(small_ref, small_in.at[0], s_s, s_r, 0, small_peers[0])]
    to_core, locals_ = [], []
    for i in range(chunks):
        part = pl.ds(i * TAIL_CHUNK, TAIL_CHUNK)
        to_core.append(
            send(dh_ref.at[pl.ds(2, 2), part], core_buf.at[:, part], core_s, core_r, i, by_core)
        )
        copy = pltpu.make_async_copy(dh_ref.at[pl.ds(0, 2), part], own_dh.at[:, part], local_sem.at[i])
        copy.start()
        locals_.append(copy)
    w_copy = {}
    w_copy["y"] = send(gw_ref.at[pl.ds(2 * (1 - y), 2)], wy, w_s, w_r, 0, by_y)
    g_copy = {}

    def g_start(p):
        for half in range(2):
            part = pl.ds(96 * half, 96)
            gsum[p, part] = (
                keep_ref[p, part].astype(f32)
                + from_y_ref[p, part].astype(f32)
                + from_x_ref[p, part].astype(f32)
                + from_xy_ref[p, part].astype(f32)
            )
        gz1s[p] = gsum[p, pl.ds(pl.multiple_of(96 * (1 - odd), 16), 96)].astype(bf16)
        g_copy["z1", p] = send(gz1s.at[p], gz1r.at[p], g_s, g_r, 5 * p, by_z1)

    mine_half = pl.multiple_of(96 * odd, 16)
    mine_quarter = pl.multiple_of(96 * odd + 48 * upper, 16)
    give_quarter = pl.multiple_of(96 * odd + 48 * (1 - upper), 16)

    def g_second(p):
        g_copy["z1", p].wait()
        gsum[p, pl.ds(mine_half, 96)] += gz1r[p].astype(f32)
        gz2s[p] = gsum[p, pl.ds(give_quarter, 48)].astype(bf16)
        g_copy["z2", p] = send(gz2s.at[p], gz2r.at[p], g_s, g_r, 5 * p + 1, by_z2)

    def g_third(p):
        g_copy["z2", p].wait()
        part = pl.ds(mine_quarter, 48)
        gfull[p, x, part] = (gsum[p, part] + gz2r[p].astype(f32)).astype(bf16)
        place_ = gfull.at[p, x, part]
        g_copy["z2b", p] = send(place_, place_, g_s, g_r, 5 * p + 2, by_z2)

    def g_fourth(p):
        g_copy["z2b", p].wait()
        place_ = gfull.at[p, x, pl.ds(mine_half, 96)]
        g_copy["z1b", p] = send(place_, place_, g_s, g_r, 5 * p + 3, by_z1)

    def g_fifth(p):
        g_copy["z1b", p].wait()
        g_copy["x", p] = send(gfull.at[p, x], gfull.at[p, x], g_s, g_r, 5 * p + 4, by_x)

    def w_second():
        w_copy["y"].wait()
        for i in range(2):
            ws[i] = gw_ref[2 * y + i].astype(f32) + wy[i].astype(f32)
        wz1s[...] = ws[1 - odd].astype(bf16)
        w_copy["z1"] = send(wz1s, wz1r, w_s, w_r, 1, by_z1)

    def w_third():
        w_copy["z1"].wait()
        ws[odd] += wz1r[...].astype(f32)
        wz2s[...] = ws[odd, pl.ds(pl.multiple_of(64 * (1 - upper), 64), 64)].astype(bf16)
        w_copy["z2"] = send(wz2s, wz2r, w_s, w_r, 2, by_z2)

    def w_fourth():
        w_copy["z2"].wait()
        part = pl.ds(pl.multiple_of(64 * upper, 64), 64)
        wfull[odd, part] = (ws[odd, part] + wz2r[...].astype(f32)).astype(bf16)
        place_ = wfull.at[odd, part]
        w_copy["z2b"] = send(place_, place_, w_s, w_r, 3, by_z2)

    def w_fifth():
        w_copy["z2b"].wait()
        w_copy["z1b"] = send(wfull.at[odd], wfull.at[odd], w_s, w_r, 4, by_z1)

    def w_sixth():
        w_copy["z1b"].wait()
        mine = 2 * x + c
        w_copy["core"] = send(wfull.at[1 - c], wall.at[mine], w_s, w_r, 5, by_core)
        w_copy["x"] = send(wfull.at[c], wall.at[mine], w_s, w_r, 6, by_x)
        w_copy["xc"] = send(wfull.at[1 - c], wall.at[mine], w_s, w_r, 7, by_xc)

    def s_next(step):
        s_copy[step].wait()
        before = small_ref[...] if step == 0 else small_out[step - 1]
        small_out[step] = before + small_in[step]
        if step + 1 < len(small_peers):
            s_copy.append(
                send(small_out.at[step], small_in.at[step + 1], s_s, s_r, step + 1, small_peers[step + 1])
            )

    x_copy, home_copy = [], []

    def add_core(i):
        part = pl.ds(i * TAIL_CHUNK, TAIL_CHUNK)
        to_core[i].wait()
        locals_[i].wait()
        x_out[part] = (own_dh[1, part].astype(f32) + core_buf[1, part].astype(f32)).astype(bf16)
        x_copy.append(send(x_out.at[part], x_buf.at[part], x_s, x_r, i, by_x))

    def finish(i):
        part = pl.ds(i * TAIL_CHUNK, TAIL_CHUNK)
        if i == 0:
            for copy in inputs:
                copy.wait()
        x_copy[i].wait()
        d_low = own_dh[0, part].astype(f32) + core_buf[0, part].astype(f32) + x_buf[part].astype(f32)
        unit, inv = norm_parts(x_ref[part].astype(f32))
        scaled = d_low * gain_ref[...]
        dx = dmid_ref[part] + inv * (
            scaled
            - jnp.mean(scaled, axis=-1, keepdims=True)
            - unit * jnp.mean(scaled * unit, axis=-1, keepdims=True)
        )
        dx_out[part] = dx.astype(bf16)
        turn, row = i // per_turn, (i % per_turn) * TAIL_CHUNK
        target = home_buf.at[upper, pl.ds(row, TAIL_CHUNK)]
        if turn == 0:
            @pl.when(stay)
            def _():
                pltpu.make_async_copy(dx_out.at[part], target, self_sem.at[i]).start()

            @pl.when(jnp.logical_not(stay))
            def _():
                send(dx_out.at[part], target, home_s, home_r, i, home[0])
        else:
            send(dx_out.at[part], target, home_s, home_r, i, home[1])

    def arrive(i):
        part = pl.ds(i * TAIL_CHUNK, TAIL_CHUNK)
        turn, row = i // per_turn, (i % per_turn) * TAIL_CHUNK
        block = odd if turn == 0 else 1 - odd
        landed = home_buf.at[block, pl.ds(row, TAIL_CHUNK)]

        def remote():
            copy = pltpu.make_async_remote_copy(
                src_ref=dx_out.at[part], dst_ref=landed, send_sem=home_s.at[i], recv_sem=home_r.at[i],
                device_id=home[turn], device_id_type=MESH,
            )
            copy.wait_send()
            copy.wait_recv()

        if turn == 0:
            @pl.when(stay)
            def _():
                pltpu.make_async_copy(dx_out.at[part], landed, self_sem.at[i]).wait()

            pl.when(jnp.logical_not(stay))(remote)
        else:
            remote()

    g_start(0)
    add_core(0)
    g_start(1)
    add_core(1)
    g_start(2)
    add_core(2)
    s_next(0)
    s_next(1)
    g_second(0)
    w_second()
    g_second(1)
    g_second(2)
    finish(0)
    add_core(3)
    s_next(2)
    g_third(0)
    finish(1)
    add_core(4)
    w_third()
    g_third(1)
    g_third(2)
    s_next(3)
    finish(2)
    add_core(5)
    g_fourth(0)
    w_fourth()
    finish(3)
    add_core(6)
    s_next(4)
    g_fourth(1)
    g_fourth(2)
    w_fifth()
    finish(4)
    add_core(7)
    g_fifth(0)
    finish(5)
    w_sixth()
    g_fifth(1)
    finish(6)
    g_fifth(2)
    finish(7)
    w_copy["core"].wait()
    w_copy["x"].wait()
    w_copy["xc"].wait()
    wall[2 * x + c] = wfull[c]
    sum_ref[...] = small_out[4]
    for i in range(chunks):
        arrive(i)
    for p in range(PIECES):
        g_copy["x", p].wait()


def tail(dh, x, dmid, gain, keep, from_y, from_x, from_xy, gw, gn, gvecs, gub):
    count, width = x.shape
    shard = gw.shape[1]
    half = count // 2
    chunks = count // TAIL_CHUNK
    sixth = keep.shape[1]
    vmem = pl.BlockSpec(memory_space=pltpu.VMEM)
    dma = pltpu.SemaphoreType.DMA
    buf = pltpu.VMEM
    return pl.pallas_call(
        tail_kernel,
        in_specs=[pl.BlockSpec(memory_space=pl.ANY)] * 3 + [vmem] * 9,
        out_specs=[vmem] * 4,
        out_shape=[
            jax.ShapeDtypeStruct((2, half, width), bf16),
            jax.ShapeDtypeStruct((PIECES, 2, sixth, width), bf16),
            jax.ShapeDtypeStruct((4, shard, 3 * PAIR), bf16),
            jax.ShapeDtypeStruct((16, width), f32),
        ],
        scratch_shapes=[
            buf((count, width), bf16),
            buf((count, width), f32),
            buf((2, count, width), bf16),
            buf((2, count, width), bf16),
            buf((count, width), bf16),
            buf((count, width), bf16),
            buf((count, width), bf16),
            buf((PIECES, sixth, width), f32),
            buf((PIECES, sixth // 2, width), bf16),
            buf((PIECES, sixth // 2, width), bf16),
            buf((PIECES, sixth // 4, width), bf16),
            buf((PIECES, sixth // 4, width), bf16),
            buf((2, shard, 3 * PAIR), bf16),
            buf((2, shard, 3 * PAIR), f32),
            buf((shard, 3 * PAIR), bf16),
            buf((shard, 3 * PAIR), bf16),
            buf((shard // 2, 3 * PAIR), bf16),
            buf((shard // 2, 3 * PAIR), bf16),
            buf((2, shard, 3 * PAIR), bf16),
            buf((16, width), f32),
            buf((5, 16, width), f32),
            buf((5, 16, width), f32),
            dma((chunks,)),
            dma((chunks // 2,)),
            dma((chunks,)),
            dma((chunks,)),
            dma((chunks,)),
            dma((chunks,)),
            dma((chunks,)),
            dma((chunks,)),
            dma((5 * PIECES,)),
            dma((5 * PIECES,)),
            dma((8,)),
            dma((8,)),
            dma((5,)),
            dma((5,)),
            dma((2,)),
        ],
        compiler_params=pltpu.CompilerParams(
            collective_id=5, has_side_effects=True, vmem_limit_bytes=56 * 1024 * 1024
        ),
        name="tail",
    )(dh, x, dmid, gain, keep, from_y, from_x, from_xy, gw, gn, gvecs, gub)

def results_kernel(
    y_ref, dx_ref, down_ref, up_ref, out_ref, wall_ref, sum_ref,
    y_out, dx_out, gd_ref, gu_ref, go_ref, gq_ref, *vectors,
):
    step = pl.program_id(0)
    width = dx_ref.shape[-1]
    y_out[:, 0] = y_ref[...]
    dx_out[:, 0] = dx_ref[...].astype(f32)
    gd_ref[...] = down_ref[...].astype(f32)
    gu_ref[...] = up_ref[...].astype(f32)
    go_ref[...] = out_ref[...].astype(f32)
    for part in range(3):
        at = pl.multiple_of(part * width + step * PAIR, PAIR)
        gq_ref[:, pl.ds(at, PAIR)] = wall_ref[0, :, part * PAIR : (part + 1) * PAIR].astype(f32)
    shard = go_ref.shape[0]
    mine = 2 * lax.axis_index("y") + lax.axis_index("c")
    for i in range(6):
        vectors[i][...] = sum_ref[i : i + 1, pl.ds(pl.multiple_of(mine * shard, shard), shard)]
    vectors[6][...] = sum_ref[pl.ds(6 + mine, 1), :]


def results(y, dx, flat, wall, sums):
    half, width = dx.shape[1:]
    shard = wall.shape[1]
    steps = 4
    flat = flat.reshape(-1, width)
    tokens = pl.BlockSpec((2, half // steps, width), lambda i: (0, i, 0))
    tokens_out = pl.BlockSpec((2, 1, half // steps, width), lambda i: (0, 0, i, 0))
    shape = jax.ShapeDtypeStruct
    return pl.pallas_call(
        results_kernel,
        grid=(steps,),
        in_specs=[
            tokens,
            tokens,
            pl.BlockSpec((shard, width), lambda i: (i, 0)),
            pl.BlockSpec((shard, width), lambda i: (steps + i, 0)),
            pl.BlockSpec((shard, width), lambda i: (2 * steps, 0)),
            pl.BlockSpec((1, shard, 3 * PAIR), lambda i: (i, 0, 0)),
            whole(sums.shape),
        ],
        out_specs=[
            tokens_out,
            tokens_out,
            pl.BlockSpec((shard, width), lambda i: (i, 0)),
            pl.BlockSpec((shard, width), lambda i: (0, i)),
            whole((shard, width)),
            whole((shard, 3 * width)),
        ]
        + [whole((1, shard))] * 6
        + [whole((1, width))],
        out_shape=[
            shape((2, 1, half, width), bf16),
            shape((2, 1, half, width), f32),
            shape((width, width), f32),
            shape((shard, 4 * width), f32),
            shape((shard, width), f32),
            shape((shard, 3 * width), f32),
        ]
        + [shape((1, shard), f32)] * 6
        + [shape((1, width), f32)],
        name="results",
    )(y, dx, flat, flat, flat, wall, sums)


def place(z, x, y, c):
    return ((z * SIZES[1] + x) * SIZES[2] + y) * SIZES[3] + c


def everyone():
    return [
        (z, x, y, c)
        for z in range(SIZES[0])
        for x in range(SIZES[1])
        for y in range(SIZES[2])
        for c in range(SIZES[3])
    ]


def swap_pairs(dx, dy, dc):
    return [(place(z, x, y, c), place(z, x ^ dx, y ^ dy, c ^ dc)) for z, x, y, c in everyone()]


def move(value, pairs):
    return lax.ppermute(value, AXES, pairs)


def swap(value, dx=0, dy=0, dc=0):
    return move(value, swap_pairs(dx, dy, dc))


def paired_body(
    inputs, out_grad, segment_ids, block_order, w_qkv, w_out, w_up, w_down,
    norm1_gain, norm1_bias, norm2_gain, norm2_bias, out_bias, up_bias, down_bias,
):
    vectors = (norm1_gain, norm1_bias, norm2_gain, norm2_bias, out_bias, down_bias, up_bias)
    (
        qt, k, kt, v, vt, unit, own_x, full_out, full_up, full_down, near_dy, w_heads, vecs, full_ubias, start, tab
    ) = head(
        inputs, out_grad, segment_ids.reshape(2, -1, 128), block_order, vectors, w_qkv, w_out, w_up, w_down
    )
    gain_one, bias_one = vecs[0:1], vecs[1:2]
    o, ot, lse = attend(tab, qt, start, k, vt)
    d_o, outputs, d_middle, keep, to_y, to_x, to_xy, g_vecs, g_ubias = feed(
        o.reshape(4, -1, PAIR), own_x, near_dy, out_grad, full_out, full_up, full_down, vecs, full_ubias, 4
    )
    from_y, from_x, from_xy = swap(to_y, dy=1), swap(to_x, dx=1), swap(to_xy, dy=1, dx=1)
    dh, g_heads, g_norm = attend_back(
        tab, k, kt, v, unit, w_heads, qt, start, d_o.reshape(-1, PAIR), ot, lse, gain_one, bias_one, 4
    )
    dx, flat, heads, sums = tail(
        dh.reshape(4, -1, dh.shape[1]), own_x, d_middle, gain_one, keep, from_y, from_x, from_xy,
        g_heads, g_norm, g_vecs, g_ubias,
    )
    outputs, input_grad, grad_down, grad_up, grad_out, grad_qkv, *vec = results(outputs, dx, flat, heads, sums)
    vec = [member.reshape(-1) for member in vec]
    return (
        outputs, input_grad, grad_qkv, grad_out, grad_up, grad_down,
        vec[0], vec[1], vec[2], vec[3], vec[4], vec[6], vec[5],
    )


def solution(mesh):
    paired = mesh.shape["ctx"] == SIZES[0] * SIZES[1] and mesh.shape["fsdp"] == SIZES[2] * SIZES[3]
    if paired:
        mesh = Mesh(mesh.devices.reshape(SIZES), AXES)
        ctx, fsdp, program = ("z", "x"), ("y", "c"), paired_body
    else:
        ctx, fsdp, program = "ctx", "fsdp", general_body
    tokens = P(None, fsdp, ctx, None)
    matrix, vector = P(fsdp, None), P(fsdp)
    return jax.shard_map(
        program,
        mesh=mesh,
        in_specs=(tokens, tokens, P(None, fsdp, ctx), P()) + (matrix,) * 4 + (vector,) * 7,
        out_specs=(tokens, tokens) + (matrix,) * 4 + (vector,) * 7,
        check_vma=False,
    )
```

```python
import functools
import math

import jax
import jax.numpy as jnp
from jax import lax
from jax.experimental import pallas as pl
from jax.experimental.pallas import tpu as pltpu
from jax.sharding import Mesh
from jax.sharding import PartitionSpec as P

H = 8
HD = 64
BLK = 256
PAIR = 2 * HD

norm_eps = 1e-05
mask_fill = -1e30
LOG2E = math.log2(math.e)
LN2 = math.log(2.0)
SCORE_SCALE = 1.0 / math.sqrt(HD)

f32 = jnp.float32
bf16 = jnp.bfloat16


def contract(a, b, da, db):
    return lax.dot_general(a, b, (((da,), (db,)), ((), ())), preferred_element_type=f32)


def norm_parts(values):
    center = values - jnp.mean(values, axis=-1, keepdims=True)
    spread = jnp.mean(center * center, axis=-1, keepdims=True)
    inv = lax.rsqrt(spread + norm_eps)
    return center * inv, inv


def whole(shape):
    zeros = (0,) * len(shape)
    return pl.BlockSpec(shape, lambda *_: zeros)


def two_heads(block):
    zero = jnp.zeros((HD, block.shape[1]), block.dtype)
    return jnp.concatenate(
        [jnp.concatenate([block[:HD], zero], axis=0), jnp.concatenate([zero, block[HD:]], axis=0)], axis=1
    )


EXTRA = 16


def attend_kernel(
    tab_ref, qt_ref, start_ref, k_ref, vt_ref, o_hbm, ot_hbm, lse_ref, acc, top, o_buf, ot_buf, out_sem
):
    blocks = start_ref.shape[0]
    row = lax.broadcasted_iota(jnp.int32, (BLK, 2 * BLK), 0)
    reach = row - jnp.bitwise_and(lax.broadcasted_iota(jnp.int32, (BLK, 2 * BLK), 1), BLK - 1)
    ones = jnp.ones((EXTRA, 2 * BLK), bf16)

    def place_of(b):
        return pl.ds(pl.multiple_of(tab_ref[2, jnp.maximum(b, 0)] * BLK, BLK), BLK)

    def visits_of(qb):
        return (qb - tab_ref[0, qb]) // 2 + 1

    def visit(qb, i, bounded):
        kb = qb - 2 * i
        both = two_heads(qt_ref[:, place_of(qb)])
        start = jnp.concatenate([start_ref[qb], start_ref[qb]], axis=1)
        places = [place_of(kb), place_of(kb - 1)]
        terms = []
        for n in range(2):
            allowed = row >= start - (kb - n) * BLK
            if n == 0:
                allowed = allowed & (reach <= (qb - kb) * BLK)
            st = jnp.dot(k_ref[places[n], :], both, preferred_element_type=f32)
            terms.append(jnp.where(allowed, st, mask_fill))
        if bounded:
            probs = [jnp.exp2(term).astype(bf16) for term in terms]
        else:
            old = top[qb]
            peak = jnp.maximum(
                jnp.max(terms[0], axis=0, keepdims=True), jnp.max(terms[1], axis=0, keepdims=True)
            )
            peak = jnp.maximum(old, peak)
            shrink = jnp.exp2(old - peak)
            top[qb] = peak
            probs = [jnp.exp2(term - peak).astype(bf16) for term in terms]
        probs = jnp.concatenate(probs, axis=0)
        vt = jnp.concatenate([vt_ref[:, places[0]], vt_ref[:, places[1]]], axis=1)
        for head in range(2):
            cols = slice(head * BLK, (head + 1) * BLK)
            left = jnp.concatenate([vt[head * HD : (head + 1) * HD], ones], axis=0)
            part = jnp.dot(left, probs[:, cols], preferred_element_type=f32)
            acc[qb, head] = part + (acc[qb, head] if bounded else acc[qb, head] * shrink[:, cols])

    def all_visits(bounded):
        count = lax.fori_loop(0, blocks, lambda b, n: n + visits_of(b), 0)

        def step(n, state):
            qb, i = state
            visit(qb, i, bounded)
            more = i + 1 < visits_of(qb)
            return jnp.where(more, qb, jnp.minimum(qb + 1, blocks - 1)), jnp.where(more, i + 1, 0)

        lax.fori_loop(0, count, step, (jnp.int32(0), jnp.int32(0)))

    small = tab_ref[3, 0] > 0
    acc[...] = jnp.zeros_like(acc)

    @pl.when(small)
    def _():
        top[...] = jnp.zeros_like(top)
        all_visits(True)

    @pl.when(jnp.logical_not(small))
    def _():
        top[...] = jnp.full_like(top, mask_fill)
        all_visits(False)

    def outgoing(b):
        at = place_of(b)
        return (
            pltpu.make_async_copy(o_buf.at[b], o_hbm.at[at], out_sem.at[0]),
            pltpu.make_async_copy(ot_buf.at[b], ot_hbm.at[b], out_sem.at[1]),
        )

    def close(b):
        total = jnp.concatenate([acc[b, 0, HD : HD + 1], acc[b, 1, HD : HD + 1]], axis=1)
        lse_ref[b] = top[b] + jnp.log2(total)
        heads = jnp.concatenate([acc[b, h, :HD] / acc[b, h, HD : HD + 1] for h in range(2)], axis=0)
        ot_buf[b] = heads
        o_buf[b] = heads.T.astype(bf16)
        for copy in outgoing(b):
            copy.start()

    def close_two(n, carry):
        close(2 * n)
        close(2 * n + 1)
        return carry

    lax.fori_loop(0, blocks // 2, close_two, 0)
    for whole_copy in (
        pltpu.make_async_copy(ot_buf, ot_hbm, out_sem.at[1]),
        pltpu.make_async_copy(o_hbm, o_hbm, out_sem.at[0]),
    ):
        whole_copy.wait()


def attend(tab, qt, start, k, vt):
    count = k.shape[0]
    blocks = count // BLK
    vmem, any_ = pl.BlockSpec(memory_space=pltpu.VMEM), pl.BlockSpec(memory_space=pl.ANY)
    return pl.pallas_call(
        attend_kernel,
        grid_spec=pltpu.PrefetchScalarGridSpec(
            num_scalar_prefetch=1,
            grid=(),
            in_specs=[vmem] * 4,
            out_specs=[any_, any_, vmem],
            scratch_shapes=[
                pltpu.VMEM((blocks, 2, HD + EXTRA, BLK), f32),
                pltpu.VMEM((blocks, 1, 2 * BLK), f32),
                pltpu.VMEM((blocks, BLK, PAIR), bf16),
                pltpu.VMEM((blocks, PAIR, BLK), f32),
                pltpu.SemaphoreType.DMA((2,)),
            ],
        ),
        out_shape=[
            jax.ShapeDtypeStruct((count, PAIR), bf16),
            jax.ShapeDtypeStruct((blocks, PAIR, BLK), f32),
            jax.ShapeDtypeStruct((blocks, 1, 2 * BLK), f32),
        ],
        name="attend",
    )(tab, qt, start, k, vt)


def split_heads(block):
    lane = lax.broadcasted_iota(jnp.int32, block.shape, 1)
    zero = jnp.zeros_like(block)
    first = lane < HD
    return jnp.concatenate([jnp.where(first, block, zero), jnp.where(first, zero, block)], axis=0)


def attend_back_kernel(
    tab_ref, k_hbm, kt_hbm, v_hbm, qt_ref, start_ref, do_ref, ot_ref, lse_ref, out_hbm,
    k_ref, kt_ref, v_ref, out_buf, dqt, dk, dv, dot, dom, qm, delta, in_sem, out_sem,
):
    blocks = start_ref.shape[0]
    row = lax.broadcasted_iota(jnp.int32, (BLK, 2 * BLK), 0)
    reach = row - jnp.bitwise_and(lax.broadcasted_iota(jnp.int32, (BLK, 2 * BLK), 1), BLK - 1)
    loads = [
        pltpu.make_async_copy(src, dst, in_sem.at[i])
        for i, (src, dst) in enumerate(((k_hbm, k_ref), (kt_hbm, kt_ref), (v_hbm, v_ref)))
    ]
    for copy in loads:
        copy.start()

    def at(b):
        return pl.ds(pl.multiple_of(tab_ref[2, b] * BLK, BLK), BLK)

    def prepare(qb):
        dqt[qb] = jnp.zeros((PAIR, BLK), f32)
        dk[qb] = jnp.zeros((BLK, PAIR), f32)
        dv[qb] = jnp.zeros((BLK, PAIR), f32)
        d_out = do_ref[at(qb), :]
        dom[qb] = split_heads(d_out)
        qm[qb] = split_heads(qt_ref[:, at(qb)].T)
        turned = d_out.astype(f32).T
        dot[qb] = turned.astype(bf16)
        both = turned * ot_ref[qb]
        delta[qb] = jnp.concatenate(
            [jnp.sum(both[:HD], axis=0, keepdims=True), jnp.sum(both[HD:], axis=0, keepdims=True)], axis=1
        )

    def prepare_two(n, carry):
        prepare(2 * n)
        prepare(2 * n + 1)
        return carry

    lax.fori_loop(0, blocks // 2, prepare_two, 0)
    for copy in loads:
        copy.wait()

    def tile(kb, qb, live):
        kt = kt_ref[:, at(kb)]
        start = jnp.concatenate([start_ref[qb], start_ref[qb]], axis=1)
        st = jnp.dot(k_ref[at(kb), :], two_heads(qt_ref[:, at(qb)]), preferred_element_type=f32)
        dpt = jnp.dot(v_ref[at(kb), :], two_heads(dot[qb]), preferred_element_type=f32)
        allowed = (row >= start - kb * BLK) & (reach <= jnp.where(live, (qb - kb) * BLK, -2 * BLK))
        pt = jnp.exp2(jnp.where(allowed, st - lse_ref[qb], mask_fill))
        dst = (pt * (dpt - delta[qb])).astype(bf16)
        part_v = jnp.dot(pt.astype(bf16), dom[qb], preferred_element_type=f32)
        part_k = jnp.dot(dst, qm[qb], preferred_element_type=f32)
        part_q = [
            jnp.dot(kt[head * HD : (head + 1) * HD], dst[:, head * BLK : (head + 1) * BLK], preferred_element_type=f32)
            for head in range(2)
        ]
        return kb, qb, part_v, part_k, jnp.concatenate(part_q, axis=0)

    def add(kb, qb, part_v, part_k, part_q):
        dv[kb] += part_v
        dk[kb] += part_k
        dqt[qb] += part_q

    def following(kb, qb):
        more = qb < tab_ref[1, kb]
        beyond = jnp.minimum(kb + 1, blocks - 1)
        return jnp.where(more, kb, beyond), jnp.where(more, qb + 1, beyond)

    tiles = lax.fori_loop(0, blocks, lambda b, n: n + tab_ref[1, b] - b + 1, 0)

    def step(n, state):
        second = following(*state)
        terms = [tile(*state, True), tile(*second, 2 * n + 1 < tiles)]
        for term in terms:
            add(*term)
        return following(*second)

    lax.fori_loop(0, (tiles + 1) // 2, step, (jnp.int32(0), jnp.int32(0)))
    def close(b):
        out_buf[b] = jnp.concatenate([(dqt[b] * SCORE_SCALE).T, dk[b] * LN2, dv[b]], axis=1).astype(bf16)
        pltpu.make_async_copy(out_buf.at[b], out_hbm.at[at(b)], out_sem.at[0]).start()

    def close_four(n, carry):
        for i in range(4):
            close(4 * n + i)
        return carry

    lax.fori_loop(0, blocks // 4, close_four, 0)
    pltpu.make_async_copy(out_hbm, out_hbm, out_sem.at[0]).wait()


def attend_back(tab, k, kt, v, qt, start, d_out, ot, lse):
    count = k.shape[0]
    blocks = count // BLK
    vmem, any_ = pl.BlockSpec(memory_space=pltpu.VMEM), pl.BlockSpec(memory_space=pl.ANY)
    buf = pltpu.VMEM
    return pl.pallas_call(
        attend_back_kernel,
        grid_spec=pltpu.PrefetchScalarGridSpec(
            num_scalar_prefetch=1,
            grid=(),
            in_specs=[any_] * 3 + [vmem] * 5,
            out_specs=any_,
            scratch_shapes=[
                buf(k.shape, bf16),
                buf(kt.shape, bf16),
                buf(v.shape, bf16),
                buf((blocks, BLK, 3 * PAIR), bf16),
                buf((blocks, PAIR, BLK), f32),
                buf((blocks, BLK, PAIR), f32),
                buf((blocks, BLK, PAIR), f32),
                buf((blocks, PAIR, BLK), bf16),
                buf((blocks, 2 * BLK, PAIR), bf16),
                buf((blocks, 2 * BLK, PAIR), bf16),
                buf((blocks, 1, 2 * BLK), f32),
                pltpu.SemaphoreType.DMA((3,)),
                pltpu.SemaphoreType.DMA((1,)),
            ],
        ),
        out_shape=jax.ShapeDtypeStruct((count, 3 * PAIR), bf16),
        compiler_params=pltpu.CompilerParams(vmem_limit_bytes=60 * 1024 * 1024),
        name="attend_back",
    )(tab, k, kt, v, qt, start, d_out, ot, lse)


def layer_norm(values, gain_vec, offset):
    center = values - jnp.mean(values, axis=-1, keepdims=True)
    spread = jnp.mean(center * center, axis=-1, keepdims=True)
    return center * lax.rsqrt(spread + norm_eps) * gain_vec + offset


def gelu_exact(values):
    return 0.5 * values * (1.0 + lax.erf(values * (1.0 / math.sqrt(2.0))))


def score_block(query_heads, key_heads, query_doc, query_pos, key_doc, key_pos):
    raw_scores = jnp.einsum(
        "qhd,khd->hqk", query_heads, key_heads, preferred_element_type=jnp.float32
    ) * (1.0 / math.sqrt(HD))
    allowed = (query_doc[:, None] == key_doc[None, :]) & (key_pos[None, :] <= query_pos[:, None])
    return (raw_scores, allowed[None])


def soft_block(raw_scores, allowed, log_norm):
    return jnp.exp(jnp.where(allowed, raw_scores, mask_fill) - log_norm[:, :, None])


def row_log_norm(query_heads, key_blocks, doc_blocks, pos_blocks, query_doc, query_pos):

    def row_visit(running, block_item):
        row_top, row_sum = running
        key_heads, key_doc, key_pos = block_item
        raw_scores, allowed = score_block(
            query_heads, key_heads, query_doc, query_pos, key_doc, key_pos
        )
        masked = jnp.where(allowed, raw_scores, mask_fill)
        new_top = jnp.maximum(row_top, jnp.max(masked, axis=-1))
        fresh = jnp.sum(jnp.where(allowed, jnp.exp(masked - new_top[:, :, None]), 0.0), axis=-1)
        return ((new_top, row_sum * jnp.exp(row_top - new_top) + fresh), None)

    query_count = query_doc.shape[0]
    start = (
        jnp.full((H, query_count), mask_fill, jnp.float32),
        jnp.zeros((H, query_count), jnp.float32),
    )
    (row_top, row_sum), unused = lax.scan(row_visit, start, (key_blocks, doc_blocks, pos_blocks))
    return row_top + jnp.log(row_sum)


def attend_all(
    query_heads, key_blocks, value_blocks, doc_blocks, pos_blocks, query_doc, query_pos, log_norm
):

    def attend_visit(accum_out, block_item):
        key_heads, value_heads, key_doc, key_pos = block_item
        raw_scores, allowed = score_block(
            query_heads, key_heads, query_doc, query_pos, key_doc, key_pos
        )
        soft_low = soft_block(raw_scores, allowed, log_norm).astype(jnp.bfloat16)
        return (
            accum_out
            + jnp.einsum("hqk,khd->qhd", soft_low, value_heads, preferred_element_type=jnp.float32),
            None,
        )

    start = jnp.zeros(query_heads.shape, jnp.float32)
    accum_out, unused = lax.scan(
        attend_visit, start, (key_blocks, value_blocks, doc_blocks, pos_blocks)
    )
    return accum_out


def grad_block(
    query_heads,
    grad_heads,
    log_norm,
    row_delta,
    query_doc,
    query_pos,
    key_heads,
    value_heads,
    key_doc,
    key_pos,
):
    raw_scores, allowed = score_block(
        query_heads, key_heads, query_doc, query_pos, key_doc, key_pos
    )
    soft = soft_block(raw_scores, allowed, log_norm)
    grad_soft = jnp.einsum(
        "qhd,khd->hqk", grad_heads, value_heads, preferred_element_type=jnp.float32
    )
    grad_scores = (soft * (grad_soft - row_delta[:, :, None])).astype(jnp.bfloat16)
    score_scale = 1.0 / math.sqrt(HD)
    part_q = (
        jnp.einsum("hqk,khd->qhd", grad_scores, key_heads, preferred_element_type=jnp.float32)
        * score_scale
    )
    part_k = (
        jnp.einsum("hqk,qhd->khd", grad_scores, query_heads, preferred_element_type=jnp.float32)
        * score_scale
    )
    part_v = jnp.einsum(
        "hqk,qhd->khd", soft.astype(jnp.bfloat16), grad_heads, preferred_element_type=jnp.float32
    )
    return (part_q, part_k, part_v)


def general_body(
    inputs,
    out_grad,
    segment_ids,
    block_order,
    w_qkv,
    w_out,
    w_up,
    w_down,
    norm1_gain,
    norm1_bias,
    norm2_gain,
    norm2_bias,
    out_bias,
    up_bias,
    down_bias,
):
    gathered = (
        lax.all_gather(w_qkv, "fsdp", axis=0, tiled=True),
        lax.all_gather(w_out, "fsdp", axis=0, tiled=True),
        lax.all_gather(w_up, "fsdp", axis=0, tiled=True),
        lax.all_gather(w_down, "fsdp", axis=0, tiled=True),
        lax.all_gather(norm1_gain, "fsdp", axis=0, tiled=True),
        lax.all_gather(norm1_bias, "fsdp", axis=0, tiled=True),
        lax.all_gather(norm2_gain, "fsdp", axis=0, tiled=True),
        lax.all_gather(norm2_bias, "fsdp", axis=0, tiled=True),
        lax.all_gather(out_bias, "fsdp", axis=0, tiled=True),
        lax.all_gather(up_bias, "fsdp", axis=0, tiled=True),
        lax.all_gather(down_bias, "fsdp", axis=0, tiled=True),
    )
    full_qkv, full_out, full_up, full_down = (gathered[0], gathered[1], gathered[2], gathered[3])
    gain_one, bias_one, gain_two, bias_two, full_obias, full_ubias, full_dbias = [
        member.astype(jnp.float32) for member in gathered[4:]
    ]
    model_width = full_qkv.shape[0]
    local_rows = inputs.shape[2]
    ctx_count = lax.axis_size("ctx")
    seq_len = local_rows * ctx_count
    key_block = min(512, seq_len)
    block_count = seq_len // key_block
    ctx_index = lax.axis_index("ctx")
    row_ids = jnp.arange(local_rows, dtype=jnp.int32)
    own_blocks = lax.dynamic_slice_in_dim(block_order, 2 * ctx_index, 2)
    own_pos = own_blocks[row_ids // BLK] * BLK + row_ids % BLK
    all_ids = jnp.arange(seq_len, dtype=jnp.int32)
    all_pos = block_order[all_ids // BLK] * BLK + all_ids % BLK
    pos_blocks = all_pos.reshape(block_count, key_block)
    grad_sums = [jnp.zeros(member.shape, jnp.float32) for member in gathered]
    outputs_list = []
    input_grads = []
    for micro_idx in range(inputs.shape[0]):
        seq_in = inputs[micro_idx, 0].astype(jnp.float32)
        normed, norm1_pull = jax.vjp(layer_norm, seq_in, gain_one, bias_one)
        normed_low = normed.astype(jnp.bfloat16)
        qkv_out = jnp.dot(normed_low, full_qkv, preferred_element_type=jnp.float32).astype(
            jnp.bfloat16
        )
        query_heads = qkv_out[:, :model_width].reshape(local_rows, H, HD)
        kv_all, doc_all = (
            lax.all_gather(qkv_out[:, model_width:], "ctx", axis=0, tiled=True),
            lax.all_gather(segment_ids[micro_idx, 0], "ctx", axis=0, tiled=True),
        )
        doc_rows = doc_all[all_pos]
        query_doc = doc_all[own_pos]
        kv_heads = kv_all.reshape(block_count, key_block, 2, H, HD)
        key_blocks = kv_heads[:, :, 0]
        value_blocks = kv_heads[:, :, 1]
        doc_blocks = doc_rows.reshape(block_count, key_block)
        log_norm = row_log_norm(query_heads, key_blocks, doc_blocks, pos_blocks, query_doc, own_pos)
        attn_acc = attend_all(
            query_heads,
            key_blocks,
            value_blocks,
            doc_blocks,
            pos_blocks,
            query_doc,
            own_pos,
            log_norm,
        )
        attn_low = attn_acc.reshape(local_rows, model_width).astype(jnp.bfloat16)
        branch = jnp.dot(attn_low, full_out, preferred_element_type=jnp.float32) + full_obias
        middle = seq_in + branch
        normed_two, norm2_pull = jax.vjp(layer_norm, middle, gain_two, bias_two)
        normed_two_low = normed_two.astype(jnp.bfloat16)
        hidden = jnp.dot(normed_two_low, full_up, preferred_element_type=jnp.float32) + full_ubias
        active, gelu_pull = jax.vjp(gelu_exact, hidden)
        active_low = active.astype(jnp.bfloat16)
        result = middle + (
            jnp.dot(active_low, full_down, preferred_element_type=jnp.float32) + full_dbias
        )
        outputs_list.append(result.astype(jnp.bfloat16))
        grad_y = out_grad[micro_idx, 0]
        grad_y32 = grad_y.astype(jnp.float32)
        grad_sums[3] = grad_sums[3] + jnp.einsum(
            "rf,rd->fd", active_low, grad_y, preferred_element_type=jnp.float32
        )
        grad_sums[10] = grad_sums[10] + jnp.sum(grad_y32, axis=0)
        grad_active = jnp.einsum("rd,fd->rf", grad_y, full_down, preferred_element_type=jnp.float32)
        (grad_hidden,) = gelu_pull(grad_active)
        grad_hidden_low = grad_hidden.astype(jnp.bfloat16)
        grad_sums[2] = grad_sums[2] + jnp.einsum(
            "rd,rf->df", normed_two_low, grad_hidden_low, preferred_element_type=jnp.float32
        )
        grad_sums[9] = grad_sums[9] + jnp.sum(grad_hidden_low.astype(jnp.float32), axis=0)
        grad_normed_two = jnp.einsum(
            "rf,df->rd", grad_hidden_low, full_up, preferred_element_type=jnp.float32
        )
        grad_mid_ln, grad_gain_two, grad_bias_two = norm2_pull(grad_normed_two)
        grad_sums[6] = grad_sums[6] + grad_gain_two
        grad_sums[7] = grad_sums[7] + grad_bias_two
        grad_mid = grad_y32 + grad_mid_ln
        grad_mid_low = grad_mid.astype(jnp.bfloat16)
        grad_sums[1] = grad_sums[1] + jnp.einsum(
            "rd,re->de", attn_low, grad_mid_low, preferred_element_type=jnp.float32
        )
        grad_sums[8] = grad_sums[8] + jnp.sum(grad_mid_low.astype(jnp.float32), axis=0)
        grad_attn_low = jnp.einsum(
            "re,de->rd", grad_mid_low, full_out, preferred_element_type=jnp.float32
        ).astype(jnp.bfloat16)
        grad_heads = grad_attn_low.reshape(local_rows, H, HD)
        row_delta = jnp.sum(grad_heads.astype(jnp.float32) * attn_acc, axis=-1).T

        def back_visit(grad_query, block_item):
            key_heads, value_heads, key_doc, key_pos = block_item
            part_q, part_k, part_v = grad_block(
                query_heads,
                grad_heads,
                log_norm,
                row_delta,
                query_doc,
                own_pos,
                key_heads,
                value_heads,
                key_doc,
                key_pos,
            )
            joined = jnp.concatenate(
                [part_k.reshape(key_block, model_width), part_v.reshape(key_block, model_width)],
                axis=1,
            )
            return (grad_query + part_q, joined)

        grad_query, kv_terms = lax.scan(
            back_visit,
            jnp.zeros((local_rows, H, HD), jnp.float32),
            (key_blocks, value_blocks, doc_blocks, pos_blocks),
        )
        kv_grad = lax.psum_scatter(
            kv_terms.reshape(seq_len, 2 * model_width).astype(jnp.bfloat16),
            "ctx",
            scatter_dimension=0,
            tiled=True,
        ).astype(jnp.float32)
        grad_qkv_low = jnp.concatenate(
            [grad_query.reshape(local_rows, model_width), kv_grad], axis=1
        ).astype(jnp.bfloat16)
        grad_sums[0] = grad_sums[0] + jnp.einsum(
            "rd,re->de", normed_low, grad_qkv_low, preferred_element_type=jnp.float32
        )
        grad_normed = jnp.einsum(
            "re,de->rd", grad_qkv_low, full_qkv, preferred_element_type=jnp.float32
        )
        grad_in_ln, grad_gain_one, grad_bias_one = norm1_pull(grad_normed)
        grad_sums[4] = grad_sums[4] + grad_gain_one
        grad_sums[5] = grad_sums[5] + grad_bias_one
        input_grads.append(grad_mid + grad_in_ln)
    owned = (
        lax.psum_scatter(
            grad_sums[0].astype(jnp.bfloat16), "fsdp", scatter_dimension=0, tiled=True
        ).astype(jnp.float32),
        lax.psum_scatter(
            grad_sums[1].astype(jnp.bfloat16), "fsdp", scatter_dimension=0, tiled=True
        ).astype(jnp.float32),
        lax.psum_scatter(
            grad_sums[2].astype(jnp.bfloat16), "fsdp", scatter_dimension=0, tiled=True
        ).astype(jnp.float32),
        lax.psum_scatter(
            grad_sums[3].astype(jnp.bfloat16), "fsdp", scatter_dimension=0, tiled=True
        ).astype(jnp.float32),
        lax.psum_scatter(
            grad_sums[4].astype(jnp.bfloat16), "fsdp", scatter_dimension=0, tiled=True
        ).astype(jnp.float32),
        lax.psum_scatter(
            grad_sums[5].astype(jnp.bfloat16), "fsdp", scatter_dimension=0, tiled=True
        ).astype(jnp.float32),
        lax.psum_scatter(
            grad_sums[6].astype(jnp.bfloat16), "fsdp", scatter_dimension=0, tiled=True
        ).astype(jnp.float32),
        lax.psum_scatter(
            grad_sums[7].astype(jnp.bfloat16), "fsdp", scatter_dimension=0, tiled=True
        ).astype(jnp.float32),
        lax.psum_scatter(
            grad_sums[8].astype(jnp.bfloat16), "fsdp", scatter_dimension=0, tiled=True
        ).astype(jnp.float32),
        lax.psum_scatter(
            grad_sums[9].astype(jnp.bfloat16), "fsdp", scatter_dimension=0, tiled=True
        ).astype(jnp.float32),
        lax.psum_scatter(
            grad_sums[10].astype(jnp.bfloat16), "fsdp", scatter_dimension=0, tiled=True
        ).astype(jnp.float32),
    )
    summed = (
        lax.psum(owned[0].astype(jnp.bfloat16), "ctx").astype(jnp.float32),
        lax.psum(owned[1].astype(jnp.bfloat16), "ctx").astype(jnp.float32),
        lax.psum(owned[2].astype(jnp.bfloat16), "ctx").astype(jnp.float32),
        lax.psum(owned[3].astype(jnp.bfloat16), "ctx").astype(jnp.float32),
        lax.psum(owned[4].astype(jnp.bfloat16), "ctx").astype(jnp.float32),
        lax.psum(owned[5].astype(jnp.bfloat16), "ctx").astype(jnp.float32),
        lax.psum(owned[6].astype(jnp.bfloat16), "ctx").astype(jnp.float32),
        lax.psum(owned[7].astype(jnp.bfloat16), "ctx").astype(jnp.float32),
        lax.psum(owned[8].astype(jnp.bfloat16), "ctx").astype(jnp.float32),
        lax.psum(owned[9].astype(jnp.bfloat16), "ctx").astype(jnp.float32),
        lax.psum(owned[10].astype(jnp.bfloat16), "ctx").astype(jnp.float32),
    )
    return (
        jnp.stack(outputs_list)[:, None],
        jnp.stack(input_grads)[:, None],
        summed[0],
        summed[1],
        summed[2],
        summed[3],
        summed[4],
        summed[5],
        summed[6],
        summed[7],
        summed[8],
        summed[9],
        summed[10],
    )


AXES = ("z", "x", "y", "c")
SIZES = (4, 2, 2, 2)


MESH = pl.DeviceIdType.MESH


def send(src, dst, sems, recv_sems, index, peer):
    copy = pltpu.make_async_remote_copy(
        src_ref=src,
        dst_ref=dst,
        send_sem=sems.at[index],
        recv_sem=recv_sems.at[index],
        device_id=peer,
        device_id_type=MESH,
    )
    copy.start()
    return copy


def greet(peers, extra, extra_on):
    barrier = pltpu.get_barrier_semaphore()
    for peer in peers:
        pl.semaphore_signal(barrier, inc=1, device_id=peer, device_id_type=MESH)

    @pl.when(extra_on)
    def _():
        for peer in extra:
            pl.semaphore_signal(barrier, inc=1, device_id=peer, device_id_type=MESH)

    pl.semaphore_wait(barrier, len(peers) + jnp.where(extra_on, len(extra), 0))


HEAD_CHUNK = 128
SAFE_SCORE = 80.0


def head_kernel(
    x_in_ref, dy_in_ref, docs_in_ref, order_ref, g1_ref, b1_ref, g2_ref, b2_ref, ob_ref, db_ref, ub_in_ref, wq_ref, wo_ref, wu_ref, wd_ref,
    qt_ref, k_ref, kt_ref, v_ref, vt_ref, ut_ref, own_ref, wo_all, wu_all, wd_all, dy_ref,
    wh_ref, vec_ref, ub_ref, start_ref, tab_ref,
    qt_buf, k_buf, kt_buf, v_buf, vt_buf, ut_buf, rows, docs, docs_true, norms, vec_in_ref, vec_all, wo_tmp, wu_tmp, wd_tmp,
    z_s, z_r, x_s, x_r, c_s, c_r, f_s, f_r, docs_s, docs_r, vec_s, vec_r, wh_s, wh_r, wh_l,
    y_s, y_r, n_s, n_r, o_s, o_r, load_sem, put_sem, self_sem, d_s, d_r, d_self, out_sem,
):
    z, x, y, c = (lax.axis_index(name) for name in AXES)
    odd, upper = lax.rem(z, 2), lax.div(z, 2)
    width = x_in_ref.shape[-1]
    chunks = rows.shape[1] // HEAD_CHUNK
    per_turn = chunks // 2
    by_core, by_x, by_y, by_yc = {"c": 1 - c}, {"x": 1 - x}, {"y": 1 - y}, {"y": 1 - y, "c": 1 - c}
    home = [{"z": 2 * c + upper, "c": odd}, {"z": 2 * c + 1 - upper, "c": odd}]
    target = [{"z": 2 * odd + c, "c": upper}, {"z": 2 * (1 - odd) + c, "c": upper}]
    block = [odd, 1 - odd]
    stay = (c == upper) & (odd == c)
    leave = jnp.logical_not(stay)
    for i, ref in enumerate((g1_ref, b1_ref, g2_ref, b2_ref, ob_ref, db_ref, ub_in_ref)):
        vec_in_ref[i : i + ref.shape[0]] = ref[...]
    greet([by_core, by_x, by_y, by_yc, home[1], target[1]], [home[0], target[0]], leave)

    def order_of(i):
        return i % 2 * per_turn + i // 2

    def piece(i):
        turn, row = order_of(i) // per_turn, (order_of(i) % per_turn) * HEAD_CHUNK
        return (
            x_in_ref.at[block[turn], 0, pl.ds(row, HEAD_CHUNK)],
            rows.at[0, pl.ds(order_of(i) * HEAD_CHUNK, HEAD_CHUNK)],
        )

    for turn in range(2):
        src, dst = docs_in_ref.at[block[turn]], docs.at[0, turn]

        def start_docs():
            send(src, dst, docs_s, docs_r, turn, target[turn])

        if turn == 0:
            pl.when(stay)(lambda: pltpu.make_async_copy(src, dst, self_sem.at[per_turn]).start())
            pl.when(leave)(start_docs)
        else:
            start_docs()
    for i in range(chunks):
        src, dst = piece(i)
        if i % 2 == 0:
            pl.when(stay)(lambda: pltpu.make_async_copy(src, dst, self_sem.at[i // 2]).start())
            pl.when(leave)(lambda: send(src, dst, z_s, z_r, i, target[0]) and None)
        else:
            send(src, dst, z_s, z_r, i, target[1])

    def piece_dy(i):
        part = pl.ds(i * HEAD_CHUNK, HEAD_CHUNK)
        return dy_in_ref.at[odd, 0, part], dy_ref.at[part]

    def send_dy(i):
        src, dst = piece_dy(i)
        pl.when(stay)(lambda: pltpu.make_async_copy(src, dst, d_self.at[i]).start())
        pl.when(leave)(lambda: send(src, dst, d_s, d_r, i, target[0]) and None)

    def land_dy(i):
        src, dst = piece_dy(i)
        pl.when(stay)(lambda: pltpu.make_async_copy(src, dst, d_self.at[i]).wait())
        pl.when(leave)(
            lambda: pltpu.make_async_remote_copy(
                src_ref=src, dst_ref=dst, send_sem=d_s.at[i], recv_sem=d_r.at[i],
                device_id=target[0], device_id_type=MESH,
            ).wait()
        )

    def landed(src, dst, sems, recv_sems, index, turn, self_index):
        def remote():
            pltpu.make_async_remote_copy(
                src_ref=src, dst_ref=dst, send_sem=sems.at[index], recv_sem=recv_sems.at[index],
                device_id=target[turn], device_id_type=MESH,
            ).wait()

        if turn == 0:
            pl.when(stay)(lambda: pltpu.make_async_copy(src, dst, self_sem.at[self_index]).wait())
            pl.when(leave)(remote)
        else:
            remote()

    mine = 2 * y + c
    vec_copy = [
        send(vec_in_ref, vec_all.at[mine], vec_s, vec_r, i, peer)
        for i, peer in enumerate((by_core, by_y, by_yc))
    ]
    vec_all[mine] = vec_in_ref[...]
    wh_copy = []
    shard = wq_ref.shape[0]
    own_rows = pl.ds(pl.multiple_of(mine * shard, shard), shard)
    for part in range(3):
        to = wh_ref.at[own_rows, pl.ds(part * PAIR, PAIR)]

        def columns(core):
            return wq_ref.at[:, pl.ds(pl.multiple_of(part * width + (2 * x + core) * PAIR, PAIR), PAIR)]

        for i, (peer, core) in enumerate(((by_core, 1 - c), (by_y, c), (by_yc, 1 - c))):
            wh_copy.append(send(columns(core), to, wh_s, wh_r, 3 * part + i, peer))
        copy = pltpu.make_async_copy(columns(c), to, wh_l.at[part])
        copy.start()
        wh_copy.append(copy)

    up_rows, down_rows = wu_ref.shape[0] // 4, wd_ref.shape[0] // 4
    parts = [(wo_ref, wo_all, wo_ref.shape[0], 0)]
    parts += [(wu_ref, wu_all, up_rows, i * up_rows) for i in range(4)]
    parts += [(wd_ref, wd_all, down_rows, i * down_rows) for i in range(4)]

    def at_owner(full, src, size, offset, owner):
        return full.at[pl.ds(pl.multiple_of(owner * src.shape[0] + offset, 32), size)]

    other = 2 * (1 - y) + c
    y_copy = []
    for i, (src, full, size, offset) in enumerate(parts):
        y_copy.append(
            send(src.at[pl.ds(offset, size)], at_owner(full, src, size, offset, mine), y_s, y_r, i, by_y)
        )
    n_copy, load_copy, put_copy = [], [], []
    for i, (src, full, tmp) in enumerate(((wo_ref, wo_all, wo_tmp), (wu_ref, wu_all, wu_tmp), (wd_ref, wd_all, wd_tmp))):
        n_copy.append(send(src, at_owner(full, src, src.shape[0], 0, mine), n_s, n_r, i, by_core))
        load_copy.append(pltpu.make_async_copy(src, tmp, load_sem.at[i]))
        load_copy[-1].start()

    def put(i):
        src, full, tmp = ((wo_ref, wo_all, wo_tmp), (wu_ref, wu_all, wu_tmp), (wd_ref, wd_all, wd_tmp))[i]
        load_copy[i].wait()
        put_copy.append(pltpu.make_async_copy(tmp, at_owner(full, src, src.shape[0], 0, mine), put_sem.at[i]))
        put_copy[-1].start()

    o_copy = []

    def forward(i):
        src, full, size, offset = parts[i]
        y_copy[i].wait()
        held = at_owner(full, src, size, offset, other)
        o_copy.append(send(held, held, o_s, o_r, i, by_core))

    blocks = order_ref.shape[0]
    lane = lax.broadcasted_iota(jnp.int32, (1, 128), 1)
    slots = jnp.zeros((1, 128), jnp.int32)
    for t in range(blocks):
        dc, dx, turn, half = t // 8, t // 4 % 2, t // 2 % 2, t % 2
        core, side = (1 - c if dc else c), (1 - x if dx else x)
        stored = 2 * (2 * (2 * core + (1 - upper if turn else upper)) + side) + half
        slots = jnp.where(lane == order_ref[stored], t, slots)

    docs_copy = {}

    def finish_docs():
        docs_copy["c"].wait()
        docs_copy["f"].wait()
        for g in range(4):
            core, side = (1 - c if g // 2 else c), (1 - x if g % 2 else x)
            for turn in range(2):
                docs_true[2 * (2 * core + (1 - upper if turn else upper)) + side] = docs[g, turn]
        numbers = docs_true[...]
        first = jnp.zeros_like(numbers)
        for d in range(1, blocks):
            before = jnp.sum((numbers < d).astype(jnp.int32), axis=(0, 1, 2), keepdims=True)
            first = jnp.where(numbers == d, before, first)
        docs_true[...] = first
        low = jnp.zeros((1, 128), jnp.int32)
        for b in range(blocks):
            line = docs_true[b // 2]
            at = 2 * (b % 2)
            line = jnp.concatenate([line[at : at + 1], line[at + 1 : at + 2]], axis=1)
            start_ref[b] = line
            low = jnp.where(lane == b, line[:, :1] // BLK, low)
        high = jnp.zeros((1, 128), jnp.int32) - 1
        for b in range(blocks):
            high = high + (low[:, b : b + 1] <= lane).astype(jnp.int32)
        tab_ref[...] = jnp.concatenate([low, high, slots, jnp.zeros((5, 128), jnp.int32)], axis=0)

    def docs_first():
        for turn in range(2):
            landed(docs_in_ref.at[block[turn]], docs.at[0, turn], docs_s, docs_r, turn, turn, per_turn)
        docs_copy["x"] = send(docs.at[0], docs.at[1], docs_s, docs_r, 2, by_x)
        docs_copy["c"] = send(docs.at[0], docs.at[2], docs_s, docs_r, 3, by_core)


    def vectors_and_weight():
        for copy in vec_copy:
            copy.wait()
        vec_width = vec_in_ref.shape[1]
        for j in range(4):
            for i in range(6):
                vec_ref[i : i + 1, j * vec_width : (j + 1) * vec_width] = vec_all[j, i : i + 1].astype(f32)
            for i in range(4):
                at = (4 * j + i) * vec_width
                ub_ref[:, at : at + vec_width] = vec_all[j, 6 + i : 7 + i].astype(f32)
        vec_ref[6:8] = jnp.zeros((2, width), f32)
        for copy in wh_copy:
            copy.wait()


    def docs_second():
        docs_copy["x"].wait()
        docs_copy["f"] = send(docs.at[1], docs.at[3], docs_s, docs_r, 4, by_core)


    x_copy, c_copy, f_copy = [], [], []

    def relay(i):
        src, dst = piece(i)
        landed(src, dst, z_s, z_r, i, i % 2, i // 2)
        part = pl.ds(order_of(i) * HEAD_CHUNK, HEAD_CHUNK)
        x_copy.append(send(rows.at[0, part], rows.at[1, part], x_s, x_r, i, by_x))
        c_copy.append(send(rows.at[0, part], rows.at[2, part], c_s, c_r, i, by_core))

    def relay_far(i):
        x_copy[i].wait()
        part = pl.ds(order_of(i) * HEAD_CHUNK, HEAD_CHUNK)
        f_copy.append(send(rows.at[1, part], rows.at[3, part], f_s, f_r, i, by_core))

    streams = (
        (qt_buf, qt_ref, 1), (k_buf, k_ref, 0), (kt_buf, kt_ref, 1), (v_buf, v_ref, 0), (vt_buf, vt_ref, 1),
        (ut_buf, ut_ref, 1),
    )

    def compute(g, i):
        count = rows.shape[1]
        chunk = order_of(i)
        unit, _ = norm_parts(rows[g, chunk * HEAD_CHUNK : (chunk + 1) * HEAD_CHUNK].astype(f32))
        at = pl.ds(g * count + chunk * HEAD_CHUNK, HEAD_CHUNK)
        ut_buf[:, at] = unit.astype(bf16).T
        low = (unit * vec_ref[0:1] + vec_ref[1:2]).astype(bf16)
        qkv = jnp.dot(low, wh_ref[...], preferred_element_type=f32)
        qt = (qkv[:, :PAIR] * (SCORE_SCALE * LOG2E)).astype(bf16).T
        qt_buf[:, at] = qt
        k = qkv[:, PAIR : 2 * PAIR].astype(bf16)
        v = qkv[:, 2 * PAIR :].astype(bf16)
        k_buf[at] = k
        v_buf[at] = v
        kt = k.T
        kt_buf[:, at] = kt
        vt_buf[:, at] = v.T
        found = []
        for block_ in (qt, kt):
            squares = block_.astype(f32) * block_.astype(f32)
            found += [jnp.sum(squares[head * HD : (head + 1) * HD], axis=0, keepdims=True) for head in range(2)]
        found = jnp.concatenate(found, axis=0)
        norms[...] = found if g == 0 and i == 0 else jnp.maximum(norms[...], found)
        for index, (source, out, columns) in enumerate(streams):
            if columns:
                source, out = source.at[:, at], out.at[:, at]
            else:
                source, out = source.at[at], out.at[at]
            pltpu.make_async_copy(source, out, out_sem.at[index]).start()

    docs_first()
    for i in range(chunks + 2):
        if i < chunks:
            if i < per_turn:
                send_dy(i)
            relay(i)
        if i == 0:
            vectors_and_weight()
            docs_second()
        if 1 <= i <= chunks:
            relay_far(i - 1)
            compute(0, i - 1)
            compute(1, i - 1)
            c_copy[i - 1].wait()
            compute(2, i - 1)
        if i >= 2:
            f_copy[i - 2].wait()
            compute(3, i - 2)
        if i == 1:
            finish_docs()
        if 2 <= i < 5:
            put(i - 2)
        if i >= 3 and i - 3 < len(parts):
            forward(i - 3)
        if i == chunks - 1:
            own_copy = pltpu.make_async_copy(rows.at[0], own_ref, out_sem.at[len(streams)])
            own_copy.start()
    largest = jnp.max(norms[...], axis=1, keepdims=True)
    bound = jnp.maximum(largest[0:1] * largest[2:3], largest[1:2] * largest[3:4])
    tab_ref[3:4] = jnp.broadcast_to((bound <= SAFE_SCORE * SAFE_SCORE).astype(jnp.int32), (1, 128))
    for i in range(chunks - 1, len(parts)):
        forward(i)
    for index, (source, out, _) in enumerate(streams):
        pltpu.make_async_copy(source, out, out_sem.at[index]).wait()
    own_copy.wait()
    for copy in n_copy + put_copy + o_copy:
        copy.wait()
    for i in range(per_turn):
        land_dy(i)


def head(x_in, dy_in, docs_in, order, vectors, w_qkv, w_out, w_up, w_down):
    width = x_in.shape[-1]
    count = 2 * x_in.shape[2]
    total = 4 * count
    shard = w_qkv.shape[0]
    chunks = count // HEAD_CHUNK
    blocks = order.shape[0]
    vmem, any_ = pl.BlockSpec(memory_space=pltpu.VMEM), pl.BlockSpec(memory_space=pl.ANY)
    smem = pl.BlockSpec(memory_space=pltpu.SMEM)
    dma, buf, shape = pltpu.SemaphoreType.DMA, pltpu.VMEM, jax.ShapeDtypeStruct
    return pl.pallas_call(
        head_kernel,
        in_specs=[any_, any_, vmem, smem] + [vmem] * 7 + [any_] * 4,
        out_specs=[any_] * 11 + [vmem] * 5,
        out_shape=[
            shape((PAIR, total), bf16),
            shape((total, PAIR), bf16),
            shape((PAIR, total), bf16),
            shape((total, PAIR), bf16),
            shape((PAIR, total), bf16),
            shape((width, total), bf16),
            shape((count, width), bf16),
            shape((4 * w_out.shape[0], w_out.shape[1]), bf16),
            shape((4 * w_up.shape[0], w_up.shape[1]), bf16),
            shape((4 * w_down.shape[0], w_down.shape[1]), bf16),
            shape((count // 2, width), bf16),
            shape((width, 3 * PAIR), bf16),
            shape((8, width), f32),
            shape((1, 4 * w_down.shape[0]), f32),
            shape((blocks, 1, BLK), jnp.int32),
            shape((8, 128), jnp.int32),
        ],
        scratch_shapes=[
            buf((PAIR, total), bf16),
            buf((total, PAIR), bf16),
            buf((PAIR, total), bf16),
            buf((total, PAIR), bf16),
            buf((PAIR, total), bf16),
            buf((width, total), bf16),
            buf((4, count, width), bf16),
            buf((4, 2) + docs_in.shape[1:], jnp.int32),
            buf((blocks // 2,) + docs_in.shape[1:], jnp.int32),
            buf((4, HEAD_CHUNK), f32),
            buf((16, shard), bf16),
            buf((4, 16, shard), bf16),
            buf(w_out.shape, bf16),
            buf(w_up.shape, bf16),
            buf(w_down.shape, bf16),
        ]
        + [dma((chunks,))] * 8
        + [dma((5,)), dma((5,)), dma((3,)), dma((3,)), dma((9,)), dma((9,)), dma((3,))]
        + [dma((9,)), dma((9,)), dma((3,)), dma((3,)), dma((9,)), dma((9,)), dma((3,)), dma((3,))]
        + [dma((chunks // 2 + 1,)), dma((chunks // 2,))] + [dma((chunks // 2,))] * 2 + [dma((7,))],
        compiler_params=pltpu.CompilerParams(
            collective_id=1, has_side_effects=True, vmem_limit_bytes=56 * 1024 * 1024
        ),
        name="head",
    )(x_in, dy_in, docs_in, order, *[v.reshape(-1, shard) for v in vectors], w_qkv, w_out, w_up, w_down)
FF_TILE = 512
PIECES = 3
feed_steps = 4


def feed_kernel(
    o_ref, x_ref, dy_near_ref, dy_in_ref, wo_ref, wu_ref, wd_ref, vec_ref, ub_ref,
    do_ref, y_home, dmid_ref, keep_ref, to_y_ref, to_x_ref, to_xy_ref, gvec_ref, gub_ref,
    attn_all, gd_ref, gu_ref, go_ref, attn_in, do_out, y_out, grad_ref, grad_in,
    dy_ref, dy_far, a_s, a_r, a_l, d_s, d_r, d_l, y_s, y_r, y_l, g_s, g_r, c_s, c_r,
):
    step = pl.program_id(0)
    steps = pl.num_programs(0)
    groups = attn_in.shape[0]
    tile = x_ref.shape[0]
    z, x, y, c = (lax.axis_index(name) for name in AXES)
    odd, upper = lax.rem(z, 2), lax.div(z, 2)
    mates = [None, {"x": 1 - x}, {"c": 1 - c}, {"x": 1 - x, "c": 1 - c}]
    pair_of = [2 * x + c, 2 * (1 - x) + c, 2 * x + 1 - c, 2 * (1 - x) + 1 - c]
    home = [{"z": 2 * c + upper, "c": odd}, {"z": 2 * c + 1 - upper, "c": odd}]
    origin = [{"z": 2 * odd + c, "c": upper}, {"z": 2 * (1 - odd) + c, "c": upper}]
    stay = (c == upper) & (odd == c)
    leave = jnp.logical_not(stay)
    half = feed_steps // 2

    def attn_copy(g, i):
        part = pl.ds(i * tile, tile)
        return pltpu.make_async_remote_copy(
            src_ref=o_ref.at[g, part], dst_ref=attn_in.at[g, part],
            send_sem=a_s.at[g - 1, i], recv_sem=a_r.at[g - 1, i], device_id=mates[g], device_id_type=MESH,
        )

    def attn_own(i):
        part = pl.ds(i * tile, tile)
        return pltpu.make_async_copy(o_ref.at[0, part], attn_in.at[0, part], a_l.at[i])

    def do_copy(g, i):
        return pltpu.make_async_remote_copy(
            src_ref=do_out.at[i, g], dst_ref=do_ref.at[g, pl.ds(i * tile, tile)],
            send_sem=d_s.at[g - 1, i], recv_sem=d_r.at[g - 1, i], device_id=mates[g], device_id_type=MESH,
        )

    def do_own(i):
        return pltpu.make_async_copy(do_out.at[i, 0], do_ref.at[0, pl.ds(i * tile, tile)], d_l.at[i])

    def y_rows(i, block):
        return y_home.at[block, pl.ds(lax.rem(i, half) * tile, tile)]

    def y_copy(i, turn, block):
        return pltpu.make_async_remote_copy(
            src_ref=y_out.at[i], dst_ref=y_rows(i, block),
            send_sem=y_s.at[i], recv_sem=y_r.at[i], device_id=home[turn], device_id_type=MESH,
        )

    def y_own(i, block):
        return pltpu.make_async_copy(y_out.at[i], y_rows(i, block), y_l.at[i])

    def grad_copy(i):
        return pltpu.make_async_remote_copy(
            src_ref=grad_ref.at[2 * i + 1 - c], dst_ref=grad_in.at[i],
            send_sem=g_s.at[i], recv_sem=g_r.at[i], device_id=mates[2], device_id_type=MESH,
        )

    def dy_copy(i):
        part = pl.ds(i * tile, tile)
        return pltpu.make_async_remote_copy(
            src_ref=dy_in_ref.at[1 - odd, 0, part], dst_ref=dy_far.at[part],
            send_sem=c_s.at[i], recv_sem=c_r.at[i], device_id=origin[1], device_id_type=MESH,
        )

    @pl.when(step == 0)
    def _():
        greet(mates[1:] + [home[1], origin[1]], [home[0], origin[0]], leave)
        for i in range(feed_steps):
            for g in (1, 3, 2):
                attn_copy(g, i).start()
            attn_own(i).start()
        for i in range(half):
            dy_copy(i).start()

    @pl.when(step == 0)
    def _():
        for ref in (gd_ref, gu_ref, go_ref, gvec_ref, gub_ref):
            ref[...] = jnp.zeros_like(ref)

    @pl.when(step < half)
    def _():
        dy_ref[...] = dy_near_ref[...]

    @pl.when(step >= half)
    def _():
        dy_copy(step - half).wait()
        dy_ref[...] = dy_far[pl.ds(pl.multiple_of((step - half) * tile, tile), tile)]

    attn_own(step).wait()
    for g in range(1, groups):
        attn_copy(g, step).wait()
    for g in range(groups):
        attn_all[:, pl.ds(pl.multiple_of(pair_of[g] * PAIR, PAIR), PAIR)] = attn_in[
            g, pl.ds(pl.multiple_of(step * tile, tile), tile)
        ]
    attn = attn_all[...]
    gain, bias, out_bias, down_bias = (vec_ref[i : i + 1, :] for i in range(2, 6))
    middle = (
        x_ref[...].astype(f32) + jnp.dot(attn, wo_ref[...], preferred_element_type=f32) + out_bias
    )
    unit, inv = norm_parts(middle)
    low = (unit * gain + bias).astype(bf16)
    dy = dy_ref[...]
    dy32 = dy.astype(f32)
    total = middle + down_bias
    d_low = jnp.zeros_like(middle)
    width = wu_ref.shape[1]
    for j in range(0, width, FF_TILE):
        part = pl.ds(j, FF_TILE)
        up = wu_ref[:, part]
        down = wd_ref[part, :]
        hidden = jnp.dot(low, up, preferred_element_type=f32) + ub_ref[:, part]
        cdf = 0.5 * (1.0 + lax.erf(hidden * (1.0 / math.sqrt(2.0))))
        active = (hidden * cdf).astype(bf16)
        slope = cdf + hidden * (jnp.exp2(hidden * hidden * (-0.5 * LOG2E)) * (1.0 / math.sqrt(2.0 * math.pi)))
        total = total + jnp.dot(active, down, preferred_element_type=f32)
        d_hidden = contract(dy, down, 1, 1) * slope
        d_hidden_low = d_hidden.astype(bf16)
        gub_ref[:, part] += jnp.sum(d_hidden, axis=0, keepdims=True)
        d_low = d_low + contract(d_hidden_low, up, 1, 1)
        gd_ref[part, :] += contract(active, dy, 0, 0)
        gu_ref[:, part] += contract(low, d_hidden_low, 0, 0)
    y_out[step] = total.astype(bf16)

    @pl.when((step < half) & stay)
    def _():
        y_own(step, upper).start()

    @pl.when((step < half) & leave)
    def _():
        y_copy(step, 0, upper).start()

    @pl.when(step >= half)
    def _():
        y_copy(step, 1, upper).start()

    scaled = d_low * gain
    d_middle = dy32 + inv * (
        scaled
        - jnp.mean(scaled, axis=-1, keepdims=True)
        - unit * jnp.mean(scaled * unit, axis=-1, keepdims=True)
    )
    dmid_ref[...] = d_middle
    branch = d_middle.astype(bf16)
    go_ref[...] += contract(attn, branch, 0, 0)
    gvec_ref[0:1, :] += jnp.sum(d_middle, axis=0, keepdims=True)
    gvec_ref[1:2, :] += jnp.sum(d_low * unit, axis=0, keepdims=True)
    gvec_ref[2:3, :] += jnp.sum(d_low, axis=0, keepdims=True)
    gvec_ref[3:4, :] += jnp.sum(dy32, axis=0, keepdims=True)
    attn_all[...] = contract(branch, wo_ref[...], 1, 1).astype(bf16)
    for g in (1, 3, 2, 0):
        do_out[step, g] = attn_all[:, pl.ds(pl.multiple_of(pair_of[g] * PAIR, PAIR), PAIR)]
        if g:
            do_copy(g, step).start()
        else:
            do_own(step).start()

    @pl.when(step == steps - 1)
    def _():
        shards = grad_ref.shape[0]
        d_model = x_ref.shape[1]
        down_rows, up_rows = gd_ref.shape[0] // shards, d_model // shards
        for j in range(shards):
            grad_ref[j, :down_rows] = gd_ref[j * down_rows : (j + 1) * down_rows].astype(bf16)
            rows = slice(j * up_rows, (j + 1) * up_rows)
            at = down_rows
            for t in range(0, width, d_model):
                grad_ref[j, at : at + up_rows] = gu_ref[rows, t : t + d_model].astype(bf16)
                at += up_rows
            grad_ref[j, at : at + up_rows] = go_ref[rows].astype(bf16)
        for j in range(2):
            grad_copy(j).start()
        for j in range(feed_steps):
            do_own(j).wait()
            for g in range(1, groups):
                do_copy(g, j).wait()
            if j < half:
                @pl.when(stay)
                def _():
                    y_own(j, odd).wait()

                @pl.when(leave)
                def _():
                    y_copy(j, 0, odd).wait()
            else:
                y_copy(j, 1, 1 - odd).wait()
        sixth = keep_ref.shape[1]
        for j in range(2):
            grad_copy(j).wait()
        for dy_, dx_, ref in ((0, 0, keep_ref), (1, 0, to_y_ref), (0, 1, to_x_ref), (1, 1, to_xy_ref)):
            row = 1 - y if dy_ else y
            side = 1 - x if dx_ else x
            for p in range(PIECES):
                part = pl.ds(pl.multiple_of((2 * p + side) * sixth, 16), sixth)
                ref[p] = (
                    grad_ref[2 * row + c, part].astype(f32) + grad_in[row, part].astype(f32)
                ).astype(bf16)


def feed(o, x, dy_near, dy_in, w_out, w_up, w_down, vecs, up_bias, shards):
    groups, count, _ = o.shape
    width = x.shape[1]
    flat = (w_out.size + w_up.size + w_down.size) // shards // width
    tile = count // feed_steps
    piece = (PIECES, flat // PIECES // 2, width)
    rows = pl.BlockSpec((tile, width), lambda i: (i, 0))
    any_ = pl.BlockSpec(memory_space=pl.ANY)
    dma, buf, shape = pltpu.SemaphoreType.DMA, pltpu.VMEM, jax.ShapeDtypeStruct
    return pl.pallas_call(
        feed_kernel,
        grid=(feed_steps,),
        in_specs=[
            any_, rows, pl.BlockSpec((tile, width), lambda i: (jnp.minimum(i, feed_steps // 2 - 1), 0)), any_, whole(w_out.shape), whole(w_up.shape), whole(w_down.shape),
            whole(vecs.shape), whole(up_bias.shape),
        ],
        out_specs=[any_, any_, rows] + [whole(piece)] * 4 + [whole(vecs.shape), whole(up_bias.shape)],
        out_shape=[
            shape((groups, count, PAIR), bf16),
            shape((2, count // 2, width), bf16),
            shape((count, width), f32),
            shape(piece, bf16),
            shape(piece, bf16),
            shape(piece, bf16),
            shape(piece, bf16),
            shape(vecs.shape, f32),
            shape(up_bias.shape, f32),
        ],
        scratch_shapes=[
            buf((tile, width), bf16),
            buf(w_down.shape, f32),
            buf(w_up.shape, f32),
            buf(w_out.shape, f32),
            buf((groups, count, PAIR), bf16),
            buf((feed_steps, groups, tile, PAIR), bf16),
            buf((feed_steps, tile, width), bf16),
            buf((shards, flat, width), bf16),
            buf((2, flat, width), bf16),
            buf((tile, width), bf16),
            buf((count // 2, width), bf16),
            dma((3, feed_steps)),
            dma((3, feed_steps)),
            dma((feed_steps,)),
            dma((3, feed_steps)),
            dma((3, feed_steps)),
            dma((feed_steps,)),
            dma((feed_steps,)),
            dma((feed_steps,)),
            dma((feed_steps,)),
            dma((2,)),
            dma((2,)),
            dma((feed_steps // 2,)),
            dma((feed_steps // 2,)),
        ],
        compiler_params=pltpu.CompilerParams(
            collective_id=3, has_side_effects=True, vmem_limit_bytes=60 * 1024 * 1024
        ),
        name="feed",
    )(o, x, dy_near, dy_in, w_out, w_up, w_down, vecs, up_bias)


TAIL_CHUNK = 128


def tail_kernel(
    d_qkv_hbm, ut_hbm, x_hbm, dmid_hbm, w_ref, gain_ref, bias_ref, keep_ref, from_y_ref, from_x_ref, from_xy_ref,
    gvecs_ref, gub_ref,
    home_buf, gfull, wall, sum_ref,
    d_qkv, ut_ref, total, sums, gw_ref, core_out, x_ref, dmid_ref, core_buf, own_dh, x_out, x_buf, dx_out,
    gsum, gz1s, gz1r, gz2s, gz2r,
    wy, ws, wz1s, wz1r, wz2s, wz2r, wfull,
    small_ref, small_out, small_in,
    load_sem, self_sem, core_s, core_r, x_s, x_r, home_s, home_r, g_s, g_r, w_s, w_r, s_s, s_r, in_sem,
):
    z, x, y, c = (lax.axis_index(name) for name in AXES)
    odd, upper = lax.rem(z, 2), lax.div(z, 2)
    width = x_ref.shape[1]
    chunks = x_ref.shape[0] // TAIL_CHUNK
    per_turn = chunks // 2
    by_core, by_x, by_y, by_xc = {"c": 1 - c}, {"x": 1 - x}, {"y": 1 - y}, {"x": 1 - x, "c": 1 - c}
    by_z1, by_z2 = {"z": z + 1 - 2 * odd}, {"z": z + 2 - 4 * upper}
    home = [{"z": 2 * c + upper, "c": odd}, {"z": 2 * c + 1 - upper, "c": odd}]
    origin = [{"z": 2 * odd + c, "c": upper}, {"z": 2 * (1 - odd) + c, "c": upper}]
    stay = (c == upper) & (odd == c)
    loads = []
    for i in range(chunks):
        part = pl.ds(i * TAIL_CHUNK, TAIL_CHUNK)
        loads.append(pltpu.make_async_copy(d_qkv_hbm.at[:, part], d_qkv.at[:, part], load_sem.at[i]))
    inputs = [
        pltpu.make_async_copy(src, dst, in_sem.at[i])
        for i, (src, dst) in enumerate(((ut_hbm, ut_ref), (x_hbm, x_ref), (dmid_hbm, dmid_ref)))
    ]
    for copy in loads + inputs:
        copy.start()
    small_ref[...] = jnp.zeros_like(small_ref)
    small_ref[2:4] = gvecs_ref[1:3]
    small_ref[4:5] = gvecs_ref[0:1]
    small_ref[5:6] = gvecs_ref[3:4]
    for i in range(4):
        small_ref[6 + i : 7 + i] = gub_ref[:, i * width : (i + 1) * width]
    greet(
        [by_core, by_x, by_y, by_xc, by_z1, by_z2, home[1], origin[1]],
        [home[0], origin[0]],
        jnp.logical_not(stay),
    )
    small_peers = [by_core, by_y, by_z1, by_z2, by_x]
    to_core, w_copy, s_copy = [], {}, []

    def share(i):
        part = pl.ds(i * TAIL_CHUNK, TAIL_CHUNK)
        loads[i].wait()
        for g in (3, 2, 1, 0):
            value = contract(d_qkv[g, part], w_ref[...], 1, 1)
            if g >= 2:
                core_out[g - 2, part] = value.astype(bf16)
            else:
                own_dh[g, part] = value
            if g == 2:
                to_core.append(
                    send(core_out.at[:, part], core_buf.at[:, part], core_s, core_r, i, by_core)
                )

    def weight(g):
        if g == 0:
            inputs[0].wait()
        rows = d_qkv[g]
        part = jnp.dot(ut_ref[:, g * rows.shape[0] : (g + 1) * rows.shape[0]], rows, preferred_element_type=f32)
        line = jnp.sum(rows.astype(f32), axis=0, keepdims=True)
        total[...] = part if g == 0 else total[...] + part
        sums[...] = line if g == 0 else sums[...] + line

    def weight_close():
        shard = gw_ref.shape[1]
        for j in range(gw_ref.shape[0]):
            part = pl.ds(j * shard, shard)
            gain, bias = (jnp.broadcast_to(ref[:, part], (shard, shard)).T[:, :1] for ref in (gain_ref, bias_ref))
            gw_ref[j] = (total[part] * gain + bias * sums[...]).astype(bf16)
            w = w_ref[part].astype(f32)
            for i, term in enumerate((w * total[part], w * sums[...])):
                column = jnp.sum(term, axis=1, keepdims=True)
                small_ref[i : i + 1, part] = jnp.broadcast_to(column, (shard, shard)).T[:1]
        s_copy.append(send(small_ref, small_in.at[0], s_s, s_r, 0, small_peers[0]))
        w_copy["y"] = send(gw_ref.at[pl.ds(2 * (1 - y), 2)], wy, w_s, w_r, 0, by_y)

    g_copy = {}

    def g_start(p):
        for half in range(2):
            part = pl.ds(96 * half, 96)
            gsum[p, part] = (
                keep_ref[p, part].astype(f32)
                + from_y_ref[p, part].astype(f32)
                + from_x_ref[p, part].astype(f32)
                + from_xy_ref[p, part].astype(f32)
            )
        gz1s[p] = gsum[p, pl.ds(pl.multiple_of(96 * (1 - odd), 16), 96)].astype(bf16)
        g_copy["z1", p] = send(gz1s.at[p], gz1r.at[p], g_s, g_r, 5 * p, by_z1)

    mine_half = pl.multiple_of(96 * odd, 16)
    mine_quarter = pl.multiple_of(96 * odd + 48 * upper, 16)
    give_quarter = pl.multiple_of(96 * odd + 48 * (1 - upper), 16)

    def g_second(p):
        g_copy["z1", p].wait()
        gsum[p, pl.ds(mine_half, 96)] += gz1r[p].astype(f32)
        gz2s[p] = gsum[p, pl.ds(give_quarter, 48)].astype(bf16)
        g_copy["z2", p] = send(gz2s.at[p], gz2r.at[p], g_s, g_r, 5 * p + 1, by_z2)

    def g_third(p):
        g_copy["z2", p].wait()
        part = pl.ds(mine_quarter, 48)
        gfull[p, x, part] = (gsum[p, part] + gz2r[p].astype(f32)).astype(bf16)
        place_ = gfull.at[p, x, part]
        g_copy["z2b", p] = send(place_, place_, g_s, g_r, 5 * p + 2, by_z2)

    def g_fourth(p):
        g_copy["z2b", p].wait()
        place_ = gfull.at[p, x, pl.ds(mine_half, 96)]
        g_copy["z1b", p] = send(place_, place_, g_s, g_r, 5 * p + 3, by_z1)

    def g_fifth(p):
        g_copy["z1b", p].wait()
        g_copy["x", p] = send(gfull.at[p, x], gfull.at[p, x], g_s, g_r, 5 * p + 4, by_x)

    def w_second():
        w_copy["y"].wait()
        for i in range(2):
            ws[i] = gw_ref[2 * y + i].astype(f32) + wy[i].astype(f32)
        wz1s[...] = ws[1 - odd].astype(bf16)
        w_copy["z1"] = send(wz1s, wz1r, w_s, w_r, 1, by_z1)

    def w_third():
        w_copy["z1"].wait()
        ws[odd] += wz1r[...].astype(f32)
        wz2s[...] = ws[odd, pl.ds(pl.multiple_of(64 * (1 - upper), 64), 64)].astype(bf16)
        w_copy["z2"] = send(wz2s, wz2r, w_s, w_r, 2, by_z2)

    def w_fourth():
        w_copy["z2"].wait()
        part = pl.ds(pl.multiple_of(64 * upper, 64), 64)
        wfull[odd, part] = (ws[odd, part] + wz2r[...].astype(f32)).astype(bf16)
        place_ = wfull.at[odd, part]
        w_copy["z2b"] = send(place_, place_, w_s, w_r, 3, by_z2)

    def w_fifth():
        w_copy["z2b"].wait()
        w_copy["z1b"] = send(wfull.at[odd], wfull.at[odd], w_s, w_r, 4, by_z1)

    def w_sixth():
        w_copy["z1b"].wait()
        mine = 2 * x + c
        w_copy["core"] = send(wfull.at[1 - c], wall.at[mine], w_s, w_r, 5, by_core)
        w_copy["x"] = send(wfull.at[c], wall.at[mine], w_s, w_r, 6, by_x)
        w_copy["xc"] = send(wfull.at[1 - c], wall.at[mine], w_s, w_r, 7, by_xc)

    def s_next(step):
        s_copy[step].wait()
        before = small_ref[...] if step == 0 else small_out[step - 1]
        small_out[step] = before + small_in[step]
        if step + 1 < len(small_peers):
            s_copy.append(
                send(small_out.at[step], small_in.at[step + 1], s_s, s_r, step + 1, small_peers[step + 1])
            )

    x_copy, home_copy = [], []

    def add_core(i):
        part = pl.ds(i * TAIL_CHUNK, TAIL_CHUNK)
        to_core[i].wait()
        x_out[part] = (own_dh[1, part] + core_buf[1, part].astype(f32)).astype(bf16)
        x_copy.append(send(x_out.at[part], x_buf.at[part], x_s, x_r, i, by_x))

    def finish(i):
        part = pl.ds(i * TAIL_CHUNK, TAIL_CHUNK)
        if i == 0:
            for copy in inputs[1:]:
                copy.wait()
        x_copy[i].wait()
        d_low = own_dh[0, part] + core_buf[0, part].astype(f32) + x_buf[part].astype(f32)
        unit, inv = norm_parts(x_ref[part].astype(f32))
        scaled = d_low * gain_ref[...]
        dx = dmid_ref[part] + inv * (
            scaled
            - jnp.mean(scaled, axis=-1, keepdims=True)
            - unit * jnp.mean(scaled * unit, axis=-1, keepdims=True)
        )
        dx_out[part] = dx.astype(bf16)
        turn, row = i // per_turn, (i % per_turn) * TAIL_CHUNK
        target = home_buf.at[upper, pl.ds(row, TAIL_CHUNK)]
        if turn == 0:
            @pl.when(stay)
            def _():
                pltpu.make_async_copy(dx_out.at[part], target, self_sem.at[i]).start()

            @pl.when(jnp.logical_not(stay))
            def _():
                send(dx_out.at[part], target, home_s, home_r, i, home[0])
        else:
            send(dx_out.at[part], target, home_s, home_r, i, home[1])

    def arrive(i):
        part = pl.ds(i * TAIL_CHUNK, TAIL_CHUNK)
        turn, row = i // per_turn, (i % per_turn) * TAIL_CHUNK
        block = odd if turn == 0 else 1 - odd
        landed = home_buf.at[block, pl.ds(row, TAIL_CHUNK)]

        def remote():
            copy = pltpu.make_async_remote_copy(
                src_ref=dx_out.at[part], dst_ref=landed, send_sem=home_s.at[i], recv_sem=home_r.at[i],
                device_id=home[turn], device_id_type=MESH,
            )
            copy.wait_send()
            copy.wait_recv()

        if turn == 0:
            @pl.when(stay)
            def _():
                pltpu.make_async_copy(dx_out.at[part], landed, self_sem.at[i]).wait()

            pl.when(jnp.logical_not(stay))(remote)
        else:
            remote()

    share(0)
    share(1)
    add_core(0)
    share(2)
    g_start(0)
    add_core(1)
    share(3)
    g_start(1)
    add_core(2)
    share(4)
    g_start(2)
    add_core(3)
    share(5)
    share(6)
    add_core(4)
    share(7)
    add_core(5)
    weight(0)
    weight(1)
    weight(2)
    weight(3)
    weight_close()
    g_second(0)
    g_second(1)
    g_second(2)
    add_core(6)
    add_core(7)
    s_next(0)
    w_second()
    finish(0)
    g_third(0)
    g_third(1)
    g_third(2)
    s_next(1)
    w_third()
    finish(1)
    g_fourth(0)
    g_fourth(1)
    g_fourth(2)
    s_next(2)
    w_fourth()
    finish(2)
    g_fifth(0)
    g_fifth(1)
    g_fifth(2)
    w_fifth()
    s_next(3)
    finish(3)
    w_sixth()
    finish(4)
    s_next(4)
    finish(5)
    finish(6)
    finish(7)
    w_copy["core"].wait()
    w_copy["x"].wait()
    w_copy["xc"].wait()
    wall[2 * x + c] = wfull[c]
    sum_ref[...] = small_out[4]
    for i in range(chunks):
        arrive(i)
    for p in range(PIECES):
        g_copy["x", p].wait()


def tail(d_qkv, unit_t, x, dmid, weight, gain, bias, keep, from_y, from_x, from_xy, gvecs, gub):
    count, width = x.shape
    shard = width // 4
    half = count // 2
    chunks = count // TAIL_CHUNK
    sixth = keep.shape[1]
    vmem = pl.BlockSpec(memory_space=pltpu.VMEM)
    dma = pltpu.SemaphoreType.DMA
    buf = pltpu.VMEM
    return pl.pallas_call(
        tail_kernel,
        in_specs=[pl.BlockSpec(memory_space=pl.ANY)] * 4 + [vmem] * 9,
        out_specs=[vmem] * 4,
        out_shape=[
            jax.ShapeDtypeStruct((2, half, width), bf16),
            jax.ShapeDtypeStruct((PIECES, 2, sixth, width), bf16),
            jax.ShapeDtypeStruct((4, shard, 3 * PAIR), bf16),
            jax.ShapeDtypeStruct((16, width), f32),
        ],
        scratch_shapes=[
            buf(d_qkv.shape, bf16),
            buf(unit_t.shape, bf16),
            buf(weight.shape, f32),
            buf((1, 3 * PAIR), f32),
            buf((4, shard, 3 * PAIR), bf16),
            buf((2, count, width), bf16),
            buf((count, width), bf16),
            buf((count, width), f32),
            buf((2, count, width), bf16),
            buf((2, count, width), f32),
            buf((count, width), bf16),
            buf((count, width), bf16),
            buf((count, width), bf16),
            buf((PIECES, sixth, width), f32),
            buf((PIECES, sixth // 2, width), bf16),
            buf((PIECES, sixth // 2, width), bf16),
            buf((PIECES, sixth // 4, width), bf16),
            buf((PIECES, sixth // 4, width), bf16),
            buf((2, shard, 3 * PAIR), bf16),
            buf((2, shard, 3 * PAIR), f32),
            buf((shard, 3 * PAIR), bf16),
            buf((shard, 3 * PAIR), bf16),
            buf((shard // 2, 3 * PAIR), bf16),
            buf((shard // 2, 3 * PAIR), bf16),
            buf((2, shard, 3 * PAIR), bf16),
            buf((16, width), f32),
            buf((5, 16, width), f32),
            buf((5, 16, width), f32),
            dma((chunks,)),
            dma((chunks // 2,)),
            dma((chunks,)),
            dma((chunks,)),
            dma((chunks,)),
            dma((chunks,)),
            dma((chunks,)),
            dma((chunks,)),
            dma((5 * PIECES,)),
            dma((5 * PIECES,)),
            dma((8,)),
            dma((8,)),
            dma((5,)),
            dma((5,)),
            dma((3,)),
        ],
        compiler_params=pltpu.CompilerParams(
            collective_id=5, has_side_effects=True, vmem_limit_bytes=56 * 1024 * 1024
        ),
        name="tail",
    )(d_qkv, unit_t, x, dmid, weight, gain, bias, keep, from_y, from_x, from_xy, gvecs, gub)

def results_kernel(
    y_ref, dx_ref, down_ref, up_ref, out_ref, wall_ref, sum_ref,
    y_out, dx_out, gd_ref, gu_ref, go_ref, gq_ref, *vectors,
):
    step = pl.program_id(0)
    width = dx_ref.shape[-1]
    y_out[:, 0] = y_ref[...]
    dx_out[:, 0] = dx_ref[...].astype(f32)
    gd_ref[...] = down_ref[...].astype(f32)
    gu_ref[...] = up_ref[...].astype(f32)
    go_ref[...] = out_ref[...].astype(f32)
    for part in range(3):
        at = pl.multiple_of(part * width + step * PAIR, PAIR)
        gq_ref[:, pl.ds(at, PAIR)] = wall_ref[0, :, part * PAIR : (part + 1) * PAIR].astype(f32)
    shard = go_ref.shape[0]
    mine = 2 * lax.axis_index("y") + lax.axis_index("c")
    for i in range(6):
        vectors[i][...] = sum_ref[i : i + 1, pl.ds(pl.multiple_of(mine * shard, shard), shard)]
    vectors[6][...] = sum_ref[pl.ds(6 + mine, 1), :]


def results(y, dx, flat, wall, sums):
    half, width = dx.shape[1:]
    shard = wall.shape[1]
    steps = 4
    flat = flat.reshape(-1, width)
    tokens = pl.BlockSpec((2, half // steps, width), lambda i: (0, i, 0))
    tokens_out = pl.BlockSpec((2, 1, half // steps, width), lambda i: (0, 0, i, 0))
    shape = jax.ShapeDtypeStruct
    return pl.pallas_call(
        results_kernel,
        grid=(steps,),
        in_specs=[
            tokens,
            tokens,
            pl.BlockSpec((shard, width), lambda i: (i, 0)),
            pl.BlockSpec((shard, width), lambda i: (steps + i, 0)),
            pl.BlockSpec((shard, width), lambda i: (2 * steps, 0)),
            pl.BlockSpec((1, shard, 3 * PAIR), lambda i: (i, 0, 0)),
            whole(sums.shape),
        ],
        out_specs=[
            tokens_out,
            tokens_out,
            pl.BlockSpec((shard, width), lambda i: (i, 0)),
            pl.BlockSpec((shard, width), lambda i: (0, i)),
            whole((shard, width)),
            whole((shard, 3 * width)),
        ]
        + [whole((1, shard))] * 6
        + [whole((1, width))],
        out_shape=[
            shape((2, 1, half, width), bf16),
            shape((2, 1, half, width), f32),
            shape((width, width), f32),
            shape((shard, 4 * width), f32),
            shape((shard, width), f32),
            shape((shard, 3 * width), f32),
        ]
        + [shape((1, shard), f32)] * 6
        + [shape((1, width), f32)],
        name="results",
    )(y, dx, flat, flat, flat, wall, sums)


def place(z, x, y, c):
    return ((z * SIZES[1] + x) * SIZES[2] + y) * SIZES[3] + c


def everyone():
    return [
        (z, x, y, c)
        for z in range(SIZES[0])
        for x in range(SIZES[1])
        for y in range(SIZES[2])
        for c in range(SIZES[3])
    ]


def swap_pairs(dx, dy, dc):
    return [(place(z, x, y, c), place(z, x ^ dx, y ^ dy, c ^ dc)) for z, x, y, c in everyone()]


def move(value, pairs):
    return lax.ppermute(value, AXES, pairs)


def swap(value, dx=0, dy=0, dc=0):
    return move(value, swap_pairs(dx, dy, dc))


def paired_body(
    inputs, out_grad, segment_ids, block_order, w_qkv, w_out, w_up, w_down,
    norm1_gain, norm1_bias, norm2_gain, norm2_bias, out_bias, up_bias, down_bias,
):
    vectors = (norm1_gain, norm1_bias, norm2_gain, norm2_bias, out_bias, down_bias, up_bias)
    (
        qt, k, kt, v, vt, unit, own_x, full_out, full_up, full_down, near_dy, w_heads, vecs, full_ubias, start, tab
    ) = head(
        inputs, out_grad, segment_ids.reshape(2, -1, 128), block_order, vectors, w_qkv, w_out, w_up, w_down
    )
    gain_one, bias_one = vecs[0:1], vecs[1:2]
    o, ot, lse = attend(tab, qt, start, k, vt)
    d_o, outputs, d_middle, keep, to_y, to_x, to_xy, g_vecs, g_ubias = feed(
        o.reshape(4, -1, PAIR), own_x, near_dy, out_grad, full_out, full_up, full_down, vecs, full_ubias, 4
    )
    from_y, from_x, from_xy = swap(to_y, dy=1), swap(to_x, dx=1), swap(to_xy, dy=1, dx=1)
    d_qkv = attend_back(tab, k, kt, v, qt, start, d_o.reshape(-1, PAIR), ot, lse)
    dx, flat, heads, sums = tail(
        d_qkv.reshape(4, -1, 3 * PAIR), unit, own_x, d_middle, w_heads, gain_one, bias_one,
        keep, from_y, from_x, from_xy, g_vecs, g_ubias,
    )
    outputs, input_grad, grad_down, grad_up, grad_out, grad_qkv, *vec = results(outputs, dx, flat, heads, sums)
    vec = [member.reshape(-1) for member in vec]
    return (
        outputs, input_grad, grad_qkv, grad_out, grad_up, grad_down,
        vec[0], vec[1], vec[2], vec[3], vec[4], vec[6], vec[5],
    )


def solution(mesh):
    paired = mesh.shape["ctx"] == SIZES[0] * SIZES[1] and mesh.shape["fsdp"] == SIZES[2] * SIZES[3]
    if paired:
        mesh = Mesh(mesh.devices.reshape(SIZES), AXES)
        ctx, fsdp, program = ("z", "x"), ("y", "c"), paired_body
    else:
        ctx, fsdp, program = "ctx", "fsdp", general_body
    tokens = P(None, fsdp, ctx, None)
    matrix, vector = P(fsdp, None), P(fsdp)
    return jax.shard_map(
        program,
        mesh=mesh,
        in_specs=(tokens, tokens, P(None, fsdp, ctx), P()) + (matrix,) * 4 + (vector,) * 7,
        out_specs=(tokens, tokens) + (matrix,) * 4 + (vector,) * 7,
        check_vma=False,
    )
```

```python
import functools
import math

import jax
import jax.numpy as jnp
from jax import lax
from jax.experimental import pallas as pl
from jax.experimental.pallas import tpu as pltpu
from jax.sharding import Mesh
from jax.sharding import PartitionSpec as P

H = 8
HD = 64
BLK = 256
PAIR = 2 * HD

norm_eps = 1e-05
mask_fill = -1e30
LOG2E = math.log2(math.e)
LN2 = math.log(2.0)
SCORE_SCALE = 1.0 / math.sqrt(HD)

f32 = jnp.float32
bf16 = jnp.bfloat16


def contract(a, b, da, db):
    return lax.dot_general(a, b, (((da,), (db,)), ((), ())), preferred_element_type=f32)


def norm_parts(values):
    center = values - jnp.mean(values, axis=-1, keepdims=True)
    spread = jnp.mean(center * center, axis=-1, keepdims=True)
    inv = lax.rsqrt(spread + norm_eps)
    return center * inv, inv


def whole(shape):
    zeros = (0,) * len(shape)
    return pl.BlockSpec(shape, lambda *_: zeros)


def two_heads(block):
    zero = jnp.zeros((HD, block.shape[1]), block.dtype)
    return jnp.concatenate(
        [jnp.concatenate([block[:HD], zero], axis=0), jnp.concatenate([zero, block[HD:]], axis=0)], axis=1
    )


EXTRA = 16


def attend_kernel(
    tab_ref, qt_ref, start_ref, k_ref, vt_ref, o_hbm, ot_hbm, lse_ref, acc, top, o_buf, ot_buf, out_sem
):
    blocks = start_ref.shape[0]
    row = lax.broadcasted_iota(jnp.int32, (BLK, 2 * BLK), 0)
    reach = row - jnp.bitwise_and(lax.broadcasted_iota(jnp.int32, (BLK, 2 * BLK), 1), BLK - 1)
    ones = jnp.ones((EXTRA, 2 * BLK), bf16)

    def place_of(b):
        return pl.ds(pl.multiple_of(tab_ref[2, jnp.maximum(b, 0)] * BLK, BLK), BLK)

    def visits_of(qb):
        return (qb - tab_ref[0, qb]) // 2 + 1

    def visit(qb, i, bounded, live=True):
        kb = qb - 2 * i
        both = two_heads(qt_ref[:, place_of(qb)])
        start = jnp.concatenate([start_ref[qb], start_ref[qb]], axis=1)
        places = [place_of(kb), place_of(kb - 1)]
        terms = []
        for n in range(2):
            first_row = start - (kb - n) * BLK
            allowed = row >= (first_row if live is True else jnp.where(live, first_row, BLK))
            if n == 0:
                allowed = allowed & (reach <= (qb - kb) * BLK)
            st = jnp.dot(k_ref[places[n], :], both, preferred_element_type=f32)
            terms.append(jnp.where(allowed, st, mask_fill))
        if bounded:
            probs = [jnp.exp2(term).astype(bf16) for term in terms]
        else:
            old = top[qb]
            peak = jnp.maximum(
                jnp.max(terms[0], axis=0, keepdims=True), jnp.max(terms[1], axis=0, keepdims=True)
            )
            peak = jnp.maximum(old, peak)
            shrink = jnp.exp2(old - peak)
            top[qb] = peak
            probs = [jnp.exp2(term - peak).astype(bf16) for term in terms]
        probs = jnp.concatenate(probs, axis=0)
        vt = jnp.concatenate([vt_ref[:, places[0]], vt_ref[:, places[1]]], axis=1)
        parts = []
        for head in range(2):
            cols = slice(head * BLK, (head + 1) * BLK)
            left = jnp.concatenate([vt[head * HD : (head + 1) * HD], ones], axis=0)
            part = jnp.dot(left, probs[:, cols], preferred_element_type=f32)
            parts.append(part)
            if not bounded:
                acc[qb, head] = part + acc[qb, head] * shrink[:, cols]
        return parts

    def all_visits(bounded):
        count = lax.fori_loop(0, blocks, lambda b, n: n + visits_of(b), 0)

        def following(qb, i):
            more = i + 1 < visits_of(qb)
            return jnp.where(more, qb, jnp.minimum(qb + 1, blocks - 1)), jnp.where(more, i + 1, 0)

        def step(n, state):
            if not bounded:
                visit(*state, False)
                return following(*state)
            second = following(*state)
            members = [visit(*state, True), visit(*second, True, 2 * n + 1 < count)]
            for (qb, _), parts in zip((state, second), members):
                for head in range(2):
                    acc[qb, head] += parts[head]
            return following(*second)

        lax.fori_loop(0, (count + 1) // 2 if bounded else count, step, (jnp.int32(0), jnp.int32(0)))

    small = tab_ref[3, 0] > 0
    acc[...] = jnp.zeros_like(acc)

    @pl.when(small)
    def _():
        top[...] = jnp.zeros_like(top)
        all_visits(True)

    @pl.when(jnp.logical_not(small))
    def _():
        top[...] = jnp.full_like(top, mask_fill)
        all_visits(False)

    def outgoing(b):
        at = place_of(b)
        return (
            pltpu.make_async_copy(o_buf.at[b], o_hbm.at[at], out_sem.at[0]),
            pltpu.make_async_copy(ot_buf.at[b], ot_hbm.at[b], out_sem.at[1]),
        )

    def close(b):
        total = jnp.concatenate([acc[b, 0, HD : HD + 1], acc[b, 1, HD : HD + 1]], axis=1)
        lse_ref[b] = top[b] + jnp.log2(total)
        heads = jnp.concatenate([acc[b, h, :HD] / acc[b, h, HD : HD + 1] for h in range(2)], axis=0)
        ot_buf[b] = heads
        o_buf[b] = heads.T.astype(bf16)
        for copy in outgoing(b):
            copy.start()

    def close_two(n, carry):
        close(2 * n)
        close(2 * n + 1)
        return carry

    lax.fori_loop(0, blocks // 2, close_two, 0)
    for whole_copy in (
        pltpu.make_async_copy(ot_buf, ot_hbm, out_sem.at[1]),
        pltpu.make_async_copy(o_hbm, o_hbm, out_sem.at[0]),
    ):
        whole_copy.wait()


def attend(tab, qt, start, k, vt):
    count = k.shape[0]
    blocks = count // BLK
    vmem, any_ = pl.BlockSpec(memory_space=pltpu.VMEM), pl.BlockSpec(memory_space=pl.ANY)
    return pl.pallas_call(
        attend_kernel,
        grid_spec=pltpu.PrefetchScalarGridSpec(
            num_scalar_prefetch=1,
            grid=(),
            in_specs=[vmem] * 4,
            out_specs=[any_, any_, vmem],
            scratch_shapes=[
                pltpu.VMEM((blocks, 2, HD + EXTRA, BLK), f32),
                pltpu.VMEM((blocks, 1, 2 * BLK), f32),
                pltpu.VMEM((blocks, BLK, PAIR), bf16),
                pltpu.VMEM((blocks, PAIR, BLK), f32),
                pltpu.SemaphoreType.DMA((2,)),
            ],
        ),
        out_shape=[
            jax.ShapeDtypeStruct((count, PAIR), bf16),
            jax.ShapeDtypeStruct((blocks, PAIR, BLK), f32),
            jax.ShapeDtypeStruct((blocks, 1, 2 * BLK), f32),
        ],
        name="attend",
    )(tab, qt, start, k, vt)


def split_heads(block):
    lane = lax.broadcasted_iota(jnp.int32, block.shape, 1)
    zero = jnp.zeros_like(block)
    first = lane < HD
    return jnp.concatenate([jnp.where(first, block, zero), jnp.where(first, zero, block)], axis=0)


def attend_back_kernel(
    tab_ref, k_hbm, kt_hbm, v_hbm, y_hbm, qt_ref, start_ref, do_ref, ot_ref, lse_ref, out_hbm, y_out,
    k_ref, kt_ref, v_ref, y_buf, out_buf, dqt, dk, dv, dot, dom, qm, delta, in_sem, out_sem,
):
    blocks = start_ref.shape[0]
    row = lax.broadcasted_iota(jnp.int32, (BLK, 2 * BLK), 0)
    reach = row - jnp.bitwise_and(lax.broadcasted_iota(jnp.int32, (BLK, 2 * BLK), 1), BLK - 1)
    loads = [
        pltpu.make_async_copy(src, dst, in_sem.at[i])
        for i, (src, dst) in enumerate(((k_hbm, k_ref), (kt_hbm, kt_ref), (v_hbm, v_ref), (y_hbm, y_buf)))
    ]
    for copy in loads:
        copy.start()

    def at(b):
        return pl.ds(pl.multiple_of(tab_ref[2, b] * BLK, BLK), BLK)

    def prepare(qb):
        dqt[qb] = jnp.zeros((PAIR, BLK), f32)
        dk[qb] = jnp.zeros((BLK, PAIR), f32)
        dv[qb] = jnp.zeros((BLK, PAIR), f32)
        d_out = do_ref[at(qb), :]
        dom[qb] = split_heads(d_out)
        qm[qb] = split_heads(qt_ref[:, at(qb)].T)
        turned = d_out.astype(f32).T
        dot[qb] = turned.astype(bf16)
        both = turned * ot_ref[qb]
        delta[qb] = jnp.concatenate(
            [jnp.sum(both[:HD], axis=0, keepdims=True), jnp.sum(both[HD:], axis=0, keepdims=True)], axis=1
        )

    def prepare_two(n, carry):
        prepare(2 * n)
        prepare(2 * n + 1)
        return carry

    lax.fori_loop(0, blocks // 2, prepare_two, 0)
    for copy in loads:
        copy.wait()
    y_copy = pltpu.make_async_copy(y_buf, y_out.at[:, 0], out_sem.at[1])
    y_copy.start()

    def tile(kb, qb, live):
        kt = kt_ref[:, at(kb)]
        start = jnp.concatenate([start_ref[qb], start_ref[qb]], axis=1)
        st = jnp.dot(k_ref[at(kb), :], two_heads(qt_ref[:, at(qb)]), preferred_element_type=f32)
        dpt = jnp.dot(v_ref[at(kb), :], two_heads(dot[qb]), preferred_element_type=f32)
        allowed = (row >= start - kb * BLK) & (reach <= jnp.where(live, (qb - kb) * BLK, -2 * BLK))
        pt = jnp.exp2(jnp.where(allowed, st - lse_ref[qb], mask_fill))
        dst = (pt * (dpt - delta[qb])).astype(bf16)
        part_v = jnp.dot(pt.astype(bf16), dom[qb], preferred_element_type=f32)
        part_k = jnp.dot(dst, qm[qb], preferred_element_type=f32)
        part_q = [
            jnp.dot(kt[head * HD : (head + 1) * HD], dst[:, head * BLK : (head + 1) * BLK], preferred_element_type=f32)
            for head in range(2)
        ]
        return kb, qb, part_v, part_k, jnp.concatenate(part_q, axis=0)

    def add(kb, qb, part_v, part_k, part_q):
        dv[kb] += part_v
        dk[kb] += part_k
        dqt[qb] += part_q

    def following(kb, qb):
        more = qb < tab_ref[1, kb]
        beyond = jnp.minimum(kb + 1, blocks - 1)
        return jnp.where(more, kb, beyond), jnp.where(more, qb + 1, beyond)

    tiles = lax.fori_loop(0, blocks, lambda b, n: n + tab_ref[1, b] - b + 1, 0)

    def step(n, state):
        second = following(*state)
        terms = [tile(*state, True), tile(*second, 2 * n + 1 < tiles)]
        for term in terms:
            add(*term)
        return following(*second)

    lax.fori_loop(0, (tiles + 1) // 2, step, (jnp.int32(0), jnp.int32(0)))
    def close(b):
        out_buf[b] = jnp.concatenate([(dqt[b] * SCORE_SCALE).T, dk[b] * LN2, dv[b]], axis=1).astype(bf16)
        pltpu.make_async_copy(out_buf.at[b], out_hbm.at[at(b)], out_sem.at[0]).start()

    def close_four(n, carry):
        for i in range(4):
            close(4 * n + i)
        return carry

    lax.fori_loop(0, blocks // 4, close_four, 0)
    pltpu.make_async_copy(out_hbm, out_hbm, out_sem.at[0]).wait()
    y_copy.wait()


def attend_back(tab, k, kt, v, y, qt, start, d_out, ot, lse):
    count = k.shape[0]
    blocks = count // BLK
    vmem, any_ = pl.BlockSpec(memory_space=pltpu.VMEM), pl.BlockSpec(memory_space=pl.ANY)
    buf = pltpu.VMEM
    return pl.pallas_call(
        attend_back_kernel,
        grid_spec=pltpu.PrefetchScalarGridSpec(
            num_scalar_prefetch=1,
            grid=(),
            in_specs=[any_] * 4 + [vmem] * 5,
            out_specs=[any_, any_],
            scratch_shapes=[
                buf(k.shape, bf16),
                buf(kt.shape, bf16),
                buf(v.shape, bf16),
                buf(y.shape, bf16),
                buf((blocks, BLK, 3 * PAIR), bf16),
                buf((blocks, PAIR, BLK), f32),
                buf((blocks, BLK, PAIR), f32),
                buf((blocks, BLK, PAIR), f32),
                buf((blocks, PAIR, BLK), bf16),
                buf((blocks, 2 * BLK, PAIR), bf16),
                buf((blocks, 2 * BLK, PAIR), bf16),
                buf((blocks, 1, 2 * BLK), f32),
                pltpu.SemaphoreType.DMA((4,)),
                pltpu.SemaphoreType.DMA((2,)),
            ],
        ),
        out_shape=[
            jax.ShapeDtypeStruct((count, 3 * PAIR), bf16),
            jax.ShapeDtypeStruct((y.shape[0], 1) + y.shape[1:], bf16),
        ],
        compiler_params=pltpu.CompilerParams(vmem_limit_bytes=60 * 1024 * 1024),
        name="attend_back",
    )(tab, k, kt, v, y, qt, start, d_out, ot, lse)


def layer_norm(values, gain_vec, offset):
    center = values - jnp.mean(values, axis=-1, keepdims=True)
    spread = jnp.mean(center * center, axis=-1, keepdims=True)
    return center * lax.rsqrt(spread + norm_eps) * gain_vec + offset


def gelu_exact(values):
    return 0.5 * values * (1.0 + lax.erf(values * (1.0 / math.sqrt(2.0))))


def score_block(query_heads, key_heads, query_doc, query_pos, key_doc, key_pos):
    raw_scores = jnp.einsum(
        "qhd,khd->hqk", query_heads, key_heads, preferred_element_type=jnp.float32
    ) * (1.0 / math.sqrt(HD))
    allowed = (query_doc[:, None] == key_doc[None, :]) & (key_pos[None, :] <= query_pos[:, None])
    return (raw_scores, allowed[None])


def soft_block(raw_scores, allowed, log_norm):
    return jnp.exp(jnp.where(allowed, raw_scores, mask_fill) - log_norm[:, :, None])


def row_log_norm(query_heads, key_blocks, doc_blocks, pos_blocks, query_doc, query_pos):

    def row_visit(running, block_item):
        row_top, row_sum = running
        key_heads, key_doc, key_pos = block_item
        raw_scores, allowed = score_block(
            query_heads, key_heads, query_doc, query_pos, key_doc, key_pos
        )
        masked = jnp.where(allowed, raw_scores, mask_fill)
        new_top = jnp.maximum(row_top, jnp.max(masked, axis=-1))
        fresh = jnp.sum(jnp.where(allowed, jnp.exp(masked - new_top[:, :, None]), 0.0), axis=-1)
        return ((new_top, row_sum * jnp.exp(row_top - new_top) + fresh), None)

    query_count = query_doc.shape[0]
    start = (
        jnp.full((H, query_count), mask_fill, jnp.float32),
        jnp.zeros((H, query_count), jnp.float32),
    )
    (row_top, row_sum), unused = lax.scan(row_visit, start, (key_blocks, doc_blocks, pos_blocks))
    return row_top + jnp.log(row_sum)


def attend_all(
    query_heads, key_blocks, value_blocks, doc_blocks, pos_blocks, query_doc, query_pos, log_norm
):

    def attend_visit(accum_out, block_item):
        key_heads, value_heads, key_doc, key_pos = block_item
        raw_scores, allowed = score_block(
            query_heads, key_heads, query_doc, query_pos, key_doc, key_pos
        )
        soft_low = soft_block(raw_scores, allowed, log_norm).astype(jnp.bfloat16)
        return (
            accum_out
            + jnp.einsum("hqk,khd->qhd", soft_low, value_heads, preferred_element_type=jnp.float32),
            None,
        )

    start = jnp.zeros(query_heads.shape, jnp.float32)
    accum_out, unused = lax.scan(
        attend_visit, start, (key_blocks, value_blocks, doc_blocks, pos_blocks)
    )
    return accum_out


def grad_block(
    query_heads,
    grad_heads,
    log_norm,
    row_delta,
    query_doc,
    query_pos,
    key_heads,
    value_heads,
    key_doc,
    key_pos,
):
    raw_scores, allowed = score_block(
        query_heads, key_heads, query_doc, query_pos, key_doc, key_pos
    )
    soft = soft_block(raw_scores, allowed, log_norm)
    grad_soft = jnp.einsum(
        "qhd,khd->hqk", grad_heads, value_heads, preferred_element_type=jnp.float32
    )
    grad_scores = (soft * (grad_soft - row_delta[:, :, None])).astype(jnp.bfloat16)
    score_scale = 1.0 / math.sqrt(HD)
    part_q = (
        jnp.einsum("hqk,khd->qhd", grad_scores, key_heads, preferred_element_type=jnp.float32)
        * score_scale
    )
    part_k = (
        jnp.einsum("hqk,qhd->khd", grad_scores, query_heads, preferred_element_type=jnp.float32)
        * score_scale
    )
    part_v = jnp.einsum(
        "hqk,qhd->khd", soft.astype(jnp.bfloat16), grad_heads, preferred_element_type=jnp.float32
    )
    return (part_q, part_k, part_v)


def general_body(
    inputs,
    out_grad,
    segment_ids,
    block_order,
    w_qkv,
    w_out,
    w_up,
    w_down,
    norm1_gain,
    norm1_bias,
    norm2_gain,
    norm2_bias,
    out_bias,
    up_bias,
    down_bias,
):
    gathered = (
        lax.all_gather(w_qkv, "fsdp", axis=0, tiled=True),
        lax.all_gather(w_out, "fsdp", axis=0, tiled=True),
        lax.all_gather(w_up, "fsdp", axis=0, tiled=True),
        lax.all_gather(w_down, "fsdp", axis=0, tiled=True),
        lax.all_gather(norm1_gain, "fsdp", axis=0, tiled=True),
        lax.all_gather(norm1_bias, "fsdp", axis=0, tiled=True),
        lax.all_gather(norm2_gain, "fsdp", axis=0, tiled=True),
        lax.all_gather(norm2_bias, "fsdp", axis=0, tiled=True),
        lax.all_gather(out_bias, "fsdp", axis=0, tiled=True),
        lax.all_gather(up_bias, "fsdp", axis=0, tiled=True),
        lax.all_gather(down_bias, "fsdp", axis=0, tiled=True),
    )
    full_qkv, full_out, full_up, full_down = (gathered[0], gathered[1], gathered[2], gathered[3])
    gain_one, bias_one, gain_two, bias_two, full_obias, full_ubias, full_dbias = [
        member.astype(jnp.float32) for member in gathered[4:]
    ]
    model_width = full_qkv.shape[0]
    local_rows = inputs.shape[2]
    ctx_count = lax.axis_size("ctx")
    seq_len = local_rows * ctx_count
    key_block = min(512, seq_len)
    block_count = seq_len // key_block
    ctx_index = lax.axis_index("ctx")
    row_ids = jnp.arange(local_rows, dtype=jnp.int32)
    own_blocks = lax.dynamic_slice_in_dim(block_order, 2 * ctx_index, 2)
    own_pos = own_blocks[row_ids // BLK] * BLK + row_ids % BLK
    all_ids = jnp.arange(seq_len, dtype=jnp.int32)
    all_pos = block_order[all_ids // BLK] * BLK + all_ids % BLK
    pos_blocks = all_pos.reshape(block_count, key_block)
    grad_sums = [jnp.zeros(member.shape, jnp.float32) for member in gathered]
    outputs_list = []
    input_grads = []
    for micro_idx in range(inputs.shape[0]):
        seq_in = inputs[micro_idx, 0].astype(jnp.float32)
        normed, norm1_pull = jax.vjp(layer_norm, seq_in, gain_one, bias_one)
        normed_low = normed.astype(jnp.bfloat16)
        qkv_out = jnp.dot(normed_low, full_qkv, preferred_element_type=jnp.float32).astype(
            jnp.bfloat16
        )
        query_heads = qkv_out[:, :model_width].reshape(local_rows, H, HD)
        kv_all, doc_all = (
            lax.all_gather(qkv_out[:, model_width:], "ctx", axis=0, tiled=True),
            lax.all_gather(segment_ids[micro_idx, 0], "ctx", axis=0, tiled=True),
        )
        doc_rows = doc_all[all_pos]
        query_doc = doc_all[own_pos]
        kv_heads = kv_all.reshape(block_count, key_block, 2, H, HD)
        key_blocks = kv_heads[:, :, 0]
        value_blocks = kv_heads[:, :, 1]
        doc_blocks = doc_rows.reshape(block_count, key_block)
        log_norm = row_log_norm(query_heads, key_blocks, doc_blocks, pos_blocks, query_doc, own_pos)
        attn_acc = attend_all(
            query_heads,
            key_blocks,
            value_blocks,
            doc_blocks,
            pos_blocks,
            query_doc,
            own_pos,
            log_norm,
        )
        attn_low = attn_acc.reshape(local_rows, model_width).astype(jnp.bfloat16)
        branch = jnp.dot(attn_low, full_out, preferred_element_type=jnp.float32) + full_obias
        middle = seq_in + branch
        normed_two, norm2_pull = jax.vjp(layer_norm, middle, gain_two, bias_two)
        normed_two_low = normed_two.astype(jnp.bfloat16)
        hidden = jnp.dot(normed_two_low, full_up, preferred_element_type=jnp.float32) + full_ubias
        active, gelu_pull = jax.vjp(gelu_exact, hidden)
        active_low = active.astype(jnp.bfloat16)
        result = middle + (
            jnp.dot(active_low, full_down, preferred_element_type=jnp.float32) + full_dbias
        )
        outputs_list.append(result.astype(jnp.bfloat16))
        grad_y = out_grad[micro_idx, 0]
        grad_y32 = grad_y.astype(jnp.float32)
        grad_sums[3] = grad_sums[3] + jnp.einsum(
            "rf,rd->fd", active_low, grad_y, preferred_element_type=jnp.float32
        )
        grad_sums[10] = grad_sums[10] + jnp.sum(grad_y32, axis=0)
        grad_active = jnp.einsum("rd,fd->rf", grad_y, full_down, preferred_element_type=jnp.float32)
        (grad_hidden,) = gelu_pull(grad_active)
        grad_hidden_low = grad_hidden.astype(jnp.bfloat16)
        grad_sums[2] = grad_sums[2] + jnp.einsum(
            "rd,rf->df", normed_two_low, grad_hidden_low, preferred_element_type=jnp.float32
        )
        grad_sums[9] = grad_sums[9] + jnp.sum(grad_hidden_low.astype(jnp.float32), axis=0)
        grad_normed_two = jnp.einsum(
            "rf,df->rd", grad_hidden_low, full_up, preferred_element_type=jnp.float32
        )
        grad_mid_ln, grad_gain_two, grad_bias_two = norm2_pull(grad_normed_two)
        grad_sums[6] = grad_sums[6] + grad_gain_two
        grad_sums[7] = grad_sums[7] + grad_bias_two
        grad_mid = grad_y32 + grad_mid_ln
        grad_mid_low = grad_mid.astype(jnp.bfloat16)
        grad_sums[1] = grad_sums[1] + jnp.einsum(
            "rd,re->de", attn_low, grad_mid_low, preferred_element_type=jnp.float32
        )
        grad_sums[8] = grad_sums[8] + jnp.sum(grad_mid_low.astype(jnp.float32), axis=0)
        grad_attn_low = jnp.einsum(
            "re,de->rd", grad_mid_low, full_out, preferred_element_type=jnp.float32
        ).astype(jnp.bfloat16)
        grad_heads = grad_attn_low.reshape(local_rows, H, HD)
        row_delta = jnp.sum(grad_heads.astype(jnp.float32) * attn_acc, axis=-1).T

        def back_visit(grad_query, block_item):
            key_heads, value_heads, key_doc, key_pos = block_item
            part_q, part_k, part_v = grad_block(
                query_heads,
                grad_heads,
                log_norm,
                row_delta,
                query_doc,
                own_pos,
                key_heads,
                value_heads,
                key_doc,
                key_pos,
            )
            joined = jnp.concatenate(
                [part_k.reshape(key_block, model_width), part_v.reshape(key_block, model_width)],
                axis=1,
            )
            return (grad_query + part_q, joined)

        grad_query, kv_terms = lax.scan(
            back_visit,
            jnp.zeros((local_rows, H, HD), jnp.float32),
            (key_blocks, value_blocks, doc_blocks, pos_blocks),
        )
        kv_grad = lax.psum_scatter(
            kv_terms.reshape(seq_len, 2 * model_width).astype(jnp.bfloat16),
            "ctx",
            scatter_dimension=0,
            tiled=True,
        ).astype(jnp.float32)
        grad_qkv_low = jnp.concatenate(
            [grad_query.reshape(local_rows, model_width), kv_grad], axis=1
        ).astype(jnp.bfloat16)
        grad_sums[0] = grad_sums[0] + jnp.einsum(
            "rd,re->de", normed_low, grad_qkv_low, preferred_element_type=jnp.float32
        )
        grad_normed = jnp.einsum(
            "re,de->rd", grad_qkv_low, full_qkv, preferred_element_type=jnp.float32
        )
        grad_in_ln, grad_gain_one, grad_bias_one = norm1_pull(grad_normed)
        grad_sums[4] = grad_sums[4] + grad_gain_one
        grad_sums[5] = grad_sums[5] + grad_bias_one
        input_grads.append(grad_mid + grad_in_ln)
    owned = (
        lax.psum_scatter(
            grad_sums[0].astype(jnp.bfloat16), "fsdp", scatter_dimension=0, tiled=True
        ).astype(jnp.float32),
        lax.psum_scatter(
            grad_sums[1].astype(jnp.bfloat16), "fsdp", scatter_dimension=0, tiled=True
        ).astype(jnp.float32),
        lax.psum_scatter(
            grad_sums[2].astype(jnp.bfloat16), "fsdp", scatter_dimension=0, tiled=True
        ).astype(jnp.float32),
        lax.psum_scatter(
            grad_sums[3].astype(jnp.bfloat16), "fsdp", scatter_dimension=0, tiled=True
        ).astype(jnp.float32),
        lax.psum_scatter(
            grad_sums[4].astype(jnp.bfloat16), "fsdp", scatter_dimension=0, tiled=True
        ).astype(jnp.float32),
        lax.psum_scatter(
            grad_sums[5].astype(jnp.bfloat16), "fsdp", scatter_dimension=0, tiled=True
        ).astype(jnp.float32),
        lax.psum_scatter(
            grad_sums[6].astype(jnp.bfloat16), "fsdp", scatter_dimension=0, tiled=True
        ).astype(jnp.float32),
        lax.psum_scatter(
            grad_sums[7].astype(jnp.bfloat16), "fsdp", scatter_dimension=0, tiled=True
        ).astype(jnp.float32),
        lax.psum_scatter(
            grad_sums[8].astype(jnp.bfloat16), "fsdp", scatter_dimension=0, tiled=True
        ).astype(jnp.float32),
        lax.psum_scatter(
            grad_sums[9].astype(jnp.bfloat16), "fsdp", scatter_dimension=0, tiled=True
        ).astype(jnp.float32),
        lax.psum_scatter(
            grad_sums[10].astype(jnp.bfloat16), "fsdp", scatter_dimension=0, tiled=True
        ).astype(jnp.float32),
    )
    summed = (
        lax.psum(owned[0].astype(jnp.bfloat16), "ctx").astype(jnp.float32),
        lax.psum(owned[1].astype(jnp.bfloat16), "ctx").astype(jnp.float32),
        lax.psum(owned[2].astype(jnp.bfloat16), "ctx").astype(jnp.float32),
        lax.psum(owned[3].astype(jnp.bfloat16), "ctx").astype(jnp.float32),
        lax.psum(owned[4].astype(jnp.bfloat16), "ctx").astype(jnp.float32),
        lax.psum(owned[5].astype(jnp.bfloat16), "ctx").astype(jnp.float32),
        lax.psum(owned[6].astype(jnp.bfloat16), "ctx").astype(jnp.float32),
        lax.psum(owned[7].astype(jnp.bfloat16), "ctx").astype(jnp.float32),
        lax.psum(owned[8].astype(jnp.bfloat16), "ctx").astype(jnp.float32),
        lax.psum(owned[9].astype(jnp.bfloat16), "ctx").astype(jnp.float32),
        lax.psum(owned[10].astype(jnp.bfloat16), "ctx").astype(jnp.float32),
    )
    return (
        jnp.stack(outputs_list)[:, None],
        jnp.stack(input_grads)[:, None],
        summed[0],
        summed[1],
        summed[2],
        summed[3],
        summed[4],
        summed[5],
        summed[6],
        summed[7],
        summed[8],
        summed[9],
        summed[10],
    )


AXES = ("z", "x", "y", "c")
SIZES = (4, 2, 2, 2)


MESH = pl.DeviceIdType.MESH


def send(src, dst, sems, recv_sems, index, peer):
    copy = pltpu.make_async_remote_copy(
        src_ref=src,
        dst_ref=dst,
        send_sem=sems.at[index],
        recv_sem=recv_sems.at[index],
        device_id=peer,
        device_id_type=MESH,
    )
    copy.start()
    return copy


def greet(peers, extra, extra_on):
    barrier = pltpu.get_barrier_semaphore()
    for peer in peers:
        pl.semaphore_signal(barrier, inc=1, device_id=peer, device_id_type=MESH)

    @pl.when(extra_on)
    def _():
        for peer in extra:
            pl.semaphore_signal(barrier, inc=1, device_id=peer, device_id_type=MESH)

    pl.semaphore_wait(barrier, len(peers) + jnp.where(extra_on, len(extra), 0))


HEAD_CHUNK = 128
SAFE_SCORE = 80.0


def head_kernel(
    x_in_ref, dy_in_ref, docs_in_ref, order_ref, g1_ref, b1_ref, g2_ref, b2_ref, ob_ref, db_ref, ub_in_ref, wq_ref, wo_ref, wu_ref, wd_ref,
    qt_ref, k_ref, kt_ref, v_ref, vt_ref, ut_ref, own_ref, wo_all, wu_all, wd_all, dy_ref,
    wh_ref, vec_ref, ub_ref, start_ref, tab_ref,
    qt_buf, k_buf, kt_buf, v_buf, vt_buf, ut_buf, rows, docs, docs_true, norms, vec_in_ref, vec_all, wo_tmp, wu_tmp, wd_tmp,
    z_s, z_r, x_s, x_r, c_s, c_r, f_s, f_r, docs_s, docs_r, vec_s, vec_r, wh_s, wh_r, wh_l,
    y_s, y_r, n_s, n_r, o_s, o_r, load_sem, put_sem, self_sem, d_s, d_r, d_self, out_sem,
):
    z, x, y, c = (lax.axis_index(name) for name in AXES)
    odd, upper = lax.rem(z, 2), lax.div(z, 2)
    width = x_in_ref.shape[-1]
    chunks = rows.shape[1] // HEAD_CHUNK
    per_turn = chunks // 2
    by_core, by_x, by_y, by_yc = {"c": 1 - c}, {"x": 1 - x}, {"y": 1 - y}, {"y": 1 - y, "c": 1 - c}
    home = [{"z": 2 * c + upper, "c": odd}, {"z": 2 * c + 1 - upper, "c": odd}]
    target = [{"z": 2 * odd + c, "c": upper}, {"z": 2 * (1 - odd) + c, "c": upper}]
    block = [odd, 1 - odd]
    stay = (c == upper) & (odd == c)
    leave = jnp.logical_not(stay)
    for i, ref in enumerate((g1_ref, b1_ref, g2_ref, b2_ref, ob_ref, db_ref, ub_in_ref)):
        vec_in_ref[i : i + ref.shape[0]] = ref[...]
    greet([by_core, by_x, by_y, by_yc, home[1], target[1]], [home[0], target[0]], leave)

    def order_of(i):
        return i % 2 * per_turn + i // 2

    def piece(i):
        turn, row = order_of(i) // per_turn, (order_of(i) % per_turn) * HEAD_CHUNK
        return (
            x_in_ref.at[block[turn], 0, pl.ds(row, HEAD_CHUNK)],
            rows.at[0, pl.ds(order_of(i) * HEAD_CHUNK, HEAD_CHUNK)],
        )

    for turn in range(2):
        src, dst = docs_in_ref.at[block[turn]], docs.at[0, turn]

        def start_docs():
            send(src, dst, docs_s, docs_r, turn, target[turn])

        if turn == 0:
            pl.when(stay)(lambda: pltpu.make_async_copy(src, dst, self_sem.at[per_turn]).start())
            pl.when(leave)(start_docs)
        else:
            start_docs()
    for i in range(chunks):
        src, dst = piece(i)
        if i % 2 == 0:
            pl.when(stay)(lambda: pltpu.make_async_copy(src, dst, self_sem.at[i // 2]).start())
            pl.when(leave)(lambda: send(src, dst, z_s, z_r, i, target[0]) and None)
        else:
            send(src, dst, z_s, z_r, i, target[1])

    def piece_dy(i):
        part = pl.ds(i * HEAD_CHUNK, HEAD_CHUNK)
        return dy_in_ref.at[odd, 0, part], dy_ref.at[part]

    def send_dy(i):
        src, dst = piece_dy(i)
        pl.when(stay)(lambda: pltpu.make_async_copy(src, dst, d_self.at[i]).start())
        pl.when(leave)(lambda: send(src, dst, d_s, d_r, i, target[0]) and None)

    def land_dy(i):
        src, dst = piece_dy(i)
        pl.when(stay)(lambda: pltpu.make_async_copy(src, dst, d_self.at[i]).wait())
        pl.when(leave)(
            lambda: pltpu.make_async_remote_copy(
                src_ref=src, dst_ref=dst, send_sem=d_s.at[i], recv_sem=d_r.at[i],
                device_id=target[0], device_id_type=MESH,
            ).wait()
        )

    def landed(src, dst, sems, recv_sems, index, turn, self_index):
        def remote():
            pltpu.make_async_remote_copy(
                src_ref=src, dst_ref=dst, send_sem=sems.at[index], recv_sem=recv_sems.at[index],
                device_id=target[turn], device_id_type=MESH,
            ).wait()

        if turn == 0:
            pl.when(stay)(lambda: pltpu.make_async_copy(src, dst, self_sem.at[self_index]).wait())
            pl.when(leave)(remote)
        else:
            remote()

    mine = 2 * y + c
    vec_copy = [
        send(vec_in_ref, vec_all.at[mine], vec_s, vec_r, i, peer)
        for i, peer in enumerate((by_core, by_y, by_yc))
    ]
    vec_all[mine] = vec_in_ref[...]
    wh_copy = []
    shard = wq_ref.shape[0]
    own_rows = pl.ds(pl.multiple_of(mine * shard, shard), shard)
    for part in range(3):
        to = wh_ref.at[own_rows, pl.ds(part * PAIR, PAIR)]

        def columns(core):
            return wq_ref.at[:, pl.ds(pl.multiple_of(part * width + (2 * x + core) * PAIR, PAIR), PAIR)]

        for i, (peer, core) in enumerate(((by_core, 1 - c), (by_y, c), (by_yc, 1 - c))):
            wh_copy.append(send(columns(core), to, wh_s, wh_r, 3 * part + i, peer))
        copy = pltpu.make_async_copy(columns(c), to, wh_l.at[part])
        copy.start()
        wh_copy.append(copy)

    up_rows, down_rows = wu_ref.shape[0] // 4, wd_ref.shape[0] // 4
    parts = [(wo_ref, wo_all, wo_ref.shape[0], 0)]
    parts += [(wu_ref, wu_all, up_rows, i * up_rows) for i in range(4)]
    parts += [(wd_ref, wd_all, down_rows, i * down_rows) for i in range(4)]

    def at_owner(full, src, size, offset, owner):
        return full.at[pl.ds(pl.multiple_of(owner * src.shape[0] + offset, 32), size)]

    other = 2 * (1 - y) + c
    y_copy = []
    for i, (src, full, size, offset) in enumerate(parts):
        y_copy.append(
            send(src.at[pl.ds(offset, size)], at_owner(full, src, size, offset, mine), y_s, y_r, i, by_y)
        )
    n_copy, load_copy, put_copy = [], [], []
    for i, (src, full, tmp) in enumerate(((wo_ref, wo_all, wo_tmp), (wu_ref, wu_all, wu_tmp), (wd_ref, wd_all, wd_tmp))):
        n_copy.append(send(src, at_owner(full, src, src.shape[0], 0, mine), n_s, n_r, i, by_core))
        load_copy.append(pltpu.make_async_copy(src, tmp, load_sem.at[i]))
        load_copy[-1].start()

    def put(i):
        src, full, tmp = ((wo_ref, wo_all, wo_tmp), (wu_ref, wu_all, wu_tmp), (wd_ref, wd_all, wd_tmp))[i]
        load_copy[i].wait()
        put_copy.append(pltpu.make_async_copy(tmp, at_owner(full, src, src.shape[0], 0, mine), put_sem.at[i]))
        put_copy[-1].start()

    o_copy = []

    def forward(i):
        src, full, size, offset = parts[i]
        y_copy[i].wait()
        held = at_owner(full, src, size, offset, other)
        o_copy.append(send(held, held, o_s, o_r, i, by_core))

    blocks = order_ref.shape[0]
    lane = lax.broadcasted_iota(jnp.int32, (1, 128), 1)
    slots = jnp.zeros((1, 128), jnp.int32)
    for t in range(blocks):
        dc, dx, turn, half = t // 8, t // 4 % 2, t // 2 % 2, t % 2
        core, side = (1 - c if dc else c), (1 - x if dx else x)
        stored = 2 * (2 * (2 * core + (1 - upper if turn else upper)) + side) + half
        slots = jnp.where(lane == order_ref[stored], t, slots)

    docs_copy = {}

    def finish_docs():
        docs_copy["c"].wait()
        docs_copy["f"].wait()
        for g in range(4):
            core, side = (1 - c if g // 2 else c), (1 - x if g % 2 else x)
            for turn in range(2):
                docs_true[2 * (2 * core + (1 - upper if turn else upper)) + side] = docs[g, turn]
        numbers = docs_true[...]
        first = jnp.zeros_like(numbers)
        for d in range(1, blocks):
            before = jnp.sum((numbers < d).astype(jnp.int32), axis=(0, 1, 2), keepdims=True)
            first = jnp.where(numbers == d, before, first)
        docs_true[...] = first
        low = jnp.zeros((1, 128), jnp.int32)
        for b in range(blocks):
            line = docs_true[b // 2]
            at = 2 * (b % 2)
            line = jnp.concatenate([line[at : at + 1], line[at + 1 : at + 2]], axis=1)
            start_ref[b] = line
            low = jnp.where(lane == b, line[:, :1] // BLK, low)
        high = jnp.zeros((1, 128), jnp.int32) - 1
        for b in range(blocks):
            high = high + (low[:, b : b + 1] <= lane).astype(jnp.int32)
        tab_ref[...] = jnp.concatenate([low, high, slots, jnp.zeros((5, 128), jnp.int32)], axis=0)

    def docs_first():
        for turn in range(2):
            landed(docs_in_ref.at[block[turn]], docs.at[0, turn], docs_s, docs_r, turn, turn, per_turn)
        docs_copy["x"] = send(docs.at[0], docs.at[1], docs_s, docs_r, 2, by_x)
        docs_copy["c"] = send(docs.at[0], docs.at[2], docs_s, docs_r, 3, by_core)


    def vectors_and_weight():
        for copy in vec_copy:
            copy.wait()
        vec_width = vec_in_ref.shape[1]
        for j in range(4):
            for i in range(6):
                vec_ref[i : i + 1, j * vec_width : (j + 1) * vec_width] = vec_all[j, i : i + 1].astype(f32)
            for i in range(4):
                at = (4 * j + i) * vec_width
                ub_ref[:, at : at + vec_width] = vec_all[j, 6 + i : 7 + i].astype(f32)
        vec_ref[6:8] = jnp.zeros((2, width), f32)
        for copy in wh_copy:
            copy.wait()


    def docs_second():
        docs_copy["x"].wait()
        docs_copy["f"] = send(docs.at[1], docs.at[3], docs_s, docs_r, 4, by_core)


    x_copy, c_copy, f_copy = [], [], []

    def relay(i):
        src, dst = piece(i)
        landed(src, dst, z_s, z_r, i, i % 2, i // 2)
        part = pl.ds(order_of(i) * HEAD_CHUNK, HEAD_CHUNK)
        x_copy.append(send(rows.at[0, part], rows.at[1, part], x_s, x_r, i, by_x))
        c_copy.append(send(rows.at[0, part], rows.at[2, part], c_s, c_r, i, by_core))

    def relay_far(i):
        x_copy[i].wait()
        part = pl.ds(order_of(i) * HEAD_CHUNK, HEAD_CHUNK)
        f_copy.append(send(rows.at[1, part], rows.at[3, part], f_s, f_r, i, by_core))

    streams = (
        (qt_buf, qt_ref, 1), (k_buf, k_ref, 0), (kt_buf, kt_ref, 1), (v_buf, v_ref, 0), (vt_buf, vt_ref, 1),
        (ut_buf, ut_ref, 1),
    )

    def compute(g, i):
        count = rows.shape[1]
        chunk = order_of(i)
        unit, _ = norm_parts(rows[g, chunk * HEAD_CHUNK : (chunk + 1) * HEAD_CHUNK].astype(f32))
        at = pl.ds(g * count + chunk * HEAD_CHUNK, HEAD_CHUNK)
        ut_buf[:, at] = unit.astype(bf16).T
        low = (unit * vec_ref[0:1] + vec_ref[1:2]).astype(bf16)
        qkv = jnp.dot(low, wh_ref[...], preferred_element_type=f32)
        qt = (qkv[:, :PAIR] * (SCORE_SCALE * LOG2E)).astype(bf16).T
        qt_buf[:, at] = qt
        k = qkv[:, PAIR : 2 * PAIR].astype(bf16)
        v = qkv[:, 2 * PAIR :].astype(bf16)
        k_buf[at] = k
        v_buf[at] = v
        kt = k.T
        kt_buf[:, at] = kt
        vt_buf[:, at] = v.T
        found = []
        for block_ in (qt, kt):
            squares = block_.astype(f32) * block_.astype(f32)
            found += [jnp.sum(squares[head * HD : (head + 1) * HD], axis=0, keepdims=True) for head in range(2)]
        found = jnp.concatenate(found, axis=0)
        norms[...] = found if g == 0 and i == 0 else jnp.maximum(norms[...], found)
        for index, (source, out, columns) in enumerate(streams):
            if columns:
                source, out = source.at[:, at], out.at[:, at]
            else:
                source, out = source.at[at], out.at[at]
            pltpu.make_async_copy(source, out, out_sem.at[index]).start()

    docs_first()
    for i in range(chunks + 2):
        if i < chunks:
            if i < per_turn:
                send_dy(i)
            relay(i)
        if i == 0:
            vectors_and_weight()
            docs_second()
        if 1 <= i <= chunks:
            relay_far(i - 1)
            compute(0, i - 1)
            compute(1, i - 1)
            c_copy[i - 1].wait()
            compute(2, i - 1)
        if i >= 2:
            f_copy[i - 2].wait()
            compute(3, i - 2)
        if i == 1:
            finish_docs()
        if 2 <= i < 5:
            put(i - 2)
        if i >= 3 and i - 3 < len(parts):
            forward(i - 3)
        if i == chunks - 1:
            own_copy = pltpu.make_async_copy(rows.at[0], own_ref, out_sem.at[len(streams)])
            own_copy.start()
    largest = jnp.max(norms[...], axis=1, keepdims=True)
    bound = jnp.maximum(largest[0:1] * largest[2:3], largest[1:2] * largest[3:4])
    tab_ref[3:4] = jnp.broadcast_to((bound <= SAFE_SCORE * SAFE_SCORE).astype(jnp.int32), (1, 128))
    for i in range(chunks - 1, len(parts)):
        forward(i)
    for index, (source, out, _) in enumerate(streams):
        pltpu.make_async_copy(source, out, out_sem.at[index]).wait()
    own_copy.wait()
    for copy in n_copy + put_copy + o_copy:
        copy.wait()
    for i in range(per_turn):
        land_dy(i)


def head(x_in, dy_in, docs_in, order, vectors, w_qkv, w_out, w_up, w_down):
    width = x_in.shape[-1]
    count = 2 * x_in.shape[2]
    total = 4 * count
    shard = w_qkv.shape[0]
    chunks = count // HEAD_CHUNK
    blocks = order.shape[0]
    vmem, any_ = pl.BlockSpec(memory_space=pltpu.VMEM), pl.BlockSpec(memory_space=pl.ANY)
    smem = pl.BlockSpec(memory_space=pltpu.SMEM)
    dma, buf, shape = pltpu.SemaphoreType.DMA, pltpu.VMEM, jax.ShapeDtypeStruct
    return pl.pallas_call(
        head_kernel,
        in_specs=[any_, any_, vmem, smem] + [vmem] * 7 + [any_] * 4,
        out_specs=[any_] * 11 + [vmem] * 5,
        out_shape=[
            shape((PAIR, total), bf16),
            shape((total, PAIR), bf16),
            shape((PAIR, total), bf16),
            shape((total, PAIR), bf16),
            shape((PAIR, total), bf16),
            shape((width, total), bf16),
            shape((count, width), bf16),
            shape((4 * w_out.shape[0], w_out.shape[1]), bf16),
            shape((4 * w_up.shape[0], w_up.shape[1]), bf16),
            shape((4 * w_down.shape[0], w_down.shape[1]), bf16),
            shape((count // 2, width), bf16),
            shape((width, 3 * PAIR), bf16),
            shape((8, width), f32),
            shape((1, 4 * w_down.shape[0]), f32),
            shape((blocks, 1, BLK), jnp.int32),
            shape((8, 128), jnp.int32),
        ],
        scratch_shapes=[
            buf((PAIR, total), bf16),
            buf((total, PAIR), bf16),
            buf((PAIR, total), bf16),
            buf((total, PAIR), bf16),
            buf((PAIR, total), bf16),
            buf((width, total), bf16),
            buf((4, count, width), bf16),
            buf((4, 2) + docs_in.shape[1:], jnp.int32),
            buf((blocks // 2,) + docs_in.shape[1:], jnp.int32),
            buf((4, HEAD_CHUNK), f32),
            buf((16, shard), bf16),
            buf((4, 16, shard), bf16),
            buf(w_out.shape, bf16),
            buf(w_up.shape, bf16),
            buf(w_down.shape, bf16),
        ]
        + [dma((chunks,))] * 8
        + [dma((5,)), dma((5,)), dma((3,)), dma((3,)), dma((9,)), dma((9,)), dma((3,))]
        + [dma((9,)), dma((9,)), dma((3,)), dma((3,)), dma((9,)), dma((9,)), dma((3,)), dma((3,))]
        + [dma((chunks // 2 + 1,)), dma((chunks // 2,))] + [dma((chunks // 2,))] * 2 + [dma((7,))],
        compiler_params=pltpu.CompilerParams(
            collective_id=1, has_side_effects=True, vmem_limit_bytes=56 * 1024 * 1024
        ),
        name="head",
    )(x_in, dy_in, docs_in, order, *[v.reshape(-1, shard) for v in vectors], w_qkv, w_out, w_up, w_down)
FF_TILE = 512
PIECES = 3
feed_steps = 4


def feed_kernel(
    o_ref, x_ref, dy_near_ref, dy_in_ref, wo_hbm, wu_hbm, wd_hbm, vec_ref, ub_ref,
    do_ref, y_home, dmid_ref, keep_ref, to_y_ref, to_x_ref, to_xy_ref, gvec_ref, gub_ref,
    attn_all, gd_ref, gu_ref, go_ref, attn_in, do_out, y_out, grad_ref, grad_in,
    wo_ref, wu_ref, wd_ref, dy_ref, dy_far, w_sem, a_s, a_r, a_l, d_s, d_r, d_l, y_s, y_r, y_l, g_s, g_r, c_s, c_r,
):
    step = pl.program_id(0)
    steps = pl.num_programs(0)
    groups = attn_in.shape[0]
    tile = x_ref.shape[0]
    z, x, y, c = (lax.axis_index(name) for name in AXES)
    odd, upper = lax.rem(z, 2), lax.div(z, 2)
    mates = [None, {"x": 1 - x}, {"c": 1 - c}, {"x": 1 - x, "c": 1 - c}]
    pair_of = [2 * x + c, 2 * (1 - x) + c, 2 * x + 1 - c, 2 * (1 - x) + 1 - c]
    home = [{"z": 2 * c + upper, "c": odd}, {"z": 2 * c + 1 - upper, "c": odd}]
    origin = [{"z": 2 * odd + c, "c": upper}, {"z": 2 * (1 - odd) + c, "c": upper}]
    stay = (c == upper) & (odd == c)
    leave = jnp.logical_not(stay)
    half = feed_steps // 2

    def attn_copy(g, i):
        part = pl.ds(i * tile, tile)
        return pltpu.make_async_remote_copy(
            src_ref=o_ref.at[g, part], dst_ref=attn_in.at[g, part],
            send_sem=a_s.at[g - 1, i], recv_sem=a_r.at[g - 1, i], device_id=mates[g], device_id_type=MESH,
        )

    def attn_own(i):
        part = pl.ds(i * tile, tile)
        return pltpu.make_async_copy(o_ref.at[0, part], attn_in.at[0, part], a_l.at[i])

    def do_copy(g, i):
        return pltpu.make_async_remote_copy(
            src_ref=do_out.at[i, g], dst_ref=do_ref.at[g, pl.ds(i * tile, tile)],
            send_sem=d_s.at[g - 1, i], recv_sem=d_r.at[g - 1, i], device_id=mates[g], device_id_type=MESH,
        )

    def do_own(i):
        return pltpu.make_async_copy(do_out.at[i, 0], do_ref.at[0, pl.ds(i * tile, tile)], d_l.at[i])

    def y_rows(i, block):
        return y_home.at[block, pl.ds(lax.rem(i, half) * tile, tile)]

    def y_copy(i, turn, block):
        return pltpu.make_async_remote_copy(
            src_ref=y_out.at[i], dst_ref=y_rows(i, block),
            send_sem=y_s.at[i], recv_sem=y_r.at[i], device_id=home[turn], device_id_type=MESH,
        )

    def y_own(i, block):
        return pltpu.make_async_copy(y_out.at[i], y_rows(i, block), y_l.at[i])

    def grad_copy(i):
        return pltpu.make_async_remote_copy(
            src_ref=grad_ref.at[2 * i + 1 - c], dst_ref=grad_in.at[i],
            send_sem=g_s.at[i], recv_sem=g_r.at[i], device_id=mates[2], device_id_type=MESH,
        )

    def dy_copy(i):
        part = pl.ds(i * tile, tile)
        return pltpu.make_async_remote_copy(
            src_ref=dy_in_ref.at[1 - odd, 0, part], dst_ref=dy_far.at[part],
            send_sem=c_s.at[i], recv_sem=c_r.at[i], device_id=origin[1], device_id_type=MESH,
        )

    w_loads = [
        pltpu.make_async_copy(src, dst, w_sem.at[i])
        for i, (src, dst) in enumerate(((wo_hbm, wo_ref), (wu_hbm, wu_ref), (wd_hbm, wd_ref)))
    ]

    @pl.when(step == 0)
    def _():
        for copy in w_loads:
            copy.start()
        greet(mates[1:] + [home[1], origin[1]], [home[0], origin[0]], leave)
        for i in range(feed_steps):
            for g in (1, 3, 2):
                attn_copy(g, i).start()
            attn_own(i).start()
        for i in range(half):
            dy_copy(i).start()

    @pl.when(step == 0)
    def _():
        for ref in (gd_ref, gu_ref, go_ref, gvec_ref, gub_ref):
            ref[...] = jnp.zeros_like(ref)

    @pl.when(step < half)
    def _():
        dy_ref[...] = dy_near_ref[...]

    @pl.when(step >= half)
    def _():
        dy_copy(step - half).wait()
        dy_ref[...] = dy_far[pl.ds(pl.multiple_of((step - half) * tile, tile), tile)]

    @pl.when(step == 0)
    def _():
        for copy in w_loads:
            copy.wait()

    attn_own(step).wait()
    for g in range(1, groups):
        attn_copy(g, step).wait()
    for g in range(groups):
        attn_all[:, pl.ds(pl.multiple_of(pair_of[g] * PAIR, PAIR), PAIR)] = attn_in[
            g, pl.ds(pl.multiple_of(step * tile, tile), tile)
        ]
    attn = attn_all[...]
    gain, bias, out_bias, down_bias = (vec_ref[i : i + 1, :] for i in range(2, 6))
    middle = (
        x_ref[...].astype(f32) + jnp.dot(attn, wo_ref[...], preferred_element_type=f32) + out_bias
    )
    unit, inv = norm_parts(middle)
    low = (unit * gain + bias).astype(bf16)
    dy = dy_ref[...]
    dy32 = dy.astype(f32)
    total = middle + down_bias
    d_low = jnp.zeros_like(middle)
    width = wu_ref.shape[1]
    for j in range(0, width, FF_TILE):
        part = pl.ds(j, FF_TILE)
        up = wu_ref[:, part]
        down = wd_ref[part, :]
        hidden = jnp.dot(low, up, preferred_element_type=f32) + ub_ref[:, part]
        cdf = 0.5 * (1.0 + lax.erf(hidden * (1.0 / math.sqrt(2.0))))
        active = (hidden * cdf).astype(bf16)
        slope = cdf + hidden * (jnp.exp2(hidden * hidden * (-0.5 * LOG2E)) * (1.0 / math.sqrt(2.0 * math.pi)))
        total = total + jnp.dot(active, down, preferred_element_type=f32)
        d_hidden = contract(dy, down, 1, 1) * slope
        d_hidden_low = d_hidden.astype(bf16)
        gub_ref[:, part] += jnp.sum(d_hidden, axis=0, keepdims=True)
        d_low = d_low + contract(d_hidden_low, up, 1, 1)
        gd_ref[part, :] += contract(active, dy, 0, 0)
        gu_ref[:, part] += contract(low, d_hidden_low, 0, 0)
    y_out[step] = total.astype(bf16)

    @pl.when((step < half) & stay)
    def _():
        y_own(step, upper).start()

    @pl.when((step < half) & leave)
    def _():
        y_copy(step, 0, upper).start()

    @pl.when(step >= half)
    def _():
        y_copy(step, 1, upper).start()

    scaled = d_low * gain
    d_middle = dy32 + inv * (
        scaled
        - jnp.mean(scaled, axis=-1, keepdims=True)
        - unit * jnp.mean(scaled * unit, axis=-1, keepdims=True)
    )
    dmid_ref[...] = d_middle
    branch = d_middle.astype(bf16)
    go_ref[...] += contract(attn, branch, 0, 0)
    gvec_ref[0:1, :] += jnp.sum(d_middle, axis=0, keepdims=True)
    gvec_ref[1:2, :] += jnp.sum(d_low * unit, axis=0, keepdims=True)
    gvec_ref[2:3, :] += jnp.sum(d_low, axis=0, keepdims=True)
    gvec_ref[3:4, :] += jnp.sum(dy32, axis=0, keepdims=True)
    attn_all[...] = contract(branch, wo_ref[...], 1, 1).astype(bf16)
    for g in (1, 3, 2, 0):
        do_out[step, g] = attn_all[:, pl.ds(pl.multiple_of(pair_of[g] * PAIR, PAIR), PAIR)]
        if g:
            do_copy(g, step).start()
        else:
            do_own(step).start()

    @pl.when(step == steps - 1)
    def _():
        shards = grad_ref.shape[0]
        d_model = x_ref.shape[1]
        down_rows, up_rows = gd_ref.shape[0] // shards, d_model // shards
        for j in range(shards):
            grad_ref[j, :down_rows] = gd_ref[j * down_rows : (j + 1) * down_rows].astype(bf16)
            rows = slice(j * up_rows, (j + 1) * up_rows)
            at = down_rows
            for t in range(0, width, d_model):
                grad_ref[j, at : at + up_rows] = gu_ref[rows, t : t + d_model].astype(bf16)
                at += up_rows
            grad_ref[j, at : at + up_rows] = go_ref[rows].astype(bf16)
        for j in range(2):
            grad_copy(j).start()
        for j in range(feed_steps):
            do_own(j).wait()
            for g in range(1, groups):
                do_copy(g, j).wait()
            if j < half:
                @pl.when(stay)
                def _():
                    y_own(j, odd).wait()

                @pl.when(leave)
                def _():
                    y_copy(j, 0, odd).wait()
            else:
                y_copy(j, 1, 1 - odd).wait()
        sixth = keep_ref.shape[1]
        for j in range(2):
            grad_copy(j).wait()
        for dy_, dx_, ref in ((0, 0, keep_ref), (1, 0, to_y_ref), (0, 1, to_x_ref), (1, 1, to_xy_ref)):
            row = 1 - y if dy_ else y
            side = 1 - x if dx_ else x
            for p in range(PIECES):
                part = pl.ds(pl.multiple_of((2 * p + side) * sixth, 16), sixth)
                ref[p] = (
                    grad_ref[2 * row + c, part].astype(f32) + grad_in[row, part].astype(f32)
                ).astype(bf16)


def feed(o, x, dy_near, dy_in, w_out, w_up, w_down, vecs, up_bias, shards):
    groups, count, _ = o.shape
    width = x.shape[1]
    flat = (w_out.size + w_up.size + w_down.size) // shards // width
    tile = count // feed_steps
    piece = (PIECES, flat // PIECES // 2, width)
    rows = pl.BlockSpec((tile, width), lambda i: (i, 0))
    any_ = pl.BlockSpec(memory_space=pl.ANY)
    dma, buf, shape = pltpu.SemaphoreType.DMA, pltpu.VMEM, jax.ShapeDtypeStruct
    return pl.pallas_call(
        feed_kernel,
        grid=(feed_steps,),
        in_specs=[
            any_, rows, pl.BlockSpec((tile, width), lambda i: (jnp.minimum(i, feed_steps // 2 - 1), 0)), any_, any_, any_, any_,
            whole(vecs.shape), whole(up_bias.shape),
        ],
        out_specs=[any_, any_, rows] + [whole(piece)] * 4 + [whole(vecs.shape), whole(up_bias.shape)],
        out_shape=[
            shape((groups, count, PAIR), bf16),
            shape((2, count // 2, width), bf16),
            shape((count, width), f32),
            shape(piece, bf16),
            shape(piece, bf16),
            shape(piece, bf16),
            shape(piece, bf16),
            shape(vecs.shape, f32),
            shape(up_bias.shape, f32),
        ],
        scratch_shapes=[
            buf((tile, width), bf16),
            buf(w_down.shape, f32),
            buf(w_up.shape, f32),
            buf(w_out.shape, f32),
            buf((groups, count, PAIR), bf16),
            buf((feed_steps, groups, tile, PAIR), bf16),
            buf((feed_steps, tile, width), bf16),
            buf((shards, flat, width), bf16),
            buf((2, flat, width), bf16),
            buf(w_out.shape, bf16),
            buf(w_up.shape, bf16),
            buf(w_down.shape, bf16),
            buf((tile, width), bf16),
            buf((count // 2, width), bf16),
            dma((3,)),
            dma((3, feed_steps)),
            dma((3, feed_steps)),
            dma((feed_steps,)),
            dma((3, feed_steps)),
            dma((3, feed_steps)),
            dma((feed_steps,)),
            dma((feed_steps,)),
            dma((feed_steps,)),
            dma((feed_steps,)),
            dma((2,)),
            dma((2,)),
            dma((feed_steps // 2,)),
            dma((feed_steps // 2,)),
        ],
        compiler_params=pltpu.CompilerParams(
            collective_id=3, has_side_effects=True, vmem_limit_bytes=60 * 1024 * 1024
        ),
        name="feed",
    )(o, x, dy_near, dy_in, w_out, w_up, w_down, vecs, up_bias)


TAIL_CHUNK = 128


def tail_kernel(
    d_qkv_hbm, ut_hbm, x_hbm, dmid_hbm, keep_hbm, from_y_hbm, from_x_hbm, from_xy_hbm, w_ref, vec_ref,
    gvecs_ref, gub_ref,
    home_buf, gfull, wall, sum_ref,
    keep_ref, from_y_ref, from_x_ref, from_xy_ref, d_qkv, ut_ref, total, sums, gw_ref, core_out, x_ref, dmid_ref, core_buf, own_dh, x_out, x_buf, dx_out,
    gsum, gz1s, gz1r, gz2s, gz2r,
    wy, ws, wz1s, wz1r, wz2s, wz2r, wfull,
    small_ref, small_out, small_in,
    load_sem, self_sem, core_s, core_r, x_s, x_r, home_s, home_r, g_s, g_r, w_s, w_r, s_s, s_r, in_sem,
):
    z, x, y, c = (lax.axis_index(name) for name in AXES)
    odd, upper = lax.rem(z, 2), lax.div(z, 2)
    width = x_ref.shape[1]
    chunks = x_ref.shape[0] // TAIL_CHUNK
    per_turn = chunks // 2
    by_core, by_x, by_y, by_xc = {"c": 1 - c}, {"x": 1 - x}, {"y": 1 - y}, {"x": 1 - x, "c": 1 - c}
    by_z1, by_z2 = {"z": z + 1 - 2 * odd}, {"z": z + 2 - 4 * upper}
    home = [{"z": 2 * c + upper, "c": odd}, {"z": 2 * c + 1 - upper, "c": odd}]
    origin = [{"z": 2 * odd + c, "c": upper}, {"z": 2 * (1 - odd) + c, "c": upper}]
    stay = (c == upper) & (odd == c)
    loads = []
    for i in range(chunks):
        part = pl.ds(i * TAIL_CHUNK, TAIL_CHUNK)
        loads.append(pltpu.make_async_copy(d_qkv_hbm.at[:, part], d_qkv.at[:, part], load_sem.at[i]))
    inputs = [
        pltpu.make_async_copy(src, dst, in_sem.at[i])
        for i, (src, dst) in enumerate(((ut_hbm, ut_ref), (x_hbm, x_ref), (dmid_hbm, dmid_ref)))
    ]
    g_loads = [
        pltpu.make_async_copy(src, dst, in_sem.at[3 + i])
        for i, (src, dst) in enumerate((
            (keep_hbm, keep_ref), (from_y_hbm, from_y_ref), (from_x_hbm, from_x_ref), (from_xy_hbm, from_xy_ref)
        ))
    ]
    for copy in loads[:2] + g_loads + loads[2:] + inputs:
        copy.start()
    small_ref[...] = jnp.zeros_like(small_ref)
    small_ref[2:4] = gvecs_ref[1:3]
    small_ref[4:5] = gvecs_ref[0:1]
    small_ref[5:6] = gvecs_ref[3:4]
    for i in range(4):
        small_ref[6 + i : 7 + i] = gub_ref[:, i * width : (i + 1) * width]
    greet(
        [by_core, by_x, by_y, by_xc, by_z1, by_z2, home[1], origin[1]],
        [home[0], origin[0]],
        jnp.logical_not(stay),
    )
    small_peers = [by_core, by_y, by_z1, by_z2, by_x]
    to_core, w_copy, s_copy = [], {}, []

    def share(i):
        part = pl.ds(i * TAIL_CHUNK, TAIL_CHUNK)
        loads[i].wait()
        for g in (3, 2, 1, 0):
            value = contract(d_qkv[g, part], w_ref[...], 1, 1)
            if g >= 2:
                core_out[g - 2, part] = value.astype(bf16)
            else:
                own_dh[g, part] = value
            if g == 2:
                to_core.append(
                    send(core_out.at[:, part], core_buf.at[:, part], core_s, core_r, i, by_core)
                )

    def weight(g):
        if g == 0:
            inputs[0].wait()
        rows = d_qkv[g]
        part = jnp.dot(ut_ref[:, g * rows.shape[0] : (g + 1) * rows.shape[0]], rows, preferred_element_type=f32)
        line = jnp.sum(rows.astype(f32), axis=0, keepdims=True)
        total[...] = part if g == 0 else total[...] + part
        sums[...] = line if g == 0 else sums[...] + line

    def weight_close():
        shard = gw_ref.shape[1]
        for j in range(gw_ref.shape[0]):
            part = pl.ds(j * shard, shard)
            gain, bias = (jnp.broadcast_to(ref[:, part], (shard, shard)).T[:, :1] for ref in (vec_ref.at[0:1], vec_ref.at[1:2]))
            gw_ref[j] = (total[part] * gain + bias * sums[...]).astype(bf16)
            w = w_ref[part].astype(f32)
            for i, term in enumerate((w * total[part], w * sums[...])):
                column = jnp.sum(term, axis=1, keepdims=True)
                small_ref[i : i + 1, part] = jnp.broadcast_to(column, (shard, shard)).T[:1]
        s_copy.append(send(small_ref, small_in.at[0], s_s, s_r, 0, small_peers[0]))
        w_copy["y"] = send(gw_ref.at[pl.ds(2 * (1 - y), 2)], wy, w_s, w_r, 0, by_y)

    g_copy = {}

    def g_start(p):
        if p == 0:
            for copy in g_loads:
                copy.wait()
        for half in range(2):
            part = pl.ds(96 * half, 96)
            gsum[p, part] = (
                keep_ref[p, part].astype(f32)
                + from_y_ref[p, part].astype(f32)
                + from_x_ref[p, part].astype(f32)
                + from_xy_ref[p, part].astype(f32)
            )
        gz1s[p] = gsum[p, pl.ds(pl.multiple_of(96 * (1 - odd), 16), 96)].astype(bf16)
        g_copy["z1", p] = send(gz1s.at[p], gz1r.at[p], g_s, g_r, 5 * p, by_z1)

    mine_half = pl.multiple_of(96 * odd, 16)
    mine_quarter = pl.multiple_of(96 * odd + 48 * upper, 16)
    give_quarter = pl.multiple_of(96 * odd + 48 * (1 - upper), 16)

    def g_second(p):
        g_copy["z1", p].wait()
        gsum[p, pl.ds(mine_half, 96)] += gz1r[p].astype(f32)
        gz2s[p] = gsum[p, pl.ds(give_quarter, 48)].astype(bf16)
        g_copy["z2", p] = send(gz2s.at[p], gz2r.at[p], g_s, g_r, 5 * p + 1, by_z2)

    def g_third(p):
        g_copy["z2", p].wait()
        part = pl.ds(mine_quarter, 48)
        gfull[p, x, part] = (gsum[p, part] + gz2r[p].astype(f32)).astype(bf16)
        place_ = gfull.at[p, x, part]
        g_copy["z2b", p] = send(place_, place_, g_s, g_r, 5 * p + 2, by_z2)

    def g_fourth(p):
        g_copy["z2b", p].wait()
        place_ = gfull.at[p, x, pl.ds(mine_half, 96)]
        g_copy["z1b", p] = send(place_, place_, g_s, g_r, 5 * p + 3, by_z1)

    def g_fifth(p):
        g_copy["z1b", p].wait()
        g_copy["x", p] = send(gfull.at[p, x], gfull.at[p, x], g_s, g_r, 5 * p + 4, by_x)

    def w_second():
        w_copy["y"].wait()
        for i in range(2):
            ws[i] = gw_ref[2 * y + i].astype(f32) + wy[i].astype(f32)
        wz1s[...] = ws[1 - odd].astype(bf16)
        w_copy["z1"] = send(wz1s, wz1r, w_s, w_r, 1, by_z1)

    def w_third():
        w_copy["z1"].wait()
        ws[odd] += wz1r[...].astype(f32)
        wz2s[...] = ws[odd, pl.ds(pl.multiple_of(64 * (1 - upper), 64), 64)].astype(bf16)
        w_copy["z2"] = send(wz2s, wz2r, w_s, w_r, 2, by_z2)

    def w_fourth():
        w_copy["z2"].wait()
        part = pl.ds(pl.multiple_of(64 * upper, 64), 64)
        wfull[odd, part] = (ws[odd, part] + wz2r[...].astype(f32)).astype(bf16)
        place_ = wfull.at[odd, part]
        w_copy["z2b"] = send(place_, place_, w_s, w_r, 3, by_z2)

    def w_fifth():
        w_copy["z2b"].wait()
        w_copy["z1b"] = send(wfull.at[odd], wfull.at[odd], w_s, w_r, 4, by_z1)

    def w_sixth():
        w_copy["z1b"].wait()
        mine = 2 * x + c
        w_copy["core"] = send(wfull.at[1 - c], wall.at[mine], w_s, w_r, 5, by_core)
        w_copy["x"] = send(wfull.at[c], wall.at[mine], w_s, w_r, 6, by_x)
        w_copy["xc"] = send(wfull.at[1 - c], wall.at[mine], w_s, w_r, 7, by_xc)

    def s_next(step):
        s_copy[step].wait()
        before = small_ref[...] if step == 0 else small_out[step - 1]
        small_out[step] = before + small_in[step]
        if step + 1 < len(small_peers):
            s_copy.append(
                send(small_out.at[step], small_in.at[step + 1], s_s, s_r, step + 1, small_peers[step + 1])
            )

    x_copy, home_copy = [], []

    def add_core(i):
        part = pl.ds(i * TAIL_CHUNK, TAIL_CHUNK)
        to_core[i].wait()
        x_out[part] = (own_dh[1, part] + core_buf[1, part].astype(f32)).astype(bf16)
        x_copy.append(send(x_out.at[part], x_buf.at[part], x_s, x_r, i, by_x))

    def finish(i):
        part = pl.ds(i * TAIL_CHUNK, TAIL_CHUNK)
        if i == 0:
            for copy in inputs[1:]:
                copy.wait()
        x_copy[i].wait()
        d_low = own_dh[0, part] + core_buf[0, part].astype(f32) + x_buf[part].astype(f32)
        unit, inv = norm_parts(x_ref[part].astype(f32))
        scaled = d_low * vec_ref[0:1]
        dx = dmid_ref[part] + inv * (
            scaled
            - jnp.mean(scaled, axis=-1, keepdims=True)
            - unit * jnp.mean(scaled * unit, axis=-1, keepdims=True)
        )
        dx_out[part] = dx.astype(bf16)
        turn, row = i // per_turn, (i % per_turn) * TAIL_CHUNK
        target = home_buf.at[upper, pl.ds(row, TAIL_CHUNK)]
        if turn == 0:
            @pl.when(stay)
            def _():
                pltpu.make_async_copy(dx_out.at[part], target, self_sem.at[i]).start()

            @pl.when(jnp.logical_not(stay))
            def _():
                send(dx_out.at[part], target, home_s, home_r, i, home[0])
        else:
            send(dx_out.at[part], target, home_s, home_r, i, home[1])

    def arrive(i):
        part = pl.ds(i * TAIL_CHUNK, TAIL_CHUNK)
        turn, row = i // per_turn, (i % per_turn) * TAIL_CHUNK
        block = odd if turn == 0 else 1 - odd
        landed = home_buf.at[block, pl.ds(row, TAIL_CHUNK)]

        def remote():
            copy = pltpu.make_async_remote_copy(
                src_ref=dx_out.at[part], dst_ref=landed, send_sem=home_s.at[i], recv_sem=home_r.at[i],
                device_id=home[turn], device_id_type=MESH,
            )
            copy.wait_send()
            copy.wait_recv()

        if turn == 0:
            @pl.when(stay)
            def _():
                pltpu.make_async_copy(dx_out.at[part], landed, self_sem.at[i]).wait()

            pl.when(jnp.logical_not(stay))(remote)
        else:
            remote()

    share(0)
    share(1)
    add_core(0)
    share(2)
    g_start(0)
    add_core(1)
    share(3)
    g_start(1)
    add_core(2)
    share(4)
    g_start(2)
    add_core(3)
    share(5)
    share(6)
    add_core(4)
    share(7)
    add_core(5)
    weight(0)
    weight(1)
    weight(2)
    weight(3)
    weight_close()
    g_second(0)
    g_second(1)
    g_second(2)
    add_core(6)
    add_core(7)
    s_next(0)
    w_second()
    finish(0)
    g_third(0)
    g_third(1)
    g_third(2)
    s_next(1)
    w_third()
    finish(1)
    g_fourth(0)
    g_fourth(1)
    g_fourth(2)
    s_next(2)
    w_fourth()
    finish(2)
    g_fifth(0)
    g_fifth(1)
    g_fifth(2)
    w_fifth()
    s_next(3)
    finish(3)
    w_sixth()
    finish(4)
    s_next(4)
    finish(5)
    finish(6)
    finish(7)
    w_copy["core"].wait()
    w_copy["x"].wait()
    w_copy["xc"].wait()
    wall[2 * x + c] = wfull[c]
    sum_ref[...] = small_out[4]
    for i in range(chunks):
        arrive(i)
    for p in range(PIECES):
        g_copy["x", p].wait()


def tail(d_qkv, unit_t, x, dmid, keep, from_y, from_x, from_xy, weight, vecs, gvecs, gub):
    count, width = x.shape
    shard = width // 4
    half = count // 2
    chunks = count // TAIL_CHUNK
    sixth = keep.shape[1]
    vmem = pl.BlockSpec(memory_space=pltpu.VMEM)
    dma = pltpu.SemaphoreType.DMA
    buf = pltpu.VMEM
    return pl.pallas_call(
        tail_kernel,
        in_specs=[pl.BlockSpec(memory_space=pl.ANY)] * 8 + [vmem] * 4,
        out_specs=[vmem] * 4,
        out_shape=[
            jax.ShapeDtypeStruct((2, half, width), bf16),
            jax.ShapeDtypeStruct((PIECES, 2, sixth, width), bf16),
            jax.ShapeDtypeStruct((4, shard, 3 * PAIR), bf16),
            jax.ShapeDtypeStruct((16, width), f32),
        ],
        scratch_shapes=[
            buf(keep.shape, bf16),
            buf(keep.shape, bf16),
            buf(keep.shape, bf16),
            buf(keep.shape, bf16),
            buf(d_qkv.shape, bf16),
            buf(unit_t.shape, bf16),
            buf(weight.shape, f32),
            buf((1, 3 * PAIR), f32),
            buf((4, shard, 3 * PAIR), bf16),
            buf((2, count, width), bf16),
            buf((count, width), bf16),
            buf((count, width), f32),
            buf((2, count, width), bf16),
            buf((2, count, width), f32),
            buf((count, width), bf16),
            buf((count, width), bf16),
            buf((count, width), bf16),
            buf((PIECES, sixth, width), f32),
            buf((PIECES, sixth // 2, width), bf16),
            buf((PIECES, sixth // 2, width), bf16),
            buf((PIECES, sixth // 4, width), bf16),
            buf((PIECES, sixth // 4, width), bf16),
            buf((2, shard, 3 * PAIR), bf16),
            buf((2, shard, 3 * PAIR), f32),
            buf((shard, 3 * PAIR), bf16),
            buf((shard, 3 * PAIR), bf16),
            buf((shard // 2, 3 * PAIR), bf16),
            buf((shard // 2, 3 * PAIR), bf16),
            buf((2, shard, 3 * PAIR), bf16),
            buf((16, width), f32),
            buf((5, 16, width), f32),
            buf((5, 16, width), f32),
            dma((chunks,)),
            dma((chunks // 2,)),
            dma((chunks,)),
            dma((chunks,)),
            dma((chunks,)),
            dma((chunks,)),
            dma((chunks,)),
            dma((chunks,)),
            dma((5 * PIECES,)),
            dma((5 * PIECES,)),
            dma((8,)),
            dma((8,)),
            dma((5,)),
            dma((5,)),
            dma((7,)),
        ],
        compiler_params=pltpu.CompilerParams(
            collective_id=5, has_side_effects=True, vmem_limit_bytes=60 * 1024 * 1024
        ),
        name="tail",
    )(d_qkv, unit_t, x, dmid, keep, from_y, from_x, from_xy, weight, vecs, gvecs, gub)

def results_kernel(
    dx_ref, down_ref, up_ref, out_ref, wall_ref, sum_ref,
    dx_out, gd_ref, gu_ref, go_ref, gq_ref, *vectors,
):
    step = pl.program_id(0)
    width = dx_ref.shape[-1]
    dx_out[:, 0] = dx_ref[...].astype(f32)
    gd_ref[...] = down_ref[...].astype(f32)
    gu_ref[...] = up_ref[...].astype(f32)
    go_ref[...] = out_ref[...].astype(f32)
    for part in range(3):
        at = pl.multiple_of(part * width + step * PAIR, PAIR)
        gq_ref[:, pl.ds(at, PAIR)] = wall_ref[0, :, part * PAIR : (part + 1) * PAIR].astype(f32)
    shard = go_ref.shape[0]
    mine = 2 * lax.axis_index("y") + lax.axis_index("c")
    for i in range(6):
        vectors[i][...] = sum_ref[i : i + 1, pl.ds(pl.multiple_of(mine * shard, shard), shard)]
    vectors[6][...] = sum_ref[pl.ds(6 + mine, 1), :]


def results(dx, flat, wall, sums):
    half, width = dx.shape[1:]
    shard = wall.shape[1]
    steps = 4
    flat = flat.reshape(-1, width)
    tokens = pl.BlockSpec((2, half // steps, width), lambda i: (0, i, 0))
    tokens_out = pl.BlockSpec((2, 1, half // steps, width), lambda i: (0, 0, i, 0))
    shape = jax.ShapeDtypeStruct
    return pl.pallas_call(
        results_kernel,
        grid=(steps,),
        in_specs=[
            tokens,
            pl.BlockSpec((shard, width), lambda i: (i, 0)),
            pl.BlockSpec((shard, width), lambda i: (steps + i, 0)),
            pl.BlockSpec((shard, width), lambda i: (2 * steps, 0)),
            pl.BlockSpec((1, shard, 3 * PAIR), lambda i: (i, 0, 0)),
            whole(sums.shape),
        ],
        out_specs=[
            tokens_out,
            pl.BlockSpec((shard, width), lambda i: (i, 0)),
            pl.BlockSpec((shard, width), lambda i: (0, i)),
            whole((shard, width)),
            whole((shard, 3 * width)),
        ]
        + [whole((1, shard))] * 6
        + [whole((1, width))],
        out_shape=[
            shape((2, 1, half, width), f32),
            shape((width, width), f32),
            shape((shard, 4 * width), f32),
            shape((shard, width), f32),
            shape((shard, 3 * width), f32),
        ]
        + [shape((1, shard), f32)] * 6
        + [shape((1, width), f32)],
        compiler_params=pltpu.CompilerParams(vmem_limit_bytes=60 * 1024 * 1024),
        name="results",
    )(dx, flat, flat, flat, wall, sums)


def place(z, x, y, c):
    return ((z * SIZES[1] + x) * SIZES[2] + y) * SIZES[3] + c


def everyone():
    return [
        (z, x, y, c)
        for z in range(SIZES[0])
        for x in range(SIZES[1])
        for y in range(SIZES[2])
        for c in range(SIZES[3])
    ]


def swap_pairs(dx, dy, dc):
    return [(place(z, x, y, c), place(z, x ^ dx, y ^ dy, c ^ dc)) for z, x, y, c in everyone()]


def move(value, pairs):
    return lax.ppermute(value, AXES, pairs)


def swap(value, dx=0, dy=0, dc=0):
    return move(value, swap_pairs(dx, dy, dc))


def paired_body(
    inputs, out_grad, segment_ids, block_order, w_qkv, w_out, w_up, w_down,
    norm1_gain, norm1_bias, norm2_gain, norm2_bias, out_bias, up_bias, down_bias,
):
    vectors = (norm1_gain, norm1_bias, norm2_gain, norm2_bias, out_bias, down_bias, up_bias)
    (
        qt, k, kt, v, vt, unit, own_x, full_out, full_up, full_down, near_dy, w_heads, vecs, full_ubias, start, tab
    ) = head(
        inputs, out_grad, segment_ids.reshape(2, -1, 128), block_order, vectors, w_qkv, w_out, w_up, w_down
    )
    o, ot, lse = attend(tab, qt, start, k, vt)
    d_o, outputs, d_middle, keep, to_y, to_x, to_xy, g_vecs, g_ubias = feed(
        o.reshape(4, -1, PAIR), own_x, near_dy, out_grad, full_out, full_up, full_down, vecs, full_ubias, 4
    )
    from_y, from_x, from_xy = swap(to_y, dy=1), swap(to_x, dx=1), swap(to_xy, dy=1, dx=1)
    d_qkv, outputs = attend_back(tab, k, kt, v, outputs, qt, start, d_o.reshape(-1, PAIR), ot, lse)
    dx, flat, heads, sums = tail(
        d_qkv.reshape(4, -1, 3 * PAIR), unit, own_x, d_middle, keep, from_y, from_x, from_xy,
        w_heads, vecs, g_vecs, g_ubias,
    )
    input_grad, grad_down, grad_up, grad_out, grad_qkv, *vec = results(dx, flat, heads, sums)
    vec = [member.reshape(-1) for member in vec]
    return (
        outputs, input_grad, grad_qkv, grad_out, grad_up, grad_down,
        vec[0], vec[1], vec[2], vec[3], vec[4], vec[6], vec[5],
    )


def solution(mesh):
    paired = mesh.shape["ctx"] == SIZES[0] * SIZES[1] and mesh.shape["fsdp"] == SIZES[2] * SIZES[3]
    if paired:
        mesh = Mesh(mesh.devices.reshape(SIZES), AXES)
        ctx, fsdp, program = ("z", "x"), ("y", "c"), paired_body
    else:
        ctx, fsdp, program = "ctx", "fsdp", general_body
    tokens = P(None, fsdp, ctx, None)
    matrix, vector = P(fsdp, None), P(fsdp)
    return jax.shard_map(
        program,
        mesh=mesh,
        in_specs=(tokens, tokens, P(None, fsdp, ctx), P()) + (matrix,) * 4 + (vector,) * 7,
        out_specs=(tokens, tokens) + (matrix,) * 4 + (vector,) * 7,
        check_vma=False,
    )
```

```python
import functools
import math

import jax
import jax.numpy as jnp
from jax import lax
from jax.experimental import pallas as pl
from jax.experimental.pallas import tpu as pltpu
from jax.sharding import Mesh
from jax.sharding import PartitionSpec as P

H = 8
HD = 64
BLK = 256
PAIR = 2 * HD

norm_eps = 1e-05
mask_fill = -1e30
LOG2E = math.log2(math.e)
LN2 = math.log(2.0)
SCORE_SCALE = 1.0 / math.sqrt(HD)

f32 = jnp.float32
bf16 = jnp.bfloat16


def contract(a, b, da, db):
    return lax.dot_general(a, b, (((da,), (db,)), ((), ())), preferred_element_type=f32)


def norm_parts(values):
    center = values - jnp.mean(values, axis=-1, keepdims=True)
    spread = jnp.mean(center * center, axis=-1, keepdims=True)
    inv = lax.rsqrt(spread + norm_eps)
    return center * inv, inv


def whole(shape):
    zeros = (0,) * len(shape)
    return pl.BlockSpec(shape, lambda *_: zeros)


def two_heads(block):
    zero = jnp.zeros((HD, block.shape[1]), block.dtype)
    return jnp.concatenate(
        [jnp.concatenate([block[:HD], zero], axis=0), jnp.concatenate([zero, block[HD:]], axis=0)], axis=1
    )


EXTRA = 16


def attend_kernel(
    tab_ref, qt_ref, start_ref, k_ref, vt_ref, o_hbm, ot_hbm, lse_ref, acc, top, o_buf, ot_buf, out_sem
):
    blocks = start_ref.shape[0]
    row = lax.broadcasted_iota(jnp.int32, (BLK, 2 * BLK), 0)
    reach = row - jnp.bitwise_and(lax.broadcasted_iota(jnp.int32, (BLK, 2 * BLK), 1), BLK - 1)
    ones = jnp.ones((EXTRA, 2 * BLK), bf16)

    def place_of(b):
        return pl.ds(pl.multiple_of(tab_ref[2, jnp.maximum(b, 0)] * BLK, BLK), BLK)

    def visits_of(qb):
        return (qb - tab_ref[0, qb]) // 2 + 1

    def visit(qb, i, bounded, live=True):
        kb = qb - 2 * i
        both = two_heads(qt_ref[:, place_of(qb)])
        start = jnp.concatenate([start_ref[qb], start_ref[qb]], axis=1)
        places = [place_of(kb), place_of(kb - 1)]
        terms = []
        for n in range(2):
            first_row = start - (kb - n) * BLK
            allowed = row >= (first_row if live is True else jnp.where(live, first_row, BLK))
            if n == 0:
                allowed = allowed & (reach <= (qb - kb) * BLK)
            st = jnp.dot(k_ref[places[n], :], both, preferred_element_type=f32)
            terms.append(jnp.where(allowed, st, mask_fill))
        if bounded:
            probs = [jnp.exp2(term).astype(bf16) for term in terms]
        else:
            old = top[qb]
            peak = jnp.maximum(
                jnp.max(terms[0], axis=0, keepdims=True), jnp.max(terms[1], axis=0, keepdims=True)
            )
            peak = jnp.maximum(old, peak)
            shrink = jnp.exp2(old - peak)
            top[qb] = peak
            probs = [jnp.exp2(term - peak).astype(bf16) for term in terms]
        probs = jnp.concatenate(probs, axis=0)
        vt = jnp.concatenate([vt_ref[:, places[0]], vt_ref[:, places[1]]], axis=1)
        parts = []
        for head in range(2):
            cols = slice(head * BLK, (head + 1) * BLK)
            left = jnp.concatenate([vt[head * HD : (head + 1) * HD], ones], axis=0)
            part = jnp.dot(left, probs[:, cols], preferred_element_type=f32)
            parts.append(part)
            if not bounded:
                acc[qb, head] = part + acc[qb, head] * shrink[:, cols]
        return parts

    def all_visits(bounded):
        count = lax.fori_loop(0, blocks, lambda b, n: n + visits_of(b), 0)

        def following(qb, i):
            more = i + 1 < visits_of(qb)
            return jnp.where(more, qb, jnp.minimum(qb + 1, blocks - 1)), jnp.where(more, i + 1, 0)

        def step(n, state):
            if not bounded:
                visit(*state, False)
                return following(*state)
            second = following(*state)
            members = [visit(*state, True), visit(*second, True, 2 * n + 1 < count)]
            for (qb, _), parts in zip((state, second), members):
                for head in range(2):
                    acc[qb, head] += parts[head]
            return following(*second)

        lax.fori_loop(0, (count + 1) // 2 if bounded else count, step, (jnp.int32(0), jnp.int32(0)))

    small = tab_ref[3, 0] > 0
    acc[...] = jnp.zeros_like(acc)

    @pl.when(small)
    def _():
        top[...] = jnp.zeros_like(top)
        all_visits(True)

    @pl.when(jnp.logical_not(small))
    def _():
        top[...] = jnp.full_like(top, mask_fill)
        all_visits(False)

    def outgoing(b):
        at = place_of(b)
        return (
            pltpu.make_async_copy(o_buf.at[b], o_hbm.at[at], out_sem.at[0]),
            pltpu.make_async_copy(ot_buf.at[b], ot_hbm.at[b], out_sem.at[1]),
        )

    def close(b):
        total = jnp.concatenate([acc[b, 0, HD : HD + 1], acc[b, 1, HD : HD + 1]], axis=1)
        lse_ref[b] = top[b] + jnp.log2(total)
        heads = jnp.concatenate([acc[b, h, :HD] / acc[b, h, HD : HD + 1] for h in range(2)], axis=0)
        ot_buf[b] = heads
        o_buf[b] = heads.T.astype(bf16)
        for copy in outgoing(b):
            copy.start()

    def close_two(n, carry):
        close(2 * n)
        close(2 * n + 1)
        return carry

    lax.fori_loop(0, blocks // 2, close_two, 0)
    for whole_copy in (
        pltpu.make_async_copy(ot_buf, ot_hbm, out_sem.at[1]),
        pltpu.make_async_copy(o_hbm, o_hbm, out_sem.at[0]),
    ):
        whole_copy.wait()


def attend(tab, qt, start, k, vt):
    count = k.shape[0]
    blocks = count // BLK
    vmem, any_ = pl.BlockSpec(memory_space=pltpu.VMEM), pl.BlockSpec(memory_space=pl.ANY)
    return pl.pallas_call(
        attend_kernel,
        grid_spec=pltpu.PrefetchScalarGridSpec(
            num_scalar_prefetch=1,
            grid=(),
            in_specs=[vmem] * 4,
            out_specs=[any_, any_, vmem],
            scratch_shapes=[
                pltpu.VMEM((blocks, 2, HD + EXTRA, BLK), f32),
                pltpu.VMEM((blocks, 1, 2 * BLK), f32),
                pltpu.VMEM((blocks, BLK, PAIR), bf16),
                pltpu.VMEM((blocks, PAIR, BLK), f32),
                pltpu.SemaphoreType.DMA((2,)),
            ],
        ),
        out_shape=[
            jax.ShapeDtypeStruct((count, PAIR), bf16),
            jax.ShapeDtypeStruct((blocks, PAIR, BLK), f32),
            jax.ShapeDtypeStruct((blocks, 1, 2 * BLK), f32),
        ],
        name="attend",
    )(tab, qt, start, k, vt)


def split_heads(block):
    lane = lax.broadcasted_iota(jnp.int32, block.shape, 1)
    zero = jnp.zeros_like(block)
    first = lane < HD
    return jnp.concatenate([jnp.where(first, block, zero), jnp.where(first, zero, block)], axis=0)


def attend_back_kernel(
    tab_ref, k_hbm, kt_hbm, v_hbm, qt_ref, start_ref, do_ref, ot_ref, lse_ref, out_hbm,
    k_ref, kt_ref, v_ref, out_buf, dqt, dk, dv, dot, dom, qm, delta, in_sem, out_sem,
):
    blocks = start_ref.shape[0]
    row = lax.broadcasted_iota(jnp.int32, (BLK, 2 * BLK), 0)
    reach = row - jnp.bitwise_and(lax.broadcasted_iota(jnp.int32, (BLK, 2 * BLK), 1), BLK - 1)
    loads = [
        pltpu.make_async_copy(src, dst, in_sem.at[i])
        for i, (src, dst) in enumerate(((k_hbm, k_ref), (kt_hbm, kt_ref), (v_hbm, v_ref)))
    ]
    for copy in loads:
        copy.start()

    def at(b):
        return pl.ds(pl.multiple_of(tab_ref[2, b] * BLK, BLK), BLK)

    def prepare(qb):
        dqt[qb] = jnp.zeros((PAIR, BLK), f32)
        dk[qb] = jnp.zeros((BLK, PAIR), f32)
        dv[qb] = jnp.zeros((BLK, PAIR), f32)
        d_out = do_ref[at(qb), :]
        dom[qb] = split_heads(d_out)
        qm[qb] = split_heads(qt_ref[:, at(qb)].T)
        turned = d_out.astype(f32).T
        dot[qb] = turned.astype(bf16)
        both = turned * ot_ref[qb]
        delta[qb] = jnp.concatenate(
            [jnp.sum(both[:HD], axis=0, keepdims=True), jnp.sum(both[HD:], axis=0, keepdims=True)], axis=1
        )

    def prepare_two(n, carry):
        prepare(2 * n)
        prepare(2 * n + 1)
        return carry

    lax.fori_loop(0, blocks // 2, prepare_two, 0)
    for copy in loads:
        copy.wait()

    def tile(kb, qb, live):
        kt = kt_ref[:, at(kb)]
        start = jnp.concatenate([start_ref[qb], start_ref[qb]], axis=1)
        st = jnp.dot(k_ref[at(kb), :], two_heads(qt_ref[:, at(qb)]), preferred_element_type=f32)
        dpt = jnp.dot(v_ref[at(kb), :], two_heads(dot[qb]), preferred_element_type=f32)
        allowed = (row >= start - kb * BLK) & (reach <= jnp.where(live, (qb - kb) * BLK, -2 * BLK))
        pt = jnp.exp2(jnp.where(allowed, st - lse_ref[qb], mask_fill))
        dst = (pt * (dpt - delta[qb])).astype(bf16)
        part_v = jnp.dot(pt.astype(bf16), dom[qb], preferred_element_type=f32)
        part_k = jnp.dot(dst, qm[qb], preferred_element_type=f32)
        part_q = [
            jnp.dot(kt[head * HD : (head + 1) * HD], dst[:, head * BLK : (head + 1) * BLK], preferred_element_type=f32)
            for head in range(2)
        ]
        return kb, qb, part_v, part_k, jnp.concatenate(part_q, axis=0)

    def add(kb, qb, part_v, part_k, part_q):
        dv[kb] += part_v
        dk[kb] += part_k
        dqt[qb] += part_q

    def following(kb, qb):
        more = qb < tab_ref[1, kb]
        beyond = jnp.minimum(kb + 1, blocks - 1)
        return jnp.where(more, kb, beyond), jnp.where(more, qb + 1, beyond)

    tiles = lax.fori_loop(0, blocks, lambda b, n: n + tab_ref[1, b] - b + 1, 0)

    def step(n, state):
        second = following(*state)
        terms = [tile(*state, True), tile(*second, 2 * n + 1 < tiles)]
        for term in terms:
            add(*term)
        return following(*second)

    lax.fori_loop(0, (tiles + 1) // 2, step, (jnp.int32(0), jnp.int32(0)))
    def close(b):
        out_buf[b] = jnp.concatenate([(dqt[b] * SCORE_SCALE).T, dk[b] * LN2, dv[b]], axis=1).astype(bf16)
        pltpu.make_async_copy(out_buf.at[b], out_hbm.at[at(b)], out_sem.at[0]).start()

    def close_four(n, carry):
        for i in range(4):
            close(4 * n + i)
        return carry

    lax.fori_loop(0, blocks // 4, close_four, 0)
    pltpu.make_async_copy(out_hbm, out_hbm, out_sem.at[0]).wait()


def attend_back(tab, k, kt, v, qt, start, d_out, ot, lse):
    count = k.shape[0]
    blocks = count // BLK
    vmem, any_ = pl.BlockSpec(memory_space=pltpu.VMEM), pl.BlockSpec(memory_space=pl.ANY)
    buf = pltpu.VMEM
    return pl.pallas_call(
        attend_back_kernel,
        grid_spec=pltpu.PrefetchScalarGridSpec(
            num_scalar_prefetch=1,
            grid=(),
            in_specs=[any_] * 3 + [vmem] * 5,
            out_specs=any_,
            scratch_shapes=[
                buf(k.shape, bf16),
                buf(kt.shape, bf16),
                buf(v.shape, bf16),
                buf((blocks, BLK, 3 * PAIR), bf16),
                buf((blocks, PAIR, BLK), f32),
                buf((blocks, BLK, PAIR), f32),
                buf((blocks, BLK, PAIR), f32),
                buf((blocks, PAIR, BLK), bf16),
                buf((blocks, 2 * BLK, PAIR), bf16),
                buf((blocks, 2 * BLK, PAIR), bf16),
                buf((blocks, 1, 2 * BLK), f32),
                pltpu.SemaphoreType.DMA((3,)),
                pltpu.SemaphoreType.DMA((1,)),
            ],
        ),
        out_shape=jax.ShapeDtypeStruct((count, 3 * PAIR), bf16),
        compiler_params=pltpu.CompilerParams(vmem_limit_bytes=60 * 1024 * 1024),
        name="attend_back",
    )(tab, k, kt, v, qt, start, d_out, ot, lse)


def layer_norm(values, gain_vec, offset):
    center = values - jnp.mean(values, axis=-1, keepdims=True)
    spread = jnp.mean(center * center, axis=-1, keepdims=True)
    return center * lax.rsqrt(spread + norm_eps) * gain_vec + offset


def gelu_exact(values):
    return 0.5 * values * (1.0 + lax.erf(values * (1.0 / math.sqrt(2.0))))


def score_block(query_heads, key_heads, query_doc, query_pos, key_doc, key_pos):
    raw_scores = jnp.einsum(
        "qhd,khd->hqk", query_heads, key_heads, preferred_element_type=jnp.float32
    ) * (1.0 / math.sqrt(HD))
    allowed = (query_doc[:, None] == key_doc[None, :]) & (key_pos[None, :] <= query_pos[:, None])
    return (raw_scores, allowed[None])


def soft_block(raw_scores, allowed, log_norm):
    return jnp.exp(jnp.where(allowed, raw_scores, mask_fill) - log_norm[:, :, None])


def row_log_norm(query_heads, key_blocks, doc_blocks, pos_blocks, query_doc, query_pos):

    def row_visit(running, block_item):
        row_top, row_sum = running
        key_heads, key_doc, key_pos = block_item
        raw_scores, allowed = score_block(
            query_heads, key_heads, query_doc, query_pos, key_doc, key_pos
        )
        masked = jnp.where(allowed, raw_scores, mask_fill)
        new_top = jnp.maximum(row_top, jnp.max(masked, axis=-1))
        fresh = jnp.sum(jnp.where(allowed, jnp.exp(masked - new_top[:, :, None]), 0.0), axis=-1)
        return ((new_top, row_sum * jnp.exp(row_top - new_top) + fresh), None)

    query_count = query_doc.shape[0]
    start = (
        jnp.full((H, query_count), mask_fill, jnp.float32),
        jnp.zeros((H, query_count), jnp.float32),
    )
    (row_top, row_sum), unused = lax.scan(row_visit, start, (key_blocks, doc_blocks, pos_blocks))
    return row_top + jnp.log(row_sum)


def attend_all(
    query_heads, key_blocks, value_blocks, doc_blocks, pos_blocks, query_doc, query_pos, log_norm
):

    def attend_visit(accum_out, block_item):
        key_heads, value_heads, key_doc, key_pos = block_item
        raw_scores, allowed = score_block(
            query_heads, key_heads, query_doc, query_pos, key_doc, key_pos
        )
        soft_low = soft_block(raw_scores, allowed, log_norm).astype(jnp.bfloat16)
        return (
            accum_out
            + jnp.einsum("hqk,khd->qhd", soft_low, value_heads, preferred_element_type=jnp.float32),
            None,
        )

    start = jnp.zeros(query_heads.shape, jnp.float32)
    accum_out, unused = lax.scan(
        attend_visit, start, (key_blocks, value_blocks, doc_blocks, pos_blocks)
    )
    return accum_out


def grad_block(
    query_heads,
    grad_heads,
    log_norm,
    row_delta,
    query_doc,
    query_pos,
    key_heads,
    value_heads,
    key_doc,
    key_pos,
):
    raw_scores, allowed = score_block(
        query_heads, key_heads, query_doc, query_pos, key_doc, key_pos
    )
    soft = soft_block(raw_scores, allowed, log_norm)
    grad_soft = jnp.einsum(
        "qhd,khd->hqk", grad_heads, value_heads, preferred_element_type=jnp.float32
    )
    grad_scores = (soft * (grad_soft - row_delta[:, :, None])).astype(jnp.bfloat16)
    score_scale = 1.0 / math.sqrt(HD)
    part_q = (
        jnp.einsum("hqk,khd->qhd", grad_scores, key_heads, preferred_element_type=jnp.float32)
        * score_scale
    )
    part_k = (
        jnp.einsum("hqk,qhd->khd", grad_scores, query_heads, preferred_element_type=jnp.float32)
        * score_scale
    )
    part_v = jnp.einsum(
        "hqk,qhd->khd", soft.astype(jnp.bfloat16), grad_heads, preferred_element_type=jnp.float32
    )
    return (part_q, part_k, part_v)


def general_body(
    inputs,
    out_grad,
    segment_ids,
    block_order,
    w_qkv,
    w_out,
    w_up,
    w_down,
    norm1_gain,
    norm1_bias,
    norm2_gain,
    norm2_bias,
    out_bias,
    up_bias,
    down_bias,
):
    gathered = (
        lax.all_gather(w_qkv, "fsdp", axis=0, tiled=True),
        lax.all_gather(w_out, "fsdp", axis=0, tiled=True),
        lax.all_gather(w_up, "fsdp", axis=0, tiled=True),
        lax.all_gather(w_down, "fsdp", axis=0, tiled=True),
        lax.all_gather(norm1_gain, "fsdp", axis=0, tiled=True),
        lax.all_gather(norm1_bias, "fsdp", axis=0, tiled=True),
        lax.all_gather(norm2_gain, "fsdp", axis=0, tiled=True),
        lax.all_gather(norm2_bias, "fsdp", axis=0, tiled=True),
        lax.all_gather(out_bias, "fsdp", axis=0, tiled=True),
        lax.all_gather(up_bias, "fsdp", axis=0, tiled=True),
        lax.all_gather(down_bias, "fsdp", axis=0, tiled=True),
    )
    full_qkv, full_out, full_up, full_down = (gathered[0], gathered[1], gathered[2], gathered[3])
    gain_one, bias_one, gain_two, bias_two, full_obias, full_ubias, full_dbias = [
        member.astype(jnp.float32) for member in gathered[4:]
    ]
    model_width = full_qkv.shape[0]
    local_rows = inputs.shape[2]
    ctx_count = lax.axis_size("ctx")
    seq_len = local_rows * ctx_count
    key_block = min(512, seq_len)
    block_count = seq_len // key_block
    ctx_index = lax.axis_index("ctx")
    row_ids = jnp.arange(local_rows, dtype=jnp.int32)
    own_blocks = lax.dynamic_slice_in_dim(block_order, 2 * ctx_index, 2)
    own_pos = own_blocks[row_ids // BLK] * BLK + row_ids % BLK
    all_ids = jnp.arange(seq_len, dtype=jnp.int32)
    all_pos = block_order[all_ids // BLK] * BLK + all_ids % BLK
    pos_blocks = all_pos.reshape(block_count, key_block)
    grad_sums = [jnp.zeros(member.shape, jnp.float32) for member in gathered]
    outputs_list = []
    input_grads = []
    for micro_idx in range(inputs.shape[0]):
        seq_in = inputs[micro_idx, 0].astype(jnp.float32)
        normed, norm1_pull = jax.vjp(layer_norm, seq_in, gain_one, bias_one)
        normed_low = normed.astype(jnp.bfloat16)
        qkv_out = jnp.dot(normed_low, full_qkv, preferred_element_type=jnp.float32).astype(
            jnp.bfloat16
        )
        query_heads = qkv_out[:, :model_width].reshape(local_rows, H, HD)
        kv_all, doc_all = (
            lax.all_gather(qkv_out[:, model_width:], "ctx", axis=0, tiled=True),
            lax.all_gather(segment_ids[micro_idx, 0], "ctx", axis=0, tiled=True),
        )
        doc_rows = doc_all[all_pos]
        query_doc = doc_all[own_pos]
        kv_heads = kv_all.reshape(block_count, key_block, 2, H, HD)
        key_blocks = kv_heads[:, :, 0]
        value_blocks = kv_heads[:, :, 1]
        doc_blocks = doc_rows.reshape(block_count, key_block)
        log_norm = row_log_norm(query_heads, key_blocks, doc_blocks, pos_blocks, query_doc, own_pos)
        attn_acc = attend_all(
            query_heads,
            key_blocks,
            value_blocks,
            doc_blocks,
            pos_blocks,
            query_doc,
            own_pos,
            log_norm,
        )
        attn_low = attn_acc.reshape(local_rows, model_width).astype(jnp.bfloat16)
        branch = jnp.dot(attn_low, full_out, preferred_element_type=jnp.float32) + full_obias
        middle = seq_in + branch
        normed_two, norm2_pull = jax.vjp(layer_norm, middle, gain_two, bias_two)
        normed_two_low = normed_two.astype(jnp.bfloat16)
        hidden = jnp.dot(normed_two_low, full_up, preferred_element_type=jnp.float32) + full_ubias
        active, gelu_pull = jax.vjp(gelu_exact, hidden)
        active_low = active.astype(jnp.bfloat16)
        result = middle + (
            jnp.dot(active_low, full_down, preferred_element_type=jnp.float32) + full_dbias
        )
        outputs_list.append(result.astype(jnp.bfloat16))
        grad_y = out_grad[micro_idx, 0]
        grad_y32 = grad_y.astype(jnp.float32)
        grad_sums[3] = grad_sums[3] + jnp.einsum(
            "rf,rd->fd", active_low, grad_y, preferred_element_type=jnp.float32
        )
        grad_sums[10] = grad_sums[10] + jnp.sum(grad_y32, axis=0)
        grad_active = jnp.einsum("rd,fd->rf", grad_y, full_down, preferred_element_type=jnp.float32)
        (grad_hidden,) = gelu_pull(grad_active)
        grad_hidden_low = grad_hidden.astype(jnp.bfloat16)
        grad_sums[2] = grad_sums[2] + jnp.einsum(
            "rd,rf->df", normed_two_low, grad_hidden_low, preferred_element_type=jnp.float32
        )
        grad_sums[9] = grad_sums[9] + jnp.sum(grad_hidden_low.astype(jnp.float32), axis=0)
        grad_normed_two = jnp.einsum(
            "rf,df->rd", grad_hidden_low, full_up, preferred_element_type=jnp.float32
        )
        grad_mid_ln, grad_gain_two, grad_bias_two = norm2_pull(grad_normed_two)
        grad_sums[6] = grad_sums[6] + grad_gain_two
        grad_sums[7] = grad_sums[7] + grad_bias_two
        grad_mid = grad_y32 + grad_mid_ln
        grad_mid_low = grad_mid.astype(jnp.bfloat16)
        grad_sums[1] = grad_sums[1] + jnp.einsum(
            "rd,re->de", attn_low, grad_mid_low, preferred_element_type=jnp.float32
        )
        grad_sums[8] = grad_sums[8] + jnp.sum(grad_mid_low.astype(jnp.float32), axis=0)
        grad_attn_low = jnp.einsum(
            "re,de->rd", grad_mid_low, full_out, preferred_element_type=jnp.float32
        ).astype(jnp.bfloat16)
        grad_heads = grad_attn_low.reshape(local_rows, H, HD)
        row_delta = jnp.sum(grad_heads.astype(jnp.float32) * attn_acc, axis=-1).T

        def back_visit(grad_query, block_item):
            key_heads, value_heads, key_doc, key_pos = block_item
            part_q, part_k, part_v = grad_block(
                query_heads,
                grad_heads,
                log_norm,
                row_delta,
                query_doc,
                own_pos,
                key_heads,
                value_heads,
                key_doc,
                key_pos,
            )
            joined = jnp.concatenate(
                [part_k.reshape(key_block, model_width), part_v.reshape(key_block, model_width)],
                axis=1,
            )
            return (grad_query + part_q, joined)

        grad_query, kv_terms = lax.scan(
            back_visit,
            jnp.zeros((local_rows, H, HD), jnp.float32),
            (key_blocks, value_blocks, doc_blocks, pos_blocks),
        )
        kv_grad = lax.psum_scatter(
            kv_terms.reshape(seq_len, 2 * model_width).astype(jnp.bfloat16),
            "ctx",
            scatter_dimension=0,
            tiled=True,
        ).astype(jnp.float32)
        grad_qkv_low = jnp.concatenate(
            [grad_query.reshape(local_rows, model_width), kv_grad], axis=1
        ).astype(jnp.bfloat16)
        grad_sums[0] = grad_sums[0] + jnp.einsum(
            "rd,re->de", normed_low, grad_qkv_low, preferred_element_type=jnp.float32
        )
        grad_normed = jnp.einsum(
            "re,de->rd", grad_qkv_low, full_qkv, preferred_element_type=jnp.float32
        )
        grad_in_ln, grad_gain_one, grad_bias_one = norm1_pull(grad_normed)
        grad_sums[4] = grad_sums[4] + grad_gain_one
        grad_sums[5] = grad_sums[5] + grad_bias_one
        input_grads.append(grad_mid + grad_in_ln)
    owned = (
        lax.psum_scatter(
            grad_sums[0].astype(jnp.bfloat16), "fsdp", scatter_dimension=0, tiled=True
        ).astype(jnp.float32),
        lax.psum_scatter(
            grad_sums[1].astype(jnp.bfloat16), "fsdp", scatter_dimension=0, tiled=True
        ).astype(jnp.float32),
        lax.psum_scatter(
            grad_sums[2].astype(jnp.bfloat16), "fsdp", scatter_dimension=0, tiled=True
        ).astype(jnp.float32),
        lax.psum_scatter(
            grad_sums[3].astype(jnp.bfloat16), "fsdp", scatter_dimension=0, tiled=True
        ).astype(jnp.float32),
        lax.psum_scatter(
            grad_sums[4].astype(jnp.bfloat16), "fsdp", scatter_dimension=0, tiled=True
        ).astype(jnp.float32),
        lax.psum_scatter(
            grad_sums[5].astype(jnp.bfloat16), "fsdp", scatter_dimension=0, tiled=True
        ).astype(jnp.float32),
        lax.psum_scatter(
            grad_sums[6].astype(jnp.bfloat16), "fsdp", scatter_dimension=0, tiled=True
        ).astype(jnp.float32),
        lax.psum_scatter(
            grad_sums[7].astype(jnp.bfloat16), "fsdp", scatter_dimension=0, tiled=True
        ).astype(jnp.float32),
        lax.psum_scatter(
            grad_sums[8].astype(jnp.bfloat16), "fsdp", scatter_dimension=0, tiled=True
        ).astype(jnp.float32),
        lax.psum_scatter(
            grad_sums[9].astype(jnp.bfloat16), "fsdp", scatter_dimension=0, tiled=True
        ).astype(jnp.float32),
        lax.psum_scatter(
            grad_sums[10].astype(jnp.bfloat16), "fsdp", scatter_dimension=0, tiled=True
        ).astype(jnp.float32),
    )
    summed = (
        lax.psum(owned[0].astype(jnp.bfloat16), "ctx").astype(jnp.float32),
        lax.psum(owned[1].astype(jnp.bfloat16), "ctx").astype(jnp.float32),
        lax.psum(owned[2].astype(jnp.bfloat16), "ctx").astype(jnp.float32),
        lax.psum(owned[3].astype(jnp.bfloat16), "ctx").astype(jnp.float32),
        lax.psum(owned[4].astype(jnp.bfloat16), "ctx").astype(jnp.float32),
        lax.psum(owned[5].astype(jnp.bfloat16), "ctx").astype(jnp.float32),
        lax.psum(owned[6].astype(jnp.bfloat16), "ctx").astype(jnp.float32),
        lax.psum(owned[7].astype(jnp.bfloat16), "ctx").astype(jnp.float32),
        lax.psum(owned[8].astype(jnp.bfloat16), "ctx").astype(jnp.float32),
        lax.psum(owned[9].astype(jnp.bfloat16), "ctx").astype(jnp.float32),
        lax.psum(owned[10].astype(jnp.bfloat16), "ctx").astype(jnp.float32),
    )
    return (
        jnp.stack(outputs_list)[:, None],
        jnp.stack(input_grads)[:, None],
        summed[0],
        summed[1],
        summed[2],
        summed[3],
        summed[4],
        summed[5],
        summed[6],
        summed[7],
        summed[8],
        summed[9],
        summed[10],
    )


AXES = ("z", "x", "y", "c")
SIZES = (4, 2, 2, 2)


MESH = pl.DeviceIdType.MESH


def send(src, dst, sems, recv_sems, index, peer):
    copy = pltpu.make_async_remote_copy(
        src_ref=src,
        dst_ref=dst,
        send_sem=sems.at[index],
        recv_sem=recv_sems.at[index],
        device_id=peer,
        device_id_type=MESH,
    )
    copy.start()
    return copy


def greet(peers, extra, extra_on):
    barrier = pltpu.get_barrier_semaphore()
    for peer in peers:
        pl.semaphore_signal(barrier, inc=1, device_id=peer, device_id_type=MESH)

    @pl.when(extra_on)
    def _():
        for peer in extra:
            pl.semaphore_signal(barrier, inc=1, device_id=peer, device_id_type=MESH)

    pl.semaphore_wait(barrier, len(peers) + jnp.where(extra_on, len(extra), 0))


HEAD_CHUNK = 128
SAFE_SCORE = 80.0


def head_kernel(
    x_in_ref, dy_in_ref, docs_in_ref, order_ref, g1_ref, b1_ref, g2_ref, b2_ref, ob_ref, db_ref, ub_in_ref, wq_ref, wo_ref, wu_ref, wd_ref,
    qt_ref, k_ref, kt_ref, v_ref, vt_ref, ut_ref, own_ref, wo_all, wu_all, wd_all, dy_ref,
    wh_ref, vec_ref, ub_ref, start_ref, tab_ref,
    qt_buf, k_buf, kt_buf, v_buf, vt_buf, ut_buf, rows, docs, docs_true, norms, vec_in_ref, vec_all, wo_tmp, wu_tmp, wd_tmp,
    z_s, z_r, x_s, x_r, c_s, c_r, f_s, f_r, docs_s, docs_r, vec_s, vec_r, wh_s, wh_r, wh_l,
    y_s, y_r, n_s, n_r, o_s, o_r, load_sem, put_sem, self_sem, d_s, d_r, d_self, out_sem,
):
    z, x, y, c = (lax.axis_index(name) for name in AXES)
    odd, upper = lax.rem(z, 2), lax.div(z, 2)
    width = x_in_ref.shape[-1]
    chunks = rows.shape[1] // HEAD_CHUNK
    per_turn = chunks // 2
    by_core, by_x, by_y, by_yc = {"c": 1 - c}, {"x": 1 - x}, {"y": 1 - y}, {"y": 1 - y, "c": 1 - c}
    home = [{"z": 2 * c + upper, "c": odd}, {"z": 2 * c + 1 - upper, "c": odd}]
    target = [{"z": 2 * odd + c, "c": upper}, {"z": 2 * (1 - odd) + c, "c": upper}]
    block = [odd, 1 - odd]
    stay = (c == upper) & (odd == c)
    leave = jnp.logical_not(stay)
    for i, ref in enumerate((g1_ref, b1_ref, g2_ref, b2_ref, ob_ref, db_ref, ub_in_ref)):
        vec_in_ref[i : i + ref.shape[0]] = ref[...]
    greet([by_core, by_x, by_y, by_yc, home[1], target[1]], [home[0], target[0]], leave)

    def order_of(i):
        return i % 2 * per_turn + i // 2

    def piece(i):
        turn, row = order_of(i) // per_turn, (order_of(i) % per_turn) * HEAD_CHUNK
        return (
            x_in_ref.at[block[turn], 0, pl.ds(row, HEAD_CHUNK)],
            rows.at[0, pl.ds(order_of(i) * HEAD_CHUNK, HEAD_CHUNK)],
        )

    for turn in range(2):
        src, dst = docs_in_ref.at[block[turn]], docs.at[0, turn]

        def start_docs():
            send(src, dst, docs_s, docs_r, turn, target[turn])

        if turn == 0:
            pl.when(stay)(lambda: pltpu.make_async_copy(src, dst, self_sem.at[per_turn]).start())
            pl.when(leave)(start_docs)
        else:
            start_docs()
    for i in range(chunks):
        src, dst = piece(i)
        if i % 2 == 0:
            pl.when(stay)(lambda: pltpu.make_async_copy(src, dst, self_sem.at[i // 2]).start())
            pl.when(leave)(lambda: send(src, dst, z_s, z_r, i, target[0]) and None)
        else:
            send(src, dst, z_s, z_r, i, target[1])

    def piece_dy(i):
        part = pl.ds(i * HEAD_CHUNK, HEAD_CHUNK)
        return dy_in_ref.at[odd, 0, part], dy_ref.at[part]

    def send_dy(i):
        src, dst = piece_dy(i)
        pl.when(stay)(lambda: pltpu.make_async_copy(src, dst, d_self.at[i]).start())
        pl.when(leave)(lambda: send(src, dst, d_s, d_r, i, target[0]) and None)

    def land_dy(i):
        src, dst = piece_dy(i)
        pl.when(stay)(lambda: pltpu.make_async_copy(src, dst, d_self.at[i]).wait())
        pl.when(leave)(
            lambda: pltpu.make_async_remote_copy(
                src_ref=src, dst_ref=dst, send_sem=d_s.at[i], recv_sem=d_r.at[i],
                device_id=target[0], device_id_type=MESH,
            ).wait()
        )

    def landed(src, dst, sems, recv_sems, index, turn, self_index):
        def remote():
            pltpu.make_async_remote_copy(
                src_ref=src, dst_ref=dst, send_sem=sems.at[index], recv_sem=recv_sems.at[index],
                device_id=target[turn], device_id_type=MESH,
            ).wait()

        if turn == 0:
            pl.when(stay)(lambda: pltpu.make_async_copy(src, dst, self_sem.at[self_index]).wait())
            pl.when(leave)(remote)
        else:
            remote()

    mine = 2 * y + c
    vec_copy = [
        send(vec_in_ref, vec_all.at[mine], vec_s, vec_r, i, peer)
        for i, peer in enumerate((by_core, by_y, by_yc))
    ]
    vec_all[mine] = vec_in_ref[...]
    wh_copy = []
    shard = wq_ref.shape[0]
    own_rows = pl.ds(pl.multiple_of(mine * shard, shard), shard)
    for part in range(3):
        to = wh_ref.at[own_rows, pl.ds(part * PAIR, PAIR)]

        def columns(core):
            return wq_ref.at[:, pl.ds(pl.multiple_of(part * width + (2 * x + core) * PAIR, PAIR), PAIR)]

        for i, (peer, core) in enumerate(((by_core, 1 - c), (by_y, c), (by_yc, 1 - c))):
            wh_copy.append(send(columns(core), to, wh_s, wh_r, 3 * part + i, peer))
        copy = pltpu.make_async_copy(columns(c), to, wh_l.at[part])
        copy.start()
        wh_copy.append(copy)

    up_rows, down_rows = wu_ref.shape[0] // 4, wd_ref.shape[0] // 4
    parts = [(wo_ref, wo_all, wo_ref.shape[0], 0)]
    parts += [(wu_ref, wu_all, up_rows, i * up_rows) for i in range(4)]
    parts += [(wd_ref, wd_all, down_rows, i * down_rows) for i in range(4)]

    def at_owner(full, src, size, offset, owner):
        return full.at[pl.ds(pl.multiple_of(owner * src.shape[0] + offset, 32), size)]

    other = 2 * (1 - y) + c
    y_copy = []
    for i, (src, full, size, offset) in enumerate(parts):
        y_copy.append(
            send(src.at[pl.ds(offset, size)], at_owner(full, src, size, offset, mine), y_s, y_r, i, by_y)
        )
    n_copy, load_copy, put_copy = [], [], []
    for i, (src, full, tmp) in enumerate(((wo_ref, wo_all, wo_tmp), (wu_ref, wu_all, wu_tmp), (wd_ref, wd_all, wd_tmp))):
        n_copy.append(send(src, at_owner(full, src, src.shape[0], 0, mine), n_s, n_r, i, by_core))
        load_copy.append(pltpu.make_async_copy(src, tmp, load_sem.at[i]))
        load_copy[-1].start()

    def put(i):
        src, full, tmp = ((wo_ref, wo_all, wo_tmp), (wu_ref, wu_all, wu_tmp), (wd_ref, wd_all, wd_tmp))[i]
        load_copy[i].wait()
        put_copy.append(pltpu.make_async_copy(tmp, at_owner(full, src, src.shape[0], 0, mine), put_sem.at[i]))
        put_copy[-1].start()

    o_copy = []

    def forward(i):
        src, full, size, offset = parts[i]
        y_copy[i].wait()
        held = at_owner(full, src, size, offset, other)
        o_copy.append(send(held, held, o_s, o_r, i, by_core))

    blocks = order_ref.shape[0]
    lane = lax.broadcasted_iota(jnp.int32, (1, 128), 1)
    slots = jnp.zeros((1, 128), jnp.int32)
    for t in range(blocks):
        dc, dx, turn, half = t // 8, t // 4 % 2, t // 2 % 2, t % 2
        core, side = (1 - c if dc else c), (1 - x if dx else x)
        stored = 2 * (2 * (2 * core + (1 - upper if turn else upper)) + side) + half
        slots = jnp.where(lane == order_ref[stored], t, slots)

    docs_copy = {}

    def finish_docs():
        docs_copy["c"].wait()
        docs_copy["f"].wait()
        for g in range(4):
            core, side = (1 - c if g // 2 else c), (1 - x if g % 2 else x)
            for turn in range(2):
                docs_true[2 * (2 * core + (1 - upper if turn else upper)) + side] = docs[g, turn]
        numbers = docs_true[...]
        first = jnp.zeros_like(numbers)
        for d in range(1, blocks):
            before = jnp.sum((numbers < d).astype(jnp.int32), axis=(0, 1, 2), keepdims=True)
            first = jnp.where(numbers == d, before, first)
        docs_true[...] = first
        low = jnp.zeros((1, 128), jnp.int32)
        for b in range(blocks):
            line = docs_true[b // 2]
            at = 2 * (b % 2)
            line = jnp.concatenate([line[at : at + 1], line[at + 1 : at + 2]], axis=1)
            start_ref[b] = line
            low = jnp.where(lane == b, line[:, :1] // BLK, low)
        high = jnp.zeros((1, 128), jnp.int32) - 1
        for b in range(blocks):
            high = high + (low[:, b : b + 1] <= lane).astype(jnp.int32)
        tab_ref[...] = jnp.concatenate([low, high, slots, jnp.zeros((5, 128), jnp.int32)], axis=0)

    def docs_first():
        for turn in range(2):
            landed(docs_in_ref.at[block[turn]], docs.at[0, turn], docs_s, docs_r, turn, turn, per_turn)
        docs_copy["x"] = send(docs.at[0], docs.at[1], docs_s, docs_r, 2, by_x)
        docs_copy["c"] = send(docs.at[0], docs.at[2], docs_s, docs_r, 3, by_core)


    def vectors_and_weight():
        for copy in vec_copy:
            copy.wait()
        vec_width = vec_in_ref.shape[1]
        for j in range(4):
            for i in range(6):
                vec_ref[i : i + 1, j * vec_width : (j + 1) * vec_width] = vec_all[j, i : i + 1].astype(f32)
            for i in range(4):
                at = (4 * j + i) * vec_width
                ub_ref[:, at : at + vec_width] = vec_all[j, 6 + i : 7 + i].astype(f32)
        vec_ref[6:8] = jnp.zeros((2, width), f32)
        for copy in wh_copy:
            copy.wait()


    def docs_second():
        docs_copy["x"].wait()
        docs_copy["f"] = send(docs.at[1], docs.at[3], docs_s, docs_r, 4, by_core)


    x_copy, c_copy, f_copy = [], [], []

    def relay(i):
        src, dst = piece(i)
        landed(src, dst, z_s, z_r, i, i % 2, i // 2)
        part = pl.ds(order_of(i) * HEAD_CHUNK, HEAD_CHUNK)
        x_copy.append(send(rows.at[0, part], rows.at[1, part], x_s, x_r, i, by_x))
        c_copy.append(send(rows.at[0, part], rows.at[2, part], c_s, c_r, i, by_core))

    def relay_far(i):
        x_copy[i].wait()
        part = pl.ds(order_of(i) * HEAD_CHUNK, HEAD_CHUNK)
        f_copy.append(send(rows.at[1, part], rows.at[3, part], f_s, f_r, i, by_core))

    streams = (
        (qt_buf, qt_ref, 1), (k_buf, k_ref, 0), (kt_buf, kt_ref, 1), (v_buf, v_ref, 0), (vt_buf, vt_ref, 1),
        (ut_buf, ut_ref, 1),
    )

    def compute(g, i):
        count = rows.shape[1]
        chunk = order_of(i)
        unit, _ = norm_parts(rows[g, chunk * HEAD_CHUNK : (chunk + 1) * HEAD_CHUNK].astype(f32))
        at = pl.ds(g * count + chunk * HEAD_CHUNK, HEAD_CHUNK)
        ut_buf[:, at] = unit.astype(bf16).T
        low = (unit * vec_ref[0:1] + vec_ref[1:2]).astype(bf16)
        qkv = jnp.dot(low, wh_ref[...], preferred_element_type=f32)
        qt = (qkv[:, :PAIR] * (SCORE_SCALE * LOG2E)).astype(bf16).T
        qt_buf[:, at] = qt
        k = qkv[:, PAIR : 2 * PAIR].astype(bf16)
        v = qkv[:, 2 * PAIR :].astype(bf16)
        k_buf[at] = k
        v_buf[at] = v
        kt = k.T
        kt_buf[:, at] = kt
        vt_buf[:, at] = v.T
        found = []
        for block_ in (qt, kt):
            squares = block_.astype(f32) * block_.astype(f32)
            found += [jnp.sum(squares[head * HD : (head + 1) * HD], axis=0, keepdims=True) for head in range(2)]
        found = jnp.concatenate(found, axis=0)
        norms[...] = found if g == 0 and i == 0 else jnp.maximum(norms[...], found)
        for index, (source, out, columns) in enumerate(streams):
            if columns:
                source, out = source.at[:, at], out.at[:, at]
            else:
                source, out = source.at[at], out.at[at]
            pltpu.make_async_copy(source, out, out_sem.at[index]).start()

    docs_first()
    for i in range(chunks + 2):
        if i < chunks:
            if i < per_turn:
                send_dy(i)
            relay(i)
        if i == 0:
            vectors_and_weight()
            docs_second()
        if 1 <= i <= chunks:
            relay_far(i - 1)
            compute(0, i - 1)
            compute(1, i - 1)
            c_copy[i - 1].wait()
            compute(2, i - 1)
        if i >= 2:
            f_copy[i - 2].wait()
            compute(3, i - 2)
        if i == 1:
            finish_docs()
        if 2 <= i < 5:
            put(i - 2)
        if i >= 3 and i - 3 < len(parts):
            forward(i - 3)
        if i == chunks - 1:
            own_copy = pltpu.make_async_copy(rows.at[0], own_ref, out_sem.at[len(streams)])
            own_copy.start()
    largest = jnp.max(norms[...], axis=1, keepdims=True)
    bound = jnp.maximum(largest[0:1] * largest[2:3], largest[1:2] * largest[3:4])
    tab_ref[3:4] = jnp.broadcast_to((bound <= SAFE_SCORE * SAFE_SCORE).astype(jnp.int32), (1, 128))
    for i in range(chunks - 1, len(parts)):
        forward(i)
    for index, (source, out, _) in enumerate(streams):
        pltpu.make_async_copy(source, out, out_sem.at[index]).wait()
    own_copy.wait()
    for copy in n_copy + put_copy + o_copy:
        copy.wait()
    for i in range(per_turn):
        land_dy(i)


def head(x_in, dy_in, docs_in, order, vectors, w_qkv, w_out, w_up, w_down):
    width = x_in.shape[-1]
    count = 2 * x_in.shape[2]
    total = 4 * count
    shard = w_qkv.shape[0]
    chunks = count // HEAD_CHUNK
    blocks = order.shape[0]
    vmem, any_ = pl.BlockSpec(memory_space=pltpu.VMEM), pl.BlockSpec(memory_space=pl.ANY)
    smem = pl.BlockSpec(memory_space=pltpu.SMEM)
    dma, buf, shape = pltpu.SemaphoreType.DMA, pltpu.VMEM, jax.ShapeDtypeStruct
    return pl.pallas_call(
        head_kernel,
        in_specs=[any_, any_, vmem, smem] + [vmem] * 7 + [any_] * 4,
        out_specs=[any_] * 11 + [vmem] * 5,
        out_shape=[
            shape((PAIR, total), bf16),
            shape((total, PAIR), bf16),
            shape((PAIR, total), bf16),
            shape((total, PAIR), bf16),
            shape((PAIR, total), bf16),
            shape((width, total), bf16),
            shape((count, width), bf16),
            shape((4 * w_out.shape[0], w_out.shape[1]), bf16),
            shape((4 * w_up.shape[0], w_up.shape[1]), bf16),
            shape((4 * w_down.shape[0], w_down.shape[1]), bf16),
            shape((count // 2, width), bf16),
            shape((width, 3 * PAIR), bf16),
            shape((8, width), f32),
            shape((1, 4 * w_down.shape[0]), f32),
            shape((blocks, 1, BLK), jnp.int32),
            shape((8, 128), jnp.int32),
        ],
        scratch_shapes=[
            buf((PAIR, total), bf16),
            buf((total, PAIR), bf16),
            buf((PAIR, total), bf16),
            buf((total, PAIR), bf16),
            buf((PAIR, total), bf16),
            buf((width, total), bf16),
            buf((4, count, width), bf16),
            buf((4, 2) + docs_in.shape[1:], jnp.int32),
            buf((blocks // 2,) + docs_in.shape[1:], jnp.int32),
            buf((4, HEAD_CHUNK), f32),
            buf((16, shard), bf16),
            buf((4, 16, shard), bf16),
            buf(w_out.shape, bf16),
            buf(w_up.shape, bf16),
            buf(w_down.shape, bf16),
        ]
        + [dma((chunks,))] * 8
        + [dma((5,)), dma((5,)), dma((3,)), dma((3,)), dma((9,)), dma((9,)), dma((3,))]
        + [dma((9,)), dma((9,)), dma((3,)), dma((3,)), dma((9,)), dma((9,)), dma((3,)), dma((3,))]
        + [dma((chunks // 2 + 1,)), dma((chunks // 2,))] + [dma((chunks // 2,))] * 2 + [dma((7,))],
        compiler_params=pltpu.CompilerParams(
            collective_id=1, has_side_effects=True, vmem_limit_bytes=56 * 1024 * 1024
        ),
        name="head",
    )(x_in, dy_in, docs_in, order, *[v.reshape(-1, shard) for v in vectors], w_qkv, w_out, w_up, w_down)
FF_TILE = 1024
PIECES = 3
feed_steps = 4


def feed_kernel(
    o_ref, x_ref, dy_near_ref, dy_in_ref, wo_hbm, wu_hbm, wd_hbm, vec_ref, ub_ref,
    do_ref, y_home, y_far_ref, dmid_ref, keep_ref, to_y_ref, to_x_ref, to_xy_ref, gvec_ref, gub_ref,
    attn_all, gd_ref, gu_ref, go_ref, attn_in, do_out, y_out, grad_ref, grad_in,
    wo_ref, wu_ref, wd_ref, dy_ref, dy_far, w_sem, a_s, a_r, a_l, d_s, d_r, d_l, y_s, y_r, y_l, g_s, g_r, c_s, c_r,
):
    step = pl.program_id(0)
    steps = pl.num_programs(0)
    groups = attn_in.shape[0]
    tile = x_ref.shape[0]
    z, x, y, c = (lax.axis_index(name) for name in AXES)
    odd, upper = lax.rem(z, 2), lax.div(z, 2)
    mates = [None, {"x": 1 - x}, {"c": 1 - c}, {"x": 1 - x, "c": 1 - c}]
    pair_of = [2 * x + c, 2 * (1 - x) + c, 2 * x + 1 - c, 2 * (1 - x) + 1 - c]
    home = [{"z": 2 * c + upper, "c": odd}, {"z": 2 * c + 1 - upper, "c": odd}]
    origin = [{"z": 2 * odd + c, "c": upper}, {"z": 2 * (1 - odd) + c, "c": upper}]
    stay = (c == upper) & (odd == c)
    leave = jnp.logical_not(stay)
    half = feed_steps // 2

    def attn_copy(g, i):
        part = pl.ds(i * tile, tile)
        return pltpu.make_async_remote_copy(
            src_ref=o_ref.at[g, part], dst_ref=attn_in.at[g, part],
            send_sem=a_s.at[g - 1, i], recv_sem=a_r.at[g - 1, i], device_id=mates[g], device_id_type=MESH,
        )

    def attn_own(i):
        part = pl.ds(i * tile, tile)
        return pltpu.make_async_copy(o_ref.at[0, part], attn_in.at[0, part], a_l.at[i])

    def do_copy(g, i):
        return pltpu.make_async_remote_copy(
            src_ref=do_out.at[i, g], dst_ref=do_ref.at[g, pl.ds(i * tile, tile)],
            send_sem=d_s.at[g - 1, i], recv_sem=d_r.at[g - 1, i], device_id=mates[g], device_id_type=MESH,
        )

    def do_own(i):
        return pltpu.make_async_copy(do_out.at[i, 0], do_ref.at[0, pl.ds(i * tile, tile)], d_l.at[i])

    def y_rows(i):
        return y_home.at[pl.ds(i * tile, tile)]

    def y_copy(i):
        return pltpu.make_async_remote_copy(
            src_ref=y_out.at[i], dst_ref=y_rows(i),
            send_sem=y_s.at[i], recv_sem=y_r.at[i], device_id=home[0], device_id_type=MESH,
        )

    def y_own(i):
        return pltpu.make_async_copy(y_out.at[i], y_rows(i), y_l.at[i])

    def grad_copy(i):
        return pltpu.make_async_remote_copy(
            src_ref=grad_ref.at[2 * i + 1 - c], dst_ref=grad_in.at[i],
            send_sem=g_s.at[i], recv_sem=g_r.at[i], device_id=mates[2], device_id_type=MESH,
        )

    def dy_copy(i):
        part = pl.ds(i * tile, tile)
        return pltpu.make_async_remote_copy(
            src_ref=dy_in_ref.at[1 - odd, 0, part], dst_ref=dy_far.at[part],
            send_sem=c_s.at[i], recv_sem=c_r.at[i], device_id=origin[1], device_id_type=MESH,
        )

    w_loads = [
        pltpu.make_async_copy(src, dst, w_sem.at[i])
        for i, (src, dst) in enumerate(((wo_hbm, wo_ref), (wu_hbm, wu_ref), (wd_hbm, wd_ref)))
    ]

    @pl.when(step == 0)
    def _():
        for copy in w_loads:
            copy.start()
        greet(mates[1:] + [home[1], origin[1]], [home[0], origin[0]], leave)
        for i in range(feed_steps):
            for g in (1, 3, 2):
                attn_copy(g, i).start()
            attn_own(i).start()
        for i in range(half):
            dy_copy(i).start()

    @pl.when(step == 0)
    def _():
        for ref in (gd_ref, gu_ref, go_ref, gvec_ref, gub_ref):
            ref[...] = jnp.zeros_like(ref)

    @pl.when(step < half)
    def _():
        dy_ref[...] = dy_near_ref[...]

    @pl.when(step >= half)
    def _():
        dy_copy(step - half).wait()
        dy_ref[...] = dy_far[pl.ds(pl.multiple_of((step - half) * tile, tile), tile)]

    @pl.when(step == 0)
    def _():
        for copy in w_loads:
            copy.wait()

    attn_own(step).wait()
    for g in range(1, groups):
        attn_copy(g, step).wait()
    for g in range(groups):
        attn_all[:, pl.ds(pl.multiple_of(pair_of[g] * PAIR, PAIR), PAIR)] = attn_in[
            g, pl.ds(pl.multiple_of(step * tile, tile), tile)
        ]
    attn = attn_all[...]
    gain, bias, out_bias, down_bias = (vec_ref[i : i + 1, :] for i in range(2, 6))
    middle = (
        x_ref[...].astype(f32) + jnp.dot(attn, wo_ref[...], preferred_element_type=f32) + out_bias
    )
    unit, inv = norm_parts(middle)
    low = (unit * gain + bias).astype(bf16)
    dy = dy_ref[...]
    dy32 = dy.astype(f32)
    total = middle + down_bias
    d_low = jnp.zeros_like(middle)
    width = wu_ref.shape[1]
    for j in range(0, width, FF_TILE):
        part = pl.ds(j, FF_TILE)
        up = wu_ref[:, part]
        down = wd_ref[part, :]
        hidden = jnp.dot(low, up, preferred_element_type=f32) + ub_ref[:, part]
        cdf = 0.5 * (1.0 + lax.erf(hidden * (1.0 / math.sqrt(2.0))))
        active = (hidden * cdf).astype(bf16)
        slope = cdf + hidden * (jnp.exp2(hidden * hidden * (-0.5 * LOG2E)) * (1.0 / math.sqrt(2.0 * math.pi)))
        total = total + jnp.dot(active, down, preferred_element_type=f32)
        d_hidden = contract(dy, down, 1, 1) * slope
        d_hidden_low = d_hidden.astype(bf16)
        gub_ref[:, part] += jnp.sum(d_hidden, axis=0, keepdims=True)
        d_low = d_low + contract(d_hidden_low, up, 1, 1)
        gd_ref[part, :] += contract(active, dy, 0, 0)
        gu_ref[:, part] += contract(low, d_hidden_low, 0, 0)
    @pl.when(step < half)
    def _():
        y_out[step] = total.astype(bf16)

        @pl.when(stay)
        def _():
            y_own(step).start()

        @pl.when(leave)
        def _():
            y_copy(step).start()

    @pl.when(step >= half)
    def _():
        y_far_ref[...] = total.astype(bf16)

    scaled = d_low * gain
    d_middle = dy32 + inv * (
        scaled
        - jnp.mean(scaled, axis=-1, keepdims=True)
        - unit * jnp.mean(scaled * unit, axis=-1, keepdims=True)
    )
    dmid_ref[...] = d_middle
    branch = d_middle.astype(bf16)
    go_ref[...] += contract(attn, branch, 0, 0)
    gvec_ref[0:1, :] += jnp.sum(d_middle, axis=0, keepdims=True)
    gvec_ref[1:2, :] += jnp.sum(d_low * unit, axis=0, keepdims=True)
    gvec_ref[2:3, :] += jnp.sum(d_low, axis=0, keepdims=True)
    gvec_ref[3:4, :] += jnp.sum(dy32, axis=0, keepdims=True)
    attn_all[...] = contract(branch, wo_ref[...], 1, 1).astype(bf16)
    for g in (1, 3, 2, 0):
        do_out[step, g] = attn_all[:, pl.ds(pl.multiple_of(pair_of[g] * PAIR, PAIR), PAIR)]
        if g:
            do_copy(g, step).start()
        else:
            do_own(step).start()

    @pl.when(step == steps - 1)
    def _():
        shards = grad_ref.shape[0]
        d_model = x_ref.shape[1]
        down_rows, up_rows = gd_ref.shape[0] // shards, d_model // shards
        for j in range(shards):
            grad_ref[j, :down_rows] = gd_ref[j * down_rows : (j + 1) * down_rows].astype(bf16)
            rows = slice(j * up_rows, (j + 1) * up_rows)
            at = down_rows
            for t in range(0, width, d_model):
                grad_ref[j, at : at + up_rows] = gu_ref[rows, t : t + d_model].astype(bf16)
                at += up_rows
            grad_ref[j, at : at + up_rows] = go_ref[rows].astype(bf16)
        for j in range(2):
            grad_copy(j).start()
        for j in range(feed_steps):
            do_own(j).wait()
            for g in range(1, groups):
                do_copy(g, j).wait()
            if j < half:
                @pl.when(stay)
                def _():
                    y_own(j).wait()

                @pl.when(leave)
                def _():
                    y_copy(j).wait()
        sixth = keep_ref.shape[1]
        for j in range(2):
            grad_copy(j).wait()
        for dy_, dx_, ref in ((0, 0, keep_ref), (1, 0, to_y_ref), (0, 1, to_x_ref), (1, 1, to_xy_ref)):
            row = 1 - y if dy_ else y
            side = 1 - x if dx_ else x
            for p in range(PIECES):
                part = pl.ds(pl.multiple_of((2 * p + side) * sixth, 16), sixth)
                ref[p] = (
                    grad_ref[2 * row + c, part].astype(f32) + grad_in[row, part].astype(f32)
                ).astype(bf16)


def feed(o, x, dy_near, dy_in, w_out, w_up, w_down, vecs, up_bias, shards):
    groups, count, _ = o.shape
    width = x.shape[1]
    flat = (w_out.size + w_up.size + w_down.size) // shards // width
    tile = count // feed_steps
    piece = (PIECES, flat // PIECES // 2, width)
    rows = pl.BlockSpec((tile, width), lambda i: (i, 0))
    any_ = pl.BlockSpec(memory_space=pl.ANY)
    dma, buf, shape = pltpu.SemaphoreType.DMA, pltpu.VMEM, jax.ShapeDtypeStruct
    return pl.pallas_call(
        feed_kernel,
        grid=(feed_steps,),
        in_specs=[
            any_, rows, pl.BlockSpec((tile, width), lambda i: (jnp.minimum(i, feed_steps // 2 - 1), 0)), any_, any_, any_, any_,
            whole(vecs.shape), whole(up_bias.shape),
        ],
        out_specs=[any_, any_, pl.BlockSpec((tile, width), lambda i: (jnp.maximum(i - feed_steps // 2, 0), 0)), rows]
        + [whole(piece)] * 4 + [whole(vecs.shape), whole(up_bias.shape)],
        out_shape=[
            shape((groups, count, PAIR), bf16),
            shape((count // 2, width), bf16),
            shape((count // 2, width), bf16),
            shape((count, width), f32),
            shape(piece, bf16),
            shape(piece, bf16),
            shape(piece, bf16),
            shape(piece, bf16),
            shape(vecs.shape, f32),
            shape(up_bias.shape, f32),
        ],
        scratch_shapes=[
            buf((tile, width), bf16),
            buf(w_down.shape, f32),
            buf(w_up.shape, f32),
            buf(w_out.shape, f32),
            buf((groups, count, PAIR), bf16),
            buf((feed_steps, groups, tile, PAIR), bf16),
            buf((feed_steps // 2, tile, width), bf16),
            buf((shards, flat, width), bf16),
            buf((2, flat, width), bf16),
            buf(w_out.shape, bf16),
            buf(w_up.shape, bf16),
            buf(w_down.shape, bf16),
            buf((tile, width), bf16),
            buf((count // 2, width), bf16),
            dma((3,)),
            dma((3, feed_steps)),
            dma((3, feed_steps)),
            dma((feed_steps,)),
            dma((3, feed_steps)),
            dma((3, feed_steps)),
            dma((feed_steps,)),
            dma((feed_steps // 2,)),
            dma((feed_steps // 2,)),
            dma((feed_steps // 2,)),
            dma((2,)),
            dma((2,)),
            dma((feed_steps // 2,)),
            dma((feed_steps // 2,)),
        ],
        compiler_params=pltpu.CompilerParams(
            collective_id=3, has_side_effects=True, vmem_limit_bytes=60 * 1024 * 1024
        ),
        name="feed",
    )(o, x, dy_near, dy_in, w_out, w_up, w_down, vecs, up_bias)


TAIL_CHUNK = 128


def tail_kernel(
    d_qkv_hbm, ut_hbm, x_hbm, dmid_hbm, keep_hbm, from_y_hbm, from_x_hbm, from_xy_hbm, w_ref, vec_ref,
    gvecs_ref, gub_ref,
    home_buf, gfull, wall, sum_ref,
    keep_ref, from_y_ref, from_x_ref, from_xy_ref, d_qkv, ut_ref, total, sums, gw_ref, core_out, x_ref, dmid_ref, core_buf, own_dh, x_out, x_buf, dx_out,
    gsum, gz1s, gz1r, gz2s, gz2r,
    wy, ws, wz1s, wz1r, wz2s, wz2r, wfull,
    small_ref, small_out, small_in,
    load_sem, self_sem, core_s, core_r, x_s, x_r, home_s, home_r, g_s, g_r, w_s, w_r, s_s, s_r, in_sem,
):
    z, x, y, c = (lax.axis_index(name) for name in AXES)
    odd, upper = lax.rem(z, 2), lax.div(z, 2)
    width = x_ref.shape[1]
    chunks = x_ref.shape[0] // TAIL_CHUNK
    per_turn = chunks // 2
    by_core, by_x, by_y, by_xc = {"c": 1 - c}, {"x": 1 - x}, {"y": 1 - y}, {"x": 1 - x, "c": 1 - c}
    by_z1, by_z2 = {"z": z + 1 - 2 * odd}, {"z": z + 2 - 4 * upper}
    home = [{"z": 2 * c + upper, "c": odd}, {"z": 2 * c + 1 - upper, "c": odd}]
    origin = [{"z": 2 * odd + c, "c": upper}, {"z": 2 * (1 - odd) + c, "c": upper}]
    stay = (c == upper) & (odd == c)
    loads = []
    for i in range(chunks):
        part = pl.ds(i * TAIL_CHUNK, TAIL_CHUNK)
        loads.append(pltpu.make_async_copy(d_qkv_hbm.at[:, part], d_qkv.at[:, part], load_sem.at[i]))
    inputs = [
        pltpu.make_async_copy(src, dst, in_sem.at[i])
        for i, (src, dst) in enumerate(((ut_hbm, ut_ref), (x_hbm, x_ref), (dmid_hbm, dmid_ref)))
    ]
    g_loads = [
        pltpu.make_async_copy(src, dst, in_sem.at[3 + i])
        for i, (src, dst) in enumerate((
            (keep_hbm, keep_ref), (from_y_hbm, from_y_ref), (from_x_hbm, from_x_ref), (from_xy_hbm, from_xy_ref)
        ))
    ]
    for copy in loads[:2] + g_loads + loads[2:] + inputs:
        copy.start()
    small_ref[...] = jnp.zeros_like(small_ref)
    small_ref[2:4] = gvecs_ref[1:3]
    small_ref[4:5] = gvecs_ref[0:1]
    small_ref[5:6] = gvecs_ref[3:4]
    for i in range(4):
        small_ref[6 + i : 7 + i] = gub_ref[:, i * width : (i + 1) * width]
    greet(
        [by_core, by_x, by_y, by_xc, by_z1, by_z2, home[1], origin[1]],
        [home[0], origin[0]],
        jnp.logical_not(stay),
    )
    small_peers = [by_core, by_y, by_z1, by_z2, by_x]
    to_core, w_copy, s_copy = [], {}, []

    def share(i):
        part = pl.ds(i * TAIL_CHUNK, TAIL_CHUNK)
        loads[i].wait()
        for g in (3, 2, 1, 0):
            value = contract(d_qkv[g, part], w_ref[...], 1, 1)
            if g >= 2:
                core_out[g - 2, part] = value.astype(bf16)
            else:
                own_dh[g, part] = value
            if g == 2:
                to_core.append(
                    send(core_out.at[:, part], core_buf.at[:, part], core_s, core_r, i, by_core)
                )

    def weight(g):
        if g == 0:
            inputs[0].wait()
        rows = d_qkv[g]
        part = jnp.dot(ut_ref[:, g * rows.shape[0] : (g + 1) * rows.shape[0]], rows, preferred_element_type=f32)
        line = jnp.sum(rows.astype(f32), axis=0, keepdims=True)
        total[...] = part if g == 0 else total[...] + part
        sums[...] = line if g == 0 else sums[...] + line

    def weight_close():
        shard = gw_ref.shape[1]
        for j in range(gw_ref.shape[0]):
            part = pl.ds(j * shard, shard)
            gain, bias = (jnp.broadcast_to(ref[:, part], (shard, shard)).T[:, :1] for ref in (vec_ref.at[0:1], vec_ref.at[1:2]))
            gw_ref[j] = (total[part] * gain + bias * sums[...]).astype(bf16)
            w = w_ref[part].astype(f32)
            for i, term in enumerate((w * total[part], w * sums[...])):
                column = jnp.sum(term, axis=1, keepdims=True)
                small_ref[i : i + 1, part] = jnp.broadcast_to(column, (shard, shard)).T[:1]
        s_copy.append(send(small_ref, small_in.at[0], s_s, s_r, 0, small_peers[0]))
        w_copy["y"] = send(gw_ref.at[pl.ds(2 * (1 - y), 2)], wy, w_s, w_r, 0, by_y)

    g_copy = {}

    def g_start(p):
        if p == 0:
            for copy in g_loads:
                copy.wait()
        for half in range(2):
            part = pl.ds(96 * half, 96)
            gsum[p, part] = (
                keep_ref[p, part].astype(f32)
                + from_y_ref[p, part].astype(f32)
                + from_x_ref[p, part].astype(f32)
                + from_xy_ref[p, part].astype(f32)
            )
        gz1s[p] = gsum[p, pl.ds(pl.multiple_of(96 * (1 - odd), 16), 96)].astype(bf16)
        g_copy["z1", p] = send(gz1s.at[p], gz1r.at[p], g_s, g_r, 5 * p, by_z1)

    mine_half = pl.multiple_of(96 * odd, 16)
    mine_quarter = pl.multiple_of(96 * odd + 48 * upper, 16)
    give_quarter = pl.multiple_of(96 * odd + 48 * (1 - upper), 16)

    def g_second(p):
        g_copy["z1", p].wait()
        gsum[p, pl.ds(mine_half, 96)] += gz1r[p].astype(f32)
        gz2s[p] = gsum[p, pl.ds(give_quarter, 48)].astype(bf16)
        g_copy["z2", p] = send(gz2s.at[p], gz2r.at[p], g_s, g_r, 5 * p + 1, by_z2)

    def g_third(p):
        g_copy["z2", p].wait()
        part = pl.ds(mine_quarter, 48)
        gfull[p, x, part] = (gsum[p, part] + gz2r[p].astype(f32)).astype(bf16)
        place_ = gfull.at[p, x, part]
        g_copy["z2b", p] = send(place_, place_, g_s, g_r, 5 * p + 2, by_z2)

    def g_fourth(p):
        g_copy["z2b", p].wait()
        place_ = gfull.at[p, x, pl.ds(mine_half, 96)]
        g_copy["z1b", p] = send(place_, place_, g_s, g_r, 5 * p + 3, by_z1)

    def g_fifth(p):
        g_copy["z1b", p].wait()
        g_copy["x", p] = send(gfull.at[p, x], gfull.at[p, x], g_s, g_r, 5 * p + 4, by_x)

    def w_second():
        w_copy["y"].wait()
        for i in range(2):
            ws[i] = gw_ref[2 * y + i].astype(f32) + wy[i].astype(f32)
        wz1s[...] = ws[1 - odd].astype(bf16)
        w_copy["z1"] = send(wz1s, wz1r, w_s, w_r, 1, by_z1)

    def w_third():
        w_copy["z1"].wait()
        ws[odd] += wz1r[...].astype(f32)
        wz2s[...] = ws[odd, pl.ds(pl.multiple_of(64 * (1 - upper), 64), 64)].astype(bf16)
        w_copy["z2"] = send(wz2s, wz2r, w_s, w_r, 2, by_z2)

    def w_fourth():
        w_copy["z2"].wait()
        part = pl.ds(pl.multiple_of(64 * upper, 64), 64)
        wfull[odd, part] = (ws[odd, part] + wz2r[...].astype(f32)).astype(bf16)
        place_ = wfull.at[odd, part]
        w_copy["z2b"] = send(place_, place_, w_s, w_r, 3, by_z2)

    def w_fifth():
        w_copy["z2b"].wait()
        w_copy["z1b"] = send(wfull.at[odd], wfull.at[odd], w_s, w_r, 4, by_z1)

    def w_sixth():
        w_copy["z1b"].wait()
        mine = 2 * x + c
        w_copy["core"] = send(wfull.at[1 - c], wall.at[mine], w_s, w_r, 5, by_core)
        w_copy["x"] = send(wfull.at[c], wall.at[mine], w_s, w_r, 6, by_x)
        w_copy["xc"] = send(wfull.at[1 - c], wall.at[mine], w_s, w_r, 7, by_xc)

    def s_next(step):
        s_copy[step].wait()
        before = small_ref[...] if step == 0 else small_out[step - 1]
        small_out[step] = before + small_in[step]
        if step + 1 < len(small_peers):
            s_copy.append(
                send(small_out.at[step], small_in.at[step + 1], s_s, s_r, step + 1, small_peers[step + 1])
            )

    x_copy, home_copy = [], []

    def add_core(i):
        part = pl.ds(i * TAIL_CHUNK, TAIL_CHUNK)
        to_core[i].wait()
        x_out[part] = (own_dh[1, part] + core_buf[1, part].astype(f32)).astype(bf16)
        x_copy.append(send(x_out.at[part], x_buf.at[part], x_s, x_r, i, by_x))

    def finish(i):
        part = pl.ds(i * TAIL_CHUNK, TAIL_CHUNK)
        if i == 0:
            for copy in inputs[1:]:
                copy.wait()
        x_copy[i].wait()
        d_low = own_dh[0, part] + core_buf[0, part].astype(f32) + x_buf[part].astype(f32)
        unit, inv = norm_parts(x_ref[part].astype(f32))
        scaled = d_low * vec_ref[0:1]
        dx = dmid_ref[part] + inv * (
            scaled
            - jnp.mean(scaled, axis=-1, keepdims=True)
            - unit * jnp.mean(scaled * unit, axis=-1, keepdims=True)
        )
        dx_out[part] = dx.astype(bf16)
        turn, row = i // per_turn, (i % per_turn) * TAIL_CHUNK
        target = home_buf.at[upper, pl.ds(row, TAIL_CHUNK)]
        if turn == 0:
            @pl.when(stay)
            def _():
                pltpu.make_async_copy(dx_out.at[part], target, self_sem.at[i]).start()

            @pl.when(jnp.logical_not(stay))
            def _():
                send(dx_out.at[part], target, home_s, home_r, i, home[0])
        else:
            send(dx_out.at[part], target, home_s, home_r, i, home[1])

    def arrive(i):
        part = pl.ds(i * TAIL_CHUNK, TAIL_CHUNK)
        turn, row = i // per_turn, (i % per_turn) * TAIL_CHUNK
        block = odd if turn == 0 else 1 - odd
        landed = home_buf.at[block, pl.ds(row, TAIL_CHUNK)]

        def remote():
            copy = pltpu.make_async_remote_copy(
                src_ref=dx_out.at[part], dst_ref=landed, send_sem=home_s.at[i], recv_sem=home_r.at[i],
                device_id=home[turn], device_id_type=MESH,
            )
            copy.wait_send()
            copy.wait_recv()

        if turn == 0:
            @pl.when(stay)
            def _():
                pltpu.make_async_copy(dx_out.at[part], landed, self_sem.at[i]).wait()

            pl.when(jnp.logical_not(stay))(remote)
        else:
            remote()

    share(0)
    share(1)
    add_core(0)
    share(2)
    g_start(0)
    add_core(1)
    share(3)
    g_start(1)
    add_core(2)
    share(4)
    g_start(2)
    add_core(3)
    share(5)
    share(6)
    add_core(4)
    share(7)
    add_core(5)
    weight(0)
    weight(1)
    weight(2)
    weight(3)
    weight_close()
    g_second(0)
    g_second(1)
    g_second(2)
    add_core(6)
    add_core(7)
    s_next(0)
    w_second()
    finish(0)
    g_third(0)
    g_third(1)
    g_third(2)
    s_next(1)
    w_third()
    finish(1)
    g_fourth(0)
    g_fourth(1)
    g_fourth(2)
    s_next(2)
    w_fourth()
    finish(2)
    g_fifth(0)
    g_fifth(1)
    g_fifth(2)
    w_fifth()
    s_next(3)
    finish(3)
    w_sixth()
    finish(4)
    s_next(4)
    finish(5)
    finish(6)
    finish(7)
    w_copy["core"].wait()
    w_copy["x"].wait()
    w_copy["xc"].wait()
    wall[2 * x + c] = wfull[c]
    sum_ref[...] = small_out[4]
    for i in range(chunks):
        arrive(i)
    for p in range(PIECES):
        g_copy["x", p].wait()


def tail(d_qkv, unit_t, x, dmid, keep, from_y, from_x, from_xy, weight, vecs, gvecs, gub):
    count, width = x.shape
    shard = width // 4
    half = count // 2
    chunks = count // TAIL_CHUNK
    sixth = keep.shape[1]
    vmem = pl.BlockSpec(memory_space=pltpu.VMEM)
    dma = pltpu.SemaphoreType.DMA
    buf = pltpu.VMEM
    return pl.pallas_call(
        tail_kernel,
        in_specs=[pl.BlockSpec(memory_space=pl.ANY)] * 8 + [vmem] * 4,
        out_specs=[vmem] * 4,
        out_shape=[
            jax.ShapeDtypeStruct((2, half, width), bf16),
            jax.ShapeDtypeStruct((PIECES, 2, sixth, width), bf16),
            jax.ShapeDtypeStruct((4, shard, 3 * PAIR), bf16),
            jax.ShapeDtypeStruct((16, width), f32),
        ],
        scratch_shapes=[
            buf(keep.shape, bf16),
            buf(keep.shape, bf16),
            buf(keep.shape, bf16),
            buf(keep.shape, bf16),
            buf(d_qkv.shape, bf16),
            buf(unit_t.shape, bf16),
            buf(weight.shape, f32),
            buf((1, 3 * PAIR), f32),
            buf((4, shard, 3 * PAIR), bf16),
            buf((2, count, width), bf16),
            buf((count, width), bf16),
            buf((count, width), f32),
            buf((2, count, width), bf16),
            buf((2, count, width), f32),
            buf((count, width), bf16),
            buf((count, width), bf16),
            buf((count, width), bf16),
            buf((PIECES, sixth, width), f32),
            buf((PIECES, sixth // 2, width), bf16),
            buf((PIECES, sixth // 2, width), bf16),
            buf((PIECES, sixth // 4, width), bf16),
            buf((PIECES, sixth // 4, width), bf16),
            buf((2, shard, 3 * PAIR), bf16),
            buf((2, shard, 3 * PAIR), f32),
            buf((shard, 3 * PAIR), bf16),
            buf((shard, 3 * PAIR), bf16),
            buf((shard // 2, 3 * PAIR), bf16),
            buf((shard // 2, 3 * PAIR), bf16),
            buf((2, shard, 3 * PAIR), bf16),
            buf((16, width), f32),
            buf((5, 16, width), f32),
            buf((5, 16, width), f32),
            dma((chunks,)),
            dma((chunks // 2,)),
            dma((chunks,)),
            dma((chunks,)),
            dma((chunks,)),
            dma((chunks,)),
            dma((chunks,)),
            dma((chunks,)),
            dma((5 * PIECES,)),
            dma((5 * PIECES,)),
            dma((8,)),
            dma((8,)),
            dma((5,)),
            dma((5,)),
            dma((7,)),
        ],
        compiler_params=pltpu.CompilerParams(
            collective_id=5, has_side_effects=True, vmem_limit_bytes=60 * 1024 * 1024
        ),
        name="tail",
    )(d_qkv, unit_t, x, dmid, keep, from_y, from_x, from_xy, weight, vecs, gvecs, gub)

def results_kernel(
    y_near_ref, y_far_ref, dx_ref, down_ref, up_ref, out_ref, wall_ref, sum_ref,
    y_out, dx_out, gd_ref, gu_ref, go_ref, gq_ref, *vectors,
):
    step = pl.program_id(0)
    width = dx_ref.shape[-1]
    odd = lax.rem(lax.axis_index("z"), 2)
    y_out[odd, 0] = y_near_ref[...]
    y_out[1 - odd, 0] = y_far_ref[...]
    dx_out[:, 0] = dx_ref[...].astype(f32)
    gd_ref[...] = down_ref[...].astype(f32)
    gu_ref[...] = up_ref[...].astype(f32)
    go_ref[...] = out_ref[...].astype(f32)
    for part in range(3):
        at = pl.multiple_of(part * width + step * PAIR, PAIR)
        gq_ref[:, pl.ds(at, PAIR)] = wall_ref[0, :, part * PAIR : (part + 1) * PAIR].astype(f32)
    shard = go_ref.shape[0]
    mine = 2 * lax.axis_index("y") + lax.axis_index("c")
    for i in range(6):
        vectors[i][...] = sum_ref[i : i + 1, pl.ds(pl.multiple_of(mine * shard, shard), shard)]
    vectors[6][...] = sum_ref[pl.ds(6 + mine, 1), :]


def results(y_near, y_far, dx, flat, wall, sums):
    half, width = dx.shape[1:]
    shard = wall.shape[1]
    steps = 4
    flat = flat.reshape(-1, width)
    tokens = pl.BlockSpec((2, half // steps, width), lambda i: (0, i, 0))
    tokens_out = pl.BlockSpec((2, 1, half // steps, width), lambda i: (0, 0, i, 0))
    shape = jax.ShapeDtypeStruct
    return pl.pallas_call(
        results_kernel,
        grid=(steps,),
        in_specs=[
            pl.BlockSpec((half // steps, width), lambda i: (i, 0)),
            pl.BlockSpec((half // steps, width), lambda i: (i, 0)),
            tokens,
            pl.BlockSpec((shard, width), lambda i: (i, 0)),
            pl.BlockSpec((shard, width), lambda i: (steps + i, 0)),
            pl.BlockSpec((shard, width), lambda i: (2 * steps, 0)),
            pl.BlockSpec((1, shard, 3 * PAIR), lambda i: (i, 0, 0)),
            whole(sums.shape),
        ],
        out_specs=[
            tokens_out,
            tokens_out,
            pl.BlockSpec((shard, width), lambda i: (i, 0)),
            pl.BlockSpec((shard, width), lambda i: (0, i)),
            whole((shard, width)),
            whole((shard, 3 * width)),
        ]
        + [whole((1, shard))] * 6
        + [whole((1, width))],
        out_shape=[
            shape((2, 1, half, width), bf16),
            shape((2, 1, half, width), f32),
            shape((width, width), f32),
            shape((shard, 4 * width), f32),
            shape((shard, width), f32),
            shape((shard, 3 * width), f32),
        ]
        + [shape((1, shard), f32)] * 6
        + [shape((1, width), f32)],
        compiler_params=pltpu.CompilerParams(vmem_limit_bytes=60 * 1024 * 1024),
        name="results",
    )(y_near, y_far, dx, flat, flat, flat, wall, sums)


def place(z, x, y, c):
    return ((z * SIZES[1] + x) * SIZES[2] + y) * SIZES[3] + c


def everyone():
    return [
        (z, x, y, c)
        for z in range(SIZES[0])
        for x in range(SIZES[1])
        for y in range(SIZES[2])
        for c in range(SIZES[3])
    ]


def swap_pairs(dx, dy, dc):
    return [(place(z, x, y, c), place(z, x ^ dx, y ^ dy, c ^ dc)) for z, x, y, c in everyone()]


def move(value, pairs):
    return lax.ppermute(value, AXES, pairs)


def swap(value, dx=0, dy=0, dc=0):
    return move(value, swap_pairs(dx, dy, dc))


def paired_body(
    inputs, out_grad, segment_ids, block_order, w_qkv, w_out, w_up, w_down,
    norm1_gain, norm1_bias, norm2_gain, norm2_bias, out_bias, up_bias, down_bias,
):
    vectors = (norm1_gain, norm1_bias, norm2_gain, norm2_bias, out_bias, down_bias, up_bias)
    (
        qt, k, kt, v, vt, unit, own_x, full_out, full_up, full_down, near_dy, w_heads, vecs, full_ubias, start, tab
    ) = head(
        inputs, out_grad, segment_ids.reshape(2, -1, 128), block_order, vectors, w_qkv, w_out, w_up, w_down
    )
    o, ot, lse = attend(tab, qt, start, k, vt)
    d_o, y_near, y_far, d_middle, keep, to_y, to_x, to_xy, g_vecs, g_ubias = feed(
        o.reshape(4, -1, PAIR), own_x, near_dy, out_grad, full_out, full_up, full_down, vecs, full_ubias, 4
    )
    y_far = move(y_far, [(place(z, x, y, c), place(2 * c + 1 - z // 2, x, y, z % 2)) for z, x, y, c in everyone()])
    from_y, from_x, from_xy = swap(to_y, dy=1), swap(to_x, dx=1), swap(to_xy, dy=1, dx=1)
    d_qkv = attend_back(tab, k, kt, v, qt, start, d_o.reshape(-1, PAIR), ot, lse)
    dx, flat, heads, sums = tail(
        d_qkv.reshape(4, -1, 3 * PAIR), unit, own_x, d_middle, keep, from_y, from_x, from_xy,
        w_heads, vecs, g_vecs, g_ubias,
    )
    outputs, input_grad, grad_down, grad_up, grad_out, grad_qkv, *vec = results(
        y_near, y_far, dx, flat, heads, sums
    )
    vec = [member.reshape(-1) for member in vec]
    return (
        outputs, input_grad, grad_qkv, grad_out, grad_up, grad_down,
        vec[0], vec[1], vec[2], vec[3], vec[4], vec[6], vec[5],
    )


def solution(mesh):
    paired = mesh.shape["ctx"] == SIZES[0] * SIZES[1] and mesh.shape["fsdp"] == SIZES[2] * SIZES[3]
    if paired:
        mesh = Mesh(mesh.devices.reshape(SIZES), AXES)
        ctx, fsdp, program = ("z", "x"), ("y", "c"), paired_body
    else:
        ctx, fsdp, program = "ctx", "fsdp", general_body
    tokens = P(None, fsdp, ctx, None)
    matrix, vector = P(fsdp, None), P(fsdp)
    return jax.shard_map(
        program,
        mesh=mesh,
        in_specs=(tokens, tokens, P(None, fsdp, ctx), P()) + (matrix,) * 4 + (vector,) * 7,
        out_specs=(tokens, tokens) + (matrix,) * 4 + (vector,) * 7,
        check_vma=False,
    )
```

```python
import functools
import math

import jax
import jax.numpy as jnp
from jax import lax
from jax.experimental import pallas as pl
from jax.experimental.pallas import tpu as pltpu
from jax.sharding import Mesh
from jax.sharding import PartitionSpec as P

H = 8
HD = 64
BLK = 256
PAIR = 2 * HD

norm_eps = 1e-05
mask_fill = -1e30
LOG2E = math.log2(math.e)
LN2 = math.log(2.0)
SCORE_SCALE = 1.0 / math.sqrt(HD)

f32 = jnp.float32
bf16 = jnp.bfloat16


def contract(a, b, da, db):
    return lax.dot_general(a, b, (((da,), (db,)), ((), ())), preferred_element_type=f32)


def norm_parts(values):
    center = values - jnp.mean(values, axis=-1, keepdims=True)
    spread = jnp.mean(center * center, axis=-1, keepdims=True)
    inv = lax.rsqrt(spread + norm_eps)
    return center * inv, inv


def whole(shape):
    zeros = (0,) * len(shape)
    return pl.BlockSpec(shape, lambda *_: zeros)


def two_heads(block):
    zero = jnp.zeros((HD, block.shape[1]), block.dtype)
    return jnp.concatenate(
        [jnp.concatenate([block[:HD], zero], axis=0), jnp.concatenate([zero, block[HD:]], axis=0)], axis=1
    )


EXTRA = 16


def attend_kernel(
    tab_ref, qt_ref, start_ref, k_ref, vt_ref, o_hbm, ot_hbm, lse_ref, acc, top, o_buf, ot_buf, out_sem
):
    blocks = start_ref.shape[0]
    row = lax.broadcasted_iota(jnp.int32, (BLK, 2 * BLK), 0)
    reach = row - jnp.bitwise_and(lax.broadcasted_iota(jnp.int32, (BLK, 2 * BLK), 1), BLK - 1)
    ones = jnp.ones((EXTRA, 2 * BLK), bf16)

    def place_of(b):
        return pl.ds(pl.multiple_of(tab_ref[2, jnp.maximum(b, 0)] * BLK, BLK), BLK)

    def visits_of(qb):
        return (qb - tab_ref[0, qb]) // 2 + 1

    def visit(qb, i, bounded, live=True):
        kb = qb - 2 * i
        both = two_heads(qt_ref[:, place_of(qb)])
        start = jnp.concatenate([start_ref[qb], start_ref[qb]], axis=1)
        places = [place_of(kb), place_of(kb - 1)]
        terms = []
        for n in range(2):
            first_row = start - (kb - n) * BLK
            allowed = row >= (first_row if live is True else jnp.where(live, first_row, BLK))
            if n == 0:
                allowed = allowed & (reach <= (qb - kb) * BLK)
            st = jnp.dot(k_ref[places[n], :], both, preferred_element_type=f32)
            terms.append(jnp.where(allowed, st, mask_fill))
        if bounded:
            probs = [jnp.exp2(term).astype(bf16) for term in terms]
        else:
            old = top[qb]
            peak = jnp.maximum(
                jnp.max(terms[0], axis=0, keepdims=True), jnp.max(terms[1], axis=0, keepdims=True)
            )
            peak = jnp.maximum(old, peak)
            shrink = jnp.exp2(old - peak)
            top[qb] = peak
            probs = [jnp.exp2(term - peak).astype(bf16) for term in terms]
        probs = jnp.concatenate(probs, axis=0)
        vt = jnp.concatenate([vt_ref[:, places[0]], vt_ref[:, places[1]]], axis=1)
        parts = []
        for head in range(2):
            cols = slice(head * BLK, (head + 1) * BLK)
            left = jnp.concatenate([vt[head * HD : (head + 1) * HD], ones], axis=0)
            part = jnp.dot(left, probs[:, cols], preferred_element_type=f32)
            parts.append(part)
            if not bounded:
                acc[qb, head] = part + acc[qb, head] * shrink[:, cols]
        return parts

    def all_visits(bounded):
        count = lax.fori_loop(0, blocks, lambda b, n: n + visits_of(b), 0)

        def following(qb, i):
            more = i + 1 < visits_of(qb)
            return jnp.where(more, qb, jnp.minimum(qb + 1, blocks - 1)), jnp.where(more, i + 1, 0)

        def step(n, state):
            if not bounded:
                visit(*state, False)
                return following(*state)
            second = following(*state)
            members = [visit(*state, True), visit(*second, True, 2 * n + 1 < count)]
            for (qb, _), parts in zip((state, second), members):
                for head in range(2):
                    acc[qb, head] += parts[head]
            return following(*second)

        lax.fori_loop(0, (count + 1) // 2 if bounded else count, step, (jnp.int32(0), jnp.int32(0)))

    small = tab_ref[3, 0] > 0
    acc[...] = jnp.zeros_like(acc)

    @pl.when(small)
    def _():
        top[...] = jnp.zeros_like(top)
        all_visits(True)

    @pl.when(jnp.logical_not(small))
    def _():
        top[...] = jnp.full_like(top, mask_fill)
        all_visits(False)

    def outgoing(b):
        at = place_of(b)
        return (
            pltpu.make_async_copy(o_buf.at[b], o_hbm.at[at], out_sem.at[0]),
            pltpu.make_async_copy(ot_buf.at[b], ot_hbm.at[b], out_sem.at[1]),
        )

    def close(b):
        total = jnp.concatenate([acc[b, 0, HD : HD + 1], acc[b, 1, HD : HD + 1]], axis=1)
        lse_ref[b] = top[b] + jnp.log2(total)
        heads = jnp.concatenate([acc[b, h, :HD] / acc[b, h, HD : HD + 1] for h in range(2)], axis=0)
        ot_buf[b] = heads
        o_buf[b] = heads.T.astype(bf16)
        for copy in outgoing(b):
            copy.start()

    def close_two(n, carry):
        close(2 * n)
        close(2 * n + 1)
        return carry

    lax.fori_loop(0, blocks // 2, close_two, 0)
    for whole_copy in (
        pltpu.make_async_copy(ot_buf, ot_hbm, out_sem.at[1]),
        pltpu.make_async_copy(o_hbm, o_hbm, out_sem.at[0]),
    ):
        whole_copy.wait()


def attend(tab, qt, start, k, vt):
    count = k.shape[0]
    blocks = count // BLK
    vmem, any_ = pl.BlockSpec(memory_space=pltpu.VMEM), pl.BlockSpec(memory_space=pl.ANY)
    return pl.pallas_call(
        attend_kernel,
        grid_spec=pltpu.PrefetchScalarGridSpec(
            num_scalar_prefetch=1,
            grid=(),
            in_specs=[vmem] * 4,
            out_specs=[any_, any_, vmem],
            scratch_shapes=[
                pltpu.VMEM((blocks, 2, HD + EXTRA, BLK), f32),
                pltpu.VMEM((blocks, 1, 2 * BLK), f32),
                pltpu.VMEM((blocks, BLK, PAIR), bf16),
                pltpu.VMEM((blocks, PAIR, BLK), f32),
                pltpu.SemaphoreType.DMA((2,)),
            ],
        ),
        out_shape=[
            jax.ShapeDtypeStruct((count, PAIR), bf16),
            jax.ShapeDtypeStruct((blocks, PAIR, BLK), f32),
            jax.ShapeDtypeStruct((blocks, 1, 2 * BLK), f32),
        ],
        name="attend",
    )(tab, qt, start, k, vt)


def split_heads(block):
    lane = lax.broadcasted_iota(jnp.int32, block.shape, 1)
    zero = jnp.zeros_like(block)
    first = lane < HD
    return jnp.concatenate([jnp.where(first, block, zero), jnp.where(first, zero, block)], axis=0)


def attend_back_kernel(
    tab_ref, k_hbm, kt_hbm, v_hbm, qt_ref, start_ref, do_ref, ot_ref, lse_ref, out_hbm,
    k_ref, kt_ref, v_ref, out_buf, dqt, dk, dv, dot, dom, qm, delta, in_sem, out_sem,
):
    blocks = start_ref.shape[0]
    row = lax.broadcasted_iota(jnp.int32, (BLK, 2 * BLK), 0)
    reach = row - jnp.bitwise_and(lax.broadcasted_iota(jnp.int32, (BLK, 2 * BLK), 1), BLK - 1)
    loads = [
        pltpu.make_async_copy(src, dst, in_sem.at[i])
        for i, (src, dst) in enumerate(((k_hbm, k_ref), (kt_hbm, kt_ref), (v_hbm, v_ref)))
    ]
    for copy in loads:
        copy.start()

    def at(b):
        return pl.ds(pl.multiple_of(tab_ref[2, b] * BLK, BLK), BLK)

    def prepare(qb):
        dqt[qb] = jnp.zeros((PAIR, BLK), f32)
        dk[qb] = jnp.zeros((BLK, PAIR), f32)
        dv[qb] = jnp.zeros((BLK, PAIR), f32)
        d_out = do_ref[at(qb), :]
        dom[qb] = split_heads(d_out)
        qm[qb] = split_heads(qt_ref[:, at(qb)].T)
        turned = d_out.astype(f32).T
        dot[qb] = turned.astype(bf16)
        both = turned * ot_ref[qb]
        delta[qb] = jnp.concatenate(
            [jnp.sum(both[:HD], axis=0, keepdims=True), jnp.sum(both[HD:], axis=0, keepdims=True)], axis=1
        )

    def prepare_two(n, carry):
        prepare(2 * n)
        prepare(2 * n + 1)
        return carry

    lax.fori_loop(0, blocks // 2, prepare_two, 0)
    for copy in loads:
        copy.wait()

    def tile(kb, qb, live):
        kt = kt_ref[:, at(kb)]
        start = jnp.concatenate([start_ref[qb], start_ref[qb]], axis=1)
        st = jnp.dot(k_ref[at(kb), :], two_heads(qt_ref[:, at(qb)]), preferred_element_type=f32)
        dpt = jnp.dot(v_ref[at(kb), :], two_heads(dot[qb]), preferred_element_type=f32)
        allowed = (row >= start - kb * BLK) & (reach <= jnp.where(live, (qb - kb) * BLK, -2 * BLK))
        pt = jnp.exp2(jnp.where(allowed, st - lse_ref[qb], mask_fill))
        dst = (pt * (dpt - delta[qb])).astype(bf16)
        part_v = jnp.dot(pt.astype(bf16), dom[qb], preferred_element_type=f32)
        part_k = jnp.dot(dst, qm[qb], preferred_element_type=f32)
        part_q = [
            jnp.dot(kt[head * HD : (head + 1) * HD], dst[:, head * BLK : (head + 1) * BLK], preferred_element_type=f32)
            for head in range(2)
        ]
        return kb, qb, part_v, part_k, jnp.concatenate(part_q, axis=0)

    def add(kb, qb, part_v, part_k, part_q):
        dv[kb] += part_v
        dk[kb] += part_k
        dqt[qb] += part_q

    def following(kb, qb):
        more = qb < tab_ref[1, kb]
        beyond = jnp.minimum(kb + 1, blocks - 1)
        return jnp.where(more, kb, beyond), jnp.where(more, qb + 1, beyond)

    tiles = lax.fori_loop(0, blocks, lambda b, n: n + tab_ref[1, b] - b + 1, 0)

    def step(n, state):
        second = following(*state)
        terms = [tile(*state, True), tile(*second, 2 * n + 1 < tiles)]
        for term in terms:
            add(*term)
        return following(*second)

    lax.fori_loop(0, (tiles + 1) // 2, step, (jnp.int32(0), jnp.int32(0)))
    def close(b):
        out_buf[b] = jnp.concatenate([(dqt[b] * SCORE_SCALE).T, dk[b] * LN2, dv[b]], axis=1).astype(bf16)
        pltpu.make_async_copy(out_buf.at[b], out_hbm.at[at(b)], out_sem.at[0]).start()

    def close_four(n, carry):
        for i in range(4):
            close(4 * n + i)
        return carry

    lax.fori_loop(0, blocks // 4, close_four, 0)
    pltpu.make_async_copy(out_hbm, out_hbm, out_sem.at[0]).wait()


def attend_back(tab, k, kt, v, qt, start, d_out, ot, lse):
    count = k.shape[0]
    blocks = count // BLK
    vmem, any_ = pl.BlockSpec(memory_space=pltpu.VMEM), pl.BlockSpec(memory_space=pl.ANY)
    buf = pltpu.VMEM
    return pl.pallas_call(
        attend_back_kernel,
        grid_spec=pltpu.PrefetchScalarGridSpec(
            num_scalar_prefetch=1,
            grid=(),
            in_specs=[any_] * 3 + [vmem] * 5,
            out_specs=any_,
            scratch_shapes=[
                buf(k.shape, bf16),
                buf(kt.shape, bf16),
                buf(v.shape, bf16),
                buf((blocks, BLK, 3 * PAIR), bf16),
                buf((blocks, PAIR, BLK), f32),
                buf((blocks, BLK, PAIR), f32),
                buf((blocks, BLK, PAIR), f32),
                buf((blocks, PAIR, BLK), bf16),
                buf((blocks, 2 * BLK, PAIR), bf16),
                buf((blocks, 2 * BLK, PAIR), bf16),
                buf((blocks, 1, 2 * BLK), f32),
                pltpu.SemaphoreType.DMA((3,)),
                pltpu.SemaphoreType.DMA((1,)),
            ],
        ),
        out_shape=jax.ShapeDtypeStruct((count, 3 * PAIR), bf16),
        compiler_params=pltpu.CompilerParams(vmem_limit_bytes=60 * 1024 * 1024),
        name="attend_back",
    )(tab, k, kt, v, qt, start, d_out, ot, lse)


def layer_norm(values, gain_vec, offset):
    center = values - jnp.mean(values, axis=-1, keepdims=True)
    spread = jnp.mean(center * center, axis=-1, keepdims=True)
    return center * lax.rsqrt(spread + norm_eps) * gain_vec + offset


def gelu_exact(values):
    return 0.5 * values * (1.0 + lax.erf(values * (1.0 / math.sqrt(2.0))))


def score_block(query_heads, key_heads, query_doc, query_pos, key_doc, key_pos):
    raw_scores = jnp.einsum(
        "qhd,khd->hqk", query_heads, key_heads, preferred_element_type=jnp.float32
    ) * (1.0 / math.sqrt(HD))
    allowed = (query_doc[:, None] == key_doc[None, :]) & (key_pos[None, :] <= query_pos[:, None])
    return (raw_scores, allowed[None])


def soft_block(raw_scores, allowed, log_norm):
    return jnp.exp(jnp.where(allowed, raw_scores, mask_fill) - log_norm[:, :, None])


def row_log_norm(query_heads, key_blocks, doc_blocks, pos_blocks, query_doc, query_pos):

    def row_visit(running, block_item):
        row_top, row_sum = running
        key_heads, key_doc, key_pos = block_item
        raw_scores, allowed = score_block(
            query_heads, key_heads, query_doc, query_pos, key_doc, key_pos
        )
        masked = jnp.where(allowed, raw_scores, mask_fill)
        new_top = jnp.maximum(row_top, jnp.max(masked, axis=-1))
        fresh = jnp.sum(jnp.where(allowed, jnp.exp(masked - new_top[:, :, None]), 0.0), axis=-1)
        return ((new_top, row_sum * jnp.exp(row_top - new_top) + fresh), None)

    query_count = query_doc.shape[0]
    start = (
        jnp.full((H, query_count), mask_fill, jnp.float32),
        jnp.zeros((H, query_count), jnp.float32),
    )
    (row_top, row_sum), unused = lax.scan(row_visit, start, (key_blocks, doc_blocks, pos_blocks))
    return row_top + jnp.log(row_sum)


def attend_all(
    query_heads, key_blocks, value_blocks, doc_blocks, pos_blocks, query_doc, query_pos, log_norm
):

    def attend_visit(accum_out, block_item):
        key_heads, value_heads, key_doc, key_pos = block_item
        raw_scores, allowed = score_block(
            query_heads, key_heads, query_doc, query_pos, key_doc, key_pos
        )
        soft_low = soft_block(raw_scores, allowed, log_norm).astype(jnp.bfloat16)
        return (
            accum_out
            + jnp.einsum("hqk,khd->qhd", soft_low, value_heads, preferred_element_type=jnp.float32),
            None,
        )

    start = jnp.zeros(query_heads.shape, jnp.float32)
    accum_out, unused = lax.scan(
        attend_visit, start, (key_blocks, value_blocks, doc_blocks, pos_blocks)
    )
    return accum_out


def grad_block(
    query_heads,
    grad_heads,
    log_norm,
    row_delta,
    query_doc,
    query_pos,
    key_heads,
    value_heads,
    key_doc,
    key_pos,
):
    raw_scores, allowed = score_block(
        query_heads, key_heads, query_doc, query_pos, key_doc, key_pos
    )
    soft = soft_block(raw_scores, allowed, log_norm)
    grad_soft = jnp.einsum(
        "qhd,khd->hqk", grad_heads, value_heads, preferred_element_type=jnp.float32
    )
    grad_scores = (soft * (grad_soft - row_delta[:, :, None])).astype(jnp.bfloat16)
    score_scale = 1.0 / math.sqrt(HD)
    part_q = (
        jnp.einsum("hqk,khd->qhd", grad_scores, key_heads, preferred_element_type=jnp.float32)
        * score_scale
    )
    part_k = (
        jnp.einsum("hqk,qhd->khd", grad_scores, query_heads, preferred_element_type=jnp.float32)
        * score_scale
    )
    part_v = jnp.einsum(
        "hqk,qhd->khd", soft.astype(jnp.bfloat16), grad_heads, preferred_element_type=jnp.float32
    )
    return (part_q, part_k, part_v)


def general_body(
    inputs,
    out_grad,
    segment_ids,
    block_order,
    w_qkv,
    w_out,
    w_up,
    w_down,
    norm1_gain,
    norm1_bias,
    norm2_gain,
    norm2_bias,
    out_bias,
    up_bias,
    down_bias,
):
    gathered = (
        lax.all_gather(w_qkv, "fsdp", axis=0, tiled=True),
        lax.all_gather(w_out, "fsdp", axis=0, tiled=True),
        lax.all_gather(w_up, "fsdp", axis=0, tiled=True),
        lax.all_gather(w_down, "fsdp", axis=0, tiled=True),
        lax.all_gather(norm1_gain, "fsdp", axis=0, tiled=True),
        lax.all_gather(norm1_bias, "fsdp", axis=0, tiled=True),
        lax.all_gather(norm2_gain, "fsdp", axis=0, tiled=True),
        lax.all_gather(norm2_bias, "fsdp", axis=0, tiled=True),
        lax.all_gather(out_bias, "fsdp", axis=0, tiled=True),
        lax.all_gather(up_bias, "fsdp", axis=0, tiled=True),
        lax.all_gather(down_bias, "fsdp", axis=0, tiled=True),
    )
    full_qkv, full_out, full_up, full_down = (gathered[0], gathered[1], gathered[2], gathered[3])
    gain_one, bias_one, gain_two, bias_two, full_obias, full_ubias, full_dbias = [
        member.astype(jnp.float32) for member in gathered[4:]
    ]
    model_width = full_qkv.shape[0]
    local_rows = inputs.shape[2]
    ctx_count = lax.axis_size("ctx")
    seq_len = local_rows * ctx_count
    key_block = min(512, seq_len)
    block_count = seq_len // key_block
    ctx_index = lax.axis_index("ctx")
    row_ids = jnp.arange(local_rows, dtype=jnp.int32)
    own_blocks = lax.dynamic_slice_in_dim(block_order, 2 * ctx_index, 2)
    own_pos = own_blocks[row_ids // BLK] * BLK + row_ids % BLK
    all_ids = jnp.arange(seq_len, dtype=jnp.int32)
    all_pos = block_order[all_ids // BLK] * BLK + all_ids % BLK
    pos_blocks = all_pos.reshape(block_count, key_block)
    grad_sums = [jnp.zeros(member.shape, jnp.float32) for member in gathered]
    outputs_list = []
    input_grads = []
    for micro_idx in range(inputs.shape[0]):
        seq_in = inputs[micro_idx, 0].astype(jnp.float32)
        normed, norm1_pull = jax.vjp(layer_norm, seq_in, gain_one, bias_one)
        normed_low = normed.astype(jnp.bfloat16)
        qkv_out = jnp.dot(normed_low, full_qkv, preferred_element_type=jnp.float32).astype(
            jnp.bfloat16
        )
        query_heads = qkv_out[:, :model_width].reshape(local_rows, H, HD)
        kv_all, doc_all = (
            lax.all_gather(qkv_out[:, model_width:], "ctx", axis=0, tiled=True),
            lax.all_gather(segment_ids[micro_idx, 0], "ctx", axis=0, tiled=True),
        )
        doc_rows = doc_all[all_pos]
        query_doc = doc_all[own_pos]
        kv_heads = kv_all.reshape(block_count, key_block, 2, H, HD)
        key_blocks = kv_heads[:, :, 0]
        value_blocks = kv_heads[:, :, 1]
        doc_blocks = doc_rows.reshape(block_count, key_block)
        log_norm = row_log_norm(query_heads, key_blocks, doc_blocks, pos_blocks, query_doc, own_pos)
        attn_acc = attend_all(
            query_heads,
            key_blocks,
            value_blocks,
            doc_blocks,
            pos_blocks,
            query_doc,
            own_pos,
            log_norm,
        )
        attn_low = attn_acc.reshape(local_rows, model_width).astype(jnp.bfloat16)
        branch = jnp.dot(attn_low, full_out, preferred_element_type=jnp.float32) + full_obias
        middle = seq_in + branch
        normed_two, norm2_pull = jax.vjp(layer_norm, middle, gain_two, bias_two)
        normed_two_low = normed_two.astype(jnp.bfloat16)
        hidden = jnp.dot(normed_two_low, full_up, preferred_element_type=jnp.float32) + full_ubias
        active, gelu_pull = jax.vjp(gelu_exact, hidden)
        active_low = active.astype(jnp.bfloat16)
        result = middle + (
            jnp.dot(active_low, full_down, preferred_element_type=jnp.float32) + full_dbias
        )
        outputs_list.append(result.astype(jnp.bfloat16))
        grad_y = out_grad[micro_idx, 0]
        grad_y32 = grad_y.astype(jnp.float32)
        grad_sums[3] = grad_sums[3] + jnp.einsum(
            "rf,rd->fd", active_low, grad_y, preferred_element_type=jnp.float32
        )
        grad_sums[10] = grad_sums[10] + jnp.sum(grad_y32, axis=0)
        grad_active = jnp.einsum("rd,fd->rf", grad_y, full_down, preferred_element_type=jnp.float32)
        (grad_hidden,) = gelu_pull(grad_active)
        grad_hidden_low = grad_hidden.astype(jnp.bfloat16)
        grad_sums[2] = grad_sums[2] + jnp.einsum(
            "rd,rf->df", normed_two_low, grad_hidden_low, preferred_element_type=jnp.float32
        )
        grad_sums[9] = grad_sums[9] + jnp.sum(grad_hidden_low.astype(jnp.float32), axis=0)
        grad_normed_two = jnp.einsum(
            "rf,df->rd", grad_hidden_low, full_up, preferred_element_type=jnp.float32
        )
        grad_mid_ln, grad_gain_two, grad_bias_two = norm2_pull(grad_normed_two)
        grad_sums[6] = grad_sums[6] + grad_gain_two
        grad_sums[7] = grad_sums[7] + grad_bias_two
        grad_mid = grad_y32 + grad_mid_ln
        grad_mid_low = grad_mid.astype(jnp.bfloat16)
        grad_sums[1] = grad_sums[1] + jnp.einsum(
            "rd,re->de", attn_low, grad_mid_low, preferred_element_type=jnp.float32
        )
        grad_sums[8] = grad_sums[8] + jnp.sum(grad_mid_low.astype(jnp.float32), axis=0)
        grad_attn_low = jnp.einsum(
            "re,de->rd", grad_mid_low, full_out, preferred_element_type=jnp.float32
        ).astype(jnp.bfloat16)
        grad_heads = grad_attn_low.reshape(local_rows, H, HD)
        row_delta = jnp.sum(grad_heads.astype(jnp.float32) * attn_acc, axis=-1).T

        def back_visit(grad_query, block_item):
            key_heads, value_heads, key_doc, key_pos = block_item
            part_q, part_k, part_v = grad_block(
                query_heads,
                grad_heads,
                log_norm,
                row_delta,
                query_doc,
                own_pos,
                key_heads,
                value_heads,
                key_doc,
                key_pos,
            )
            joined = jnp.concatenate(
                [part_k.reshape(key_block, model_width), part_v.reshape(key_block, model_width)],
                axis=1,
            )
            return (grad_query + part_q, joined)

        grad_query, kv_terms = lax.scan(
            back_visit,
            jnp.zeros((local_rows, H, HD), jnp.float32),
            (key_blocks, value_blocks, doc_blocks, pos_blocks),
        )
        kv_grad = lax.psum_scatter(
            kv_terms.reshape(seq_len, 2 * model_width).astype(jnp.bfloat16),
            "ctx",
            scatter_dimension=0,
            tiled=True,
        ).astype(jnp.float32)
        grad_qkv_low = jnp.concatenate(
            [grad_query.reshape(local_rows, model_width), kv_grad], axis=1
        ).astype(jnp.bfloat16)
        grad_sums[0] = grad_sums[0] + jnp.einsum(
            "rd,re->de", normed_low, grad_qkv_low, preferred_element_type=jnp.float32
        )
        grad_normed = jnp.einsum(
            "re,de->rd", grad_qkv_low, full_qkv, preferred_element_type=jnp.float32
        )
        grad_in_ln, grad_gain_one, grad_bias_one = norm1_pull(grad_normed)
        grad_sums[4] = grad_sums[4] + grad_gain_one
        grad_sums[5] = grad_sums[5] + grad_bias_one
        input_grads.append(grad_mid + grad_in_ln)
    owned = (
        lax.psum_scatter(
            grad_sums[0].astype(jnp.bfloat16), "fsdp", scatter_dimension=0, tiled=True
        ).astype(jnp.float32),
        lax.psum_scatter(
            grad_sums[1].astype(jnp.bfloat16), "fsdp", scatter_dimension=0, tiled=True
        ).astype(jnp.float32),
        lax.psum_scatter(
            grad_sums[2].astype(jnp.bfloat16), "fsdp", scatter_dimension=0, tiled=True
        ).astype(jnp.float32),
        lax.psum_scatter(
            grad_sums[3].astype(jnp.bfloat16), "fsdp", scatter_dimension=0, tiled=True
        ).astype(jnp.float32),
        lax.psum_scatter(
            grad_sums[4].astype(jnp.bfloat16), "fsdp", scatter_dimension=0, tiled=True
        ).astype(jnp.float32),
        lax.psum_scatter(
            grad_sums[5].astype(jnp.bfloat16), "fsdp", scatter_dimension=0, tiled=True
        ).astype(jnp.float32),
        lax.psum_scatter(
            grad_sums[6].astype(jnp.bfloat16), "fsdp", scatter_dimension=0, tiled=True
        ).astype(jnp.float32),
        lax.psum_scatter(
            grad_sums[7].astype(jnp.bfloat16), "fsdp", scatter_dimension=0, tiled=True
        ).astype(jnp.float32),
        lax.psum_scatter(
            grad_sums[8].astype(jnp.bfloat16), "fsdp", scatter_dimension=0, tiled=True
        ).astype(jnp.float32),
        lax.psum_scatter(
            grad_sums[9].astype(jnp.bfloat16), "fsdp", scatter_dimension=0, tiled=True
        ).astype(jnp.float32),
        lax.psum_scatter(
            grad_sums[10].astype(jnp.bfloat16), "fsdp", scatter_dimension=0, tiled=True
        ).astype(jnp.float32),
    )
    summed = (
        lax.psum(owned[0].astype(jnp.bfloat16), "ctx").astype(jnp.float32),
        lax.psum(owned[1].astype(jnp.bfloat16), "ctx").astype(jnp.float32),
        lax.psum(owned[2].astype(jnp.bfloat16), "ctx").astype(jnp.float32),
        lax.psum(owned[3].astype(jnp.bfloat16), "ctx").astype(jnp.float32),
        lax.psum(owned[4].astype(jnp.bfloat16), "ctx").astype(jnp.float32),
        lax.psum(owned[5].astype(jnp.bfloat16), "ctx").astype(jnp.float32),
        lax.psum(owned[6].astype(jnp.bfloat16), "ctx").astype(jnp.float32),
        lax.psum(owned[7].astype(jnp.bfloat16), "ctx").astype(jnp.float32),
        lax.psum(owned[8].astype(jnp.bfloat16), "ctx").astype(jnp.float32),
        lax.psum(owned[9].astype(jnp.bfloat16), "ctx").astype(jnp.float32),
        lax.psum(owned[10].astype(jnp.bfloat16), "ctx").astype(jnp.float32),
    )
    return (
        jnp.stack(outputs_list)[:, None],
        jnp.stack(input_grads)[:, None],
        summed[0],
        summed[1],
        summed[2],
        summed[3],
        summed[4],
        summed[5],
        summed[6],
        summed[7],
        summed[8],
        summed[9],
        summed[10],
    )


AXES = ("z", "x", "y", "c")
SIZES = (4, 2, 2, 2)


MESH = pl.DeviceIdType.MESH


def send(src, dst, sems, recv_sems, index, peer):
    copy = pltpu.make_async_remote_copy(
        src_ref=src,
        dst_ref=dst,
        send_sem=sems.at[index],
        recv_sem=recv_sems.at[index],
        device_id=peer,
        device_id_type=MESH,
    )
    copy.start()
    return copy


def greet(peers, extra, extra_on):
    barrier = pltpu.get_barrier_semaphore()
    for peer in peers:
        pl.semaphore_signal(barrier, inc=1, device_id=peer, device_id_type=MESH)

    @pl.when(extra_on)
    def _():
        for peer in extra:
            pl.semaphore_signal(barrier, inc=1, device_id=peer, device_id_type=MESH)

    pl.semaphore_wait(barrier, len(peers) + jnp.where(extra_on, len(extra), 0))


HEAD_CHUNK = 128
SAFE_SCORE = 80.0


def head_kernel(
    x_in_ref, dy_in_ref, docs_in_ref, order_ref, g1_ref, b1_ref, g2_ref, b2_ref, ob_ref, db_ref, ub_in_ref, wq_ref, wo_ref, wu_ref, wd_ref,
    qt_ref, k_ref, kt_ref, v_ref, vt_ref, ut_ref, own_ref, wo_all, wu_all, wd_all, dy_ref,
    wh_ref, vec_ref, ub_ref, start_ref, tab_ref,
    qt_buf, k_buf, kt_buf, v_buf, vt_buf, ut_buf, rows, docs, docs_true, norms, vec_in_ref, vec_all, wo_tmp, wu_tmp, wd_tmp,
    z_s, z_r, x_s, x_r, c_s, c_r, f_s, f_r, docs_s, docs_r, vec_s, vec_r, wh_s, wh_r, wh_l,
    y_s, y_r, n_s, n_r, o_s, o_r, load_sem, put_sem, self_sem, d_s, d_r, d_self, out_sem,
):
    z, x, y, c = (lax.axis_index(name) for name in AXES)
    odd, upper = lax.rem(z, 2), lax.div(z, 2)
    width = x_in_ref.shape[-1]
    chunks = rows.shape[1] // HEAD_CHUNK
    per_turn = chunks // 2
    by_core, by_x, by_y, by_yc = {"c": 1 - c}, {"x": 1 - x}, {"y": 1 - y}, {"y": 1 - y, "c": 1 - c}
    home = [{"z": 2 * c + upper, "c": odd}, {"z": 2 * c + 1 - upper, "c": odd}]
    target = [{"z": 2 * odd + c, "c": upper}, {"z": 2 * (1 - odd) + c, "c": upper}]
    block = [odd, 1 - odd]
    stay = (c == upper) & (odd == c)
    leave = jnp.logical_not(stay)
    for i, ref in enumerate((g1_ref, b1_ref, g2_ref, b2_ref, ob_ref, db_ref, ub_in_ref)):
        vec_in_ref[i : i + ref.shape[0]] = ref[...]
    greet([by_core, by_x, by_y, by_yc, home[1], target[1]], [home[0], target[0]], leave)

    def order_of(i):
        return i % 2 * per_turn + i // 2

    def piece(i):
        turn, row = order_of(i) // per_turn, (order_of(i) % per_turn) * HEAD_CHUNK
        return (
            x_in_ref.at[block[turn], 0, pl.ds(row, HEAD_CHUNK)],
            rows.at[0, pl.ds(order_of(i) * HEAD_CHUNK, HEAD_CHUNK)],
        )

    for turn in range(2):
        src, dst = docs_in_ref.at[block[turn]], docs.at[0, turn]

        def start_docs():
            send(src, dst, docs_s, docs_r, turn, target[turn])

        if turn == 0:
            pl.when(stay)(lambda: pltpu.make_async_copy(src, dst, self_sem.at[per_turn]).start())
            pl.when(leave)(start_docs)
        else:
            start_docs()
    for i in range(chunks):
        src, dst = piece(i)
        if i % 2 == 0:
            pl.when(stay)(lambda: pltpu.make_async_copy(src, dst, self_sem.at[i // 2]).start())
            pl.when(leave)(lambda: send(src, dst, z_s, z_r, i, target[0]) and None)
        else:
            send(src, dst, z_s, z_r, i, target[1])

    def piece_dy(i):
        part = pl.ds(i * HEAD_CHUNK, HEAD_CHUNK)
        return dy_in_ref.at[odd, 0, part], dy_ref.at[part]

    def send_dy(i):
        src, dst = piece_dy(i)
        pl.when(stay)(lambda: pltpu.make_async_copy(src, dst, d_self.at[i]).start())
        pl.when(leave)(lambda: send(src, dst, d_s, d_r, i, target[0]) and None)

    def land_dy(i):
        src, dst = piece_dy(i)
        pl.when(stay)(lambda: pltpu.make_async_copy(src, dst, d_self.at[i]).wait())
        pl.when(leave)(
            lambda: pltpu.make_async_remote_copy(
                src_ref=src, dst_ref=dst, send_sem=d_s.at[i], recv_sem=d_r.at[i],
                device_id=target[0], device_id_type=MESH,
            ).wait()
        )

    def landed(src, dst, sems, recv_sems, index, turn, self_index):
        def remote():
            pltpu.make_async_remote_copy(
                src_ref=src, dst_ref=dst, send_sem=sems.at[index], recv_sem=recv_sems.at[index],
                device_id=target[turn], device_id_type=MESH,
            ).wait()

        if turn == 0:
            pl.when(stay)(lambda: pltpu.make_async_copy(src, dst, self_sem.at[self_index]).wait())
            pl.when(leave)(remote)
        else:
            remote()

    mine = 2 * y + c
    vec_copy = [
        send(vec_in_ref, vec_all.at[mine], vec_s, vec_r, i, peer)
        for i, peer in enumerate((by_core, by_y, by_yc))
    ]
    vec_all[mine] = vec_in_ref[...]
    wh_copy = []
    shard = wq_ref.shape[0]
    own_rows = pl.ds(pl.multiple_of(mine * shard, shard), shard)
    for part in range(3):
        to = wh_ref.at[own_rows, pl.ds(part * PAIR, PAIR)]

        def columns(core):
            return wq_ref.at[:, pl.ds(pl.multiple_of(part * width + (2 * x + core) * PAIR, PAIR), PAIR)]

        for i, (peer, core) in enumerate(((by_core, 1 - c), (by_y, c), (by_yc, 1 - c))):
            wh_copy.append(send(columns(core), to, wh_s, wh_r, 3 * part + i, peer))
        copy = pltpu.make_async_copy(columns(c), to, wh_l.at[part])
        copy.start()
        wh_copy.append(copy)

    up_rows, down_rows = wu_ref.shape[0] // 4, wd_ref.shape[0] // 4
    parts = [(wo_ref, wo_all, wo_ref.shape[0], 0)]
    parts += [(wu_ref, wu_all, up_rows, i * up_rows) for i in range(4)]
    parts += [(wd_ref, wd_all, down_rows, i * down_rows) for i in range(4)]

    def at_owner(full, src, size, offset, owner):
        return full.at[pl.ds(pl.multiple_of(owner * src.shape[0] + offset, 32), size)]

    other = 2 * (1 - y) + c
    y_copy = []
    for i, (src, full, size, offset) in enumerate(parts):
        y_copy.append(
            send(src.at[pl.ds(offset, size)], at_owner(full, src, size, offset, mine), y_s, y_r, i, by_y)
        )
    n_copy, load_copy, put_copy = [], [], []
    for i, (src, full, tmp) in enumerate(((wo_ref, wo_all, wo_tmp), (wu_ref, wu_all, wu_tmp), (wd_ref, wd_all, wd_tmp))):
        n_copy.append(send(src, at_owner(full, src, src.shape[0], 0, mine), n_s, n_r, i, by_core))
        load_copy.append(pltpu.make_async_copy(src, tmp, load_sem.at[i]))
        load_copy[-1].start()

    def put(i):
        src, full, tmp = ((wo_ref, wo_all, wo_tmp), (wu_ref, wu_all, wu_tmp), (wd_ref, wd_all, wd_tmp))[i]
        load_copy[i].wait()
        put_copy.append(pltpu.make_async_copy(tmp, at_owner(full, src, src.shape[0], 0, mine), put_sem.at[i]))
        put_copy[-1].start()

    o_copy = []

    def forward(i):
        src, full, size, offset = parts[i]
        y_copy[i].wait()
        held = at_owner(full, src, size, offset, other)
        o_copy.append(send(held, held, o_s, o_r, i, by_core))

    blocks = order_ref.shape[0]
    lane = lax.broadcasted_iota(jnp.int32, (1, 128), 1)
    slots = jnp.zeros((1, 128), jnp.int32)
    for t in range(blocks):
        dc, dx, turn, half = t // 8, t // 4 % 2, t // 2 % 2, t % 2
        core, side = (1 - c if dc else c), (1 - x if dx else x)
        stored = 2 * (2 * (2 * core + (1 - upper if turn else upper)) + side) + half
        slots = jnp.where(lane == order_ref[stored], t, slots)

    docs_copy = {}

    def finish_docs():
        docs_copy["c"].wait()
        docs_copy["f"].wait()
        for g in range(4):
            core, side = (1 - c if g // 2 else c), (1 - x if g % 2 else x)
            for turn in range(2):
                docs_true[2 * (2 * core + (1 - upper if turn else upper)) + side] = docs[g, turn]
        numbers = docs_true[...]
        first = jnp.zeros_like(numbers)
        for d in range(1, blocks):
            before = jnp.sum((numbers < d).astype(jnp.int32), axis=(0, 1, 2), keepdims=True)
            first = jnp.where(numbers == d, before, first)
        docs_true[...] = first
        low = jnp.zeros((1, 128), jnp.int32)
        for b in range(blocks):
            line = docs_true[b // 2]
            at = 2 * (b % 2)
            line = jnp.concatenate([line[at : at + 1], line[at + 1 : at + 2]], axis=1)
            start_ref[b] = line
            low = jnp.where(lane == b, line[:, :1] // BLK, low)
        high = jnp.zeros((1, 128), jnp.int32) - 1
        for b in range(blocks):
            high = high + (low[:, b : b + 1] <= lane).astype(jnp.int32)
        tab_ref[...] = jnp.concatenate([low, high, slots, jnp.zeros((5, 128), jnp.int32)], axis=0)

    def docs_first():
        for turn in range(2):
            landed(docs_in_ref.at[block[turn]], docs.at[0, turn], docs_s, docs_r, turn, turn, per_turn)
        docs_copy["x"] = send(docs.at[0], docs.at[1], docs_s, docs_r, 2, by_x)
        docs_copy["c"] = send(docs.at[0], docs.at[2], docs_s, docs_r, 3, by_core)


    def vectors_and_weight():
        for copy in vec_copy:
            copy.wait()
        vec_width = vec_in_ref.shape[1]
        for j in range(4):
            for i in range(6):
                vec_ref[i : i + 1, j * vec_width : (j + 1) * vec_width] = vec_all[j, i : i + 1].astype(f32)
            for i in range(4):
                at = (4 * j + i) * vec_width
                ub_ref[:, at : at + vec_width] = vec_all[j, 6 + i : 7 + i].astype(f32)
        vec_ref[6:8] = jnp.zeros((2, width), f32)
        for copy in wh_copy:
            copy.wait()


    def docs_second():
        docs_copy["x"].wait()
        docs_copy["f"] = send(docs.at[1], docs.at[3], docs_s, docs_r, 4, by_core)


    x_copy, c_copy, f_copy = [], [], []

    def relay(i):
        src, dst = piece(i)
        landed(src, dst, z_s, z_r, i, i % 2, i // 2)
        part = pl.ds(order_of(i) * HEAD_CHUNK, HEAD_CHUNK)
        x_copy.append(send(rows.at[0, part], rows.at[1, part], x_s, x_r, i, by_x))
        c_copy.append(send(rows.at[0, part], rows.at[2, part], c_s, c_r, i, by_core))

    def relay_far(i):
        x_copy[i].wait()
        part = pl.ds(order_of(i) * HEAD_CHUNK, HEAD_CHUNK)
        f_copy.append(send(rows.at[1, part], rows.at[3, part], f_s, f_r, i, by_core))

    streams = (
        (qt_buf, qt_ref, 1), (k_buf, k_ref, 0), (kt_buf, kt_ref, 1), (v_buf, v_ref, 0), (vt_buf, vt_ref, 1),
        (ut_buf, ut_ref, 1),
    )

    def compute(g, i):
        count = rows.shape[1]
        chunk = order_of(i)
        unit, _ = norm_parts(rows[g, chunk * HEAD_CHUNK : (chunk + 1) * HEAD_CHUNK].astype(f32))
        at = pl.ds(g * count + chunk * HEAD_CHUNK, HEAD_CHUNK)
        ut_buf[:, at] = unit.astype(bf16).T
        low = (unit * vec_ref[0:1] + vec_ref[1:2]).astype(bf16)
        qkv = jnp.dot(low, wh_ref[...], preferred_element_type=f32)
        qt = (qkv[:, :PAIR] * (SCORE_SCALE * LOG2E)).astype(bf16).T
        qt_buf[:, at] = qt
        k = qkv[:, PAIR : 2 * PAIR].astype(bf16)
        v = qkv[:, 2 * PAIR :].astype(bf16)
        k_buf[at] = k
        v_buf[at] = v
        kt = k.T
        kt_buf[:, at] = kt
        vt_buf[:, at] = v.T
        found = []
        for block_ in (qt, kt):
            squares = block_.astype(f32) * block_.astype(f32)
            found += [jnp.sum(squares[head * HD : (head + 1) * HD], axis=0, keepdims=True) for head in range(2)]
        found = jnp.concatenate(found, axis=0)
        norms[...] = found if g == 0 and i == 0 else jnp.maximum(norms[...], found)
        for index, (source, out, columns) in enumerate(streams):
            if columns:
                source, out = source.at[:, at], out.at[:, at]
            else:
                source, out = source.at[at], out.at[at]
            pltpu.make_async_copy(source, out, out_sem.at[index]).start()

    docs_first()
    for i in range(chunks + 2):
        if i < chunks:
            if i < per_turn:
                send_dy(i)
            relay(i)
        if i == 0:
            vectors_and_weight()
            docs_second()
        if 1 <= i <= chunks:
            relay_far(i - 1)
            compute(0, i - 1)
            compute(1, i - 1)
            c_copy[i - 1].wait()
            compute(2, i - 1)
        if i >= 2:
            f_copy[i - 2].wait()
            compute(3, i - 2)
        if i == 1:
            finish_docs()
        if 2 <= i < 5:
            put(i - 2)
        if i >= 3 and i - 3 < len(parts):
            forward(i - 3)
        if i == chunks - 1:
            own_copy = pltpu.make_async_copy(rows.at[0], own_ref, out_sem.at[len(streams)])
            own_copy.start()
    largest = jnp.max(norms[...], axis=1, keepdims=True)
    bound = jnp.maximum(largest[0:1] * largest[2:3], largest[1:2] * largest[3:4])
    tab_ref[3:4] = jnp.broadcast_to((bound <= SAFE_SCORE * SAFE_SCORE).astype(jnp.int32), (1, 128))
    for i in range(chunks - 1, len(parts)):
        forward(i)
    for index, (source, out, _) in enumerate(streams):
        pltpu.make_async_copy(source, out, out_sem.at[index]).wait()
    own_copy.wait()
    for copy in n_copy + put_copy + o_copy:
        copy.wait()
    for i in range(per_turn):
        land_dy(i)


def head(x_in, dy_in, docs_in, order, vectors, w_qkv, w_out, w_up, w_down):
    width = x_in.shape[-1]
    count = 2 * x_in.shape[2]
    total = 4 * count
    shard = w_qkv.shape[0]
    chunks = count // HEAD_CHUNK
    blocks = order.shape[0]
    vmem, any_ = pl.BlockSpec(memory_space=pltpu.VMEM), pl.BlockSpec(memory_space=pl.ANY)
    smem = pl.BlockSpec(memory_space=pltpu.SMEM)
    dma, buf, shape = pltpu.SemaphoreType.DMA, pltpu.VMEM, jax.ShapeDtypeStruct
    return pl.pallas_call(
        head_kernel,
        in_specs=[any_, any_, vmem, smem] + [vmem] * 7 + [any_] * 4,
        out_specs=[any_] * 11 + [vmem] * 5,
        out_shape=[
            shape((PAIR, total), bf16),
            shape((total, PAIR), bf16),
            shape((PAIR, total), bf16),
            shape((total, PAIR), bf16),
            shape((PAIR, total), bf16),
            shape((width, total), bf16),
            shape((count, width), bf16),
            shape((4 * w_out.shape[0], w_out.shape[1]), bf16),
            shape((4 * w_up.shape[0], w_up.shape[1]), bf16),
            shape((4 * w_down.shape[0], w_down.shape[1]), bf16),
            shape((count // 2, width), bf16),
            shape((width, 3 * PAIR), bf16),
            shape((8, width), f32),
            shape((1, 4 * w_down.shape[0]), f32),
            shape((blocks, 1, BLK), jnp.int32),
            shape((8, 128), jnp.int32),
        ],
        scratch_shapes=[
            buf((PAIR, total), bf16),
            buf((total, PAIR), bf16),
            buf((PAIR, total), bf16),
            buf((total, PAIR), bf16),
            buf((PAIR, total), bf16),
            buf((width, total), bf16),
            buf((4, count, width), bf16),
            buf((4, 2) + docs_in.shape[1:], jnp.int32),
            buf((blocks // 2,) + docs_in.shape[1:], jnp.int32),
            buf((4, HEAD_CHUNK), f32),
            buf((16, shard), bf16),
            buf((4, 16, shard), bf16),
            buf(w_out.shape, bf16),
            buf(w_up.shape, bf16),
            buf(w_down.shape, bf16),
        ]
        + [dma((chunks,))] * 8
        + [dma((5,)), dma((5,)), dma((3,)), dma((3,)), dma((9,)), dma((9,)), dma((3,))]
        + [dma((9,)), dma((9,)), dma((3,)), dma((3,)), dma((9,)), dma((9,)), dma((3,)), dma((3,))]
        + [dma((chunks // 2 + 1,)), dma((chunks // 2,))] + [dma((chunks // 2,))] * 2 + [dma((7,))],
        compiler_params=pltpu.CompilerParams(
            collective_id=1, has_side_effects=True, vmem_limit_bytes=56 * 1024 * 1024
        ),
        name="head",
    )(x_in, dy_in, docs_in, order, *[v.reshape(-1, shard) for v in vectors], w_qkv, w_out, w_up, w_down)
FF_TILE = 1024
PIECES = 3
feed_steps = 4


def feed_kernel(
    o_ref, x_ref, dy_near_ref, dy_in_ref, wo_hbm, wu_hbm, wd_hbm, vec_ref, ub_ref,
    do_ref, y_home, y_far_ref, dmid_ref, keep_ref, to_y_ref, to_x_ref, to_xy_ref, gvec_ref, gub_ref,
    attn_all, gd_ref, gu_ref, go_ref, attn_in, do_out, y_out, grad_ref, grad_in,
    wo_ref, wu_ref, wd_ref, dy_ref, dy_far, w_sem, a_s, a_r, a_l, d_s, d_r, d_l, y_s, y_r, y_l, g_s, g_r, c_s, c_r,
):
    step = pl.program_id(0)
    steps = pl.num_programs(0)
    groups = attn_in.shape[0]
    tile = x_ref.shape[0]
    z, x, y, c = (lax.axis_index(name) for name in AXES)
    odd, upper = lax.rem(z, 2), lax.div(z, 2)
    mates = [None, {"x": 1 - x}, {"c": 1 - c}, {"x": 1 - x, "c": 1 - c}]
    pair_of = [2 * x + c, 2 * (1 - x) + c, 2 * x + 1 - c, 2 * (1 - x) + 1 - c]
    home = [{"z": 2 * c + upper, "c": odd}, {"z": 2 * c + 1 - upper, "c": odd}]
    origin = [{"z": 2 * odd + c, "c": upper}, {"z": 2 * (1 - odd) + c, "c": upper}]
    stay = (c == upper) & (odd == c)
    leave = jnp.logical_not(stay)
    half = feed_steps // 2

    def attn_copy(g, i):
        part = pl.ds(i * tile, tile)
        return pltpu.make_async_remote_copy(
            src_ref=o_ref.at[g, part], dst_ref=attn_in.at[g, part],
            send_sem=a_s.at[g - 1, i], recv_sem=a_r.at[g - 1, i], device_id=mates[g], device_id_type=MESH,
        )

    def attn_own(i):
        part = pl.ds(i * tile, tile)
        return pltpu.make_async_copy(o_ref.at[0, part], attn_in.at[0, part], a_l.at[i])

    def do_copy(g, i):
        return pltpu.make_async_remote_copy(
            src_ref=do_out.at[i, g], dst_ref=do_ref.at[g, pl.ds(i * tile, tile)],
            send_sem=d_s.at[g - 1, i], recv_sem=d_r.at[g - 1, i], device_id=mates[g], device_id_type=MESH,
        )

    def do_own(i):
        return pltpu.make_async_copy(do_out.at[i, 0], do_ref.at[0, pl.ds(i * tile, tile)], d_l.at[i])

    def y_rows(i):
        return y_home.at[pl.ds(i * tile, tile)]

    def y_copy(i):
        return pltpu.make_async_remote_copy(
            src_ref=y_out.at[i], dst_ref=y_rows(i),
            send_sem=y_s.at[i], recv_sem=y_r.at[i], device_id=home[0], device_id_type=MESH,
        )

    def y_own(i):
        return pltpu.make_async_copy(y_out.at[i], y_rows(i), y_l.at[i])

    def grad_copy(i):
        return pltpu.make_async_remote_copy(
            src_ref=grad_ref.at[2 * i + 1 - c], dst_ref=grad_in.at[i],
            send_sem=g_s.at[i], recv_sem=g_r.at[i], device_id=mates[2], device_id_type=MESH,
        )

    def dy_copy(i):
        part = pl.ds(i * tile, tile)
        return pltpu.make_async_remote_copy(
            src_ref=dy_in_ref.at[1 - odd, 0, part], dst_ref=dy_far.at[part],
            send_sem=c_s.at[i], recv_sem=c_r.at[i], device_id=origin[1], device_id_type=MESH,
        )

    w_loads = [
        pltpu.make_async_copy(src, dst, w_sem.at[i])
        for i, (src, dst) in enumerate(((wo_hbm, wo_ref), (wu_hbm, wu_ref), (wd_hbm, wd_ref)))
    ]

    @pl.when(step == 0)
    def _():
        for copy in w_loads:
            copy.start()
        greet(mates[1:] + [home[1], origin[1]], [home[0], origin[0]], leave)
        for i in range(feed_steps):
            for g in (1, 3, 2):
                attn_copy(g, i).start()
            attn_own(i).start()
        for i in range(half):
            dy_copy(i).start()

    @pl.when(step == 0)
    def _():
        for ref in (gd_ref, gu_ref, go_ref, gvec_ref, gub_ref):
            ref[...] = jnp.zeros_like(ref)

    @pl.when(step < half)
    def _():
        dy_ref[...] = dy_near_ref[...]

    @pl.when(step >= half)
    def _():
        dy_copy(step - half).wait()
        dy_ref[...] = dy_far[pl.ds(pl.multiple_of((step - half) * tile, tile), tile)]

    @pl.when(step == 0)
    def _():
        for copy in w_loads:
            copy.wait()

    attn_own(step).wait()
    for g in range(1, groups):
        attn_copy(g, step).wait()
    for g in range(groups):
        attn_all[:, pl.ds(pl.multiple_of(pair_of[g] * PAIR, PAIR), PAIR)] = attn_in[
            g, pl.ds(pl.multiple_of(step * tile, tile), tile)
        ]
    attn = attn_all[...]
    gain, bias, out_bias, down_bias = (vec_ref[i : i + 1, :] for i in range(2, 6))
    middle = (
        x_ref[...].astype(f32) + jnp.dot(attn, wo_ref[...], preferred_element_type=f32) + out_bias
    )
    unit, inv = norm_parts(middle)
    low = (unit * gain + bias).astype(bf16)
    dy = dy_ref[...]
    dy32 = dy.astype(f32)
    total = middle + down_bias
    d_low = jnp.zeros_like(middle)
    width = wu_ref.shape[1]
    for j in range(0, width, FF_TILE):
        part = pl.ds(j, FF_TILE)
        up = wu_ref[:, part]
        down = wd_ref[part, :]
        hidden = jnp.dot(low, up, preferred_element_type=f32) + ub_ref[:, part]
        cdf = 0.5 * (1.0 + lax.erf(hidden * (1.0 / math.sqrt(2.0))))
        active = (hidden * cdf).astype(bf16)
        slope = cdf + hidden * (jnp.exp2(hidden * hidden * (-0.5 * LOG2E)) * (1.0 / math.sqrt(2.0 * math.pi)))
        total = total + jnp.dot(active, down, preferred_element_type=f32)
        d_hidden = contract(dy, down, 1, 1) * slope
        d_hidden_low = d_hidden.astype(bf16)
        gub_ref[:, part] += jnp.sum(d_hidden, axis=0, keepdims=True)
        d_low = d_low + contract(d_hidden_low, up, 1, 1)
        gd_ref[part, :] += contract(active, dy, 0, 0)
        gu_ref[:, part] += contract(low, d_hidden_low, 0, 0)
    @pl.when(step < half)
    def _():
        y_out[step] = total.astype(bf16)

        @pl.when(stay)
        def _():
            y_own(step).start()

        @pl.when(leave)
        def _():
            y_copy(step).start()

    @pl.when(step >= half)
    def _():
        y_far_ref[...] = total.astype(bf16)

    scaled = d_low * gain
    d_middle = dy32 + inv * (
        scaled
        - jnp.mean(scaled, axis=-1, keepdims=True)
        - unit * jnp.mean(scaled * unit, axis=-1, keepdims=True)
    )
    dmid_ref[...] = d_middle
    branch = d_middle.astype(bf16)
    go_ref[...] += contract(attn, branch, 0, 0)
    gvec_ref[0:1, :] += jnp.sum(d_middle, axis=0, keepdims=True)
    gvec_ref[1:2, :] += jnp.sum(d_low * unit, axis=0, keepdims=True)
    gvec_ref[2:3, :] += jnp.sum(d_low, axis=0, keepdims=True)
    gvec_ref[3:4, :] += jnp.sum(dy32, axis=0, keepdims=True)
    attn_all[...] = contract(branch, wo_ref[...], 1, 1).astype(bf16)
    for g in (1, 3, 2, 0):
        do_out[step, g] = attn_all[:, pl.ds(pl.multiple_of(pair_of[g] * PAIR, PAIR), PAIR)]
        if g:
            do_copy(g, step).start()
        else:
            do_own(step).start()

    @pl.when(step == steps - 1)
    def _():
        shards = grad_ref.shape[0]
        d_model = x_ref.shape[1]
        down_rows, up_rows = gd_ref.shape[0] // shards, d_model // shards
        for j in range(shards):
            grad_ref[j, :down_rows] = gd_ref[j * down_rows : (j + 1) * down_rows].astype(bf16)
            rows = slice(j * up_rows, (j + 1) * up_rows)
            at = down_rows
            for t in range(0, width, d_model):
                grad_ref[j, at : at + up_rows] = gu_ref[rows, t : t + d_model].astype(bf16)
                at += up_rows
            grad_ref[j, at : at + up_rows] = go_ref[rows].astype(bf16)
        for j in range(2):
            grad_copy(j).start()
        for j in range(feed_steps):
            do_own(j).wait()
            for g in range(1, groups):
                do_copy(g, j).wait()
            if j < half:
                @pl.when(stay)
                def _():
                    y_own(j).wait()

                @pl.when(leave)
                def _():
                    y_copy(j).wait()
        sixth = keep_ref.shape[1]
        for j in range(2):
            grad_copy(j).wait()
        for dy_, dx_, ref in ((0, 0, keep_ref), (1, 0, to_y_ref), (0, 1, to_x_ref), (1, 1, to_xy_ref)):
            row = 1 - y if dy_ else y
            side = 1 - x if dx_ else x
            for p in range(PIECES):
                part = pl.ds(pl.multiple_of((2 * p + side) * sixth, 16), sixth)
                ref[p] = (
                    grad_ref[2 * row + c, part].astype(f32) + grad_in[row, part].astype(f32)
                ).astype(bf16)


def feed(o, x, dy_near, dy_in, w_out, w_up, w_down, vecs, up_bias, shards):
    groups, count, _ = o.shape
    width = x.shape[1]
    flat = (w_out.size + w_up.size + w_down.size) // shards // width
    tile = count // feed_steps
    piece = (PIECES, flat // PIECES // 2, width)
    rows = pl.BlockSpec((tile, width), lambda i: (i, 0))
    any_ = pl.BlockSpec(memory_space=pl.ANY)
    dma, buf, shape = pltpu.SemaphoreType.DMA, pltpu.VMEM, jax.ShapeDtypeStruct
    return pl.pallas_call(
        feed_kernel,
        grid=(feed_steps,),
        in_specs=[
            any_, rows, pl.BlockSpec((tile, width), lambda i: (jnp.minimum(i, feed_steps // 2 - 1), 0)), any_, any_, any_, any_,
            whole(vecs.shape), whole(up_bias.shape),
        ],
        out_specs=[any_, any_, pl.BlockSpec((tile, width), lambda i: (jnp.maximum(i - feed_steps // 2, 0), 0)), rows]
        + [whole(piece)] * 4 + [whole(vecs.shape), whole(up_bias.shape)],
        out_shape=[
            shape((groups, count, PAIR), bf16),
            shape((count // 2, width), bf16),
            shape((count // 2, width), bf16),
            shape((count, width), f32),
            shape(piece, bf16),
            shape(piece, bf16),
            shape(piece, bf16),
            shape(piece, bf16),
            shape(vecs.shape, f32),
            shape(up_bias.shape, f32),
        ],
        scratch_shapes=[
            buf((tile, width), bf16),
            buf(w_down.shape, f32),
            buf(w_up.shape, f32),
            buf(w_out.shape, f32),
            buf((groups, count, PAIR), bf16),
            buf((feed_steps, groups, tile, PAIR), bf16),
            buf((feed_steps // 2, tile, width), bf16),
            buf((shards, flat, width), bf16),
            buf((2, flat, width), bf16),
            buf(w_out.shape, bf16),
            buf(w_up.shape, bf16),
            buf(w_down.shape, bf16),
            buf((tile, width), bf16),
            buf((count // 2, width), bf16),
            dma((3,)),
            dma((3, feed_steps)),
            dma((3, feed_steps)),
            dma((feed_steps,)),
            dma((3, feed_steps)),
            dma((3, feed_steps)),
            dma((feed_steps,)),
            dma((feed_steps // 2,)),
            dma((feed_steps // 2,)),
            dma((feed_steps // 2,)),
            dma((2,)),
            dma((2,)),
            dma((feed_steps // 2,)),
            dma((feed_steps // 2,)),
        ],
        compiler_params=pltpu.CompilerParams(
            collective_id=3, has_side_effects=True, vmem_limit_bytes=60 * 1024 * 1024
        ),
        name="feed",
    )(o, x, dy_near, dy_in, w_out, w_up, w_down, vecs, up_bias)


TAIL_CHUNK = 128


def tail_kernel(
    d_qkv_hbm, ut_hbm, x_hbm, dmid_hbm, keep_hbm, from_y_hbm, from_x_hbm, from_xy_hbm, w_ref, vec_ref,
    gvecs_ref, gub_ref,
    home_buf, gfull, wall, sum_ref,
    keep_ref, from_y_ref, from_x_ref, from_xy_ref, d_qkv, ut_ref, total, sums, gw_ref, core_out, x_ref, dmid_ref, core_buf, own_dh, x_out, x_buf, dx_out,
    gsum, gz1s, gz1r, gz2s, gz2r,
    wy, ws, wz1s, wz1r, wz2s, wz2r, wfull,
    small_ref, small_out, small_in,
    load_sem, self_sem, core_s, core_r, x_s, x_r, home_s, home_r, g_s, g_r, w_s, w_r, s_s, s_r, in_sem,
):
    z, x, y, c = (lax.axis_index(name) for name in AXES)
    odd, upper = lax.rem(z, 2), lax.div(z, 2)
    width = x_ref.shape[1]
    chunks = x_ref.shape[0] // TAIL_CHUNK
    per_turn = chunks // 2
    by_core, by_x, by_y, by_xc = {"c": 1 - c}, {"x": 1 - x}, {"y": 1 - y}, {"x": 1 - x, "c": 1 - c}
    by_z1, by_z2 = {"z": z + 1 - 2 * odd}, {"z": z + 2 - 4 * upper}
    home = [{"z": 2 * c + upper, "c": odd}, {"z": 2 * c + 1 - upper, "c": odd}]
    origin = [{"z": 2 * odd + c, "c": upper}, {"z": 2 * (1 - odd) + c, "c": upper}]
    stay = (c == upper) & (odd == c)
    loads = []
    for i in range(chunks):
        part = pl.ds(i * TAIL_CHUNK, TAIL_CHUNK)
        loads.append(pltpu.make_async_copy(d_qkv_hbm.at[:, part], d_qkv.at[:, part], load_sem.at[i]))
    inputs = [
        pltpu.make_async_copy(src, dst, in_sem.at[i])
        for i, (src, dst) in enumerate(((ut_hbm, ut_ref), (x_hbm, x_ref), (dmid_hbm, dmid_ref)))
    ]
    g_loads = [
        pltpu.make_async_copy(src, dst, in_sem.at[3 + i])
        for i, (src, dst) in enumerate((
            (keep_hbm, keep_ref), (from_y_hbm, from_y_ref), (from_x_hbm, from_x_ref), (from_xy_hbm, from_xy_ref)
        ))
    ]
    for copy in loads[:2] + g_loads + loads[2:] + inputs:
        copy.start()
    small_ref[...] = jnp.zeros_like(small_ref)
    small_ref[2:4] = gvecs_ref[1:3]
    small_ref[4:5] = gvecs_ref[0:1]
    small_ref[5:6] = gvecs_ref[3:4]
    for i in range(4):
        small_ref[6 + i : 7 + i] = gub_ref[:, i * width : (i + 1) * width]
    greet(
        [by_core, by_x, by_y, by_xc, by_z1, by_z2, home[1], origin[1]],
        [home[0], origin[0]],
        jnp.logical_not(stay),
    )
    small_peers = [by_core, by_y, by_z1, by_z2, by_x]
    to_core, w_copy, s_copy = [], {}, []

    def share(i):
        part = pl.ds(i * TAIL_CHUNK, TAIL_CHUNK)
        loads[i].wait()
        for g in (3, 2, 1, 0):
            value = contract(d_qkv[g, part], w_ref[...], 1, 1)
            if g >= 2:
                core_out[g - 2, part] = value.astype(bf16)
            else:
                own_dh[g, part] = value
            if g == 2:
                to_core.append(
                    send(core_out.at[:, part], core_buf.at[:, part], core_s, core_r, i, by_core)
                )

    def weight(g):
        if g == 0:
            inputs[0].wait()
        rows = d_qkv[g]
        part = jnp.dot(ut_ref[:, g * rows.shape[0] : (g + 1) * rows.shape[0]], rows, preferred_element_type=f32)
        line = jnp.sum(rows.astype(f32), axis=0, keepdims=True)
        total[...] = part if g == 0 else total[...] + part
        sums[...] = line if g == 0 else sums[...] + line

    def weight_close():
        shard = gw_ref.shape[1]
        for j in range(gw_ref.shape[0]):
            part = pl.ds(j * shard, shard)
            gain, bias = (jnp.broadcast_to(ref[:, part], (shard, shard)).T[:, :1] for ref in (vec_ref.at[0:1], vec_ref.at[1:2]))
            gw_ref[j] = (total[part] * gain + bias * sums[...]).astype(bf16)
            w = w_ref[part].astype(f32)
            for i, term in enumerate((w * total[part], w * sums[...])):
                column = jnp.sum(term, axis=1, keepdims=True)
                small_ref[i : i + 1, part] = jnp.broadcast_to(column, (shard, shard)).T[:1]
        s_copy.append(send(small_ref, small_in.at[0], s_s, s_r, 0, small_peers[0]))
        w_copy["y"] = send(gw_ref.at[pl.ds(2 * (1 - y), 2)], wy, w_s, w_r, 0, by_y)

    g_copy = {}

    def g_start(p):
        if p == 0:
            for copy in g_loads:
                copy.wait()
        for half in range(2):
            part = pl.ds(96 * half, 96)
            gsum[p, part] = (
                keep_ref[p, part].astype(f32)
                + from_y_ref[p, part].astype(f32)
                + from_x_ref[p, part].astype(f32)
                + from_xy_ref[p, part].astype(f32)
            )
        gz1s[p] = gsum[p, pl.ds(pl.multiple_of(96 * (1 - odd), 16), 96)].astype(bf16)
        g_copy["z1", p] = send(gz1s.at[p], gz1r.at[p], g_s, g_r, 5 * p, by_z1)

    mine_half = pl.multiple_of(96 * odd, 16)
    mine_quarter = pl.multiple_of(96 * odd + 48 * upper, 16)
    give_quarter = pl.multiple_of(96 * odd + 48 * (1 - upper), 16)

    def g_second(p):
        g_copy["z1", p].wait()
        gsum[p, pl.ds(mine_half, 96)] += gz1r[p].astype(f32)
        gz2s[p] = gsum[p, pl.ds(give_quarter, 48)].astype(bf16)
        g_copy["z2", p] = send(gz2s.at[p], gz2r.at[p], g_s, g_r, 5 * p + 1, by_z2)

    def g_third(p):
        g_copy["z2", p].wait()
        part = pl.ds(mine_quarter, 48)
        gfull[p, x, part] = (gsum[p, part] + gz2r[p].astype(f32)).astype(bf16)
        place_ = gfull.at[p, x, part]
        g_copy["z2b", p] = send(place_, place_, g_s, g_r, 5 * p + 2, by_z2)

    def g_fourth(p):
        g_copy["z2b", p].wait()
        place_ = gfull.at[p, x, pl.ds(mine_half, 96)]
        g_copy["z1b", p] = send(place_, place_, g_s, g_r, 5 * p + 3, by_z1)

    def g_fifth(p):
        g_copy["z1b", p].wait()
        g_copy["x", p] = send(gfull.at[p, x], gfull.at[p, x], g_s, g_r, 5 * p + 4, by_x)

    def w_second():
        w_copy["y"].wait()
        for i in range(2):
            ws[i] = gw_ref[2 * y + i].astype(f32) + wy[i].astype(f32)
        wz1s[...] = ws[1 - odd].astype(bf16)
        w_copy["z1"] = send(wz1s, wz1r, w_s, w_r, 1, by_z1)

    def w_third():
        w_copy["z1"].wait()
        ws[odd] += wz1r[...].astype(f32)
        wz2s[...] = ws[odd, pl.ds(pl.multiple_of(64 * (1 - upper), 64), 64)].astype(bf16)
        w_copy["z2"] = send(wz2s, wz2r, w_s, w_r, 2, by_z2)

    def w_fourth():
        w_copy["z2"].wait()
        part = pl.ds(pl.multiple_of(64 * upper, 64), 64)
        wfull[odd, part] = (ws[odd, part] + wz2r[...].astype(f32)).astype(bf16)
        place_ = wfull.at[odd, part]
        w_copy["z2b"] = send(place_, place_, w_s, w_r, 3, by_z2)

    def w_fifth():
        w_copy["z2b"].wait()
        w_copy["z1b"] = send(wfull.at[odd], wfull.at[odd], w_s, w_r, 4, by_z1)

    def w_sixth():
        w_copy["z1b"].wait()
        mine = 2 * x + c
        w_copy["core"] = send(wfull.at[1 - c], wall.at[mine], w_s, w_r, 5, by_core)
        w_copy["x"] = send(wfull.at[c], wall.at[mine], w_s, w_r, 6, by_x)
        w_copy["xc"] = send(wfull.at[1 - c], wall.at[mine], w_s, w_r, 7, by_xc)

    def s_next(step):
        s_copy[step].wait()
        before = small_ref[...] if step == 0 else small_out[step - 1]
        small_out[step] = before + small_in[step]
        if step + 1 < len(small_peers):
            s_copy.append(
                send(small_out.at[step], small_in.at[step + 1], s_s, s_r, step + 1, small_peers[step + 1])
            )

    x_copy, home_copy = [], []

    def add_core(i):
        part = pl.ds(i * TAIL_CHUNK, TAIL_CHUNK)
        to_core[i].wait()
        x_out[part] = (own_dh[1, part] + core_buf[1, part].astype(f32)).astype(bf16)
        x_copy.append(send(x_out.at[part], x_buf.at[part], x_s, x_r, i, by_x))

    def finish(i):
        part = pl.ds(i * TAIL_CHUNK, TAIL_CHUNK)
        if i == 0:
            for copy in inputs[1:]:
                copy.wait()
        x_copy[i].wait()
        d_low = own_dh[0, part] + core_buf[0, part].astype(f32) + x_buf[part].astype(f32)
        unit, inv = norm_parts(x_ref[part].astype(f32))
        scaled = d_low * vec_ref[0:1]
        dx = dmid_ref[part] + inv * (
            scaled
            - jnp.mean(scaled, axis=-1, keepdims=True)
            - unit * jnp.mean(scaled * unit, axis=-1, keepdims=True)
        )
        dx_out[part] = dx.astype(bf16)
        turn, row = i // per_turn, (i % per_turn) * TAIL_CHUNK
        target = home_buf.at[upper, pl.ds(row, TAIL_CHUNK)]
        if turn == 0:
            @pl.when(stay)
            def _():
                pltpu.make_async_copy(dx_out.at[part], target, self_sem.at[i]).start()

            @pl.when(jnp.logical_not(stay))
            def _():
                send(dx_out.at[part], target, home_s, home_r, i, home[0])
        else:
            send(dx_out.at[part], target, home_s, home_r, i, home[1])

    def arrive(i):
        part = pl.ds(i * TAIL_CHUNK, TAIL_CHUNK)
        turn, row = i // per_turn, (i % per_turn) * TAIL_CHUNK
        block = odd if turn == 0 else 1 - odd
        landed = home_buf.at[block, pl.ds(row, TAIL_CHUNK)]

        def remote():
            copy = pltpu.make_async_remote_copy(
                src_ref=dx_out.at[part], dst_ref=landed, send_sem=home_s.at[i], recv_sem=home_r.at[i],
                device_id=home[turn], device_id_type=MESH,
            )
            copy.wait_send()
            copy.wait_recv()

        if turn == 0:
            @pl.when(stay)
            def _():
                pltpu.make_async_copy(dx_out.at[part], landed, self_sem.at[i]).wait()

            pl.when(jnp.logical_not(stay))(remote)
        else:
            remote()

    share(0)
    share(1)
    add_core(0)
    share(2)
    g_start(0)
    add_core(1)
    share(3)
    g_start(1)
    add_core(2)
    share(4)
    g_start(2)
    add_core(3)
    share(5)
    share(6)
    add_core(4)
    share(7)
    weight(0)
    finish(0)
    weight(1)
    g_second(0)
    g_second(1)
    g_second(2)
    weight(2)
    finish(1)
    add_core(5)
    weight(3)
    weight_close()
    add_core(6)
    s_next(0)
    w_second()
    g_third(0)
    g_third(1)
    g_third(2)
    finish(2)
    add_core(7)
    s_next(1)
    w_third()
    g_fourth(0)
    g_fourth(1)
    g_fourth(2)
    finish(3)
    s_next(2)
    w_fourth()
    g_fifth(0)
    g_fifth(1)
    g_fifth(2)
    finish(4)
    w_fifth()
    s_next(3)
    w_sixth()
    finish(5)
    s_next(4)
    finish(6)
    finish(7)
    w_copy["core"].wait()
    w_copy["x"].wait()
    w_copy["xc"].wait()
    wall[2 * x + c] = wfull[c]
    sum_ref[...] = small_out[4]
    for i in range(chunks):
        arrive(i)
    for p in range(PIECES):
        g_copy["x", p].wait()


def tail(d_qkv, unit_t, x, dmid, keep, from_y, from_x, from_xy, weight, vecs, gvecs, gub):
    count, width = x.shape
    shard = width // 4
    half = count // 2
    chunks = count // TAIL_CHUNK
    sixth = keep.shape[1]
    vmem = pl.BlockSpec(memory_space=pltpu.VMEM)
    dma = pltpu.SemaphoreType.DMA
    buf = pltpu.VMEM
    return pl.pallas_call(
        tail_kernel,
        in_specs=[pl.BlockSpec(memory_space=pl.ANY)] * 8 + [vmem] * 4,
        out_specs=[vmem] * 4,
        out_shape=[
            jax.ShapeDtypeStruct((2, half, width), bf16),
            jax.ShapeDtypeStruct((PIECES, 2, sixth, width), bf16),
            jax.ShapeDtypeStruct((4, shard, 3 * PAIR), bf16),
            jax.ShapeDtypeStruct((16, width), f32),
        ],
        scratch_shapes=[
            buf(keep.shape, bf16),
            buf(keep.shape, bf16),
            buf(keep.shape, bf16),
            buf(keep.shape, bf16),
            buf(d_qkv.shape, bf16),
            buf(unit_t.shape, bf16),
            buf(weight.shape, f32),
            buf((1, 3 * PAIR), f32),
            buf((4, shard, 3 * PAIR), bf16),
            buf((2, count, width), bf16),
            buf((count, width), bf16),
            buf((count, width), f32),
            buf((2, count, width), bf16),
            buf((2, count, width), f32),
            buf((count, width), bf16),
            buf((count, width), bf16),
            buf((count, width), bf16),
            buf((PIECES, sixth, width), f32),
            buf((PIECES, sixth // 2, width), bf16),
            buf((PIECES, sixth // 2, width), bf16),
            buf((PIECES, sixth // 4, width), bf16),
            buf((PIECES, sixth // 4, width), bf16),
            buf((2, shard, 3 * PAIR), bf16),
            buf((2, shard, 3 * PAIR), f32),
            buf((shard, 3 * PAIR), bf16),
            buf((shard, 3 * PAIR), bf16),
            buf((shard // 2, 3 * PAIR), bf16),
            buf((shard // 2, 3 * PAIR), bf16),
            buf((2, shard, 3 * PAIR), bf16),
            buf((16, width), f32),
            buf((5, 16, width), f32),
            buf((5, 16, width), f32),
            dma((chunks,)),
            dma((chunks // 2,)),
            dma((chunks,)),
            dma((chunks,)),
            dma((chunks,)),
            dma((chunks,)),
            dma((chunks,)),
            dma((chunks,)),
            dma((5 * PIECES,)),
            dma((5 * PIECES,)),
            dma((8,)),
            dma((8,)),
            dma((5,)),
            dma((5,)),
            dma((7,)),
        ],
        compiler_params=pltpu.CompilerParams(
            collective_id=5, has_side_effects=True, vmem_limit_bytes=60 * 1024 * 1024
        ),
        name="tail",
    )(d_qkv, unit_t, x, dmid, keep, from_y, from_x, from_xy, weight, vecs, gvecs, gub)

def results_kernel(
    y_near_ref, y_far_ref, dx_ref, down_ref, up_ref, out_ref, wall_ref, sum_ref,
    y_out, dx_out, gd_ref, gu_ref, go_ref, gq_ref, *vectors,
):
    step = pl.program_id(0)
    width = dx_ref.shape[-1]
    odd = lax.rem(lax.axis_index("z"), 2)
    y_out[odd, 0] = y_near_ref[...]
    y_out[1 - odd, 0] = y_far_ref[...]
    dx_out[:, 0] = dx_ref[...].astype(f32)
    gd_ref[...] = down_ref[...].astype(f32)
    gu_ref[...] = up_ref[...].astype(f32)
    go_ref[...] = out_ref[...].astype(f32)
    for part in range(3):
        at = pl.multiple_of(part * width + step * PAIR, PAIR)
        gq_ref[:, pl.ds(at, PAIR)] = wall_ref[0, :, part * PAIR : (part + 1) * PAIR].astype(f32)
    shard = go_ref.shape[0]
    mine = 2 * lax.axis_index("y") + lax.axis_index("c")
    for i in range(6):
        vectors[i][...] = sum_ref[i : i + 1, pl.ds(pl.multiple_of(mine * shard, shard), shard)]
    vectors[6][...] = sum_ref[pl.ds(6 + mine, 1), :]


def results(y_near, y_far, dx, flat, wall, sums):
    half, width = dx.shape[1:]
    shard = wall.shape[1]
    steps = 4
    flat = flat.reshape(-1, width)
    tokens = pl.BlockSpec((2, half // steps, width), lambda i: (0, i, 0))
    tokens_out = pl.BlockSpec((2, 1, half // steps, width), lambda i: (0, 0, i, 0))
    shape = jax.ShapeDtypeStruct
    return pl.pallas_call(
        results_kernel,
        grid=(steps,),
        in_specs=[
            pl.BlockSpec((half // steps, width), lambda i: (i, 0)),
            pl.BlockSpec((half // steps, width), lambda i: (i, 0)),
            tokens,
            pl.BlockSpec((shard, width), lambda i: (i, 0)),
            pl.BlockSpec((shard, width), lambda i: (steps + i, 0)),
            pl.BlockSpec((shard, width), lambda i: (2 * steps, 0)),
            pl.BlockSpec((1, shard, 3 * PAIR), lambda i: (i, 0, 0)),
            whole(sums.shape),
        ],
        out_specs=[
            tokens_out,
            tokens_out,
            pl.BlockSpec((shard, width), lambda i: (i, 0)),
            pl.BlockSpec((shard, width), lambda i: (0, i)),
            whole((shard, width)),
            whole((shard, 3 * width)),
        ]
        + [whole((1, shard))] * 6
        + [whole((1, width))],
        out_shape=[
            shape((2, 1, half, width), bf16),
            shape((2, 1, half, width), f32),
            shape((width, width), f32),
            shape((shard, 4 * width), f32),
            shape((shard, width), f32),
            shape((shard, 3 * width), f32),
        ]
        + [shape((1, shard), f32)] * 6
        + [shape((1, width), f32)],
        compiler_params=pltpu.CompilerParams(vmem_limit_bytes=60 * 1024 * 1024),
        name="results",
    )(y_near, y_far, dx, flat, flat, flat, wall, sums)


def place(z, x, y, c):
    return ((z * SIZES[1] + x) * SIZES[2] + y) * SIZES[3] + c


def everyone():
    return [
        (z, x, y, c)
        for z in range(SIZES[0])
        for x in range(SIZES[1])
        for y in range(SIZES[2])
        for c in range(SIZES[3])
    ]


def swap_pairs(dx, dy, dc):
    return [(place(z, x, y, c), place(z, x ^ dx, y ^ dy, c ^ dc)) for z, x, y, c in everyone()]


def move(value, pairs):
    return lax.ppermute(value, AXES, pairs)


def swap(value, dx=0, dy=0, dc=0):
    return move(value, swap_pairs(dx, dy, dc))


def paired_body(
    inputs, out_grad, segment_ids, block_order, w_qkv, w_out, w_up, w_down,
    norm1_gain, norm1_bias, norm2_gain, norm2_bias, out_bias, up_bias, down_bias,
):
    vectors = (norm1_gain, norm1_bias, norm2_gain, norm2_bias, out_bias, down_bias, up_bias)
    (
        qt, k, kt, v, vt, unit, own_x, full_out, full_up, full_down, near_dy, w_heads, vecs, full_ubias, start, tab
    ) = head(
        inputs, out_grad, segment_ids.reshape(2, -1, 128), block_order, vectors, w_qkv, w_out, w_up, w_down
    )
    o, ot, lse = attend(tab, qt, start, k, vt)
    d_o, y_near, y_far, d_middle, keep, to_y, to_x, to_xy, g_vecs, g_ubias = feed(
        o.reshape(4, -1, PAIR), own_x, near_dy, out_grad, full_out, full_up, full_down, vecs, full_ubias, 4
    )
    y_far = move(y_far, [(place(z, x, y, c), place(2 * c + 1 - z // 2, x, y, z % 2)) for z, x, y, c in everyone()])
    from_y, from_x, from_xy = swap(to_y, dy=1), swap(to_x, dx=1), swap(to_xy, dy=1, dx=1)
    d_qkv = attend_back(tab, k, kt, v, qt, start, d_o.reshape(-1, PAIR), ot, lse)
    dx, flat, heads, sums = tail(
        d_qkv.reshape(4, -1, 3 * PAIR), unit, own_x, d_middle, keep, from_y, from_x, from_xy,
        w_heads, vecs, g_vecs, g_ubias,
    )
    outputs, input_grad, grad_down, grad_up, grad_out, grad_qkv, *vec = results(
        y_near, y_far, dx, flat, heads, sums
    )
    vec = [member.reshape(-1) for member in vec]
    return (
        outputs, input_grad, grad_qkv, grad_out, grad_up, grad_down,
        vec[0], vec[1], vec[2], vec[3], vec[4], vec[6], vec[5],
    )


def solution(mesh):
    paired = mesh.shape["ctx"] == SIZES[0] * SIZES[1] and mesh.shape["fsdp"] == SIZES[2] * SIZES[3]
    if paired:
        mesh = Mesh(mesh.devices.reshape(SIZES), AXES)
        ctx, fsdp, program = ("z", "x"), ("y", "c"), paired_body
    else:
        ctx, fsdp, program = "ctx", "fsdp", general_body
    tokens = P(None, fsdp, ctx, None)
    matrix, vector = P(fsdp, None), P(fsdp)
    return jax.shard_map(
        program,
        mesh=mesh,
        in_specs=(tokens, tokens, P(None, fsdp, ctx), P()) + (matrix,) * 4 + (vector,) * 7,
        out_specs=(tokens, tokens) + (matrix,) * 4 + (vector,) * 7,
        check_vma=False,
    )
```

```python
import functools
import math

import jax
import jax.numpy as jnp
from jax import lax
from jax.experimental import pallas as pl
from jax.experimental.pallas import tpu as pltpu
from jax.sharding import Mesh
from jax.sharding import PartitionSpec as P

H = 8
HD = 64
BLK = 256
PAIR = 2 * HD

norm_eps = 1e-05
mask_fill = -1e30
LOG2E = math.log2(math.e)
LN2 = math.log(2.0)
SCORE_SCALE = 1.0 / math.sqrt(HD)

f32 = jnp.float32
bf16 = jnp.bfloat16


def contract(a, b, da, db):
    return lax.dot_general(a, b, (((da,), (db,)), ((), ())), preferred_element_type=f32)


def norm_parts(values):
    center = values - jnp.mean(values, axis=-1, keepdims=True)
    spread = jnp.mean(center * center, axis=-1, keepdims=True)
    inv = lax.rsqrt(spread + norm_eps)
    return center * inv, inv


def whole(shape):
    zeros = (0,) * len(shape)
    return pl.BlockSpec(shape, lambda *_: zeros)


def two_heads(block):
    zero = jnp.zeros((HD, block.shape[1]), block.dtype)
    return jnp.concatenate(
        [jnp.concatenate([block[:HD], zero], axis=0), jnp.concatenate([zero, block[HD:]], axis=0)], axis=1
    )


EXTRA = 16


def attend_kernel(
    tab_ref, qt_ref, start_ref, k_ref, vt_ref, o_hbm, ot_hbm, lse_ref, acc, top, o_buf, ot_buf, out_sem
):
    blocks = start_ref.shape[0]
    row = lax.broadcasted_iota(jnp.int32, (BLK, 2 * BLK), 0)
    reach = row - jnp.bitwise_and(lax.broadcasted_iota(jnp.int32, (BLK, 2 * BLK), 1), BLK - 1)
    ones = jnp.ones((EXTRA, 2 * BLK), bf16)

    def place_of(b):
        return pl.ds(pl.multiple_of(tab_ref[2, jnp.maximum(b, 0)] * BLK, BLK), BLK)

    def visits_of(qb):
        return (qb - tab_ref[0, qb]) // 2 + 1

    def visit(qb, i, bounded, live=True):
        kb = qb - 2 * i
        both = two_heads(qt_ref[:, place_of(qb)])
        start = jnp.concatenate([start_ref[qb], start_ref[qb]], axis=1)
        places = [place_of(kb), place_of(kb - 1)]
        terms = []
        for n in range(2):
            first_row = start - (kb - n) * BLK
            allowed = row >= (first_row if live is True else jnp.where(live, first_row, BLK))
            if n == 0:
                allowed = allowed & (reach <= (qb - kb) * BLK)
            st = jnp.dot(k_ref[places[n], :], both, preferred_element_type=f32)
            terms.append(jnp.where(allowed, st, mask_fill))
        if bounded:
            probs = [jnp.exp2(term).astype(bf16) for term in terms]
        else:
            old = top[qb]
            peak = jnp.maximum(
                jnp.max(terms[0], axis=0, keepdims=True), jnp.max(terms[1], axis=0, keepdims=True)
            )
            peak = jnp.maximum(old, peak)
            shrink = jnp.exp2(old - peak)
            top[qb] = peak
            probs = [jnp.exp2(term - peak).astype(bf16) for term in terms]
        probs = jnp.concatenate(probs, axis=0)
        vt = jnp.concatenate([vt_ref[:, places[0]], vt_ref[:, places[1]]], axis=1)
        parts = []
        for head in range(2):
            cols = slice(head * BLK, (head + 1) * BLK)
            left = jnp.concatenate([vt[head * HD : (head + 1) * HD], ones], axis=0)
            part = jnp.dot(left, probs[:, cols], preferred_element_type=f32)
            parts.append(part)
            if not bounded:
                acc[qb, head] = part + acc[qb, head] * shrink[:, cols]
        return parts

    def all_visits(bounded):
        count = lax.fori_loop(0, blocks, lambda b, n: n + visits_of(b), 0)

        def following(qb, i):
            more = i + 1 < visits_of(qb)
            return jnp.where(more, qb, jnp.minimum(qb + 1, blocks - 1)), jnp.where(more, i + 1, 0)

        def step(n, state):
            if not bounded:
                visit(*state, False)
                return following(*state)
            second = following(*state)
            members = [visit(*state, True), visit(*second, True, 2 * n + 1 < count)]
            for (qb, _), parts in zip((state, second), members):
                for head in range(2):
                    acc[qb, head] += parts[head]
            return following(*second)

        lax.fori_loop(0, (count + 1) // 2 if bounded else count, step, (jnp.int32(0), jnp.int32(0)))

    small = tab_ref[3, 0] > 0
    acc[...] = jnp.zeros_like(acc)

    @pl.when(small)
    def _():
        top[...] = jnp.zeros_like(top)
        all_visits(True)

    @pl.when(jnp.logical_not(small))
    def _():
        top[...] = jnp.full_like(top, mask_fill)
        all_visits(False)

    def outgoing(b):
        at = place_of(b)
        return (
            pltpu.make_async_copy(o_buf.at[b], o_hbm.at[at], out_sem.at[0]),
            pltpu.make_async_copy(ot_buf.at[b], ot_hbm.at[b], out_sem.at[1]),
        )

    def close(b):
        total = jnp.concatenate([acc[b, 0, HD : HD + 1], acc[b, 1, HD : HD + 1]], axis=1)
        lse_ref[b] = top[b] + jnp.log2(total)
        heads = jnp.concatenate([acc[b, h, :HD] / acc[b, h, HD : HD + 1] for h in range(2)], axis=0)
        ot_buf[b] = heads
        o_buf[b] = heads.T.astype(bf16)
        for copy in outgoing(b):
            copy.start()

    def close_two(n, carry):
        close(2 * n)
        close(2 * n + 1)
        return carry

    lax.fori_loop(0, blocks // 2, close_two, 0)
    for whole_copy in (
        pltpu.make_async_copy(ot_buf, ot_hbm, out_sem.at[1]),
        pltpu.make_async_copy(o_hbm, o_hbm, out_sem.at[0]),
    ):
        whole_copy.wait()


def attend(tab, qt, start, k, vt):
    count = k.shape[0]
    blocks = count // BLK
    vmem, any_ = pl.BlockSpec(memory_space=pltpu.VMEM), pl.BlockSpec(memory_space=pl.ANY)
    return pl.pallas_call(
        attend_kernel,
        grid_spec=pltpu.PrefetchScalarGridSpec(
            num_scalar_prefetch=1,
            grid=(),
            in_specs=[vmem] * 4,
            out_specs=[any_, any_, vmem],
            scratch_shapes=[
                pltpu.VMEM((blocks, 2, HD + EXTRA, BLK), f32),
                pltpu.VMEM((blocks, 1, 2 * BLK), f32),
                pltpu.VMEM((blocks, BLK, PAIR), bf16),
                pltpu.VMEM((blocks, PAIR, BLK), f32),
                pltpu.SemaphoreType.DMA((2,)),
            ],
        ),
        out_shape=[
            jax.ShapeDtypeStruct((count, PAIR), bf16),
            jax.ShapeDtypeStruct((blocks, PAIR, BLK), f32),
            jax.ShapeDtypeStruct((blocks, 1, 2 * BLK), f32),
        ],
        name="attend",
    )(tab, qt, start, k, vt)


def split_heads(block):
    lane = lax.broadcasted_iota(jnp.int32, block.shape, 1)
    zero = jnp.zeros_like(block)
    first = lane < HD
    return jnp.concatenate([jnp.where(first, block, zero), jnp.where(first, zero, block)], axis=0)


def attend_back_kernel(
    tab_ref, k_hbm, kt_hbm, v_hbm, qt_ref, start_ref, do_ref, ot_ref, lse_ref, out_hbm,
    k_ref, kt_ref, v_ref, out_buf, dqt, dk, dv, dot, dom, qm, delta, in_sem, out_sem,
):
    blocks = start_ref.shape[0]
    row = lax.broadcasted_iota(jnp.int32, (BLK, 2 * BLK), 0)
    reach = row - jnp.bitwise_and(lax.broadcasted_iota(jnp.int32, (BLK, 2 * BLK), 1), BLK - 1)
    loads = [
        pltpu.make_async_copy(src, dst, in_sem.at[i])
        for i, (src, dst) in enumerate(((k_hbm, k_ref), (kt_hbm, kt_ref), (v_hbm, v_ref)))
    ]
    for copy in loads:
        copy.start()

    def at(b):
        return pl.ds(pl.multiple_of(tab_ref[2, b] * BLK, BLK), BLK)

    def prepare(qb):
        dqt[qb] = jnp.zeros((PAIR, BLK), f32)
        dk[qb] = jnp.zeros((BLK, PAIR), f32)
        dv[qb] = jnp.zeros((BLK, PAIR), f32)
        d_out = do_ref[at(qb), :]
        dom[qb] = split_heads(d_out)
        qm[qb] = split_heads(qt_ref[:, at(qb)].T)
        turned = d_out.astype(f32).T
        dot[qb] = turned.astype(bf16)
        both = turned * ot_ref[qb]
        delta[qb] = jnp.concatenate(
            [jnp.sum(both[:HD], axis=0, keepdims=True), jnp.sum(both[HD:], axis=0, keepdims=True)], axis=1
        )

    def prepare_four(n, carry):
        for i in range(4):
            prepare(4 * n + i)
        return carry

    lax.fori_loop(0, blocks // 4, prepare_four, 0)
    for copy in loads:
        copy.wait()

    def tile(kb, qb, live):
        kt = kt_ref[:, at(kb)]
        start = jnp.concatenate([start_ref[qb], start_ref[qb]], axis=1)
        st = jnp.dot(k_ref[at(kb), :], two_heads(qt_ref[:, at(qb)]), preferred_element_type=f32)
        dpt = jnp.dot(v_ref[at(kb), :], two_heads(dot[qb]), preferred_element_type=f32)
        allowed = (row >= start - kb * BLK) & (reach <= jnp.where(live, (qb - kb) * BLK, -2 * BLK))
        pt = jnp.exp2(jnp.where(allowed, st - lse_ref[qb], mask_fill))
        dst = (pt * (dpt - delta[qb])).astype(bf16)
        part_v = jnp.dot(pt.astype(bf16), dom[qb], preferred_element_type=f32)
        part_k = jnp.dot(dst, qm[qb], preferred_element_type=f32)
        part_q = [
            jnp.dot(kt[head * HD : (head + 1) * HD], dst[:, head * BLK : (head + 1) * BLK], preferred_element_type=f32)
            for head in range(2)
        ]
        return kb, qb, part_v, part_k, jnp.concatenate(part_q, axis=0)

    def add(kb, qb, part_v, part_k, part_q):
        dv[kb] += part_v
        dk[kb] += part_k
        dqt[qb] += part_q

    def following(kb, qb):
        more = qb < tab_ref[1, kb]
        beyond = jnp.minimum(kb + 1, blocks - 1)
        return jnp.where(more, kb, beyond), jnp.where(more, qb + 1, beyond)

    tiles = lax.fori_loop(0, blocks, lambda b, n: n + tab_ref[1, b] - b + 1, 0)

    def step(n, state):
        second = following(*state)
        terms = [tile(*state, True), tile(*second, 2 * n + 1 < tiles)]
        for term in terms:
            add(*term)
        return following(*second)

    lax.fori_loop(0, (tiles + 1) // 2, step, (jnp.int32(0), jnp.int32(0)))
    def close(b):
        out_buf[b] = jnp.concatenate([(dqt[b] * SCORE_SCALE).T, dk[b] * LN2, dv[b]], axis=1).astype(bf16)
        pltpu.make_async_copy(out_buf.at[b], out_hbm.at[at(b)], out_sem.at[0]).start()

    def close_four(n, carry):
        for i in range(4):
            close(4 * n + i)
        return carry

    lax.fori_loop(0, blocks // 4, close_four, 0)
    pltpu.make_async_copy(out_hbm, out_hbm, out_sem.at[0]).wait()


def attend_back(tab, k, kt, v, qt, start, d_out, ot, lse):
    count = k.shape[0]
    blocks = count // BLK
    vmem, any_ = pl.BlockSpec(memory_space=pltpu.VMEM), pl.BlockSpec(memory_space=pl.ANY)
    buf = pltpu.VMEM
    return pl.pallas_call(
        attend_back_kernel,
        grid_spec=pltpu.PrefetchScalarGridSpec(
            num_scalar_prefetch=1,
            grid=(),
            in_specs=[any_] * 3 + [vmem] * 5,
            out_specs=any_,
            scratch_shapes=[
                buf(k.shape, bf16),
                buf(kt.shape, bf16),
                buf(v.shape, bf16),
                buf((blocks, BLK, 3 * PAIR), bf16),
                buf((blocks, PAIR, BLK), f32),
                buf((blocks, BLK, PAIR), f32),
                buf((blocks, BLK, PAIR), f32),
                buf((blocks, PAIR, BLK), bf16),
                buf((blocks, 2 * BLK, PAIR), bf16),
                buf((blocks, 2 * BLK, PAIR), bf16),
                buf((blocks, 1, 2 * BLK), f32),
                pltpu.SemaphoreType.DMA((3,)),
                pltpu.SemaphoreType.DMA((1,)),
            ],
        ),
        out_shape=jax.ShapeDtypeStruct((count, 3 * PAIR), bf16),
        compiler_params=pltpu.CompilerParams(vmem_limit_bytes=60 * 1024 * 1024),
        name="attend_back",
    )(tab, k, kt, v, qt, start, d_out, ot, lse)


def layer_norm(values, gain_vec, offset):
    center = values - jnp.mean(values, axis=-1, keepdims=True)
    spread = jnp.mean(center * center, axis=-1, keepdims=True)
    return center * lax.rsqrt(spread + norm_eps) * gain_vec + offset


def gelu_exact(values):
    return 0.5 * values * (1.0 + lax.erf(values * (1.0 / math.sqrt(2.0))))


def score_block(query_heads, key_heads, query_doc, query_pos, key_doc, key_pos):
    raw_scores = jnp.einsum(
        "qhd,khd->hqk", query_heads, key_heads, preferred_element_type=jnp.float32
    ) * (1.0 / math.sqrt(HD))
    allowed = (query_doc[:, None] == key_doc[None, :]) & (key_pos[None, :] <= query_pos[:, None])
    return (raw_scores, allowed[None])


def soft_block(raw_scores, allowed, log_norm):
    return jnp.exp(jnp.where(allowed, raw_scores, mask_fill) - log_norm[:, :, None])


def row_log_norm(query_heads, key_blocks, doc_blocks, pos_blocks, query_doc, query_pos):

    def row_visit(running, block_item):
        row_top, row_sum = running
        key_heads, key_doc, key_pos = block_item
        raw_scores, allowed = score_block(
            query_heads, key_heads, query_doc, query_pos, key_doc, key_pos
        )
        masked = jnp.where(allowed, raw_scores, mask_fill)
        new_top = jnp.maximum(row_top, jnp.max(masked, axis=-1))
        fresh = jnp.sum(jnp.where(allowed, jnp.exp(masked - new_top[:, :, None]), 0.0), axis=-1)
        return ((new_top, row_sum * jnp.exp(row_top - new_top) + fresh), None)

    query_count = query_doc.shape[0]
    start = (
        jnp.full((H, query_count), mask_fill, jnp.float32),
        jnp.zeros((H, query_count), jnp.float32),
    )
    (row_top, row_sum), unused = lax.scan(row_visit, start, (key_blocks, doc_blocks, pos_blocks))
    return row_top + jnp.log(row_sum)


def attend_all(
    query_heads, key_blocks, value_blocks, doc_blocks, pos_blocks, query_doc, query_pos, log_norm
):

    def attend_visit(accum_out, block_item):
        key_heads, value_heads, key_doc, key_pos = block_item
        raw_scores, allowed = score_block(
            query_heads, key_heads, query_doc, query_pos, key_doc, key_pos
        )
        soft_low = soft_block(raw_scores, allowed, log_norm).astype(jnp.bfloat16)
        return (
            accum_out
            + jnp.einsum("hqk,khd->qhd", soft_low, value_heads, preferred_element_type=jnp.float32),
            None,
        )

    start = jnp.zeros(query_heads.shape, jnp.float32)
    accum_out, unused = lax.scan(
        attend_visit, start, (key_blocks, value_blocks, doc_blocks, pos_blocks)
    )
    return accum_out


def grad_block(
    query_heads,
    grad_heads,
    log_norm,
    row_delta,
    query_doc,
    query_pos,
    key_heads,
    value_heads,
    key_doc,
    key_pos,
):
    raw_scores, allowed = score_block(
        query_heads, key_heads, query_doc, query_pos, key_doc, key_pos
    )
    soft = soft_block(raw_scores, allowed, log_norm)
    grad_soft = jnp.einsum(
        "qhd,khd->hqk", grad_heads, value_heads, preferred_element_type=jnp.float32
    )
    grad_scores = (soft * (grad_soft - row_delta[:, :, None])).astype(jnp.bfloat16)
    score_scale = 1.0 / math.sqrt(HD)
    part_q = (
        jnp.einsum("hqk,khd->qhd", grad_scores, key_heads, preferred_element_type=jnp.float32)
        * score_scale
    )
    part_k = (
        jnp.einsum("hqk,qhd->khd", grad_scores, query_heads, preferred_element_type=jnp.float32)
        * score_scale
    )
    part_v = jnp.einsum(
        "hqk,qhd->khd", soft.astype(jnp.bfloat16), grad_heads, preferred_element_type=jnp.float32
    )
    return (part_q, part_k, part_v)


def general_body(
    inputs,
    out_grad,
    segment_ids,
    block_order,
    w_qkv,
    w_out,
    w_up,
    w_down,
    norm1_gain,
    norm1_bias,
    norm2_gain,
    norm2_bias,
    out_bias,
    up_bias,
    down_bias,
):
    gathered = (
        lax.all_gather(w_qkv, "fsdp", axis=0, tiled=True),
        lax.all_gather(w_out, "fsdp", axis=0, tiled=True),
        lax.all_gather(w_up, "fsdp", axis=0, tiled=True),
        lax.all_gather(w_down, "fsdp", axis=0, tiled=True),
        lax.all_gather(norm1_gain, "fsdp", axis=0, tiled=True),
        lax.all_gather(norm1_bias, "fsdp", axis=0, tiled=True),
        lax.all_gather(norm2_gain, "fsdp", axis=0, tiled=True),
        lax.all_gather(norm2_bias, "fsdp", axis=0, tiled=True),
        lax.all_gather(out_bias, "fsdp", axis=0, tiled=True),
        lax.all_gather(up_bias, "fsdp", axis=0, tiled=True),
        lax.all_gather(down_bias, "fsdp", axis=0, tiled=True),
    )
    full_qkv, full_out, full_up, full_down = (gathered[0], gathered[1], gathered[2], gathered[3])
    gain_one, bias_one, gain_two, bias_two, full_obias, full_ubias, full_dbias = [
        member.astype(jnp.float32) for member in gathered[4:]
    ]
    model_width = full_qkv.shape[0]
    local_rows = inputs.shape[2]
    ctx_count = lax.axis_size("ctx")
    seq_len = local_rows * ctx_count
    key_block = min(512, seq_len)
    block_count = seq_len // key_block
    ctx_index = lax.axis_index("ctx")
    row_ids = jnp.arange(local_rows, dtype=jnp.int32)
    own_blocks = lax.dynamic_slice_in_dim(block_order, 2 * ctx_index, 2)
    own_pos = own_blocks[row_ids // BLK] * BLK + row_ids % BLK
    all_ids = jnp.arange(seq_len, dtype=jnp.int32)
    all_pos = block_order[all_ids // BLK] * BLK + all_ids % BLK
    pos_blocks = all_pos.reshape(block_count, key_block)
    grad_sums = [jnp.zeros(member.shape, jnp.float32) for member in gathered]
    outputs_list = []
    input_grads = []
    for micro_idx in range(inputs.shape[0]):
        seq_in = inputs[micro_idx, 0].astype(jnp.float32)
        normed, norm1_pull = jax.vjp(layer_norm, seq_in, gain_one, bias_one)
        normed_low = normed.astype(jnp.bfloat16)
        qkv_out = jnp.dot(normed_low, full_qkv, preferred_element_type=jnp.float32).astype(
            jnp.bfloat16
        )
        query_heads = qkv_out[:, :model_width].reshape(local_rows, H, HD)
        kv_all, doc_all = (
            lax.all_gather(qkv_out[:, model_width:], "ctx", axis=0, tiled=True),
            lax.all_gather(segment_ids[micro_idx, 0], "ctx", axis=0, tiled=True),
        )
        doc_rows = doc_all[all_pos]
        query_doc = doc_all[own_pos]
        kv_heads = kv_all.reshape(block_count, key_block, 2, H, HD)
        key_blocks = kv_heads[:, :, 0]
        value_blocks = kv_heads[:, :, 1]
        doc_blocks = doc_rows.reshape(block_count, key_block)
        log_norm = row_log_norm(query_heads, key_blocks, doc_blocks, pos_blocks, query_doc, own_pos)
        attn_acc = attend_all(
            query_heads,
            key_blocks,
            value_blocks,
            doc_blocks,
            pos_blocks,
            query_doc,
            own_pos,
            log_norm,
        )
        attn_low = attn_acc.reshape(local_rows, model_width).astype(jnp.bfloat16)
        branch = jnp.dot(attn_low, full_out, preferred_element_type=jnp.float32) + full_obias
        middle = seq_in + branch
        normed_two, norm2_pull = jax.vjp(layer_norm, middle, gain_two, bias_two)
        normed_two_low = normed_two.astype(jnp.bfloat16)
        hidden = jnp.dot(normed_two_low, full_up, preferred_element_type=jnp.float32) + full_ubias
        active, gelu_pull = jax.vjp(gelu_exact, hidden)
        active_low = active.astype(jnp.bfloat16)
        result = middle + (
            jnp.dot(active_low, full_down, preferred_element_type=jnp.float32) + full_dbias
        )
        outputs_list.append(result.astype(jnp.bfloat16))
        grad_y = out_grad[micro_idx, 0]
        grad_y32 = grad_y.astype(jnp.float32)
        grad_sums[3] = grad_sums[3] + jnp.einsum(
            "rf,rd->fd", active_low, grad_y, preferred_element_type=jnp.float32
        )
        grad_sums[10] = grad_sums[10] + jnp.sum(grad_y32, axis=0)
        grad_active = jnp.einsum("rd,fd->rf", grad_y, full_down, preferred_element_type=jnp.float32)
        (grad_hidden,) = gelu_pull(grad_active)
        grad_hidden_low = grad_hidden.astype(jnp.bfloat16)
        grad_sums[2] = grad_sums[2] + jnp.einsum(
            "rd,rf->df", normed_two_low, grad_hidden_low, preferred_element_type=jnp.float32
        )
        grad_sums[9] = grad_sums[9] + jnp.sum(grad_hidden_low.astype(jnp.float32), axis=0)
        grad_normed_two = jnp.einsum(
            "rf,df->rd", grad_hidden_low, full_up, preferred_element_type=jnp.float32
        )
        grad_mid_ln, grad_gain_two, grad_bias_two = norm2_pull(grad_normed_two)
        grad_sums[6] = grad_sums[6] + grad_gain_two
        grad_sums[7] = grad_sums[7] + grad_bias_two
        grad_mid = grad_y32 + grad_mid_ln
        grad_mid_low = grad_mid.astype(jnp.bfloat16)
        grad_sums[1] = grad_sums[1] + jnp.einsum(
            "rd,re->de", attn_low, grad_mid_low, preferred_element_type=jnp.float32
        )
        grad_sums[8] = grad_sums[8] + jnp.sum(grad_mid_low.astype(jnp.float32), axis=0)
        grad_attn_low = jnp.einsum(
            "re,de->rd", grad_mid_low, full_out, preferred_element_type=jnp.float32
        ).astype(jnp.bfloat16)
        grad_heads = grad_attn_low.reshape(local_rows, H, HD)
        row_delta = jnp.sum(grad_heads.astype(jnp.float32) * attn_acc, axis=-1).T

        def back_visit(grad_query, block_item):
            key_heads, value_heads, key_doc, key_pos = block_item
            part_q, part_k, part_v = grad_block(
                query_heads,
                grad_heads,
                log_norm,
                row_delta,
                query_doc,
                own_pos,
                key_heads,
                value_heads,
                key_doc,
                key_pos,
            )
            joined = jnp.concatenate(
                [part_k.reshape(key_block, model_width), part_v.reshape(key_block, model_width)],
                axis=1,
            )
            return (grad_query + part_q, joined)

        grad_query, kv_terms = lax.scan(
            back_visit,
            jnp.zeros((local_rows, H, HD), jnp.float32),
            (key_blocks, value_blocks, doc_blocks, pos_blocks),
        )
        kv_grad = lax.psum_scatter(
            kv_terms.reshape(seq_len, 2 * model_width).astype(jnp.bfloat16),
            "ctx",
            scatter_dimension=0,
            tiled=True,
        ).astype(jnp.float32)
        grad_qkv_low = jnp.concatenate(
            [grad_query.reshape(local_rows, model_width), kv_grad], axis=1
        ).astype(jnp.bfloat16)
        grad_sums[0] = grad_sums[0] + jnp.einsum(
            "rd,re->de", normed_low, grad_qkv_low, preferred_element_type=jnp.float32
        )
        grad_normed = jnp.einsum(
            "re,de->rd", grad_qkv_low, full_qkv, preferred_element_type=jnp.float32
        )
        grad_in_ln, grad_gain_one, grad_bias_one = norm1_pull(grad_normed)
        grad_sums[4] = grad_sums[4] + grad_gain_one
        grad_sums[5] = grad_sums[5] + grad_bias_one
        input_grads.append(grad_mid + grad_in_ln)
    owned = (
        lax.psum_scatter(
            grad_sums[0].astype(jnp.bfloat16), "fsdp", scatter_dimension=0, tiled=True
        ).astype(jnp.float32),
        lax.psum_scatter(
            grad_sums[1].astype(jnp.bfloat16), "fsdp", scatter_dimension=0, tiled=True
        ).astype(jnp.float32),
        lax.psum_scatter(
            grad_sums[2].astype(jnp.bfloat16), "fsdp", scatter_dimension=0, tiled=True
        ).astype(jnp.float32),
        lax.psum_scatter(
            grad_sums[3].astype(jnp.bfloat16), "fsdp", scatter_dimension=0, tiled=True
        ).astype(jnp.float32),
        lax.psum_scatter(
            grad_sums[4].astype(jnp.bfloat16), "fsdp", scatter_dimension=0, tiled=True
        ).astype(jnp.float32),
        lax.psum_scatter(
            grad_sums[5].astype(jnp.bfloat16), "fsdp", scatter_dimension=0, tiled=True
        ).astype(jnp.float32),
        lax.psum_scatter(
            grad_sums[6].astype(jnp.bfloat16), "fsdp", scatter_dimension=0, tiled=True
        ).astype(jnp.float32),
        lax.psum_scatter(
            grad_sums[7].astype(jnp.bfloat16), "fsdp", scatter_dimension=0, tiled=True
        ).astype(jnp.float32),
        lax.psum_scatter(
            grad_sums[8].astype(jnp.bfloat16), "fsdp", scatter_dimension=0, tiled=True
        ).astype(jnp.float32),
        lax.psum_scatter(
            grad_sums[9].astype(jnp.bfloat16), "fsdp", scatter_dimension=0, tiled=True
        ).astype(jnp.float32),
        lax.psum_scatter(
            grad_sums[10].astype(jnp.bfloat16), "fsdp", scatter_dimension=0, tiled=True
        ).astype(jnp.float32),
    )
    summed = (
        lax.psum(owned[0].astype(jnp.bfloat16), "ctx").astype(jnp.float32),
        lax.psum(owned[1].astype(jnp.bfloat16), "ctx").astype(jnp.float32),
        lax.psum(owned[2].astype(jnp.bfloat16), "ctx").astype(jnp.float32),
        lax.psum(owned[3].astype(jnp.bfloat16), "ctx").astype(jnp.float32),
        lax.psum(owned[4].astype(jnp.bfloat16), "ctx").astype(jnp.float32),
        lax.psum(owned[5].astype(jnp.bfloat16), "ctx").astype(jnp.float32),
        lax.psum(owned[6].astype(jnp.bfloat16), "ctx").astype(jnp.float32),
        lax.psum(owned[7].astype(jnp.bfloat16), "ctx").astype(jnp.float32),
        lax.psum(owned[8].astype(jnp.bfloat16), "ctx").astype(jnp.float32),
        lax.psum(owned[9].astype(jnp.bfloat16), "ctx").astype(jnp.float32),
        lax.psum(owned[10].astype(jnp.bfloat16), "ctx").astype(jnp.float32),
    )
    return (
        jnp.stack(outputs_list)[:, None],
        jnp.stack(input_grads)[:, None],
        summed[0],
        summed[1],
        summed[2],
        summed[3],
        summed[4],
        summed[5],
        summed[6],
        summed[7],
        summed[8],
        summed[9],
        summed[10],
    )


AXES = ("z", "x", "y", "c")
SIZES = (4, 2, 2, 2)


MESH = pl.DeviceIdType.MESH


def send(src, dst, sems, recv_sems, index, peer):
    copy = pltpu.make_async_remote_copy(
        src_ref=src,
        dst_ref=dst,
        send_sem=sems.at[index],
        recv_sem=recv_sems.at[index],
        device_id=peer,
        device_id_type=MESH,
    )
    copy.start()
    return copy


def greet(peers, extra, extra_on):
    barrier = pltpu.get_barrier_semaphore()
    for peer in peers:
        pl.semaphore_signal(barrier, inc=1, device_id=peer, device_id_type=MESH)

    @pl.when(extra_on)
    def _():
        for peer in extra:
            pl.semaphore_signal(barrier, inc=1, device_id=peer, device_id_type=MESH)

    pl.semaphore_wait(barrier, len(peers) + jnp.where(extra_on, len(extra), 0))


HEAD_CHUNK = 128
SAFE_SCORE = 80.0


def head_kernel(
    x_in_ref, dy_in_ref, docs_in_ref, order_ref, g1_ref, b1_ref, g2_ref, b2_ref, ob_ref, db_ref, ub_in_ref, wq_ref, wo_ref, wu_ref, wd_ref,
    qt_ref, k_ref, kt_ref, v_ref, vt_ref, ut_ref, own_ref, wo_all, wu_all, wd_all, dy_ref,
    wh_ref, vec_ref, ub_ref, start_ref, tab_ref,
    qt_buf, k_buf, kt_buf, v_buf, vt_buf, ut_buf, rows, docs, docs_true, norms, vec_in_ref, vec_all, wo_tmp, wu_tmp, wd_tmp,
    z_s, z_r, x_s, x_r, c_s, c_r, f_s, f_r, docs_s, docs_r, vec_s, vec_r, wh_s, wh_r, wh_l,
    y_s, y_r, n_s, n_r, o_s, o_r, load_sem, put_sem, self_sem, d_s, d_r, d_self, out_sem,
):
    z, x, y, c = (lax.axis_index(name) for name in AXES)
    odd, upper = lax.rem(z, 2), lax.div(z, 2)
    width = x_in_ref.shape[-1]
    chunks = rows.shape[1] // HEAD_CHUNK
    per_turn = chunks // 2
    by_core, by_x, by_y, by_yc = {"c": 1 - c}, {"x": 1 - x}, {"y": 1 - y}, {"y": 1 - y, "c": 1 - c}
    home = [{"z": 2 * c + upper, "c": odd}, {"z": 2 * c + 1 - upper, "c": odd}]
    target = [{"z": 2 * odd + c, "c": upper}, {"z": 2 * (1 - odd) + c, "c": upper}]
    block = [odd, 1 - odd]
    stay = (c == upper) & (odd == c)
    leave = jnp.logical_not(stay)
    for i, ref in enumerate((g1_ref, b1_ref, g2_ref, b2_ref, ob_ref, db_ref, ub_in_ref)):
        vec_in_ref[i : i + ref.shape[0]] = ref[...]
    greet([by_core, by_x, by_y, by_yc, home[1], target[1]], [home[0], target[0]], leave)

    def order_of(i):
        return i % 2 * per_turn + i // 2

    def piece(i):
        turn, row = order_of(i) // per_turn, (order_of(i) % per_turn) * HEAD_CHUNK
        return (
            x_in_ref.at[block[turn], 0, pl.ds(row, HEAD_CHUNK)],
            rows.at[0, pl.ds(order_of(i) * HEAD_CHUNK, HEAD_CHUNK)],
        )

    for turn in range(2):
        src, dst = docs_in_ref.at[block[turn]], docs.at[0, turn]

        def start_docs():
            send(src, dst, docs_s, docs_r, turn, target[turn])

        if turn == 0:
            pl.when(stay)(lambda: pltpu.make_async_copy(src, dst, self_sem.at[per_turn]).start())
            pl.when(leave)(start_docs)
        else:
            start_docs()
    for i in range(chunks):
        src, dst = piece(i)
        if i % 2 == 0:
            pl.when(stay)(lambda: pltpu.make_async_copy(src, dst, self_sem.at[i // 2]).start())
            pl.when(leave)(lambda: send(src, dst, z_s, z_r, i, target[0]) and None)
        else:
            send(src, dst, z_s, z_r, i, target[1])

    def piece_dy(i):
        part = pl.ds(i * HEAD_CHUNK, HEAD_CHUNK)
        return dy_in_ref.at[odd, 0, part], dy_ref.at[part]

    def send_dy(i):
        src, dst = piece_dy(i)
        pl.when(stay)(lambda: pltpu.make_async_copy(src, dst, d_self.at[i]).start())
        pl.when(leave)(lambda: send(src, dst, d_s, d_r, i, target[0]) and None)

    def land_dy(i):
        src, dst = piece_dy(i)
        pl.when(stay)(lambda: pltpu.make_async_copy(src, dst, d_self.at[i]).wait())
        pl.when(leave)(
            lambda: pltpu.make_async_remote_copy(
                src_ref=src, dst_ref=dst, send_sem=d_s.at[i], recv_sem=d_r.at[i],
                device_id=target[0], device_id_type=MESH,
            ).wait()
        )

    def landed(src, dst, sems, recv_sems, index, turn, self_index):
        def remote():
            pltpu.make_async_remote_copy(
                src_ref=src, dst_ref=dst, send_sem=sems.at[index], recv_sem=recv_sems.at[index],
                device_id=target[turn], device_id_type=MESH,
            ).wait()

        if turn == 0:
            pl.when(stay)(lambda: pltpu.make_async_copy(src, dst, self_sem.at[self_index]).wait())
            pl.when(leave)(remote)
        else:
            remote()

    mine = 2 * y + c
    vec_copy = [
        send(vec_in_ref, vec_all.at[mine], vec_s, vec_r, i, peer)
        for i, peer in enumerate((by_core, by_y, by_yc))
    ]
    vec_all[mine] = vec_in_ref[...]
    wh_copy = []
    shard = wq_ref.shape[0]
    own_rows = pl.ds(pl.multiple_of(mine * shard, shard), shard)
    for part in range(3):
        to = wh_ref.at[own_rows, pl.ds(part * PAIR, PAIR)]

        def columns(core):
            return wq_ref.at[:, pl.ds(pl.multiple_of(part * width + (2 * x + core) * PAIR, PAIR), PAIR)]

        for i, (peer, core) in enumerate(((by_core, 1 - c), (by_y, c), (by_yc, 1 - c))):
            wh_copy.append(send(columns(core), to, wh_s, wh_r, 3 * part + i, peer))
        copy = pltpu.make_async_copy(columns(c), to, wh_l.at[part])
        copy.start()
        wh_copy.append(copy)

    up_rows, down_rows = wu_ref.shape[0] // 4, wd_ref.shape[0] // 4
    parts = [(wo_ref, wo_all, wo_ref.shape[0], 0)]
    parts += [(wu_ref, wu_all, up_rows, i * up_rows) for i in range(4)]
    parts += [(wd_ref, wd_all, down_rows, i * down_rows) for i in range(4)]

    def at_owner(full, src, size, offset, owner):
        return full.at[pl.ds(pl.multiple_of(owner * src.shape[0] + offset, 32), size)]

    other = 2 * (1 - y) + c
    y_copy = []
    for i, (src, full, size, offset) in enumerate(parts):
        y_copy.append(
            send(src.at[pl.ds(offset, size)], at_owner(full, src, size, offset, mine), y_s, y_r, i, by_y)
        )
    n_copy, load_copy, put_copy = [], [], []
    for i, (src, full, tmp) in enumerate(((wo_ref, wo_all, wo_tmp), (wu_ref, wu_all, wu_tmp), (wd_ref, wd_all, wd_tmp))):
        n_copy.append(send(src, at_owner(full, src, src.shape[0], 0, mine), n_s, n_r, i, by_core))
        load_copy.append(pltpu.make_async_copy(src, tmp, load_sem.at[i]))
        load_copy[-1].start()

    def put(i):
        src, full, tmp = ((wo_ref, wo_all, wo_tmp), (wu_ref, wu_all, wu_tmp), (wd_ref, wd_all, wd_tmp))[i]
        load_copy[i].wait()
        put_copy.append(pltpu.make_async_copy(tmp, at_owner(full, src, src.shape[0], 0, mine), put_sem.at[i]))
        put_copy[-1].start()

    o_copy = []

    def forward(i):
        src, full, size, offset = parts[i]
        y_copy[i].wait()
        held = at_owner(full, src, size, offset, other)
        o_copy.append(send(held, held, o_s, o_r, i, by_core))

    blocks = order_ref.shape[0]
    lane = lax.broadcasted_iota(jnp.int32, (1, 128), 1)
    slots = jnp.zeros((1, 128), jnp.int32)
    for t in range(blocks):
        dc, dx, turn, half = t // 8, t // 4 % 2, t // 2 % 2, t % 2
        core, side = (1 - c if dc else c), (1 - x if dx else x)
        stored = 2 * (2 * (2 * core + (1 - upper if turn else upper)) + side) + half
        slots = jnp.where(lane == order_ref[stored], t, slots)

    docs_copy = {}

    def finish_docs():
        docs_copy["c"].wait()
        docs_copy["f"].wait()
        for g in range(4):
            core, side = (1 - c if g // 2 else c), (1 - x if g % 2 else x)
            for turn in range(2):
                docs_true[2 * (2 * core + (1 - upper if turn else upper)) + side] = docs[g, turn]
        numbers = docs_true[...]
        first = jnp.zeros_like(numbers)
        for d in range(1, blocks):
            before = jnp.sum((numbers < d).astype(jnp.int32), axis=(0, 1, 2), keepdims=True)
            first = jnp.where(numbers == d, before, first)
        docs_true[...] = first
        low = jnp.zeros((1, 128), jnp.int32)
        for b in range(blocks):
            line = docs_true[b // 2]
            at = 2 * (b % 2)
            line = jnp.concatenate([line[at : at + 1], line[at + 1 : at + 2]], axis=1)
            start_ref[b] = line
            low = jnp.where(lane == b, line[:, :1] // BLK, low)
        high = jnp.zeros((1, 128), jnp.int32) - 1
        for b in range(blocks):
            high = high + (low[:, b : b + 1] <= lane).astype(jnp.int32)
        tab_ref[...] = jnp.concatenate([low, high, slots, jnp.zeros((5, 128), jnp.int32)], axis=0)

    def docs_first():
        for turn in range(2):
            landed(docs_in_ref.at[block[turn]], docs.at[0, turn], docs_s, docs_r, turn, turn, per_turn)
        docs_copy["x"] = send(docs.at[0], docs.at[1], docs_s, docs_r, 2, by_x)
        docs_copy["c"] = send(docs.at[0], docs.at[2], docs_s, docs_r, 3, by_core)


    def vectors_and_weight():
        for copy in vec_copy:
            copy.wait()
        vec_width = vec_in_ref.shape[1]
        for j in range(4):
            for i in range(6):
                vec_ref[i : i + 1, j * vec_width : (j + 1) * vec_width] = vec_all[j, i : i + 1].astype(f32)
            for i in range(4):
                at = (4 * j + i) * vec_width
                ub_ref[:, at : at + vec_width] = vec_all[j, 6 + i : 7 + i].astype(f32)
        vec_ref[6:8] = jnp.zeros((2, width), f32)
        for copy in wh_copy:
            copy.wait()


    def docs_second():
        docs_copy["x"].wait()
        docs_copy["f"] = send(docs.at[1], docs.at[3], docs_s, docs_r, 4, by_core)


    x_copy, c_copy, f_copy = [], [], []

    def relay(i):
        src, dst = piece(i)
        landed(src, dst, z_s, z_r, i, i % 2, i // 2)
        part = pl.ds(order_of(i) * HEAD_CHUNK, HEAD_CHUNK)
        x_copy.append(send(rows.at[0, part], rows.at[1, part], x_s, x_r, i, by_x))
        c_copy.append(send(rows.at[0, part], rows.at[2, part], c_s, c_r, i, by_core))

    def relay_far(i):
        x_copy[i].wait()
        part = pl.ds(order_of(i) * HEAD_CHUNK, HEAD_CHUNK)
        f_copy.append(send(rows.at[1, part], rows.at[3, part], f_s, f_r, i, by_core))

    streams = (
        (qt_buf, qt_ref, 1), (k_buf, k_ref, 0), (kt_buf, kt_ref, 1), (v_buf, v_ref, 0), (vt_buf, vt_ref, 1),
        (ut_buf, ut_ref, 1),
    )

    def compute(g, i):
        count = rows.shape[1]
        chunk = order_of(i)
        unit, _ = norm_parts(rows[g, chunk * HEAD_CHUNK : (chunk + 1) * HEAD_CHUNK].astype(f32))
        at = pl.ds(g * count + chunk * HEAD_CHUNK, HEAD_CHUNK)
        ut_buf[:, at] = unit.astype(bf16).T
        low = (unit * vec_ref[0:1] + vec_ref[1:2]).astype(bf16)
        qkv = jnp.dot(low, wh_ref[...], preferred_element_type=f32)
        qt = (qkv[:, :PAIR] * (SCORE_SCALE * LOG2E)).astype(bf16).T
        qt_buf[:, at] = qt
        k = qkv[:, PAIR : 2 * PAIR].astype(bf16)
        v = qkv[:, 2 * PAIR :].astype(bf16)
        k_buf[at] = k
        v_buf[at] = v
        kt = k.T
        kt_buf[:, at] = kt
        vt_buf[:, at] = v.T
        found = []
        for block_ in (qt, kt):
            squares = block_.astype(f32) * block_.astype(f32)
            found += [jnp.sum(squares[head * HD : (head + 1) * HD], axis=0, keepdims=True) for head in range(2)]
        found = jnp.concatenate(found, axis=0)
        norms[...] = found if g == 0 and i == 0 else jnp.maximum(norms[...], found)
        for index, (source, out, columns) in enumerate(streams):
            if columns:
                source, out = source.at[:, at], out.at[:, at]
            else:
                source, out = source.at[at], out.at[at]
            pltpu.make_async_copy(source, out, out_sem.at[index]).start()

    docs_first()
    for i in range(chunks + 2):
        if i < chunks:
            if i < per_turn:
                send_dy(i)
            relay(i)
        if i == 0:
            vectors_and_weight()
            docs_second()
        if 1 <= i <= chunks:
            relay_far(i - 1)
            compute(0, i - 1)
            compute(1, i - 1)
            c_copy[i - 1].wait()
            compute(2, i - 1)
        if i >= 2:
            f_copy[i - 2].wait()
            compute(3, i - 2)
        if i == 1:
            finish_docs()
        if 2 <= i < 5:
            put(i - 2)
        if i >= 3 and i - 3 < len(parts):
            forward(i - 3)
        if i == chunks - 1:
            own_copy = pltpu.make_async_copy(rows.at[0], own_ref, out_sem.at[len(streams)])
            own_copy.start()
    largest = jnp.max(norms[...], axis=1, keepdims=True)
    bound = jnp.maximum(largest[0:1] * largest[2:3], largest[1:2] * largest[3:4])
    tab_ref[3:4] = jnp.broadcast_to((bound <= SAFE_SCORE * SAFE_SCORE).astype(jnp.int32), (1, 128))
    for i in range(chunks - 1, len(parts)):
        forward(i)
    for index, (source, out, _) in enumerate(streams):
        pltpu.make_async_copy(source, out, out_sem.at[index]).wait()
    own_copy.wait()
    for copy in n_copy + put_copy + o_copy:
        copy.wait()
    for i in range(per_turn):
        land_dy(i)


def head(x_in, dy_in, docs_in, order, vectors, w_qkv, w_out, w_up, w_down):
    width = x_in.shape[-1]
    count = 2 * x_in.shape[2]
    total = 4 * count
    shard = w_qkv.shape[0]
    chunks = count // HEAD_CHUNK
    blocks = order.shape[0]
    vmem, any_ = pl.BlockSpec(memory_space=pltpu.VMEM), pl.BlockSpec(memory_space=pl.ANY)
    smem = pl.BlockSpec(memory_space=pltpu.SMEM)
    dma, buf, shape = pltpu.SemaphoreType.DMA, pltpu.VMEM, jax.ShapeDtypeStruct
    return pl.pallas_call(
        head_kernel,
        in_specs=[any_, any_, vmem, smem] + [vmem] * 7 + [any_] * 4,
        out_specs=[any_] * 11 + [vmem] * 5,
        out_shape=[
            shape((PAIR, total), bf16),
            shape((total, PAIR), bf16),
            shape((PAIR, total), bf16),
            shape((total, PAIR), bf16),
            shape((PAIR, total), bf16),
            shape((width, total), bf16),
            shape((count, width), bf16),
            shape((4 * w_out.shape[0], w_out.shape[1]), bf16),
            shape((4 * w_up.shape[0], w_up.shape[1]), bf16),
            shape((4 * w_down.shape[0], w_down.shape[1]), bf16),
            shape((count // 2, width), bf16),
            shape((width, 3 * PAIR), bf16),
            shape((8, width), f32),
            shape((1, 4 * w_down.shape[0]), f32),
            shape((blocks, 1, BLK), jnp.int32),
            shape((8, 128), jnp.int32),
        ],
        scratch_shapes=[
            buf((PAIR, total), bf16),
            buf((total, PAIR), bf16),
            buf((PAIR, total), bf16),
            buf((total, PAIR), bf16),
            buf((PAIR, total), bf16),
            buf((width, total), bf16),
            buf((4, count, width), bf16),
            buf((4, 2) + docs_in.shape[1:], jnp.int32),
            buf((blocks // 2,) + docs_in.shape[1:], jnp.int32),
            buf((4, HEAD_CHUNK), f32),
            buf((16, shard), bf16),
            buf((4, 16, shard), bf16),
            buf(w_out.shape, bf16),
            buf(w_up.shape, bf16),
            buf(w_down.shape, bf16),
        ]
        + [dma((chunks,))] * 8
        + [dma((5,)), dma((5,)), dma((3,)), dma((3,)), dma((9,)), dma((9,)), dma((3,))]
        + [dma((9,)), dma((9,)), dma((3,)), dma((3,)), dma((9,)), dma((9,)), dma((3,)), dma((3,))]
        + [dma((chunks // 2 + 1,)), dma((chunks // 2,))] + [dma((chunks // 2,))] * 2 + [dma((7,))],
        compiler_params=pltpu.CompilerParams(
            collective_id=1, has_side_effects=True, vmem_limit_bytes=56 * 1024 * 1024
        ),
        name="head",
    )(x_in, dy_in, docs_in, order, *[v.reshape(-1, shard) for v in vectors], w_qkv, w_out, w_up, w_down)
FF_TILE = 1024
PIECES = 3
feed_steps = 4


def feed_kernel(
    o_ref, x_ref, dy_near_ref, dy_in_ref, wo_hbm, wu_hbm, wd_hbm, vec_ref, ub_ref,
    do_ref, y_home, y_far_ref, dmid_ref, keep_ref, to_y_ref, to_x_ref, to_xy_ref, gvec_ref, gub_ref,
    attn_all, gd_ref, gu_ref, go_ref, attn_in, do_out, y_out, grad_ref, grad_in,
    wo_ref, wu_ref, wd_ref, dy_ref, dy_far, w_sem, a_s, a_r, a_l, d_s, d_r, d_l, y_s, y_r, y_l, g_s, g_r, c_s, c_r,
):
    step = pl.program_id(0)
    steps = pl.num_programs(0)
    groups = attn_in.shape[0]
    tile = x_ref.shape[0]
    z, x, y, c = (lax.axis_index(name) for name in AXES)
    odd, upper = lax.rem(z, 2), lax.div(z, 2)
    mates = [None, {"x": 1 - x}, {"c": 1 - c}, {"x": 1 - x, "c": 1 - c}]
    pair_of = [2 * x + c, 2 * (1 - x) + c, 2 * x + 1 - c, 2 * (1 - x) + 1 - c]
    home = [{"z": 2 * c + upper, "c": odd}, {"z": 2 * c + 1 - upper, "c": odd}]
    origin = [{"z": 2 * odd + c, "c": upper}, {"z": 2 * (1 - odd) + c, "c": upper}]
    stay = (c == upper) & (odd == c)
    leave = jnp.logical_not(stay)
    half = feed_steps // 2

    def attn_copy(g, i):
        part = pl.ds(i * tile, tile)
        return pltpu.make_async_remote_copy(
            src_ref=o_ref.at[g, part], dst_ref=attn_in.at[g, part],
            send_sem=a_s.at[g - 1, i], recv_sem=a_r.at[g - 1, i], device_id=mates[g], device_id_type=MESH,
        )

    def attn_own(i):
        part = pl.ds(i * tile, tile)
        return pltpu.make_async_copy(o_ref.at[0, part], attn_in.at[0, part], a_l.at[i])

    def do_copy(g, i):
        return pltpu.make_async_remote_copy(
            src_ref=do_out.at[i, g], dst_ref=do_ref.at[g, pl.ds(i * tile, tile)],
            send_sem=d_s.at[g - 1, i], recv_sem=d_r.at[g - 1, i], device_id=mates[g], device_id_type=MESH,
        )

    def do_own(i):
        return pltpu.make_async_copy(do_out.at[i, 0], do_ref.at[0, pl.ds(i * tile, tile)], d_l.at[i])

    def y_rows(i):
        return y_home.at[pl.ds(i * tile, tile)]

    def y_copy(i):
        return pltpu.make_async_remote_copy(
            src_ref=y_out.at[i], dst_ref=y_rows(i),
            send_sem=y_s.at[i], recv_sem=y_r.at[i], device_id=home[0], device_id_type=MESH,
        )

    def y_own(i):
        return pltpu.make_async_copy(y_out.at[i], y_rows(i), y_l.at[i])

    def grad_copy(i):
        return pltpu.make_async_remote_copy(
            src_ref=grad_ref.at[2 * i + 1 - c], dst_ref=grad_in.at[i],
            send_sem=g_s.at[i], recv_sem=g_r.at[i], device_id=mates[2], device_id_type=MESH,
        )

    def dy_copy(i):
        part = pl.ds(i * tile, tile)
        return pltpu.make_async_remote_copy(
            src_ref=dy_in_ref.at[1 - odd, 0, part], dst_ref=dy_far.at[part],
            send_sem=c_s.at[i], recv_sem=c_r.at[i], device_id=origin[1], device_id_type=MESH,
        )

    w_loads = [
        pltpu.make_async_copy(src, dst, w_sem.at[i])
        for i, (src, dst) in enumerate(((wo_hbm, wo_ref), (wu_hbm, wu_ref), (wd_hbm, wd_ref)))
    ]

    @pl.when(step == 0)
    def _():
        for copy in w_loads:
            copy.start()
        greet(mates[1:] + [home[1], origin[1]], [home[0], origin[0]], leave)
        for i in range(feed_steps):
            for g in (1, 3, 2):
                attn_copy(g, i).start()
            attn_own(i).start()
        for i in range(half):
            dy_copy(i).start()

    @pl.when(step == 0)
    def _():
        for ref in (gd_ref, gu_ref, go_ref, gvec_ref, gub_ref):
            ref[...] = jnp.zeros_like(ref)

    @pl.when(step < half)
    def _():
        dy_ref[...] = dy_near_ref[...]

    @pl.when(step >= half)
    def _():
        dy_copy(step - half).wait()
        dy_ref[...] = dy_far[pl.ds(pl.multiple_of((step - half) * tile, tile), tile)]

    @pl.when(step == 0)
    def _():
        for copy in w_loads:
            copy.wait()

    attn_own(step).wait()
    for g in range(1, groups):
        attn_copy(g, step).wait()
    for g in range(groups):
        attn_all[:, pl.ds(pl.multiple_of(pair_of[g] * PAIR, PAIR), PAIR)] = attn_in[
            g, pl.ds(pl.multiple_of(step * tile, tile), tile)
        ]
    attn = attn_all[...]
    gain, bias, out_bias, down_bias = (vec_ref[i : i + 1, :] for i in range(2, 6))
    middle = (
        x_ref[...].astype(f32) + jnp.dot(attn, wo_ref[...], preferred_element_type=f32) + out_bias
    )
    unit, inv = norm_parts(middle)
    low = (unit * gain + bias).astype(bf16)
    dy = dy_ref[...]
    dy32 = dy.astype(f32)
    total = middle + down_bias
    d_low = jnp.zeros_like(middle)
    width = wu_ref.shape[1]
    for j in range(0, width, FF_TILE):
        part = pl.ds(j, FF_TILE)
        up = wu_ref[:, part]
        down = wd_ref[part, :]
        hidden = jnp.dot(low, up, preferred_element_type=f32) + ub_ref[:, part]
        cdf = 0.5 * (1.0 + lax.erf(hidden * (1.0 / math.sqrt(2.0))))
        active = (hidden * cdf).astype(bf16)
        slope = cdf + hidden * (jnp.exp2(hidden * hidden * (-0.5 * LOG2E)) * (1.0 / math.sqrt(2.0 * math.pi)))
        total = total + jnp.dot(active, down, preferred_element_type=f32)
        d_hidden = contract(dy, down, 1, 1) * slope
        d_hidden_low = d_hidden.astype(bf16)
        gub_ref[:, part] += jnp.sum(d_hidden, axis=0, keepdims=True)
        d_low = d_low + contract(d_hidden_low, up, 1, 1)
        gd_ref[part, :] += contract(active, dy, 0, 0)
        gu_ref[:, part] += contract(low, d_hidden_low, 0, 0)
    @pl.when(step < half)
    def _():
        y_out[step] = total.astype(bf16)

        @pl.when(stay)
        def _():
            y_own(step).start()

        @pl.when(leave)
        def _():
            y_copy(step).start()

    @pl.when(step >= half)
    def _():
        y_far_ref[...] = total.astype(bf16)

    scaled = d_low * gain
    d_middle = dy32 + inv * (
        scaled
        - jnp.mean(scaled, axis=-1, keepdims=True)
        - unit * jnp.mean(scaled * unit, axis=-1, keepdims=True)
    )
    dmid_ref[...] = d_middle
    branch = d_middle.astype(bf16)
    go_ref[...] += contract(attn, branch, 0, 0)
    gvec_ref[0:1, :] += jnp.sum(d_middle, axis=0, keepdims=True)
    gvec_ref[1:2, :] += jnp.sum(d_low * unit, axis=0, keepdims=True)
    gvec_ref[2:3, :] += jnp.sum(d_low, axis=0, keepdims=True)
    gvec_ref[3:4, :] += jnp.sum(dy32, axis=0, keepdims=True)
    attn_all[...] = contract(branch, wo_ref[...], 1, 1).astype(bf16)
    for g in (1, 3, 2, 0):
        do_out[step, g] = attn_all[:, pl.ds(pl.multiple_of(pair_of[g] * PAIR, PAIR), PAIR)]
        if g:
            do_copy(g, step).start()
        else:
            do_own(step).start()

    @pl.when(step == steps - 1)
    def _():
        shards = grad_ref.shape[0]
        d_model = x_ref.shape[1]
        down_rows, up_rows = gd_ref.shape[0] // shards, d_model // shards
        for j in range(shards):
            grad_ref[j, :down_rows] = gd_ref[j * down_rows : (j + 1) * down_rows].astype(bf16)
            rows = slice(j * up_rows, (j + 1) * up_rows)
            at = down_rows
            for t in range(0, width, d_model):
                grad_ref[j, at : at + up_rows] = gu_ref[rows, t : t + d_model].astype(bf16)
                at += up_rows
            grad_ref[j, at : at + up_rows] = go_ref[rows].astype(bf16)
        for j in range(2):
            grad_copy(j).start()
        for j in range(feed_steps):
            do_own(j).wait()
            for g in range(1, groups):
                do_copy(g, j).wait()
            if j < half:
                @pl.when(stay)
                def _():
                    y_own(j).wait()

                @pl.when(leave)
                def _():
                    y_copy(j).wait()
        sixth = keep_ref.shape[1]
        for j in range(2):
            grad_copy(j).wait()
        for dy_, dx_, ref in ((0, 0, keep_ref), (1, 0, to_y_ref), (0, 1, to_x_ref), (1, 1, to_xy_ref)):
            row = 1 - y if dy_ else y
            side = 1 - x if dx_ else x
            for p in range(PIECES):
                part = pl.ds(pl.multiple_of((2 * p + side) * sixth, 16), sixth)
                ref[p] = (
                    grad_ref[2 * row + c, part].astype(f32) + grad_in[row, part].astype(f32)
                ).astype(bf16)


def feed(o, x, dy_near, dy_in, w_out, w_up, w_down, vecs, up_bias, shards):
    groups, count, _ = o.shape
    width = x.shape[1]
    flat = (w_out.size + w_up.size + w_down.size) // shards // width
    tile = count // feed_steps
    piece = (PIECES, flat // PIECES // 2, width)
    rows = pl.BlockSpec((tile, width), lambda i: (i, 0))
    any_ = pl.BlockSpec(memory_space=pl.ANY)
    dma, buf, shape = pltpu.SemaphoreType.DMA, pltpu.VMEM, jax.ShapeDtypeStruct
    return pl.pallas_call(
        feed_kernel,
        grid=(feed_steps,),
        in_specs=[
            any_, rows, pl.BlockSpec((tile, width), lambda i: (jnp.minimum(i, feed_steps // 2 - 1), 0)), any_, any_, any_, any_,
            whole(vecs.shape), whole(up_bias.shape),
        ],
        out_specs=[any_, any_, pl.BlockSpec((tile, width), lambda i: (jnp.maximum(i - feed_steps // 2, 0), 0)), rows]
        + [whole(piece)] * 4 + [whole(vecs.shape), whole(up_bias.shape)],
        out_shape=[
            shape((groups, count, PAIR), bf16),
            shape((count // 2, width), bf16),
            shape((count // 2, width), bf16),
            shape((count, width), f32),
            shape(piece, bf16),
            shape(piece, bf16),
            shape(piece, bf16),
            shape(piece, bf16),
            shape(vecs.shape, f32),
            shape(up_bias.shape, f32),
        ],
        scratch_shapes=[
            buf((tile, width), bf16),
            buf(w_down.shape, f32),
            buf(w_up.shape, f32),
            buf(w_out.shape, f32),
            buf((groups, count, PAIR), bf16),
            buf((feed_steps, groups, tile, PAIR), bf16),
            buf((feed_steps // 2, tile, width), bf16),
            buf((shards, flat, width), bf16),
            buf((2, flat, width), bf16),
            buf(w_out.shape, bf16),
            buf(w_up.shape, bf16),
            buf(w_down.shape, bf16),
            buf((tile, width), bf16),
            buf((count // 2, width), bf16),
            dma((3,)),
            dma((3, feed_steps)),
            dma((3, feed_steps)),
            dma((feed_steps,)),
            dma((3, feed_steps)),
            dma((3, feed_steps)),
            dma((feed_steps,)),
            dma((feed_steps // 2,)),
            dma((feed_steps // 2,)),
            dma((feed_steps // 2,)),
            dma((2,)),
            dma((2,)),
            dma((feed_steps // 2,)),
            dma((feed_steps // 2,)),
        ],
        compiler_params=pltpu.CompilerParams(
            collective_id=3, has_side_effects=True, vmem_limit_bytes=60 * 1024 * 1024
        ),
        name="feed",
    )(o, x, dy_near, dy_in, w_out, w_up, w_down, vecs, up_bias)


TAIL_CHUNK = 128


def tail_kernel(
    d_qkv_hbm, ut_hbm, x_hbm, dmid_hbm, keep_hbm, from_y_hbm, from_x_hbm, from_xy_hbm, w_ref, vec_ref,
    gvecs_ref, gub_ref,
    home_buf, gfull, wall, sum_ref,
    keep_ref, from_y_ref, from_x_ref, from_xy_ref, d_qkv, ut_ref, total, sums, gw_ref, core_out, x_ref, dmid_ref, core_buf, own_dh, x_out, x_buf, dx_out,
    gsum, gz1s, gz1r, gz2s, gz2r,
    wy, ws, wz1s, wz1r, wz2s, wz2r, wfull,
    small_ref, small_out, small_in,
    load_sem, self_sem, core_s, core_r, x_s, x_r, home_s, home_r, g_s, g_r, w_s, w_r, s_s, s_r, in_sem,
):
    z, x, y, c = (lax.axis_index(name) for name in AXES)
    odd, upper = lax.rem(z, 2), lax.div(z, 2)
    width = x_ref.shape[1]
    chunks = x_ref.shape[0] // TAIL_CHUNK
    per_turn = chunks // 2
    by_core, by_x, by_y, by_xc = {"c": 1 - c}, {"x": 1 - x}, {"y": 1 - y}, {"x": 1 - x, "c": 1 - c}
    by_z1, by_z2 = {"z": z + 1 - 2 * odd}, {"z": z + 2 - 4 * upper}
    home = [{"z": 2 * c + upper, "c": odd}, {"z": 2 * c + 1 - upper, "c": odd}]
    origin = [{"z": 2 * odd + c, "c": upper}, {"z": 2 * (1 - odd) + c, "c": upper}]
    stay = (c == upper) & (odd == c)
    loads = []
    for i in range(chunks):
        part = pl.ds(i * TAIL_CHUNK, TAIL_CHUNK)
        loads.append(pltpu.make_async_copy(d_qkv_hbm.at[:, part], d_qkv.at[:, part], load_sem.at[i]))
    inputs = [
        pltpu.make_async_copy(src, dst, in_sem.at[i])
        for i, (src, dst) in enumerate(((ut_hbm, ut_ref), (x_hbm, x_ref), (dmid_hbm, dmid_ref)))
    ]
    g_loads = [
        pltpu.make_async_copy(src, dst, in_sem.at[3 + i])
        for i, (src, dst) in enumerate((
            (keep_hbm, keep_ref), (from_y_hbm, from_y_ref), (from_x_hbm, from_x_ref), (from_xy_hbm, from_xy_ref)
        ))
    ]
    for copy in loads[:2] + g_loads + loads[2:] + inputs:
        copy.start()
    small_ref[...] = jnp.zeros_like(small_ref)
    small_ref[2:4] = gvecs_ref[1:3]
    small_ref[4:5] = gvecs_ref[0:1]
    small_ref[5:6] = gvecs_ref[3:4]
    for i in range(4):
        small_ref[6 + i : 7 + i] = gub_ref[:, i * width : (i + 1) * width]
    greet(
        [by_core, by_x, by_y, by_xc, by_z1, by_z2, home[1], origin[1]],
        [home[0], origin[0]],
        jnp.logical_not(stay),
    )
    small_peers = [by_core, by_y, by_z1, by_z2, by_x]
    to_core, w_copy, s_copy = [], {}, []

    def share(i):
        part = pl.ds(i * TAIL_CHUNK, TAIL_CHUNK)
        loads[i].wait()
        for g in (3, 2, 1, 0):
            value = contract(d_qkv[g, part], w_ref[...], 1, 1)
            if g >= 2:
                core_out[g - 2, part] = value.astype(bf16)
            else:
                own_dh[g, part] = value
            if g == 2:
                to_core.append(
                    send(core_out.at[:, part], core_buf.at[:, part], core_s, core_r, i, by_core)
                )

    def weight(g):
        if g == 0:
            inputs[0].wait()
        rows = d_qkv[g]
        part = jnp.dot(ut_ref[:, g * rows.shape[0] : (g + 1) * rows.shape[0]], rows, preferred_element_type=f32)
        line = jnp.sum(rows.astype(f32), axis=0, keepdims=True)
        total[...] = part if g == 0 else total[...] + part
        sums[...] = line if g == 0 else sums[...] + line

    def weight_close():
        shard = gw_ref.shape[1]
        for j in range(gw_ref.shape[0]):
            part = pl.ds(j * shard, shard)
            gain, bias = (jnp.broadcast_to(ref[:, part], (shard, shard)).T[:, :1] for ref in (vec_ref.at[0:1], vec_ref.at[1:2]))
            gw_ref[j] = (total[part] * gain + bias * sums[...]).astype(bf16)
            w = w_ref[part].astype(f32)
            for i, term in enumerate((w * total[part], w * sums[...])):
                column = jnp.sum(term, axis=1, keepdims=True)
                small_ref[i : i + 1, part] = jnp.broadcast_to(column, (shard, shard)).T[:1]
        s_copy.append(send(small_ref, small_in.at[0], s_s, s_r, 0, small_peers[0]))
        w_copy["y"] = send(gw_ref.at[pl.ds(2 * (1 - y), 2)], wy, w_s, w_r, 0, by_y)

    g_copy = {}

    def g_start(p):
        if p == 0:
            for copy in g_loads:
                copy.wait()
        for half in range(2):
            part = pl.ds(96 * half, 96)
            gsum[p, part] = (
                keep_ref[p, part].astype(f32)
                + from_y_ref[p, part].astype(f32)
                + from_x_ref[p, part].astype(f32)
                + from_xy_ref[p, part].astype(f32)
            )
        gz1s[p] = gsum[p, pl.ds(pl.multiple_of(96 * (1 - odd), 16), 96)].astype(bf16)
        g_copy["z1", p] = send(gz1s.at[p], gz1r.at[p], g_s, g_r, 5 * p, by_z1)

    mine_half = pl.multiple_of(96 * odd, 16)
    mine_quarter = pl.multiple_of(96 * odd + 48 * upper, 16)
    give_quarter = pl.multiple_of(96 * odd + 48 * (1 - upper), 16)

    def g_second(p):
        g_copy["z1", p].wait()
        gsum[p, pl.ds(mine_half, 96)] += gz1r[p].astype(f32)
        gz2s[p] = gsum[p, pl.ds(give_quarter, 48)].astype(bf16)
        g_copy["z2", p] = send(gz2s.at[p], gz2r.at[p], g_s, g_r, 5 * p + 1, by_z2)

    def g_third(p):
        g_copy["z2", p].wait()
        part = pl.ds(mine_quarter, 48)
        gfull[p, x, part] = (gsum[p, part] + gz2r[p].astype(f32)).astype(bf16)
        place_ = gfull.at[p, x, part]
        g_copy["z2b", p] = send(place_, place_, g_s, g_r, 5 * p + 2, by_z2)

    def g_fourth(p):
        g_copy["z2b", p].wait()
        place_ = gfull.at[p, x, pl.ds(mine_half, 96)]
        g_copy["z1b", p] = send(place_, place_, g_s, g_r, 5 * p + 3, by_z1)

    def g_fifth(p):
        g_copy["z1b", p].wait()
        g_copy["x", p] = send(gfull.at[p, x], gfull.at[p, x], g_s, g_r, 5 * p + 4, by_x)

    def w_second():
        w_copy["y"].wait()
        for i in range(2):
            ws[i] = gw_ref[2 * y + i].astype(f32) + wy[i].astype(f32)
        wz1s[...] = ws[1 - odd].astype(bf16)
        w_copy["z1"] = send(wz1s, wz1r, w_s, w_r, 1, by_z1)

    def w_third():
        w_copy["z1"].wait()
        ws[odd] += wz1r[...].astype(f32)
        wz2s[...] = ws[odd, pl.ds(pl.multiple_of(64 * (1 - upper), 64), 64)].astype(bf16)
        w_copy["z2"] = send(wz2s, wz2r, w_s, w_r, 2, by_z2)

    def w_fourth():
        w_copy["z2"].wait()
        part = pl.ds(pl.multiple_of(64 * upper, 64), 64)
        wfull[odd, part] = (ws[odd, part] + wz2r[...].astype(f32)).astype(bf16)
        place_ = wfull.at[odd, part]
        w_copy["z2b"] = send(place_, place_, w_s, w_r, 3, by_z2)

    def w_fifth():
        w_copy["z2b"].wait()
        w_copy["z1b"] = send(wfull.at[odd], wfull.at[odd], w_s, w_r, 4, by_z1)

    def w_sixth():
        w_copy["z1b"].wait()
        mine = 2 * x + c
        w_copy["core"] = send(wfull.at[1 - c], wall.at[mine], w_s, w_r, 5, by_core)
        w_copy["x"] = send(wfull.at[c], wall.at[mine], w_s, w_r, 6, by_x)
        w_copy["xc"] = send(wfull.at[1 - c], wall.at[mine], w_s, w_r, 7, by_xc)

    def s_next(step):
        s_copy[step].wait()
        before = small_ref[...] if step == 0 else small_out[step - 1]
        small_out[step] = before + small_in[step]
        if step + 1 < len(small_peers):
            s_copy.append(
                send(small_out.at[step], small_in.at[step + 1], s_s, s_r, step + 1, small_peers[step + 1])
            )

    x_copy, home_copy = [], []

    def add_core(i):
        part = pl.ds(i * TAIL_CHUNK, TAIL_CHUNK)
        to_core[i].wait()
        x_out[part] = (own_dh[1, part] + core_buf[1, part].astype(f32)).astype(bf16)
        x_copy.append(send(x_out.at[part], x_buf.at[part], x_s, x_r, i, by_x))

    def finish(i):
        part = pl.ds(i * TAIL_CHUNK, TAIL_CHUNK)
        if i == 0:
            for copy in inputs[1:]:
                copy.wait()
        x_copy[i].wait()
        d_low = own_dh[0, part] + core_buf[0, part].astype(f32) + x_buf[part].astype(f32)
        unit, inv = norm_parts(x_ref[part].astype(f32))
        scaled = d_low * vec_ref[0:1]
        dx = dmid_ref[part] + inv * (
            scaled
            - jnp.mean(scaled, axis=-1, keepdims=True)
            - unit * jnp.mean(scaled * unit, axis=-1, keepdims=True)
        )
        dx_out[part] = dx.astype(bf16)
        turn, row = i // per_turn, (i % per_turn) * TAIL_CHUNK
        target = home_buf.at[upper, pl.ds(row, TAIL_CHUNK)]
        if turn == 0:
            @pl.when(stay)
            def _():
                pltpu.make_async_copy(dx_out.at[part], target, self_sem.at[i]).start()

            @pl.when(jnp.logical_not(stay))
            def _():
                send(dx_out.at[part], target, home_s, home_r, i, home[0])
        else:
            send(dx_out.at[part], target, home_s, home_r, i, home[1])

    def arrive(i):
        part = pl.ds(i * TAIL_CHUNK, TAIL_CHUNK)
        turn, row = i // per_turn, (i % per_turn) * TAIL_CHUNK
        block = odd if turn == 0 else 1 - odd
        landed = home_buf.at[block, pl.ds(row, TAIL_CHUNK)]

        def remote():
            copy = pltpu.make_async_remote_copy(
                src_ref=dx_out.at[part], dst_ref=landed, send_sem=home_s.at[i], recv_sem=home_r.at[i],
                device_id=home[turn], device_id_type=MESH,
            )
            copy.wait_send()
            copy.wait_recv()

        if turn == 0:
            @pl.when(stay)
            def _():
                pltpu.make_async_copy(dx_out.at[part], landed, self_sem.at[i]).wait()

            pl.when(jnp.logical_not(stay))(remote)
        else:
            remote()

    share(0)
    share(1)
    add_core(0)
    share(2)
    g_start(0)
    add_core(1)
    share(3)
    g_start(1)
    add_core(2)
    share(4)
    g_start(2)
    add_core(3)
    share(5)
    share(6)
    add_core(4)
    share(7)
    weight(0)
    finish(0)
    weight(1)
    g_second(0)
    g_second(1)
    g_second(2)
    weight(2)
    finish(1)
    add_core(5)
    weight(3)
    weight_close()
    add_core(6)
    s_next(0)
    w_second()
    g_third(0)
    g_third(1)
    g_third(2)
    finish(2)
    add_core(7)
    s_next(1)
    w_third()
    g_fourth(0)
    g_fourth(1)
    g_fourth(2)
    finish(3)
    s_next(2)
    w_fourth()
    g_fifth(0)
    g_fifth(1)
    g_fifth(2)
    finish(4)
    w_fifth()
    s_next(3)
    w_sixth()
    finish(5)
    s_next(4)
    finish(6)
    finish(7)
    w_copy["core"].wait()
    w_copy["x"].wait()
    w_copy["xc"].wait()
    wall[2 * x + c] = wfull[c]
    sum_ref[...] = small_out[4]
    for i in range(chunks):
        arrive(i)
    for p in range(PIECES):
        g_copy["x", p].wait()


def tail(d_qkv, unit_t, x, dmid, keep, from_y, from_x, from_xy, weight, vecs, gvecs, gub):
    count, width = x.shape
    shard = width // 4
    half = count // 2
    chunks = count // TAIL_CHUNK
    sixth = keep.shape[1]
    vmem = pl.BlockSpec(memory_space=pltpu.VMEM)
    dma = pltpu.SemaphoreType.DMA
    buf = pltpu.VMEM
    return pl.pallas_call(
        tail_kernel,
        in_specs=[pl.BlockSpec(memory_space=pl.ANY)] * 8 + [vmem] * 4,
        out_specs=[vmem] * 4,
        out_shape=[
            jax.ShapeDtypeStruct((2, half, width), bf16),
            jax.ShapeDtypeStruct((PIECES, 2, sixth, width), bf16),
            jax.ShapeDtypeStruct((4, shard, 3 * PAIR), bf16),
            jax.ShapeDtypeStruct((16, width), f32),
        ],
        scratch_shapes=[
            buf(keep.shape, bf16),
            buf(keep.shape, bf16),
            buf(keep.shape, bf16),
            buf(keep.shape, bf16),
            buf(d_qkv.shape, bf16),
            buf(unit_t.shape, bf16),
            buf(weight.shape, f32),
            buf((1, 3 * PAIR), f32),
            buf((4, shard, 3 * PAIR), bf16),
            buf((2, count, width), bf16),
            buf((count, width), bf16),
            buf((count, width), f32),
            buf((2, count, width), bf16),
            buf((2, count, width), f32),
            buf((count, width), bf16),
            buf((count, width), bf16),
            buf((count, width), bf16),
            buf((PIECES, sixth, width), f32),
            buf((PIECES, sixth // 2, width), bf16),
            buf((PIECES, sixth // 2, width), bf16),
            buf((PIECES, sixth // 4, width), bf16),
            buf((PIECES, sixth // 4, width), bf16),
            buf((2, shard, 3 * PAIR), bf16),
            buf((2, shard, 3 * PAIR), f32),
            buf((shard, 3 * PAIR), bf16),
            buf((shard, 3 * PAIR), bf16),
            buf((shard // 2, 3 * PAIR), bf16),
            buf((shard // 2, 3 * PAIR), bf16),
            buf((2, shard, 3 * PAIR), bf16),
            buf((16, width), f32),
            buf((5, 16, width), f32),
            buf((5, 16, width), f32),
            dma((chunks,)),
            dma((chunks // 2,)),
            dma((chunks,)),
            dma((chunks,)),
            dma((chunks,)),
            dma((chunks,)),
            dma((chunks,)),
            dma((chunks,)),
            dma((5 * PIECES,)),
            dma((5 * PIECES,)),
            dma((8,)),
            dma((8,)),
            dma((5,)),
            dma((5,)),
            dma((7,)),
        ],
        compiler_params=pltpu.CompilerParams(
            collective_id=5, has_side_effects=True, vmem_limit_bytes=60 * 1024 * 1024
        ),
        name="tail",
    )(d_qkv, unit_t, x, dmid, keep, from_y, from_x, from_xy, weight, vecs, gvecs, gub)

def results_kernel(
    y_near_ref, y_far_ref, dx_ref, down_ref, up_ref, out_ref, wall_ref, sum_ref,
    y_out, dx_out, gd_ref, gu_ref, go_ref, gq_ref, *vectors,
):
    step = pl.program_id(0)
    width = dx_ref.shape[-1]
    odd = lax.rem(lax.axis_index("z"), 2)
    y_out[odd, 0] = y_near_ref[...]
    y_out[1 - odd, 0] = y_far_ref[...]
    dx_out[:, 0] = dx_ref[...].astype(f32)
    gd_ref[...] = down_ref[...].astype(f32)
    gu_ref[...] = up_ref[...].astype(f32)
    go_ref[...] = out_ref[...].astype(f32)
    for part in range(3):
        at = pl.multiple_of(part * width + step * PAIR, PAIR)
        gq_ref[:, pl.ds(at, PAIR)] = wall_ref[0, :, part * PAIR : (part + 1) * PAIR].astype(f32)
    shard = go_ref.shape[0]
    mine = 2 * lax.axis_index("y") + lax.axis_index("c")
    for i in range(6):
        vectors[i][...] = sum_ref[i : i + 1, pl.ds(pl.multiple_of(mine * shard, shard), shard)]
    vectors[6][...] = sum_ref[pl.ds(6 + mine, 1), :]


def results(y_near, y_far, dx, flat, wall, sums):
    half, width = dx.shape[1:]
    shard = wall.shape[1]
    steps = 4
    flat = flat.reshape(-1, width)
    tokens = pl.BlockSpec((2, half // steps, width), lambda i: (0, i, 0))
    tokens_out = pl.BlockSpec((2, 1, half // steps, width), lambda i: (0, 0, i, 0))
    shape = jax.ShapeDtypeStruct
    return pl.pallas_call(
        results_kernel,
        grid=(steps,),
        in_specs=[
            pl.BlockSpec((half // steps, width), lambda i: (i, 0)),
            pl.BlockSpec((half // steps, width), lambda i: (i, 0)),
            tokens,
            pl.BlockSpec((shard, width), lambda i: (i, 0)),
            pl.BlockSpec((shard, width), lambda i: (steps + i, 0)),
            pl.BlockSpec((shard, width), lambda i: (2 * steps, 0)),
            pl.BlockSpec((1, shard, 3 * PAIR), lambda i: (i, 0, 0)),
            whole(sums.shape),
        ],
        out_specs=[
            tokens_out,
            tokens_out,
            pl.BlockSpec((shard, width), lambda i: (i, 0)),
            pl.BlockSpec((shard, width), lambda i: (0, i)),
            whole((shard, width)),
            whole((shard, 3 * width)),
        ]
        + [whole((1, shard))] * 6
        + [whole((1, width))],
        out_shape=[
            shape((2, 1, half, width), bf16),
            shape((2, 1, half, width), f32),
            shape((width, width), f32),
            shape((shard, 4 * width), f32),
            shape((shard, width), f32),
            shape((shard, 3 * width), f32),
        ]
        + [shape((1, shard), f32)] * 6
        + [shape((1, width), f32)],
        compiler_params=pltpu.CompilerParams(vmem_limit_bytes=60 * 1024 * 1024),
        name="results",
    )(y_near, y_far, dx, flat, flat, flat, wall, sums)


def place(z, x, y, c):
    return ((z * SIZES[1] + x) * SIZES[2] + y) * SIZES[3] + c


def everyone():
    return [
        (z, x, y, c)
        for z in range(SIZES[0])
        for x in range(SIZES[1])
        for y in range(SIZES[2])
        for c in range(SIZES[3])
    ]


def swap_pairs(dx, dy, dc):
    return [(place(z, x, y, c), place(z, x ^ dx, y ^ dy, c ^ dc)) for z, x, y, c in everyone()]


def move(value, pairs):
    return lax.ppermute(value, AXES, pairs)


def swap(value, dx=0, dy=0, dc=0):
    return move(value, swap_pairs(dx, dy, dc))


def paired_body(
    inputs, out_grad, segment_ids, block_order, w_qkv, w_out, w_up, w_down,
    norm1_gain, norm1_bias, norm2_gain, norm2_bias, out_bias, up_bias, down_bias,
):
    vectors = (norm1_gain, norm1_bias, norm2_gain, norm2_bias, out_bias, down_bias, up_bias)
    (
        qt, k, kt, v, vt, unit, own_x, full_out, full_up, full_down, near_dy, w_heads, vecs, full_ubias, start, tab
    ) = head(
        inputs, out_grad, segment_ids.reshape(2, -1, 128), block_order, vectors, w_qkv, w_out, w_up, w_down
    )
    o, ot, lse = attend(tab, qt, start, k, vt)
    d_o, y_near, y_far, d_middle, keep, to_y, to_x, to_xy, g_vecs, g_ubias = feed(
        o.reshape(4, -1, PAIR), own_x, near_dy, out_grad, full_out, full_up, full_down, vecs, full_ubias, 4
    )
    y_far = move(y_far, [(place(z, x, y, c), place(2 * c + 1 - z // 2, x, y, z % 2)) for z, x, y, c in everyone()])
    from_y, from_x, from_xy = swap(to_y, dy=1), swap(to_x, dx=1), swap(to_xy, dy=1, dx=1)
    d_qkv = attend_back(tab, k, kt, v, qt, start, d_o.reshape(-1, PAIR), ot, lse)
    dx, flat, heads, sums = tail(
        d_qkv.reshape(4, -1, 3 * PAIR), unit, own_x, d_middle, keep, from_y, from_x, from_xy,
        w_heads, vecs, g_vecs, g_ubias,
    )
    outputs, input_grad, grad_down, grad_up, grad_out, grad_qkv, *vec = results(
        y_near, y_far, dx, flat, heads, sums
    )
    vec = [member.reshape(-1) for member in vec]
    return (
        outputs, input_grad, grad_qkv, grad_out, grad_up, grad_down,
        vec[0], vec[1], vec[2], vec[3], vec[4], vec[6], vec[5],
    )


def solution(mesh):
    paired = mesh.shape["ctx"] == SIZES[0] * SIZES[1] and mesh.shape["fsdp"] == SIZES[2] * SIZES[3]
    if paired:
        mesh = Mesh(mesh.devices.reshape(SIZES), AXES)
        ctx, fsdp, program = ("z", "x"), ("y", "c"), paired_body
    else:
        ctx, fsdp, program = "ctx", "fsdp", general_body
    tokens = P(None, fsdp, ctx, None)
    matrix, vector = P(fsdp, None), P(fsdp)
    return jax.shard_map(
        program,
        mesh=mesh,
        in_specs=(tokens, tokens, P(None, fsdp, ctx), P()) + (matrix,) * 4 + (vector,) * 7,
        out_specs=(tokens, tokens) + (matrix,) * 4 + (vector,) * 7,
        check_vma=False,
    )
```
